32 devices in a mesh: dp: 32 (over z, y, x, core).
Axes of the slice: x: 2, y: 2, z: 4, core: 2. Of those that a mesh axis runs over, the one named last changes fastest.
Arguments:
- tokens: bfloat16 [4096, 2048], P('dp'), may hold values from -6 to 6
- cotangent: bfloat16 [4096, 2048], P('dp'), may hold values from -6 to 6
- lengths: int32 [32], replicated, may hold values from 1 to 160, 4096 in all
- wq: bfloat16 [2048, 2048], P('dp'), may hold values from -0.125 to 0.125
- bq: bfloat16 [2048], P('dp'), may hold values from -3 to 3
- wk: bfloat16 [2048, 2048], P('dp'), may hold values from -0.125 to 0.125
- wv: bfloat16 [2048, 2048], P('dp'), may hold values from -0.125 to 0.125
- bv: bfloat16 [2048], P('dp'), may hold values from -3 to 3
- wo: bfloat16 [2048, 2048], P('dp'), may hold values from -0.5 to 0.5
- bo: bfloat16 [2048], P('dp'), may hold values from -3 to 3
- norm1_gain: bfloat16 [2048], P('dp'), may hold values from 0.5 to 1.5
- norm1_bias: bfloat16 [2048], P('dp'), may hold values from -2 to 2
- w1: bfloat16 [2048, 8192], P('dp'), may hold values from -0.125 to 0.125
- b1: bfloat16 [8192], P('dp'), may hold values from -3 to 3
- w2: bfloat16 [8192, 2048], P('dp'), may hold values from -0.0625 to 0.0625
- b2: bfloat16 [2048], P('dp'), may hold values from -3 to 3
- norm2_gain: bfloat16 [2048], P('dp'), may hold values from 0.5 to 1.5
- norm2_bias: bfloat16 [2048], P('dp'), may hold values from -2 to 2
Outputs:
- output: bfloat16 [4096, 2048], P('dp')
- input_grad: bfloat16 [4096, 2048], P('dp')
- grad_wq: float32 [2048, 2048], P('dp')
- grad_bq: float32 [2048], P('dp')
- grad_wk: float32 [2048, 2048], P('dp')
- grad_wv: float32 [2048, 2048], P('dp')
- grad_bv: float32 [2048], P('dp')
- grad_wo: float32 [2048, 2048], P('dp')
- grad_bo: float32 [2048], P('dp')
- grad_norm1_gain: float32 [2048], P('dp')
- grad_norm1_bias: float32 [2048], P('dp')
- grad_w1: float32 [2048, 8192], P('dp')
- grad_b1: float32 [8192], P('dp')
- grad_w2: float32 [8192, 2048], P('dp')
- grad_b2: float32 [2048], P('dp')
- grad_norm2_gain: float32 [2048], P('dp')
- grad_norm2_bias: float32 [2048], P('dp')
The draws below stay inside these ranges and needn't reach their ends.
Inputs may be any that keep to these rules, and one draw needn't show every extreme that they name: The lengths sum to 4096; the longest is exactly 160.
All inputs are finite; a program needn't handle non-finite values.
Results may differ from the reference program's by a relative error of at most 0.015.
Values may be sent and summed in bfloat16 or wider, within the bound.
A program may use at most 448 MiB of HBM per device.

```python
import math
import jax
import jax.numpy as jnp
import numpy as np
from jax import lax

D = 2048
HEADS = 16
HEAD_DIM = 128
FF = 8192
SEQ_MAX = 160
SEQS = 32
TOKENS = 4096


def levels(own_key, extent, split, low, high):
    gain, own = 1.0, jax.random.fold_in(own_key, 6)
    for axis_at, blocks in split:
        steps = jnp.exp(jax.random.uniform(jax.random.fold_in(own, axis_at), (blocks,), jnp.float32, low / len(split), high / len(split)))
        gain = gain * jnp.repeat(steps, extent[axis_at] // blocks).reshape([-1 if axis == axis_at else 1 for axis in range(len(extent))])
    return gain


def profile(count, total, limit, slope):
    portions = [(1 << 20) // math.isqrt(grade ** slope) + 1 for grade in range(2, count + 1)]
    surplus, counts = total - limit - (count - 1), [1] * (count - 1)
    while surplus > 0:
        candidates = [i for i in range(count - 1) if counts[i] < limit]
        whole, remaining = sum([portions[i] for i in candidates]), surplus
        for i in candidates:
            extra = min(limit - counts[i], max(1, remaining * portions[i] // whole), surplus)
            counts[i] = counts[i] + extra
            surplus = surplus - extra
    return np.array([limit] + counts)


def ragged_sizes(key, amount, total, reach, slope):
    if amount == 2:
        one = jax.random.randint(key, (), max(1, total - reach), min(reach, total - 1) + 1)
        return jnp.stack([one, total - one])
    tallies = jnp.asarray(profile(amount, total, reach, slope), jnp.int32)
    couples = (amount - 1) // 2
    donor, receiver = tallies[1:1 + 2 * couples:2], tallies[2:2 + 2 * couples:2]
    room = jnp.minimum(donor - 1, reach - receiver)
    moved = jax.random.randint(jax.random.fold_in(key, 1), (couples,), 0, 1 << 20) % (room + 1)
    tallies = tallies.at[1:1 + 2 * couples:2].set(donor - moved).at[2:2 + 2 * couples:2].set(receiver + moved)
    return tallies[jax.random.permutation(jax.random.fold_in(key, 2), amount)]


def normal_values(key, extent, width, limit, pieces=(), kind=jnp.bfloat16):
    gain = levels(key, extent, pieces, -0.22, 0.18) if pieces else 1.0
    values = jax.random.normal(key, extent, jnp.float32) * width * gain
    return jnp.minimum(jnp.maximum(values, -limit), limit).astype(kind)


def setup_inputs(seed: int = 0) -> dict:
    seeds = jax.random.split(jax.random.key(seed), 19)
    tokens = normal_values(seeds[0], (TOKENS, D), 1.0, 6.0, ((0, 32),))
    cotangent = normal_values(seeds[1], (TOKENS, D), 1.0, 6.0, ((0, 32),))
    lengths = ragged_sizes(seeds[2], SEQS, TOKENS, SEQ_MAX, 1).astype(jnp.int32)
    wq = normal_values(seeds[3], (D, D), D ** -0.5, 0.125, ((0, 32),))
    bq = normal_values(seeds[4], (D,), 0.5, 3.0, ((0, 32),))
    wk = normal_values(seeds[5], (D, D), D ** -0.5, 0.125, ((0, 32),))
    wv = normal_values(seeds[6], (D, D), D ** -0.5, 0.125, ((0, 32),))
    bv = normal_values(seeds[7], (D,), 0.5, 3.0, ((0, 32),))
    wo = normal_values(seeds[8], (D, D), (D // 16) ** -0.5, 0.5, ((0, 32),))
    bo = normal_values(seeds[9], (D,), 0.5, 3.0, ((0, 32),))
    norm1_gain = jnp.clip(1.0 + 0.1 * jax.random.normal(seeds[10], (D,), jnp.float32), 0.5, 1.5).astype(jnp.bfloat16)
    norm1_bias = normal_values(seeds[11], (D,), 0.3, 2.0, ((0, 32),))
    w1 = normal_values(seeds[12], (D, FF), D ** -0.5, 0.125, ((0, 32),))
    b1 = normal_values(seeds[13], (FF,), 0.5, 3.0, ((0, 32),))
    w2 = normal_values(seeds[14], (FF, D), FF ** -0.5, 0.0625, ((0, 32),))
    b2 = normal_values(seeds[15], (D,), 0.5, 3.0, ((0, 32),))
    norm2_gain = jnp.clip(1.0 + 0.1 * jax.random.normal(seeds[16], (D,), jnp.float32), 0.5, 1.5).astype(jnp.bfloat16)
    norm2_bias = normal_values(seeds[17], (D,), 0.3, 2.0, ((0, 32),))
    return {"tokens": tokens, "cotangent": cotangent, "lengths": lengths, "wq": wq, "bq": bq, "wk": wk, "wv": wv, "bv": bv, "wo": wo, "bo": bo, "norm1_gain": norm1_gain, "norm1_bias": norm1_bias, "w1": w1, "b1": b1, "w2": w2, "b2": b2, "norm2_gain": norm2_gain, "norm2_bias": norm2_bias}


@jax.custom_vjp
def low(v):
    return lax.optimization_barrier(v.astype(jnp.bfloat16)).astype(jnp.float32)

@jax.custom_vjp
def low_back(v):
    return v

def low_keep(v):
    return (low(v), None)

def low_pass(kept, grad):
    return (grad,)

def back_keep(v):
    return (v, None)

def back_low(kept, grad):
    return (low(grad),)
low.defvjp(low_keep, low_pass)
low_back.defvjp(back_keep, back_low)
norm_eps = 1e-05

def matmul_hi(left, right):
    return jnp.dot(left, right, precision=lax.Precision.HIGHEST)

def layer_norm(residual, gain_vec, shift_vec):
    mean_val = lax.optimization_barrier(jnp.mean(residual, axis=-1, keepdims=True))
    centred = residual - mean_val
    var_val = lax.optimization_barrier(jnp.mean(centred * centred, axis=-1, keepdims=True))
    return centred * lax.rsqrt(var_val + norm_eps) * gain_vec + shift_vec

def sequence_layer(rows, valid_rows, params):
    wq, bq, wk, wv, bv, wo, bo, gain_one, shift_one, w1, b1, w2, b2, gain_two, shift_two = params
    slot_count = rows.shape[0]
    score_scale = HEAD_DIM ** (-0.5)
    queries = low_back(low(matmul_hi(rows, wq) + bq)).reshape(slot_count, HEADS, HEAD_DIM)
    keys_low = low_back(low(matmul_hi(rows, wk))).reshape(slot_count, HEADS, HEAD_DIM)
    values_low = low_back(low(matmul_hi(rows, wv) + bv)).reshape(slot_count, HEADS, HEAD_DIM)
    scores = low_back(jnp.einsum('qhd,khd->hqk', queries, keys_low, precision=lax.Precision.HIGHEST) * score_scale)
    scores = jnp.where(valid_rows[None, None, :], scores, -1e+30)
    attn_probs = low(jax.nn.softmax(scores, axis=-1))
    attended = jnp.einsum('hqk,khd->qhd', attn_probs, values_low, precision=lax.Precision.HIGHEST)
    attended = low_back(low(attended.reshape(slot_count, HEADS * HEAD_DIM)))
    branch = low_back(matmul_hi(attended, wo) + bo)
    hidden = layer_norm(rows + branch, gain_one, shift_one)
    upward = low_back(matmul_hi(low(hidden), w1) + b1)
    activ = low(jax.nn.gelu(upward, approximate=True))
    mixed = low_back(matmul_hi(activ, w2) + b2)
    normed = layer_norm(hidden + mixed, gain_two, shift_two)
    return jnp.where(valid_rows[:, None], normed, 0.0)

def reference(tokens, cotangent, lengths, wq, bq, wk, wv, bv, wo, bo, norm1_gain, norm1_bias, w1, b1, w2, b2, norm2_gain, norm2_bias):
    total_rows = tokens.shape[0]
    starts = (jnp.cumsum(lengths) - lengths).astype(jnp.int32)
    places = jnp.arange(SEQ_MAX, dtype=jnp.int32)
    row_ids = jnp.arange(total_rows, dtype=jnp.int32)
    seq_of = (lax.optimization_barrier(jnp.sum((row_ids[:, None] >= starts[None, :]).astype(jnp.int32), 1)) - 1).astype(jnp.int32)
    flat_index = (seq_of * SEQ_MAX + row_ids - starts[seq_of]).astype(jnp.int32)
    params = tuple((item.astype(jnp.float32) for item in (wq, bq, wk, wv, bv, wo, bo, norm1_gain, norm1_bias, w1, b1, w2, b2, norm2_gain, norm2_bias)))

    def forward_all(tok_rows, weights):
        padded = jnp.concatenate([tok_rows, jnp.zeros((SEQ_MAX, tok_rows.shape[1]), tok_rows.dtype)], 0)

        def per_sequence(carry, item):
            start_row, seq_len = item
            rows = lax.dynamic_slice_in_dim(padded, start_row, SEQ_MAX, 0)
            valid_rows = places < seq_len
            rows = jnp.where(valid_rows[:, None], rows, 0.0)
            return (carry, jax.checkpoint(sequence_layer)(rows, valid_rows, weights))
        _, stacked = lax.scan(per_sequence, jnp.zeros((), jnp.float32), (starts, lengths))
        return stacked.reshape(-1, tok_rows.shape[1])[flat_index]
    result, pullback = jax.vjp(forward_all, tokens.astype(jnp.float32), params)
    grad_tokens, grads = pullback(cotangent.astype(jnp.float32))
    gq, gbq, gk, gv, gbv, go, gbo, gg1, gb1n, gw1, gb1, gw2, gb2, gg2, gb2n = grads
    return (result.astype(jnp.bfloat16), grad_tokens.astype(jnp.bfloat16), gq, gbq, gk, gv, gbv, go, gbo, gg1, gb1n, gw1, gb1, gw2, gb2, gg2, gb2n)
```

```python
import functools

import jax
import jax.numpy as jnp
from jax import lax
from jax.experimental import pallas as pl
from jax.experimental.pallas import tpu as pltpu
from jax.sharding import PartitionSpec as P

HEADS = 16
HEAD_DIM = 128
SEQ_MAX = 160
SPAN = 3

GROUP = 16
HALO = 256
WINDOW = 512
TILE = 128
MESH_ID = pl.DeviceIdType.MESH
VMEM_LIMIT = 60 << 20
PORTIONS = ((0, 48), (48, 48), (96, 32))
ORDERS = ((0, 1, 2), (1, 2, 0), (2, 0, 1))


norm_eps = 1e-05


def layer_norm(residual, gain_vec, shift_vec):
    mean_val = jnp.mean(residual, axis=-1, keepdims=True)
    centred = residual - mean_val
    var_val = jnp.mean(centred * centred, axis=-1, keepdims=True)
    return centred * lax.rsqrt(var_val + norm_eps) * gain_vec + shift_vec


def gelu_tanh(values):
    return jax.nn.gelu(values, approximate=True)


def plan_layout(lengths, tok_dev):
    starts = jnp.cumsum(lengths) - lengths
    owner_first = starts // tok_dev
    return (starts, starts, lengths, owner_first)


def to_owners(shard, layout, dev_count, piece_rows):
    starts, owner_start, owner_length, owner_first = layout
    tok_dev = shard.shape[0]
    feat_width = shard.shape[1]
    device = lax.axis_index("dp")
    held_rows = lax.all_to_all(
        shard.reshape(dev_count, piece_rows, feat_width),
        "dp",
        split_axis=0,
        concat_axis=0,
        tiled=True,
    )
    held_rows = held_rows.reshape(dev_count * piece_rows, feat_width)
    slot_ids = jnp.arange(SPAN * piece_rows, dtype=jnp.int32)
    shard_step = slot_ids // piece_rows
    within = slot_ids % piece_rows
    source = owner_first[:, None] + shard_step[None, :]
    global_row = source * tok_dev + device * piece_rows + within[None, :]
    inside = (
        (global_row >= owner_start[:, None])
        & (global_row < (owner_start + owner_length)[:, None])
        & (source < dev_count)
    )
    picked = held_rows[jnp.clip(source, 0, dev_count - 1) * piece_rows + within[None, :]]
    outgoing = jnp.where(inside[:, :, None], picked, jnp.zeros((), picked.dtype))
    arrived = lax.all_to_all(outgoing, "dp", split_axis=0, concat_axis=0, tiled=True)
    arrived = arrived.reshape(dev_count * SPAN * piece_rows, feat_width)
    my_start = owner_start[device]
    my_length = owner_length[device]
    my_first = owner_first[device]
    places = jnp.arange(SEQ_MAX, dtype=jnp.int32)
    global_pos = my_start + places
    shard_of = global_pos // tok_dev
    offset_in = global_pos % tok_dev
    slot_index = (
        offset_in // piece_rows * (SPAN * piece_rows)
        + (shard_of - my_first) * piece_rows
        + offset_in % piece_rows
    )
    valid_rows = places < my_length
    slot_index = jnp.where(valid_rows, slot_index, 0)
    owned = jnp.where(valid_rows[:, None], arrived[slot_index], jnp.zeros((), arrived.dtype))
    return (owned, valid_rows)


def to_order(owned, layout, dev_count, piece_rows, tok_dev):
    starts, owner_start, owner_length, owner_first = layout
    feat_width = owned.shape[1]
    device = lax.axis_index("dp")
    my_start = owner_start[device]
    my_length = owner_length[device]
    my_first = owner_first[device]
    slot_ids = jnp.arange(SPAN * piece_rows, dtype=jnp.int32)
    shard_step = slot_ids // piece_rows
    within = slot_ids % piece_rows
    targets = jnp.arange(dev_count, dtype=jnp.int32)
    global_row = (
        (my_first + shard_step)[None, :] * tok_dev + targets[:, None] * piece_rows + within[None, :]
    )
    place_row = global_row - my_start
    inside = (place_row >= 0) & (place_row < my_length)
    picked = owned[jnp.clip(place_row, 0, owned.shape[0] - 1)]
    outgoing = jnp.where(inside[:, :, None], picked, jnp.zeros((), picked.dtype))
    returned = lax.all_to_all(outgoing, "dp", split_axis=0, concat_axis=0, tiled=True)
    returned = returned.reshape(dev_count * SPAN * piece_rows, feat_width)
    sources = jnp.arange(dev_count, dtype=jnp.int32)
    within_piece = jnp.arange(piece_rows, dtype=jnp.int32)
    row_ids = sources[:, None] * tok_dev + device * piece_rows + within_piece[None, :]
    seq_of = jnp.sum((row_ids[:, :, None] >= starts[None, None, :]).astype(jnp.int32), 2) - 1
    slot_index = (
        seq_of * (SPAN * piece_rows)
        + (sources[:, None] - owner_first[seq_of]) * piece_rows
        + within_piece[None, :]
    )
    pieces = returned[slot_index]
    ordered = lax.all_to_all(pieces, "dp", split_axis=0, concat_axis=0, tiled=True)
    return ordered.reshape(tok_dev, feat_width)


def per_device(
    tokens,
    cotangent,
    lengths,
    wq,
    bq,
    wk,
    wv,
    bv,
    wo,
    bo,
    norm1_gain,
    norm1_bias,
    w1,
    b1,
    w2,
    b2,
    norm2_gain,
    norm2_bias,
):
    f32 = jnp.float32
    bf16 = jnp.bfloat16
    dev_count = lax.axis_size("dp")
    tok_dev = tokens.shape[0]
    feat_width = tokens.shape[1]
    piece_rows = tok_dev // dev_count
    layout = plan_layout(lengths, tok_dev)
    joined, valid_rows = to_owners(
        jnp.concatenate([tokens, cotangent], 1), layout, dev_count, piece_rows
    )
    inputs = joined[:, :feat_width]
    upstream = joined[:, feat_width:].astype(f32)
    slot_count = inputs.shape[0]
    score_scale = HEAD_DIM ** (-0.5)
    full_wq, full_wk, full_wv, full_wo, full_bq, full_bv, full_bo, gain_one, shift_one = (
        lax.all_gather(wq, "dp", axis=0, tiled=True),
        lax.all_gather(wk, "dp", axis=0, tiled=True),
        lax.all_gather(wv, "dp", axis=0, tiled=True),
        lax.all_gather(wo, "dp", axis=0, tiled=True),
        lax.all_gather(bq, "dp", axis=0, tiled=True),
        lax.all_gather(bv, "dp", axis=0, tiled=True),
        lax.all_gather(bo, "dp", axis=0, tiled=True),
        lax.all_gather(norm1_gain, "dp", axis=0, tiled=True),
        lax.all_gather(norm1_bias, "dp", axis=0, tiled=True),
    )
    queries = (
        (jnp.dot(inputs, full_wq, preferred_element_type=f32) + full_bq.astype(f32))
        .astype(bf16)
        .reshape(slot_count, HEADS, HEAD_DIM)
    )
    keys_low = (
        jnp.dot(inputs, full_wk, preferred_element_type=f32)
        .astype(bf16)
        .reshape(slot_count, HEADS, HEAD_DIM)
    )
    values_low = (
        (jnp.dot(inputs, full_wv, preferred_element_type=f32) + full_bv.astype(f32))
        .astype(bf16)
        .reshape(slot_count, HEADS, HEAD_DIM)
    )
    scores = jnp.einsum("qhd,khd->hqk", queries, keys_low, preferred_element_type=f32) * score_scale
    scores = jnp.where(valid_rows[None, None, :], scores, -1e30)
    row_max = jnp.max(scores, -1, keepdims=True)
    row_total = jnp.sum(jnp.exp(scores - row_max), -1, keepdims=True)
    log_total = row_max + jnp.log(row_total)
    attn_probs = jnp.exp(scores - log_total).astype(bf16)
    attended = jnp.einsum("hqk,khd->qhd", attn_probs, values_low, preferred_element_type=f32)
    attended = attended.reshape(slot_count, feat_width).astype(bf16)
    branch = jnp.dot(attended, full_wo, preferred_element_type=f32) + full_bo.astype(f32)
    resid_one = inputs.astype(f32) + branch
    hidden, norm_one_back = jax.vjp(
        layer_norm, resid_one, gain_one.astype(f32), shift_one.astype(f32)
    )
    hidden_low = hidden.astype(bf16)
    full_w1, full_w2, full_b1, full_b2, gain_two, shift_two = (
        lax.all_gather(w1, "dp", axis=0, tiled=True),
        lax.all_gather(w2, "dp", axis=0, tiled=True),
        lax.all_gather(b1, "dp", axis=0, tiled=True),
        lax.all_gather(b2, "dp", axis=0, tiled=True),
        lax.all_gather(norm2_gain, "dp", axis=0, tiled=True),
        lax.all_gather(norm2_bias, "dp", axis=0, tiled=True),
    )
    upward = jnp.dot(hidden_low, full_w1, preferred_element_type=f32) + full_b1.astype(f32)
    activ, gelu_back = jax.vjp(gelu_tanh, upward)
    activ_low = activ.astype(bf16)
    mixed = jnp.dot(activ_low, full_w2, preferred_element_type=f32) + full_b2.astype(f32)
    resid_two = hidden + mixed
    normed, norm_two_back = jax.vjp(
        layer_norm, resid_two, gain_two.astype(f32), shift_two.astype(f32)
    )
    result = jnp.where(valid_rows[:, None], normed, 0.0).astype(bf16)
    output = to_order(result, layout, dev_count, piece_rows, tok_dev)
    back_w1, back_w2 = (
        lax.all_gather(w1, "dp", axis=0, tiled=True),
        lax.all_gather(w2, "dp", axis=0, tiled=True),
    )
    grad_resid_two, grad_gain_two, grad_shift_two = norm_two_back(upstream)
    grad_mixed = grad_resid_two.astype(bf16)
    grad_bias_two = jnp.sum(grad_mixed.astype(f32), 0)
    grad_activ = jnp.einsum("td,fd->tf", grad_mixed, back_w2, preferred_element_type=f32)
    grad_upward = gelu_back(grad_activ)[0].astype(bf16)
    grad_bias_one = jnp.sum(grad_upward.astype(f32), 0)
    grad_hidden = grad_resid_two + jnp.einsum(
        "tf,df->td", grad_upward, back_w1, preferred_element_type=f32
    )
    grad_w2 = jnp.einsum("tf,td->fd", activ_low, grad_mixed, preferred_element_type=f32)
    grad_w1 = jnp.einsum("td,tf->df", hidden_low, grad_upward, preferred_element_type=f32)
    mlp_grads = (
        lax.psum_scatter(grad_w1, "dp", scatter_dimension=0, tiled=True),
        lax.psum_scatter(grad_w2, "dp", scatter_dimension=0, tiled=True),
        lax.psum_scatter(grad_bias_one, "dp", scatter_dimension=0, tiled=True),
        lax.psum_scatter(grad_bias_two, "dp", scatter_dimension=0, tiled=True),
        lax.psum_scatter(grad_gain_two, "dp", scatter_dimension=0, tiled=True),
        lax.psum_scatter(grad_shift_two, "dp", scatter_dimension=0, tiled=True),
    )
    back_wq, back_wk, back_wv, back_wo = (
        lax.all_gather(wq, "dp", axis=0, tiled=True),
        lax.all_gather(wk, "dp", axis=0, tiled=True),
        lax.all_gather(wv, "dp", axis=0, tiled=True),
        lax.all_gather(wo, "dp", axis=0, tiled=True),
    )
    grad_resid_one, grad_gain_one, grad_shift_one = norm_one_back(grad_hidden)
    grad_branch = grad_resid_one.astype(bf16)
    grad_bo = jnp.sum(grad_branch.astype(f32), 0)
    grad_wo = jnp.einsum("tc,td->cd", attended, grad_branch, preferred_element_type=f32)
    grad_attended = jnp.einsum(
        "td,cd->tc", grad_branch, back_wo, preferred_element_type=f32
    ).astype(bf16)
    grad_attended = grad_attended.reshape(slot_count, HEADS, HEAD_DIM)
    re_scores = (
        jnp.einsum("qhd,khd->hqk", queries, keys_low, preferred_element_type=f32) * score_scale
    )
    re_scores = jnp.where(valid_rows[None, None, :], re_scores, -1e30)
    re_probs = jnp.exp(re_scores - log_total)
    re_probs_low = re_probs.astype(bf16)
    grad_values = jnp.einsum(
        "hqk,qhd->khd", re_probs_low, grad_attended, preferred_element_type=f32
    ).astype(bf16)
    grad_probs = jnp.einsum("qhd,khd->hqk", grad_attended, values_low, preferred_element_type=f32)
    grad_scores = re_probs * (grad_probs - jnp.sum(re_probs * grad_probs, -1, keepdims=True))
    grad_scores_low = grad_scores.astype(bf16)
    grad_queries = (
        jnp.einsum("hqk,khd->qhd", grad_scores_low, keys_low, preferred_element_type=f32)
        * score_scale
    ).astype(bf16)
    grad_keys = (
        jnp.einsum("hqk,qhd->khd", grad_scores_low, queries, preferred_element_type=f32)
        * score_scale
    ).astype(bf16)
    grad_queries = grad_queries.reshape(slot_count, feat_width)
    grad_keys = grad_keys.reshape(slot_count, feat_width)
    grad_values = grad_values.reshape(slot_count, feat_width)
    grad_bq = jnp.sum(grad_queries.astype(f32), 0)
    grad_bv = jnp.sum(grad_values.astype(f32), 0)
    grad_wq = jnp.einsum("tc,td->cd", inputs, grad_queries, preferred_element_type=f32)
    grad_wk = jnp.einsum("tc,td->cd", inputs, grad_keys, preferred_element_type=f32)
    grad_wv = jnp.einsum("tc,td->cd", inputs, grad_values, preferred_element_type=f32)
    grad_input = grad_resid_one + jnp.einsum(
        "td,cd->tc", grad_queries, back_wq, preferred_element_type=f32
    )
    grad_input = grad_input + jnp.einsum(
        "td,cd->tc", grad_keys, back_wk, preferred_element_type=f32
    )
    grad_input = grad_input + jnp.einsum(
        "td,cd->tc", grad_values, back_wv, preferred_element_type=f32
    )
    grad_input = jnp.where(valid_rows[:, None], grad_input, 0.0).astype(bf16)
    attn_grads = (
        lax.psum_scatter(grad_wq, "dp", scatter_dimension=0, tiled=True),
        lax.psum_scatter(grad_wk, "dp", scatter_dimension=0, tiled=True),
        lax.psum_scatter(grad_wv, "dp", scatter_dimension=0, tiled=True),
        lax.psum_scatter(grad_wo, "dp", scatter_dimension=0, tiled=True),
        lax.psum_scatter(grad_bq, "dp", scatter_dimension=0, tiled=True),
        lax.psum_scatter(grad_bv, "dp", scatter_dimension=0, tiled=True),
        lax.psum_scatter(grad_bo, "dp", scatter_dimension=0, tiled=True),
        lax.psum_scatter(grad_gain_one, "dp", scatter_dimension=0, tiled=True),
        lax.psum_scatter(grad_shift_one, "dp", scatter_dimension=0, tiled=True),
    )
    sum_w1, sum_w2, sum_b1, sum_b2, sum_g2, sum_s2 = mlp_grads
    sum_wq, sum_wk, sum_wv, sum_wo, sum_bq, sum_bv, sum_bo, sum_g1, sum_s1 = attn_grads
    input_grad = to_order(grad_input, layout, dev_count, piece_rows, tok_dev)
    return (
        output,
        input_grad,
        sum_wq,
        sum_bq,
        sum_wk,
        sum_wv,
        sum_bv,
        sum_wo,
        sum_bo,
        sum_g1,
        sum_s1,
        sum_w1,
        sum_b1,
        sum_w2,
        sum_b2,
        sum_g2,
        sum_s2,
    )


def flip(device, bit):
    step = 1 << bit
    return device + step - 2 * step * ((device // step) % 2)


def chip_bits(device):
    return [(device // 2) % 2, (device // 4) % 2, (device // 8) % 2]


def enter(partners):
    barrier = pltpu.get_barrier_semaphore()
    for partner in partners:
        pl.semaphore_signal(barrier, inc=1, device_id=(partner,), device_id_type=MESH_ID)
    pl.semaphore_wait(barrier, len(partners))


def push(src, dst, send_sem, recv_sem, device):
    return pltpu.make_async_remote_copy(
        src_ref=src,
        dst_ref=dst,
        send_sem=send_sem,
        recv_sem=recv_sem,
        device_id=(device,),
        device_id_type=MESH_ID,
    )


def gather_kernel(x_ref, o_ref, local_sem, send_sem, recv_sem, pair_send, pair_recv):
    device = lax.axis_index("dp")
    core = device % 2
    bits = chip_bits(device)
    partners = [flip(device, 1), flip(device, 2), flip(device, 3)]
    pair = flip(device, 0)
    enter(partners + [pair])

    def at(values, rows):
        return o_ref.at[values[2], values[1], values[0], core, rows, slice(None)]

    own = o_ref.at[bits[2], bits[1], bits[0], core]
    local = pltpu.make_async_copy(x_ref, own, local_sem)
    local.start()
    hops, shares = {}, {}

    def hop(part, step):
        first, count = PORTIONS[part]
        rows = pl.ds(first, count)
        values = list(bits)
        for dim in ORDERS[part][:step]:
            values[dim] = slice(None)
        dst = at(values, rows)
        src = x_ref.at[rows, :] if step == 0 else dst
        copy = push(
            src, dst, send_sem.at[part, step], recv_sem.at[part, step], partners[ORDERS[part][step]]
        )
        copy.start()
        hops[part, step] = copy

    def share(part, step):
        first, count = PORTIONS[part]
        rows = pl.ds(first, count)
        values = list(bits)
        if step:
            for dim in ORDERS[part][: step - 1]:
                values[dim] = slice(None)
            dim = ORDERS[part][step - 1]
            values[dim] = 1 - bits[dim]
        dst = at(values, rows)
        src = dst if step else x_ref.at[rows, :]
        copy = push(src, dst, pair_send.at[part, step], pair_recv.at[part, step], pair)
        copy.start()
        shares[part, step] = copy

    for part in range(3):
        hop(part, 0)
    for part in range(3):
        share(part, 0)
    local.wait()
    for step in (1, 2, 3):
        for part in range(3):
            hops[part, step - 1].wait_recv()
            if step < 3:
                hop(part, step)
            share(part, step)
    for copy in shares.values():
        copy.wait()
    for copy in hops.values():
        copy.wait_send()


def group_gather(rows, name, collective_id):
    count, width = rows.shape
    vmem = pl.BlockSpec(memory_space=pltpu.VMEM)
    sems = pltpu.SemaphoreType.DMA
    out = pl.pallas_call(
        gather_kernel,
        out_shape=jax.ShapeDtypeStruct((2, 2, 2, 2, count, width), rows.dtype),
        in_specs=[vmem],
        out_specs=vmem,
        scratch_shapes=[sems, sems((3, 3)), sems((3, 3)), sems((3, 4)), sems((3, 4))],
        compiler_params=pltpu.CompilerParams(
            collective_id=collective_id, has_side_effects=True, vmem_limit_bytes=VMEM_LIMIT
        ),
        name=name,
    )(rows)
    return out.reshape(GROUP * count, width)


def scatter_kernel(
    x_ref, o_ref, pair_in, sums, in_one, in_two, in_three, send_sem, recv_sem, pair_send, pair_recv
):
    device = lax.axis_index("dp")
    core = device % 2
    bits = chip_bits(device)
    partners = [flip(device, 1), flip(device, 2), flip(device, 3)]
    pair = flip(device, 0)
    width = x_ref.shape[-1]
    f32 = jnp.float32
    incoming = (in_one, in_two, in_three)
    enter(partners + [pair])

    def view(ref, values, rows, with_core=None):
        where = (values[2], values[1], values[0])
        if with_core is not None:
            where = where + (with_core,)
        return ref.at[where + (rows, slice(None))]

    shares, hops = {}, {}
    for half in range(2):
        for part in range(3):
            first, count = PORTIONS[part]
            rows = pl.ds(first, count)
            dim = ORDERS[part][0]
            values = [slice(None)] * 3
            values[dim] = 1 - bits[dim] if half == 0 else bits[dim]
            copy = push(
                view(x_ref, values, rows, 1 - core),
                view(pair_in, values, rows),
                pair_send.at[part, half],
                pair_recv.at[part, half],
                pair,
            )
            copy.start()
            shares[part, half] = copy

    def add_up(part, values, arrived, store):
        first, count = PORTIONS[part]

        def body(index, carry):
            rows = pl.ds(pl.multiple_of(first + index * 16, 16), 16)
            where = (values[2], values[1], values[0])
            total = x_ref[where + (core, rows, slice(None))].astype(f32)
            total = total + pair_in[where + (rows, slice(None))].astype(f32)
            for ref in incoming[:arrived]:
                total = total + ref[where + (rows, slice(None))].astype(f32)
            store(where, rows, total)
            return carry

        lax.fori_loop(0, count // 16, body, 0)

    def keep_sum(where, rows, total):
        sums[where + (rows, slice(None))] = total.astype(sums.dtype)

    def finish(where, rows, total):
        o_ref[rows, :] = total

    def hop(part, step):
        first, count = PORTIONS[part]
        order = ORDERS[part]
        values = list(bits)
        values[order[step]] = 1 - bits[order[step]]
        free = order[step + 1 :]
        for mask in range(1 << len(free)):
            slot = list(values)
            for place, dim in enumerate(free):
                slot[dim] = (mask >> place) & 1
            add_up(part, slot, step, keep_sum)
        for dim in free:
            values[dim] = slice(None)
        rows = pl.ds(first, count)
        copy = push(
            view(sums, values, rows),
            view(incoming[step], values, rows),
            send_sem.at[part, step],
            recv_sem.at[part, step],
            partners[order[step]],
        )
        copy.start()
        hops[part, step] = copy

    for part in range(3):
        shares[part, 0].wait_recv()
        hop(part, 0)
    for part in range(3):
        shares[part, 1].wait_recv()
        hops[part, 0].wait_recv()
        hop(part, 1)
    for part in range(3):
        hops[part, 1].wait_recv()
        hop(part, 2)
    for part in range(3):
        hops[part, 2].wait_recv()
        add_up(part, bits, 3, finish)
    for copy in shares.values():
        copy.wait_send()
    for copy in hops.values():
        copy.wait_send()


def group_scatter(partial, name, collective_id):
    width = partial.shape[-1]
    count = partial.shape[0] // GROUP
    low = partial.dtype
    vmem = pl.BlockSpec(memory_space=pltpu.VMEM)
    sems = pltpu.SemaphoreType.DMA
    slots = pltpu.VMEM((2, 2, 2, count, width), low)
    return pl.pallas_call(
        scatter_kernel,
        out_shape=jax.ShapeDtypeStruct((count, width), jnp.float32),
        in_specs=[vmem],
        out_specs=vmem,
        scratch_shapes=[
            slots, slots, slots, slots, slots,
            sems((3, 3)), sems((3, 3)), sems((3, 2)), sems((3, 2)),
        ],
        compiler_params=pltpu.CompilerParams(
            collective_id=collective_id, has_side_effects=True, vmem_limit_bytes=VMEM_LIMIT
        ),
        name=name,
    )(partial.reshape(2, 2, 2, 2, count, width))


def exchange_kernel(arrays, *refs):
    ins, outs = refs[:arrays], refs[arrays : 2 * arrays]
    local_sem, send_sem, recv_sem = refs[2 * arrays :]
    device = lax.axis_index("dp")
    base = device // GROUP * GROUP
    mine = device % GROUP
    others = [base + (mine + step) % GROUP for step in range(1, GROUP)]
    enter(others)
    copies, locals_ = [], []
    for at in range(arrays):
        for step, other in enumerate(others):
            copy = push(
                ins[at].at[other - base],
                outs[at].at[mine],
                send_sem.at[at, step],
                recv_sem.at[at, step],
                other,
            )
            copy.start()
            copies.append(copy)
        local = pltpu.make_async_copy(ins[at].at[mine], outs[at].at[mine], local_sem.at[at])
        local.start()
        locals_.append(local)
    for copy in locals_:
        copy.wait()
    for copy in copies:
        copy.wait()


def group_exchange(arrays, name, collective_id):
    count = len(arrays)
    anywhere = pl.BlockSpec(memory_space=pl.ANY)
    sems = pltpu.SemaphoreType.DMA
    return pl.pallas_call(
        functools.partial(exchange_kernel, count),
        out_shape=[jax.ShapeDtypeStruct(item.shape, item.dtype) for item in arrays],
        in_specs=[anywhere] * count,
        out_specs=[anywhere] * count,
        scratch_shapes=[sems((count,)), sems((count, GROUP - 1)), sems((count, GROUP - 1))],
        compiler_params=pltpu.CompilerParams(
            collective_id=collective_id, has_side_effects=True, vmem_limit_bytes=VMEM_LIMIT
        ),
        name=name,
    )(*arrays)


def window_start(row, total):
    start = jnp.minimum(jnp.maximum(row - (WINDOW - TILE) // 2, 0), total - WINDOW)
    return pl.multiple_of(start, 64)


def tile_probs(qkv_ref, row, start, seg_q, seg_k):
    f32 = jnp.float32
    queries = qkv_ref[pl.ds(row, TILE), 0:HEAD_DIM]
    keys = qkv_ref[pl.ds(start, WINDOW), HEAD_DIM : 2 * HEAD_DIM]
    scores = lax.dot_general(queries, keys, (((1,), (1,)), ((), ())), preferred_element_type=f32)
    scores = jnp.where(seg_q == seg_k, scores * HEAD_DIM ** (-0.5), -1e30)
    weights = jnp.exp(scores - jnp.max(scores, -1, keepdims=True))
    return queries, keys, weights / jnp.sum(weights, -1, keepdims=True)


def attend_kernel(offset_ref, qkv_ref, seg_q_ref, seg_k_ref, o_ref):
    total = qkv_ref.shape[0]
    offset = offset_ref[0]

    def body(tile, carry):
        row = pl.multiple_of(offset + tile * TILE, TILE)
        start = window_start(row, total)
        _, _, probs = tile_probs(
            qkv_ref, row, start, seg_q_ref[pl.ds(row, TILE), :], seg_k_ref[row // TILE]
        )
        values = qkv_ref[pl.ds(start, WINDOW), 2 * HEAD_DIM : 3 * HEAD_DIM]
        out = jnp.dot(probs.astype(values.dtype), values, preferred_element_type=jnp.float32)
        o_ref[pl.ds(pl.multiple_of(tile * TILE, TILE), TILE), :] = out.astype(o_ref.dtype)
        return carry

    lax.fori_loop(0, o_ref.shape[0] // TILE, body, 0, unroll=2)


def attend_back_kernel(qkv_ref, grad_ref, seg_q_ref, seg_k_ref, o_ref, dq_sum, dk_sum, dv_sum):
    total = qkv_ref.shape[0]
    f32 = jnp.float32
    low = qkv_ref.dtype
    scale = HEAD_DIM ** (-0.5)
    dk_sum[...] = jnp.zeros_like(dk_sum)
    dv_sum[...] = jnp.zeros_like(dv_sum)

    def body(tile, carry):
        row = pl.multiple_of(tile * TILE, TILE)
        start = window_start(row, total)
        queries, keys, probs = tile_probs(
            qkv_ref, row, start, seg_q_ref[pl.ds(row, TILE), :], seg_k_ref[tile]
        )
        window = pl.ds(start, WINDOW)
        values = qkv_ref[window, 2 * HEAD_DIM : 3 * HEAD_DIM]
        grads = grad_ref[pl.ds(row, TILE), :]
        grad_probs = lax.dot_general(
            grads, values, (((1,), (1,)), ((), ())), preferred_element_type=f32
        )
        inner = jnp.sum(probs * grad_probs, -1, keepdims=True)
        grad_scores = (probs * (grad_probs - inner)).astype(low)
        dq_sum[pl.ds(row, TILE), :] = jnp.dot(grad_scores, keys, preferred_element_type=f32)
        dk_sum[window, :] += lax.dot_general(
            grad_scores, queries, (((0,), (0,)), ((), ())), preferred_element_type=f32
        )
        dv_sum[window, :] += lax.dot_general(
            probs.astype(low), grads, (((0,), (0,)), ((), ())), preferred_element_type=f32
        )
        return carry

    lax.fori_loop(0, total // TILE, body, 0, unroll=2)
    o_ref[:, 0:HEAD_DIM] = (dq_sum[...] * scale).astype(low)
    o_ref[:, HEAD_DIM : 2 * HEAD_DIM] = (dk_sum[...] * scale).astype(low)
    o_ref[:, 2 * HEAD_DIM : 3 * HEAD_DIM] = dv_sum[...].astype(low)


def attend(offset, qkv, seg_q, seg_k, rows):
    vmem = pl.BlockSpec(memory_space=pltpu.VMEM)
    return pl.pallas_call(
        attend_kernel,
        out_shape=jax.ShapeDtypeStruct((rows, HEAD_DIM), qkv.dtype),
        in_specs=[pl.BlockSpec(memory_space=pltpu.SMEM), vmem, vmem, vmem],
        out_specs=vmem,
        compiler_params=pltpu.CompilerParams(vmem_limit_bytes=VMEM_LIMIT),
        name="attend",
    )(offset, qkv, seg_q, seg_k)


def attend_back(qkv, grads, seg_q, seg_k):
    vmem = pl.BlockSpec(memory_space=pltpu.VMEM)
    total = qkv.shape[0]
    acc = pltpu.VMEM((total, HEAD_DIM), jnp.float32)
    return pl.pallas_call(
        attend_back_kernel,
        out_shape=jax.ShapeDtypeStruct(qkv.shape, qkv.dtype),
        in_specs=[vmem, vmem, vmem, vmem],
        out_specs=vmem,
        scratch_shapes=[acc, acc, acc],
        compiler_params=pltpu.CompilerParams(vmem_limit_bytes=VMEM_LIMIT),
        name="attend_back",
    )(qkv, grads, seg_q, seg_k)


def grouped_device(
    tokens,
    cotangent,
    lengths,
    wq,
    bq,
    wk,
    wv,
    bv,
    wo,
    bo,
    norm1_gain,
    norm1_bias,
    w1,
    b1,
    w2,
    b2,
    norm2_gain,
    norm2_bias,
):
    f32 = jnp.float32
    bf16 = jnp.bfloat16
    devices = lax.axis_size("dp")
    block, width = tokens.shape
    own_rows = GROUP * block
    total_tokens = devices * block
    weight_rows = wq.shape[0]
    unit_rows, units = w2.shape[0], w1.shape[1]
    device = lax.axis_index("dp")
    group, member = device // GROUP, device % GROUP
    chip, core = member // 2, member % 2
    head = core * 8 + chip
    first_group = group == 0
    across = [(at, (at + GROUP) % devices) for at in range(devices)]
    beside = [(at, at + 1 - 2 * (at % 2)) for at in range(devices)]

    def swap(own, other):
        return jnp.where(first_group, own, other), jnp.where(first_group, other, own)

    def in_order(own, other):
        return jnp.concatenate(swap(own, other), 0)

    def by_head(weight):
        return weight.reshape(weight_rows, 2, 8, HEAD_DIM).transpose(2, 1, 0, 3).reshape(
            GROUP, weight_rows, HEAD_DIM
        )

    pack_qkv = jnp.concatenate([by_head(wq), by_head(wk), by_head(wv)], -1)
    pack_w1 = w1.reshape(weight_rows, 2, GROUP, unit_rows).transpose(2, 0, 1, 3).reshape(
        GROUP, weight_rows, 2 * unit_rows
    )
    own_qkv, own_w1 = group_exchange([pack_qkv, pack_w1], "weights_out", 1)
    own_qkv = own_qkv.reshape(GROUP * weight_rows, 3 * HEAD_DIM)
    own_w1 = own_w1.reshape(GROUP * weight_rows, 2 * unit_rows)
    full_qkv = in_order(own_qkv, lax.ppermute(own_qkv, "dp", across))
    wo_beside = lax.ppermute(wo, "dp", beside)
    chip_wo = jnp.concatenate(
        [jnp.where(core == 0, wo, wo_beside), jnp.where(core == 0, wo_beside, wo)], 0
    )
    wo_pairs = [
        (GROUP * g + 2 * k + g, GROUP * (1 - g) + 2 * k + g) for g in range(2) for k in range(8)
    ]
    full_wo = jnp.where(core == group, chip_wo, lax.ppermute(chip_wo, "dp", wo_pairs))
    full_w1 = in_order(own_w1, lax.ppermute(own_w1, "dp", across))
    full_w2 = in_order(w2, lax.ppermute(w2, "dp", across))

    vectors = [bq, bv, bo, norm1_gain, norm1_bias, b2, norm2_gain, norm2_bias, b1]
    sizes = [item.shape[0] for item in vectors]
    gathered = lax.all_gather(jnp.concatenate(vectors), "dp", axis=0).astype(f32)
    whole, at = [], 0
    for size in sizes:
        whole.append(gathered[:, at : at + size].reshape(-1))
        at += size
    all_bq, all_bv, all_bo, gain_one, shift_one, all_b2, gain_two, shift_two, all_b1 = whole
    my_b1 = lax.dynamic_index_in_dim(
        all_b1.reshape(2, GROUP, unit_rows), member, 1, keepdims=False
    ).reshape(-1)
    my_bq = lax.dynamic_slice_in_dim(all_bq, head * HEAD_DIM, HEAD_DIM)
    my_bv = lax.dynamic_slice_in_dim(all_bv, head * HEAD_DIM, HEAD_DIM)
    my_bqkv = jnp.concatenate([my_bq, jnp.zeros_like(my_bq), my_bv])

    ext_rows = own_rows + HALO
    ext_first = group * (own_rows - HALO)
    offset = group * HALO
    starts = jnp.cumsum(lengths) - lengths
    ext_ids = ext_first + jnp.arange(ext_rows, dtype=jnp.int32)
    seg = jnp.sum((ext_ids[:, None] >= starts[None, :]).astype(jnp.int32), 1)
    tile_rows = jnp.arange(ext_rows // TILE, dtype=jnp.int32) * TILE
    tile_starts = jnp.clip(tile_rows - (WINDOW - TILE) // 2, 0, ext_rows - WINDOW)
    key_ids = ext_first + tile_starts[:, None] + jnp.arange(WINDOW, dtype=jnp.int32)[None, :]
    seg_k = jnp.sum((key_ids[:, :, None] >= starts[None, None, :]).astype(jnp.int32), 2)
    seg_k = seg_k[:, None, :]
    seg_q = seg[:, None]

    def with_halo(rows):
        edge = jnp.where(first_group, rows[own_rows - HALO :], rows[:HALO])
        halo = lax.ppermute(edge, "dp", across)
        return jnp.where(
            first_group, jnp.concatenate([rows, halo], 0), jnp.concatenate([halo, rows], 0)
        )

    all_tokens = group_gather(tokens, "gather_tokens", 2)
    qkv = (jnp.dot(all_tokens, full_qkv, preferred_element_type=f32) + my_bqkv).astype(bf16)
    qkv_ext = with_halo(qkv)
    attended = attend(offset.reshape(1), qkv_ext, seg_q, seg_k, own_rows)
    branch_part = jnp.dot(attended, full_wo, preferred_element_type=f32).astype(bf16)
    branch = group_scatter(branch_part, "scatter_branch", 3) + all_bo
    resid_one = tokens.astype(f32) + branch
    hidden, norm_one_back = jax.vjp(layer_norm, resid_one, gain_one, shift_one)

    all_hidden = group_gather(hidden.astype(bf16), "gather_hidden", 4)
    upward = jnp.dot(all_hidden, full_w1, preferred_element_type=f32) + my_b1
    activ, gelu_back = jax.vjp(gelu_tanh, upward)
    activ_low = activ.astype(bf16)
    mixed_part = jnp.dot(activ_low, full_w2, preferred_element_type=f32).astype(bf16)
    mixed = group_scatter(mixed_part, "scatter_mixed", 5) + all_b2
    normed, norm_two_back = jax.vjp(layer_norm, hidden + mixed, gain_two, shift_two)
    output = normed.astype(bf16)

    grad_resid_two, grad_gain_two, grad_shift_two = norm_two_back(cotangent.astype(f32))
    grad_mixed = grad_resid_two.astype(bf16)
    grad_b2 = jnp.sum(grad_mixed.astype(f32), 0)
    all_grad_mixed = group_gather(grad_mixed, "gather_grad_mixed", 6)
    grad_activ = jnp.einsum("td,fd->tf", all_grad_mixed, full_w2, preferred_element_type=f32)
    grad_upward = gelu_back(grad_activ)[0].astype(bf16)
    grad_b1 = jnp.sum(grad_upward.astype(f32), 0)
    hidden_part = jnp.einsum(
        "tf,df->td", grad_upward, full_w1, preferred_element_type=f32
    ).astype(bf16)
    grad_w2 = jnp.einsum("tf,td->fd", activ_low, all_grad_mixed, preferred_element_type=f32)
    grad_w1 = jnp.einsum("td,tf->df", all_hidden, grad_upward, preferred_element_type=f32)

    def across_sum(grad):
        halves = grad.reshape((2, grad.shape[0] // 2) + grad.shape[1:])
        mine = jnp.where(first_group, halves[0], halves[1])
        theirs = jnp.where(first_group, halves[1], halves[0]).astype(bf16)
        return mine + lax.ppermute(theirs, "dp", across).astype(f32)

    out_w2 = across_sum(grad_w2)
    sum_w1 = across_sum(grad_w1)
    grad_hidden = grad_resid_two + group_scatter(hidden_part, "scatter_grad_hidden", 7)

    grad_resid_one, grad_gain_one, grad_shift_one = norm_one_back(grad_hidden)
    grad_branch = grad_resid_one.astype(bf16)
    grad_bo = jnp.sum(grad_branch.astype(f32), 0)
    all_grad_branch = group_gather(grad_branch, "gather_grad_branch", 8)
    grad_attended = jnp.einsum(
        "td,cd->tc", all_grad_branch, full_wo, preferred_element_type=f32
    ).astype(bf16)
    grad_wo = jnp.einsum("tc,td->cd", attended, all_grad_branch, preferred_element_type=f32)
    grad_qkv_ext = attend_back(qkv_ext, with_halo(grad_attended), seg_q, seg_k)
    grad_qkv = lax.dynamic_slice_in_dim(grad_qkv_ext, offset, own_rows, 0)
    grad_bqkv = jnp.sum(grad_qkv.astype(f32), 0)
    input_part = jnp.einsum("tf,df->td", grad_qkv, full_qkv, preferred_element_type=f32)
    grad_wqkv = jnp.einsum("td,tf->df", all_tokens, grad_qkv, preferred_element_type=f32)
    sum_qkv = across_sum(grad_wqkv)
    input_sum = group_scatter(input_part.astype(bf16), "scatter_input", 9)
    input_grad = (grad_resid_one + input_sum).astype(bf16)

    back_pairs = [(dst, src) for src, dst in wo_pairs]
    sum_wo = grad_wo + lax.ppermute(grad_wo.astype(bf16), "dp", back_pairs).astype(f32)
    halves = sum_wo.reshape(2, weight_rows, width)
    mine_wo = jnp.where(core == 0, halves[0], halves[1])
    theirs_wo = jnp.where(core == 0, halves[1], halves[0])
    out_wo = jnp.where(core == group, mine_wo, lax.ppermute(theirs_wo, "dp", beside))
    rows_w1, rows_qkv = group_exchange(
        [
            sum_w1.astype(bf16).reshape(GROUP, weight_rows, 2 * unit_rows),
            sum_qkv.astype(bf16).reshape(GROUP, weight_rows, 3 * HEAD_DIM),
        ],
        "weights_back",
        10,
    )
    out_w1 = (
        rows_w1.reshape(GROUP, weight_rows, 2, unit_rows)
        .transpose(1, 2, 0, 3)
        .reshape(weight_rows, units)
        .astype(f32)
    )
    out_q, out_k, out_v = [
        rows_qkv[:, :, at * HEAD_DIM : (at + 1) * HEAD_DIM]
        .reshape(8, 2, weight_rows, HEAD_DIM)
        .transpose(2, 1, 0, 3)
        .reshape(weight_rows, width)
        .astype(f32)
        for at in range(3)
    ]

    def place_head(vector):
        return lax.dynamic_update_slice_in_dim(
            jnp.zeros((width,), f32), vector, head * HEAD_DIM, 0
        )

    spread_b1 = lax.dynamic_update_slice_in_dim(
        jnp.zeros((2, GROUP, unit_rows), f32), grad_b1.reshape(2, 1, unit_rows), member, 1
    )

    def reduce_vectors(items):
        parts = jnp.concatenate([item.reshape(devices, -1) for item in items], 1)
        mine = lax.psum_scatter(parts.reshape(-1), "dp", scatter_dimension=0, tiled=True)
        result, at = [], 0
        for item in items:
            size = item.size // devices
            result.append(mine[at : at + size])
            at += size
        return result

    out_b1, out_b2, out_g2, out_s2, out_bo, out_g1, out_s1 = reduce_vectors(
        [spread_b1, grad_b2, grad_gain_two, grad_shift_two, grad_bo, grad_gain_one, grad_shift_one]
    )
    out_bq, out_bv = reduce_vectors(
        [place_head(grad_bqkv[:HEAD_DIM]), place_head(grad_bqkv[2 * HEAD_DIM :])]
    )
    return (
        output, input_grad, out_q, out_bq, out_k, out_v, out_bv, out_wo, out_bo, out_g1, out_s1,
        out_w1, out_b1, out_w2, out_b2, out_g2, out_s2,
    )


def solution(mesh):
    in_specs = (
        P("dp", None),
        P("dp", None),
        P(),
        P("dp", None),
        P("dp"),
        P("dp", None),
        P("dp", None),
        P("dp"),
        P("dp", None),
        P("dp"),
        P("dp"),
        P("dp"),
        P("dp", None),
        P("dp"),
        P("dp", None),
        P("dp"),
        P("dp"),
        P("dp"),
    )
    out_specs = (
        P("dp", None),
        P("dp", None),
        P("dp", None),
        P("dp"),
        P("dp", None),
        P("dp", None),
        P("dp"),
        P("dp", None),
        P("dp"),
        P("dp"),
        P("dp"),
        P("dp", None),
        P("dp"),
        P("dp", None),
        P("dp"),
        P("dp"),
        P("dp"),
    )
    two_groups = mesh.shape["dp"] == 2 * GROUP
    return jax.shard_map(
        grouped_device if two_groups else per_device, mesh=mesh, in_specs=in_specs, out_specs=out_specs, check_vma=False
    )
```

```python
import functools

import jax
import jax.numpy as jnp
from jax import lax
from jax.experimental import pallas as pl
from jax.experimental.pallas import tpu as pltpu
from jax.sharding import PartitionSpec as P

HEADS = 16
HEAD_DIM = 128
SEQ_MAX = 160
SPAN = 3

GROUP = 16
HALO = 256
WINDOW = 512
TILE = 128
MESH_ID = pl.DeviceIdType.MESH
VMEM_LIMIT = 60 << 20
PORTIONS = ((0, 48), (48, 48), (96, 32))
ORDERS = ((0, 1, 2), (1, 2, 0), (2, 0, 1))


norm_eps = 1e-05


def layer_norm(residual, gain_vec, shift_vec):
    mean_val = jnp.mean(residual, axis=-1, keepdims=True)
    centred = residual - mean_val
    var_val = jnp.mean(centred * centred, axis=-1, keepdims=True)
    return centred * lax.rsqrt(var_val + norm_eps) * gain_vec + shift_vec


def gelu_tanh(values):
    return jax.nn.gelu(values, approximate=True)


def plan_layout(lengths, tok_dev):
    starts = jnp.cumsum(lengths) - lengths
    owner_first = starts // tok_dev
    return (starts, starts, lengths, owner_first)


def to_owners(shard, layout, dev_count, piece_rows):
    starts, owner_start, owner_length, owner_first = layout
    tok_dev = shard.shape[0]
    feat_width = shard.shape[1]
    device = lax.axis_index("dp")
    held_rows = lax.all_to_all(
        shard.reshape(dev_count, piece_rows, feat_width),
        "dp",
        split_axis=0,
        concat_axis=0,
        tiled=True,
    )
    held_rows = held_rows.reshape(dev_count * piece_rows, feat_width)
    slot_ids = jnp.arange(SPAN * piece_rows, dtype=jnp.int32)
    shard_step = slot_ids // piece_rows
    within = slot_ids % piece_rows
    source = owner_first[:, None] + shard_step[None, :]
    global_row = source * tok_dev + device * piece_rows + within[None, :]
    inside = (
        (global_row >= owner_start[:, None])
        & (global_row < (owner_start + owner_length)[:, None])
        & (source < dev_count)
    )
    picked = held_rows[jnp.clip(source, 0, dev_count - 1) * piece_rows + within[None, :]]
    outgoing = jnp.where(inside[:, :, None], picked, jnp.zeros((), picked.dtype))
    arrived = lax.all_to_all(outgoing, "dp", split_axis=0, concat_axis=0, tiled=True)
    arrived = arrived.reshape(dev_count * SPAN * piece_rows, feat_width)
    my_start = owner_start[device]
    my_length = owner_length[device]
    my_first = owner_first[device]
    places = jnp.arange(SEQ_MAX, dtype=jnp.int32)
    global_pos = my_start + places
    shard_of = global_pos // tok_dev
    offset_in = global_pos % tok_dev
    slot_index = (
        offset_in // piece_rows * (SPAN * piece_rows)
        + (shard_of - my_first) * piece_rows
        + offset_in % piece_rows
    )
    valid_rows = places < my_length
    slot_index = jnp.where(valid_rows, slot_index, 0)
    owned = jnp.where(valid_rows[:, None], arrived[slot_index], jnp.zeros((), arrived.dtype))
    return (owned, valid_rows)


def to_order(owned, layout, dev_count, piece_rows, tok_dev):
    starts, owner_start, owner_length, owner_first = layout
    feat_width = owned.shape[1]
    device = lax.axis_index("dp")
    my_start = owner_start[device]
    my_length = owner_length[device]
    my_first = owner_first[device]
    slot_ids = jnp.arange(SPAN * piece_rows, dtype=jnp.int32)
    shard_step = slot_ids // piece_rows
    within = slot_ids % piece_rows
    targets = jnp.arange(dev_count, dtype=jnp.int32)
    global_row = (
        (my_first + shard_step)[None, :] * tok_dev + targets[:, None] * piece_rows + within[None, :]
    )
    place_row = global_row - my_start
    inside = (place_row >= 0) & (place_row < my_length)
    picked = owned[jnp.clip(place_row, 0, owned.shape[0] - 1)]
    outgoing = jnp.where(inside[:, :, None], picked, jnp.zeros((), picked.dtype))
    returned = lax.all_to_all(outgoing, "dp", split_axis=0, concat_axis=0, tiled=True)
    returned = returned.reshape(dev_count * SPAN * piece_rows, feat_width)
    sources = jnp.arange(dev_count, dtype=jnp.int32)
    within_piece = jnp.arange(piece_rows, dtype=jnp.int32)
    row_ids = sources[:, None] * tok_dev + device * piece_rows + within_piece[None, :]
    seq_of = jnp.sum((row_ids[:, :, None] >= starts[None, None, :]).astype(jnp.int32), 2) - 1
    slot_index = (
        seq_of * (SPAN * piece_rows)
        + (sources[:, None] - owner_first[seq_of]) * piece_rows
        + within_piece[None, :]
    )
    pieces = returned[slot_index]
    ordered = lax.all_to_all(pieces, "dp", split_axis=0, concat_axis=0, tiled=True)
    return ordered.reshape(tok_dev, feat_width)


def per_device(
    tokens,
    cotangent,
    lengths,
    wq,
    bq,
    wk,
    wv,
    bv,
    wo,
    bo,
    norm1_gain,
    norm1_bias,
    w1,
    b1,
    w2,
    b2,
    norm2_gain,
    norm2_bias,
):
    f32 = jnp.float32
    bf16 = jnp.bfloat16
    dev_count = lax.axis_size("dp")
    tok_dev = tokens.shape[0]
    feat_width = tokens.shape[1]
    piece_rows = tok_dev // dev_count
    layout = plan_layout(lengths, tok_dev)
    joined, valid_rows = to_owners(
        jnp.concatenate([tokens, cotangent], 1), layout, dev_count, piece_rows
    )
    inputs = joined[:, :feat_width]
    upstream = joined[:, feat_width:].astype(f32)
    slot_count = inputs.shape[0]
    score_scale = HEAD_DIM ** (-0.5)
    full_wq, full_wk, full_wv, full_wo, full_bq, full_bv, full_bo, gain_one, shift_one = (
        lax.all_gather(wq, "dp", axis=0, tiled=True),
        lax.all_gather(wk, "dp", axis=0, tiled=True),
        lax.all_gather(wv, "dp", axis=0, tiled=True),
        lax.all_gather(wo, "dp", axis=0, tiled=True),
        lax.all_gather(bq, "dp", axis=0, tiled=True),
        lax.all_gather(bv, "dp", axis=0, tiled=True),
        lax.all_gather(bo, "dp", axis=0, tiled=True),
        lax.all_gather(norm1_gain, "dp", axis=0, tiled=True),
        lax.all_gather(norm1_bias, "dp", axis=0, tiled=True),
    )
    queries = (
        (jnp.dot(inputs, full_wq, preferred_element_type=f32) + full_bq.astype(f32))
        .astype(bf16)
        .reshape(slot_count, HEADS, HEAD_DIM)
    )
    keys_low = (
        jnp.dot(inputs, full_wk, preferred_element_type=f32)
        .astype(bf16)
        .reshape(slot_count, HEADS, HEAD_DIM)
    )
    values_low = (
        (jnp.dot(inputs, full_wv, preferred_element_type=f32) + full_bv.astype(f32))
        .astype(bf16)
        .reshape(slot_count, HEADS, HEAD_DIM)
    )
    scores = jnp.einsum("qhd,khd->hqk", queries, keys_low, preferred_element_type=f32) * score_scale
    scores = jnp.where(valid_rows[None, None, :], scores, -1e30)
    row_max = jnp.max(scores, -1, keepdims=True)
    row_total = jnp.sum(jnp.exp(scores - row_max), -1, keepdims=True)
    log_total = row_max + jnp.log(row_total)
    attn_probs = jnp.exp(scores - log_total).astype(bf16)
    attended = jnp.einsum("hqk,khd->qhd", attn_probs, values_low, preferred_element_type=f32)
    attended = attended.reshape(slot_count, feat_width).astype(bf16)
    branch = jnp.dot(attended, full_wo, preferred_element_type=f32) + full_bo.astype(f32)
    resid_one = inputs.astype(f32) + branch
    hidden, norm_one_back = jax.vjp(
        layer_norm, resid_one, gain_one.astype(f32), shift_one.astype(f32)
    )
    hidden_low = hidden.astype(bf16)
    full_w1, full_w2, full_b1, full_b2, gain_two, shift_two = (
        lax.all_gather(w1, "dp", axis=0, tiled=True),
        lax.all_gather(w2, "dp", axis=0, tiled=True),
        lax.all_gather(b1, "dp", axis=0, tiled=True),
        lax.all_gather(b2, "dp", axis=0, tiled=True),
        lax.all_gather(norm2_gain, "dp", axis=0, tiled=True),
        lax.all_gather(norm2_bias, "dp", axis=0, tiled=True),
    )
    upward = jnp.dot(hidden_low, full_w1, preferred_element_type=f32) + full_b1.astype(f32)
    activ, gelu_back = jax.vjp(gelu_tanh, upward)
    activ_low = activ.astype(bf16)
    mixed = jnp.dot(activ_low, full_w2, preferred_element_type=f32) + full_b2.astype(f32)
    resid_two = hidden + mixed
    normed, norm_two_back = jax.vjp(
        layer_norm, resid_two, gain_two.astype(f32), shift_two.astype(f32)
    )
    result = jnp.where(valid_rows[:, None], normed, 0.0).astype(bf16)
    output = to_order(result, layout, dev_count, piece_rows, tok_dev)
    back_w1, back_w2 = (
        lax.all_gather(w1, "dp", axis=0, tiled=True),
        lax.all_gather(w2, "dp", axis=0, tiled=True),
    )
    grad_resid_two, grad_gain_two, grad_shift_two = norm_two_back(upstream)
    grad_mixed = grad_resid_two.astype(bf16)
    grad_bias_two = jnp.sum(grad_mixed.astype(f32), 0)
    grad_activ = jnp.einsum("td,fd->tf", grad_mixed, back_w2, preferred_element_type=f32)
    grad_upward = gelu_back(grad_activ)[0].astype(bf16)
    grad_bias_one = jnp.sum(grad_upward.astype(f32), 0)
    grad_hidden = grad_resid_two + jnp.einsum(
        "tf,df->td", grad_upward, back_w1, preferred_element_type=f32
    )
    grad_w2 = jnp.einsum("tf,td->fd", activ_low, grad_mixed, preferred_element_type=f32)
    grad_w1 = jnp.einsum("td,tf->df", hidden_low, grad_upward, preferred_element_type=f32)
    mlp_grads = (
        lax.psum_scatter(grad_w1, "dp", scatter_dimension=0, tiled=True),
        lax.psum_scatter(grad_w2, "dp", scatter_dimension=0, tiled=True),
        lax.psum_scatter(grad_bias_one, "dp", scatter_dimension=0, tiled=True),
        lax.psum_scatter(grad_bias_two, "dp", scatter_dimension=0, tiled=True),
        lax.psum_scatter(grad_gain_two, "dp", scatter_dimension=0, tiled=True),
        lax.psum_scatter(grad_shift_two, "dp", scatter_dimension=0, tiled=True),
    )
    back_wq, back_wk, back_wv, back_wo = (
        lax.all_gather(wq, "dp", axis=0, tiled=True),
        lax.all_gather(wk, "dp", axis=0, tiled=True),
        lax.all_gather(wv, "dp", axis=0, tiled=True),
        lax.all_gather(wo, "dp", axis=0, tiled=True),
    )
    grad_resid_one, grad_gain_one, grad_shift_one = norm_one_back(grad_hidden)
    grad_branch = grad_resid_one.astype(bf16)
    grad_bo = jnp.sum(grad_branch.astype(f32), 0)
    grad_wo = jnp.einsum("tc,td->cd", attended, grad_branch, preferred_element_type=f32)
    grad_attended = jnp.einsum(
        "td,cd->tc", grad_branch, back_wo, preferred_element_type=f32
    ).astype(bf16)
    grad_attended = grad_attended.reshape(slot_count, HEADS, HEAD_DIM)
    re_scores = (
        jnp.einsum("qhd,khd->hqk", queries, keys_low, preferred_element_type=f32) * score_scale
    )
    re_scores = jnp.where(valid_rows[None, None, :], re_scores, -1e30)
    re_probs = jnp.exp(re_scores - log_total)
    re_probs_low = re_probs.astype(bf16)
    grad_values = jnp.einsum(
        "hqk,qhd->khd", re_probs_low, grad_attended, preferred_element_type=f32
    ).astype(bf16)
    grad_probs = jnp.einsum("qhd,khd->hqk", grad_attended, values_low, preferred_element_type=f32)
    grad_scores = re_probs * (grad_probs - jnp.sum(re_probs * grad_probs, -1, keepdims=True))
    grad_scores_low = grad_scores.astype(bf16)
    grad_queries = (
        jnp.einsum("hqk,khd->qhd", grad_scores_low, keys_low, preferred_element_type=f32)
        * score_scale
    ).astype(bf16)
    grad_keys = (
        jnp.einsum("hqk,qhd->khd", grad_scores_low, queries, preferred_element_type=f32)
        * score_scale
    ).astype(bf16)
    grad_queries = grad_queries.reshape(slot_count, feat_width)
    grad_keys = grad_keys.reshape(slot_count, feat_width)
    grad_values = grad_values.reshape(slot_count, feat_width)
    grad_bq = jnp.sum(grad_queries.astype(f32), 0)
    grad_bv = jnp.sum(grad_values.astype(f32), 0)
    grad_wq = jnp.einsum("tc,td->cd", inputs, grad_queries, preferred_element_type=f32)
    grad_wk = jnp.einsum("tc,td->cd", inputs, grad_keys, preferred_element_type=f32)
    grad_wv = jnp.einsum("tc,td->cd", inputs, grad_values, preferred_element_type=f32)
    grad_input = grad_resid_one + jnp.einsum(
        "td,cd->tc", grad_queries, back_wq, preferred_element_type=f32
    )
    grad_input = grad_input + jnp.einsum(
        "td,cd->tc", grad_keys, back_wk, preferred_element_type=f32
    )
    grad_input = grad_input + jnp.einsum(
        "td,cd->tc", grad_values, back_wv, preferred_element_type=f32
    )
    grad_input = jnp.where(valid_rows[:, None], grad_input, 0.0).astype(bf16)
    attn_grads = (
        lax.psum_scatter(grad_wq, "dp", scatter_dimension=0, tiled=True),
        lax.psum_scatter(grad_wk, "dp", scatter_dimension=0, tiled=True),
        lax.psum_scatter(grad_wv, "dp", scatter_dimension=0, tiled=True),
        lax.psum_scatter(grad_wo, "dp", scatter_dimension=0, tiled=True),
        lax.psum_scatter(grad_bq, "dp", scatter_dimension=0, tiled=True),
        lax.psum_scatter(grad_bv, "dp", scatter_dimension=0, tiled=True),
        lax.psum_scatter(grad_bo, "dp", scatter_dimension=0, tiled=True),
        lax.psum_scatter(grad_gain_one, "dp", scatter_dimension=0, tiled=True),
        lax.psum_scatter(grad_shift_one, "dp", scatter_dimension=0, tiled=True),
    )
    sum_w1, sum_w2, sum_b1, sum_b2, sum_g2, sum_s2 = mlp_grads
    sum_wq, sum_wk, sum_wv, sum_wo, sum_bq, sum_bv, sum_bo, sum_g1, sum_s1 = attn_grads
    input_grad = to_order(grad_input, layout, dev_count, piece_rows, tok_dev)
    return (
        output,
        input_grad,
        sum_wq,
        sum_bq,
        sum_wk,
        sum_wv,
        sum_bv,
        sum_wo,
        sum_bo,
        sum_g1,
        sum_s1,
        sum_w1,
        sum_b1,
        sum_w2,
        sum_b2,
        sum_g2,
        sum_s2,
    )


def flip(device, bit):
    step = 1 << bit
    return device + step - 2 * step * ((device // step) % 2)


def chip_bits(device):
    return [(device // 2) % 2, (device // 4) % 2, (device // 8) % 2]


def enter(partners):
    barrier = pltpu.get_barrier_semaphore()
    for partner in partners:
        pl.semaphore_signal(barrier, inc=1, device_id=(partner,), device_id_type=MESH_ID)
    pl.semaphore_wait(barrier, len(partners))


def push(src, dst, send_sem, recv_sem, device):
    return pltpu.make_async_remote_copy(
        src_ref=src,
        dst_ref=dst,
        send_sem=send_sem,
        recv_sem=recv_sem,
        device_id=(device,),
        device_id_type=MESH_ID,
    )


def gather_kernel(x_ref, o_ref, local_sem, send_sem, recv_sem, pair_send, pair_recv):
    device = lax.axis_index("dp")
    core = device % 2
    bits = chip_bits(device)
    partners = [flip(device, 1), flip(device, 2), flip(device, 3)]
    pair = flip(device, 0)
    enter(partners + [pair])

    def at(values, rows):
        return o_ref.at[values[2], values[1], values[0], core, rows, slice(None)]

    own = o_ref.at[bits[2], bits[1], bits[0], core]
    local = pltpu.make_async_copy(x_ref, own, local_sem)
    local.start()
    hops, shares = {}, {}

    def hop(part, step):
        first, count = PORTIONS[part]
        rows = pl.ds(first, count)
        values = list(bits)
        for dim in ORDERS[part][:step]:
            values[dim] = slice(None)
        dst = at(values, rows)
        src = x_ref.at[rows, :] if step == 0 else dst
        copy = push(
            src, dst, send_sem.at[part, step], recv_sem.at[part, step], partners[ORDERS[part][step]]
        )
        copy.start()
        hops[part, step] = copy

    def share(part, step):
        first, count = PORTIONS[part]
        rows = pl.ds(first, count)
        values = list(bits)
        if step:
            for dim in ORDERS[part][: step - 1]:
                values[dim] = slice(None)
            dim = ORDERS[part][step - 1]
            values[dim] = 1 - bits[dim]
        dst = at(values, rows)
        src = dst if step else x_ref.at[rows, :]
        copy = push(src, dst, pair_send.at[part, step], pair_recv.at[part, step], pair)
        copy.start()
        shares[part, step] = copy

    for part in range(3):
        hop(part, 0)
    for part in range(3):
        share(part, 0)
    local.wait()
    for step in (1, 2, 3):
        for part in range(3):
            hops[part, step - 1].wait_recv()
            if step < 3:
                hop(part, step)
            share(part, step)
    for copy in shares.values():
        copy.wait()
    for copy in hops.values():
        copy.wait_send()


def group_gather(rows, name, collective_id):
    count, width = rows.shape
    vmem = pl.BlockSpec(memory_space=pltpu.VMEM)
    sems = pltpu.SemaphoreType.DMA
    out = pl.pallas_call(
        gather_kernel,
        out_shape=jax.ShapeDtypeStruct((2, 2, 2, 2, count, width), rows.dtype),
        in_specs=[vmem],
        out_specs=vmem,
        scratch_shapes=[sems, sems((3, 3)), sems((3, 3)), sems((3, 4)), sems((3, 4))],
        compiler_params=pltpu.CompilerParams(
            collective_id=collective_id, has_side_effects=True, vmem_limit_bytes=VMEM_LIMIT
        ),
        name=name,
    )(rows)
    return out.reshape(GROUP * count, width)


def scatter_kernel(
    x_ref, o_ref, pair_in, sums, in_one, in_two, in_three, send_sem, recv_sem, pair_send, pair_recv
):
    device = lax.axis_index("dp")
    core = device % 2
    bits = chip_bits(device)
    partners = [flip(device, 1), flip(device, 2), flip(device, 3)]
    pair = flip(device, 0)
    width = x_ref.shape[-1]
    f32 = jnp.float32
    incoming = (in_one, in_two, in_three)
    enter(partners + [pair])

    def view(ref, values, rows, with_core=None):
        where = (values[2], values[1], values[0])
        if with_core is not None:
            where = where + (with_core,)
        return ref.at[where + (rows, slice(None))]

    shares, hops = {}, {}
    for half in range(2):
        for part in range(3):
            first, count = PORTIONS[part]
            rows = pl.ds(first, count)
            dim = ORDERS[part][0]
            values = [slice(None)] * 3
            values[dim] = 1 - bits[dim] if half == 0 else bits[dim]
            copy = push(
                view(x_ref, values, rows, 1 - core),
                view(pair_in, values, rows),
                pair_send.at[part, half],
                pair_recv.at[part, half],
                pair,
            )
            copy.start()
            shares[part, half] = copy

    def add_up(part, values, arrived, store):
        first, count = PORTIONS[part]

        def body(index, carry):
            rows = pl.ds(pl.multiple_of(first + index * 16, 16), 16)
            where = (values[2], values[1], values[0])
            total = x_ref[where + (core, rows, slice(None))].astype(f32)
            total = total + pair_in[where + (rows, slice(None))].astype(f32)
            for ref in incoming[:arrived]:
                total = total + ref[where + (rows, slice(None))].astype(f32)
            store(where, rows, total)
            return carry

        lax.fori_loop(0, count // 16, body, 0)

    def keep_sum(where, rows, total):
        sums[where + (rows, slice(None))] = total.astype(sums.dtype)

    def finish(where, rows, total):
        o_ref[rows, :] = total

    def hop(part, step):
        first, count = PORTIONS[part]
        order = ORDERS[part]
        values = list(bits)
        values[order[step]] = 1 - bits[order[step]]
        free = order[step + 1 :]
        for mask in range(1 << len(free)):
            slot = list(values)
            for place, dim in enumerate(free):
                slot[dim] = (mask >> place) & 1
            add_up(part, slot, step, keep_sum)
        for dim in free:
            values[dim] = slice(None)
        rows = pl.ds(first, count)
        copy = push(
            view(sums, values, rows),
            view(incoming[step], values, rows),
            send_sem.at[part, step],
            recv_sem.at[part, step],
            partners[order[step]],
        )
        copy.start()
        hops[part, step] = copy

    for part in range(3):
        shares[part, 0].wait_recv()
        hop(part, 0)
    for part in range(3):
        shares[part, 1].wait_recv()
        hops[part, 0].wait_recv()
        hop(part, 1)
    for part in range(3):
        hops[part, 1].wait_recv()
        hop(part, 2)
    for part in range(3):
        hops[part, 2].wait_recv()
        add_up(part, bits, 3, finish)
    for copy in shares.values():
        copy.wait_send()
    for copy in hops.values():
        copy.wait_send()


def group_scatter(partial, name, collective_id):
    width = partial.shape[-1]
    count = partial.shape[0] // GROUP
    low = partial.dtype
    vmem = pl.BlockSpec(memory_space=pltpu.VMEM)
    sems = pltpu.SemaphoreType.DMA
    slots = pltpu.VMEM((2, 2, 2, count, width), low)
    return pl.pallas_call(
        scatter_kernel,
        out_shape=jax.ShapeDtypeStruct((count, width), jnp.float32),
        in_specs=[vmem],
        out_specs=vmem,
        scratch_shapes=[
            slots, slots, slots, slots, slots,
            sems((3, 3)), sems((3, 3)), sems((3, 2)), sems((3, 2)),
        ],
        compiler_params=pltpu.CompilerParams(
            collective_id=collective_id, has_side_effects=True, vmem_limit_bytes=VMEM_LIMIT
        ),
        name=name,
    )(partial.reshape(2, 2, 2, 2, count, width))


def exchange_blocks(pairs, sems, base, mine, others):
    local_sem, send_sem, recv_sem = sems
    copies = []
    for at, (src, dst) in enumerate(pairs):
        for step, other in enumerate(others):
            copy = push(
                src.at[other - base],
                dst.at[mine],
                send_sem.at[at, step],
                recv_sem.at[at, step],
                other,
            )
            copy.start()
            copies.append(copy)
        local = pltpu.make_async_copy(src.at[mine], dst.at[mine], local_sem.at[at])
        local.start()
        copies.append(local)
    return copies


def group_places():
    device = lax.axis_index("dp")
    base = device // GROUP * GROUP
    mine = device % GROUP
    others = [base + (mine + step) % GROUP for step in range(1, GROUP)]
    across = (device + GROUP) % (2 * GROUP)
    return device // GROUP, base, mine, others, across


def weights_out_kernel(
    qkv_ref, w1_ref, vec_ref, qkv_out, w1_out, vec_out,
    local_sem, send_sem, recv_sem, vec_local, far_send, far_recv, vec_send, vec_recv,
):
    group, base, mine, others, across = group_places()
    enter(others + [across])
    far = push(vec_ref, vec_out.at[group, mine], far_send, far_recv, across)
    far.start()
    local = pltpu.make_async_copy(vec_ref, vec_out.at[group, mine], vec_local)
    local.start()
    copies = exchange_blocks(
        [(qkv_ref, qkv_out), (w1_ref, w1_out)], (local_sem, send_sem, recv_sem), base, mine, others
    )
    local.wait()
    far.wait()
    both = vec_out.at[:, mine]
    for step, other in enumerate(others):
        copy = push(both, both, vec_send.at[step], vec_recv.at[step], other)
        copy.start()
        copies.append(copy)
    for copy in copies:
        copy.wait()


def weights_out(pack_qkv, pack_w1, vector):
    anywhere = pl.BlockSpec(memory_space=pl.ANY)
    vmem = pl.BlockSpec(memory_space=pltpu.VMEM)
    sems = pltpu.SemaphoreType.DMA
    peers = GROUP - 1
    return pl.pallas_call(
        weights_out_kernel,
        out_shape=[
            jax.ShapeDtypeStruct(pack_qkv.shape, pack_qkv.dtype),
            jax.ShapeDtypeStruct(pack_w1.shape, pack_w1.dtype),
            jax.ShapeDtypeStruct((2, GROUP) + vector.shape, vector.dtype),
        ],
        in_specs=[anywhere, anywhere, vmem],
        out_specs=[anywhere, anywhere, vmem],
        scratch_shapes=[
            sems((2,)), sems((2, peers)), sems((2, peers)),
            sems, sems, sems, sems((peers,)), sems((peers,)),
        ],
        compiler_params=pltpu.CompilerParams(
            collective_id=1, has_side_effects=True, vmem_limit_bytes=VMEM_LIMIT
        ),
        name="weights_out",
    )(pack_qkv, pack_w1, vector)


def weights_back_kernel(
    w1_ref, qkv_ref, vec_ref, w1_out, qkv_out, vec_out,
    arrived, theirs, far_in, local_sem, send_sem, recv_sem, vec_sems, vec_send, vec_recv,
    far_send, far_recv,
):
    group, base, mine, others, across = group_places()
    enter(others + [across])
    first = exchange_blocks(
        [(vec_ref, arrived)], (vec_sems, vec_send, vec_recv), base, mine, others
    )
    copies = exchange_blocks(
        [(w1_ref, w1_out), (qkv_ref, qkv_out)], (local_sem, send_sem, recv_sem), base, mine, others
    )
    for copy in first:
        copy.wait()
    total = arrived[0]
    for at in range(1, GROUP):
        total = total + arrived[at]
    rows = total.shape[0] // 2
    low, high = total[:rows], total[rows:]
    theirs[...] = jnp.where(group == 0, high, low)
    far = push(theirs, far_in, far_send, far_recv, across)
    far.start()
    own = jnp.where(group == 0, low, high)
    far.wait()
    vec_out[...] = own + far_in[...]
    for copy in copies:
        copy.wait()


def weights_back(rows_w1, rows_qkv, vectors):
    anywhere = pl.BlockSpec(memory_space=pl.ANY)
    vmem = pl.BlockSpec(memory_space=pltpu.VMEM)
    sems = pltpu.SemaphoreType.DMA
    peers = GROUP - 1
    half = (vectors.shape[1] // 2, vectors.shape[2])
    return pl.pallas_call(
        weights_back_kernel,
        out_shape=[
            jax.ShapeDtypeStruct(rows_w1.shape, rows_w1.dtype),
            jax.ShapeDtypeStruct(rows_qkv.shape, rows_qkv.dtype),
            jax.ShapeDtypeStruct(half, vectors.dtype),
        ],
        in_specs=[anywhere, anywhere, vmem],
        out_specs=[anywhere, anywhere, vmem],
        scratch_shapes=[
            pltpu.VMEM(vectors.shape, vectors.dtype),
            pltpu.VMEM(half, vectors.dtype),
            pltpu.VMEM(half, vectors.dtype),
            sems((2,)), sems((2, peers)), sems((2, peers)),
            sems((1,)), sems((1, peers)), sems((1, peers)), sems, sems,
        ],
        compiler_params=pltpu.CompilerParams(
            collective_id=10, has_side_effects=True, vmem_limit_bytes=VMEM_LIMIT
        ),
        name="weights_back",
    )(rows_w1, rows_qkv, vectors)


def window_start(row, total):
    start = jnp.minimum(jnp.maximum(row - (WINDOW - TILE) // 2, 0), total - WINDOW)
    return pl.multiple_of(start, 64)


def tile_probs(qkv_ref, row, start, seg_q, seg_k):
    f32 = jnp.float32
    queries = qkv_ref[pl.ds(row, TILE), 0:HEAD_DIM]
    keys = qkv_ref[pl.ds(start, WINDOW), HEAD_DIM : 2 * HEAD_DIM]
    scores = lax.dot_general(queries, keys, (((1,), (1,)), ((), ())), preferred_element_type=f32)
    scores = jnp.where(seg_q == seg_k, scores * HEAD_DIM ** (-0.5), -1e30)
    weights = jnp.exp(scores - jnp.max(scores, -1, keepdims=True))
    return queries, keys, weights / jnp.sum(weights, -1, keepdims=True)


def attend_kernel(offset_ref, qkv_ref, seg_q_ref, seg_k_ref, o_ref):
    total = qkv_ref.shape[0]
    offset = offset_ref[0]

    def body(tile, carry):
        row = pl.multiple_of(offset + tile * TILE, TILE)
        start = window_start(row, total)
        _, _, probs = tile_probs(
            qkv_ref, row, start, seg_q_ref[pl.ds(row, TILE), :], seg_k_ref[row // TILE]
        )
        values = qkv_ref[pl.ds(start, WINDOW), 2 * HEAD_DIM : 3 * HEAD_DIM]
        out = jnp.dot(probs.astype(values.dtype), values, preferred_element_type=jnp.float32)
        o_ref[pl.ds(pl.multiple_of(tile * TILE, TILE), TILE), :] = out.astype(o_ref.dtype)
        return carry

    lax.fori_loop(0, o_ref.shape[0] // TILE, body, 0, unroll=2)


def attend_back_kernel(qkv_ref, grad_ref, seg_q_ref, seg_k_ref, o_ref, dq_sum, dk_sum, dv_sum):
    total = qkv_ref.shape[0]
    f32 = jnp.float32
    low = qkv_ref.dtype
    scale = HEAD_DIM ** (-0.5)
    dk_sum[...] = jnp.zeros_like(dk_sum)
    dv_sum[...] = jnp.zeros_like(dv_sum)

    def body(tile, carry):
        row = pl.multiple_of(tile * TILE, TILE)
        start = window_start(row, total)
        queries, keys, probs = tile_probs(
            qkv_ref, row, start, seg_q_ref[pl.ds(row, TILE), :], seg_k_ref[tile]
        )
        window = pl.ds(start, WINDOW)
        values = qkv_ref[window, 2 * HEAD_DIM : 3 * HEAD_DIM]
        grads = grad_ref[pl.ds(row, TILE), :]
        grad_probs = lax.dot_general(
            grads, values, (((1,), (1,)), ((), ())), preferred_element_type=f32
        )
        inner = jnp.sum(probs * grad_probs, -1, keepdims=True)
        grad_scores = (probs * (grad_probs - inner)).astype(low)
        dq_sum[pl.ds(row, TILE), :] = jnp.dot(grad_scores, keys, preferred_element_type=f32)
        dk_sum[window, :] += lax.dot_general(
            grad_scores, queries, (((0,), (0,)), ((), ())), preferred_element_type=f32
        )
        dv_sum[window, :] += lax.dot_general(
            probs.astype(low), grads, (((0,), (0,)), ((), ())), preferred_element_type=f32
        )
        return carry

    lax.fori_loop(0, total // TILE, body, 0, unroll=2)
    o_ref[:, 0:HEAD_DIM] = (dq_sum[...] * scale).astype(low)
    o_ref[:, HEAD_DIM : 2 * HEAD_DIM] = (dk_sum[...] * scale).astype(low)
    o_ref[:, 2 * HEAD_DIM : 3 * HEAD_DIM] = dv_sum[...].astype(low)


def attend(offset, qkv, seg_q, seg_k, rows):
    vmem = pl.BlockSpec(memory_space=pltpu.VMEM)
    return pl.pallas_call(
        attend_kernel,
        out_shape=jax.ShapeDtypeStruct((rows, HEAD_DIM), qkv.dtype),
        in_specs=[pl.BlockSpec(memory_space=pltpu.SMEM), vmem, vmem, vmem],
        out_specs=vmem,
        compiler_params=pltpu.CompilerParams(vmem_limit_bytes=VMEM_LIMIT),
        name="attend",
    )(offset, qkv, seg_q, seg_k)


def attend_back(qkv, grads, seg_q, seg_k):
    vmem = pl.BlockSpec(memory_space=pltpu.VMEM)
    total = qkv.shape[0]
    acc = pltpu.VMEM((total, HEAD_DIM), jnp.float32)
    return pl.pallas_call(
        attend_back_kernel,
        out_shape=jax.ShapeDtypeStruct(qkv.shape, qkv.dtype),
        in_specs=[vmem, vmem, vmem, vmem],
        out_specs=vmem,
        scratch_shapes=[acc, acc, acc],
        compiler_params=pltpu.CompilerParams(vmem_limit_bytes=VMEM_LIMIT),
        name="attend_back",
    )(qkv, grads, seg_q, seg_k)


def grouped_device(
    tokens,
    cotangent,
    lengths,
    wq,
    bq,
    wk,
    wv,
    bv,
    wo,
    bo,
    norm1_gain,
    norm1_bias,
    w1,
    b1,
    w2,
    b2,
    norm2_gain,
    norm2_bias,
):
    f32 = jnp.float32
    bf16 = jnp.bfloat16
    devices = lax.axis_size("dp")
    block, width = tokens.shape
    own_rows = GROUP * block
    total_tokens = devices * block
    weight_rows = wq.shape[0]
    unit_rows, units = w2.shape[0], w1.shape[1]
    device = lax.axis_index("dp")
    group, member = device // GROUP, device % GROUP
    chip, core = member // 2, member % 2
    head = core * 8 + chip
    first_group = group == 0
    across = [(at, (at + GROUP) % devices) for at in range(devices)]
    beside = [(at, at + 1 - 2 * (at % 2)) for at in range(devices)]

    def swap(own, other):
        return jnp.where(first_group, own, other), jnp.where(first_group, other, own)

    def in_order(own, other):
        return jnp.concatenate(swap(own, other), 0)

    def by_head(weight):
        return weight.reshape(weight_rows, 2, 8, HEAD_DIM).transpose(2, 1, 0, 3).reshape(
            GROUP, weight_rows, HEAD_DIM
        )

    pack_qkv = jnp.concatenate([by_head(wq), by_head(wk), by_head(wv)], -1)
    pack_w1 = w1.reshape(weight_rows, 2, GROUP, unit_rows).transpose(2, 0, 1, 3).reshape(
        GROUP, weight_rows, 2 * unit_rows
    )
    vectors = [bq, bv, bo, norm1_gain, norm1_bias, b2, norm2_gain, norm2_bias, b1]
    sizes = [item.shape[0] for item in vectors]
    vector = jnp.concatenate(vectors).astype(f32)
    vector = jnp.pad(vector, (0, 1024 - vector.shape[0])).reshape(8, 128)
    own_qkv, own_w1, gathered = weights_out(pack_qkv, pack_w1, vector)
    own_qkv = own_qkv.reshape(GROUP * weight_rows, 3 * HEAD_DIM)
    own_w1 = own_w1.reshape(GROUP * weight_rows, 2 * unit_rows)
    full_qkv = in_order(own_qkv, lax.ppermute(own_qkv, "dp", across))
    wo_beside = lax.ppermute(wo, "dp", beside)
    chip_wo = jnp.concatenate(
        [jnp.where(core == 0, wo, wo_beside), jnp.where(core == 0, wo_beside, wo)], 0
    )
    wo_pairs = [
        (GROUP * g + 2 * k + g, GROUP * (1 - g) + 2 * k + g) for g in range(2) for k in range(8)
    ]
    full_wo = jnp.where(core == group, chip_wo, lax.ppermute(chip_wo, "dp", wo_pairs))
    full_w1 = in_order(own_w1, lax.ppermute(own_w1, "dp", across))
    full_w2 = in_order(w2, lax.ppermute(w2, "dp", across))

    gathered = gathered.reshape(devices, -1)
    whole, at = [], 0
    for size in sizes:
        whole.append(gathered[:, at : at + size].reshape(-1))
        at += size
    all_bq, all_bv, all_bo, gain_one, shift_one, all_b2, gain_two, shift_two, all_b1 = whole
    my_b1 = lax.dynamic_index_in_dim(
        all_b1.reshape(2, GROUP, unit_rows), member, 1, keepdims=False
    ).reshape(-1)
    my_bq = lax.dynamic_slice_in_dim(all_bq, head * HEAD_DIM, HEAD_DIM)
    my_bv = lax.dynamic_slice_in_dim(all_bv, head * HEAD_DIM, HEAD_DIM)
    my_bqkv = jnp.concatenate([my_bq, jnp.zeros_like(my_bq), my_bv])

    ext_rows = own_rows + HALO
    ext_first = group * (own_rows - HALO)
    offset = group * HALO
    starts = jnp.cumsum(lengths) - lengths
    ext_ids = ext_first + jnp.arange(ext_rows, dtype=jnp.int32)
    seg = jnp.sum((ext_ids[:, None] >= starts[None, :]).astype(jnp.int32), 1)
    tile_rows = jnp.arange(ext_rows // TILE, dtype=jnp.int32) * TILE
    tile_starts = jnp.clip(tile_rows - (WINDOW - TILE) // 2, 0, ext_rows - WINDOW)
    key_ids = ext_first + tile_starts[:, None] + jnp.arange(WINDOW, dtype=jnp.int32)[None, :]
    seg_k = jnp.sum((key_ids[:, :, None] >= starts[None, None, :]).astype(jnp.int32), 2)
    seg_k = seg_k[:, None, :]
    seg_q = seg[:, None]

    def with_halo(rows):
        edge = jnp.where(first_group, rows[own_rows - HALO :], rows[:HALO])
        halo = lax.ppermute(edge, "dp", across)
        return jnp.where(
            first_group, jnp.concatenate([rows, halo], 0), jnp.concatenate([halo, rows], 0)
        )

    all_tokens = group_gather(tokens, "gather_tokens", 2)
    qkv = (jnp.dot(all_tokens, full_qkv, preferred_element_type=f32) + my_bqkv).astype(bf16)
    qkv_ext = with_halo(qkv)
    attended = attend(offset.reshape(1), qkv_ext, seg_q, seg_k, own_rows)
    branch_part = jnp.dot(attended, full_wo, preferred_element_type=f32).astype(bf16)
    branch = group_scatter(branch_part, "scatter_branch", 3) + all_bo
    resid_one = tokens.astype(f32) + branch
    hidden, norm_one_back = jax.vjp(layer_norm, resid_one, gain_one, shift_one)

    all_hidden = group_gather(hidden.astype(bf16), "gather_hidden", 4)
    upward = jnp.dot(all_hidden, full_w1, preferred_element_type=f32) + my_b1
    activ, gelu_back = jax.vjp(gelu_tanh, upward)
    activ_low = activ.astype(bf16)
    mixed_part = jnp.dot(activ_low, full_w2, preferred_element_type=f32).astype(bf16)
    mixed = group_scatter(mixed_part, "scatter_mixed", 5) + all_b2
    normed, norm_two_back = jax.vjp(layer_norm, hidden + mixed, gain_two, shift_two)
    output = normed.astype(bf16)

    grad_resid_two, grad_gain_two, grad_shift_two = norm_two_back(cotangent.astype(f32))
    grad_mixed = grad_resid_two.astype(bf16)
    grad_b2 = jnp.sum(grad_mixed.astype(f32), 0)
    all_grad_mixed = group_gather(grad_mixed, "gather_grad_mixed", 6)
    grad_activ = jnp.einsum("td,fd->tf", all_grad_mixed, full_w2, preferred_element_type=f32)
    grad_upward = gelu_back(grad_activ)[0].astype(bf16)
    grad_b1 = jnp.sum(grad_upward.astype(f32), 0)
    hidden_part = jnp.einsum(
        "tf,df->td", grad_upward, full_w1, preferred_element_type=f32
    ).astype(bf16)
    grad_w2 = jnp.einsum("tf,td->fd", activ_low, all_grad_mixed, preferred_element_type=f32)
    grad_w1 = jnp.einsum("td,tf->df", all_hidden, grad_upward, preferred_element_type=f32)

    def across_sum(grad):
        halves = grad.reshape((2, grad.shape[0] // 2) + grad.shape[1:])
        mine = jnp.where(first_group, halves[0], halves[1])
        theirs = jnp.where(first_group, halves[1], halves[0]).astype(bf16)
        return mine + lax.ppermute(theirs, "dp", across).astype(f32)

    out_w2 = across_sum(grad_w2)
    sum_w1 = across_sum(grad_w1)
    grad_hidden = grad_resid_two + group_scatter(hidden_part, "scatter_grad_hidden", 7)

    grad_resid_one, grad_gain_one, grad_shift_one = norm_one_back(grad_hidden)
    grad_branch = grad_resid_one.astype(bf16)
    grad_bo = jnp.sum(grad_branch.astype(f32), 0)
    all_grad_branch = group_gather(grad_branch, "gather_grad_branch", 8)
    grad_attended = jnp.einsum(
        "td,cd->tc", all_grad_branch, full_wo, preferred_element_type=f32
    ).astype(bf16)
    grad_wo = jnp.einsum("tc,td->cd", attended, all_grad_branch, preferred_element_type=f32)
    grad_qkv_ext = attend_back(qkv_ext, with_halo(grad_attended), seg_q, seg_k)
    grad_qkv = lax.dynamic_slice_in_dim(grad_qkv_ext, offset, own_rows, 0)
    grad_bqkv = jnp.sum(grad_qkv.astype(f32), 0)
    input_part = jnp.einsum("tf,df->td", grad_qkv, full_qkv, preferred_element_type=f32)
    grad_wqkv = jnp.einsum("td,tf->df", all_tokens, grad_qkv, preferred_element_type=f32)
    sum_qkv = across_sum(grad_wqkv)
    input_sum = group_scatter(input_part.astype(bf16), "scatter_input", 9)
    input_grad = (grad_resid_one + input_sum).astype(bf16)

    back_pairs = [(dst, src) for src, dst in wo_pairs]
    sum_wo = grad_wo + lax.ppermute(grad_wo.astype(bf16), "dp", back_pairs).astype(f32)
    halves = sum_wo.reshape(2, weight_rows, width)
    mine_wo = jnp.where(core == 0, halves[0], halves[1])
    theirs_wo = jnp.where(core == 0, halves[1], halves[0])
    out_wo = jnp.where(core == group, mine_wo, lax.ppermute(theirs_wo, "dp", beside))
    def place_head(vector):
        return lax.dynamic_update_slice_in_dim(
            jnp.zeros((width,), f32), vector, head * HEAD_DIM, 0
        )

    spread_b1 = lax.dynamic_update_slice_in_dim(
        jnp.zeros((2, GROUP, unit_rows), f32), grad_b1.reshape(2, 1, unit_rows), member, 1
    )
    items = [
        place_head(grad_bqkv[:HEAD_DIM]), place_head(grad_bqkv[2 * HEAD_DIM :]), grad_bo,
        grad_gain_one, grad_shift_one, grad_b2, grad_gain_two, grad_shift_two, spread_b1,
    ]
    parts = jnp.concatenate([item.reshape(2, GROUP, -1) for item in items], 2)
    parts = jnp.pad(parts, ((0, 0), (0, 0), (0, 1024 - parts.shape[2])))
    parts = parts.transpose(1, 0, 2).reshape(GROUP, 16, 128)
    rows_w1, rows_qkv, sums = weights_back(
        sum_w1.astype(bf16).reshape(GROUP, weight_rows, 2 * unit_rows),
        sum_qkv.astype(bf16).reshape(GROUP, weight_rows, 3 * HEAD_DIM),
        parts,
    )
    sums, at = sums.reshape(-1), 0
    small = []
    for size in sizes:
        small.append(sums[at : at + size])
        at += size
    out_bq, out_bv, out_bo, out_g1, out_s1, out_b2, out_g2, out_s2, out_b1 = small
    out_w1 = (
        rows_w1.reshape(GROUP, weight_rows, 2, unit_rows)
        .transpose(1, 2, 0, 3)
        .reshape(weight_rows, units)
        .astype(f32)
    )
    out_q, out_k, out_v = [
        rows_qkv[:, :, at * HEAD_DIM : (at + 1) * HEAD_DIM]
        .reshape(8, 2, weight_rows, HEAD_DIM)
        .transpose(2, 1, 0, 3)
        .reshape(weight_rows, width)
        .astype(f32)
        for at in range(3)
    ]

    return (
        output, input_grad, out_q, out_bq, out_k, out_v, out_bv, out_wo, out_bo, out_g1, out_s1,
        out_w1, out_b1, out_w2, out_b2, out_g2, out_s2,
    )


def solution(mesh):
    in_specs = (
        P("dp", None),
        P("dp", None),
        P(),
        P("dp", None),
        P("dp"),
        P("dp", None),
        P("dp", None),
        P("dp"),
        P("dp", None),
        P("dp"),
        P("dp"),
        P("dp"),
        P("dp", None),
        P("dp"),
        P("dp", None),
        P("dp"),
        P("dp"),
        P("dp"),
    )
    out_specs = (
        P("dp", None),
        P("dp", None),
        P("dp", None),
        P("dp"),
        P("dp", None),
        P("dp", None),
        P("dp"),
        P("dp", None),
        P("dp"),
        P("dp"),
        P("dp"),
        P("dp", None),
        P("dp"),
        P("dp", None),
        P("dp"),
        P("dp"),
        P("dp"),
    )
    two_groups = mesh.shape["dp"] == 2 * GROUP
    return jax.shard_map(
        grouped_device if two_groups else per_device, mesh=mesh, in_specs=in_specs, out_specs=out_specs, check_vma=False
    )
```

```python
import functools

import jax
import jax.numpy as jnp
from jax import lax
from jax.experimental import pallas as pl
from jax.experimental.pallas import tpu as pltpu
from jax.sharding import PartitionSpec as P

HEADS = 16
HEAD_DIM = 128
SEQ_MAX = 160
SPAN = 3

GROUP = 16
HALO = 256
WINDOW = 512
TILE = 128
MESH_ID = pl.DeviceIdType.MESH
VMEM_LIMIT = 60 << 20
PORTIONS = ((0, 48), (48, 48), (96, 32))
ORDERS = ((0, 1, 2), (1, 2, 0), (2, 0, 1))


norm_eps = 1e-05


def layer_norm(residual, gain_vec, shift_vec):
    mean_val = jnp.mean(residual, axis=-1, keepdims=True)
    centred = residual - mean_val
    var_val = jnp.mean(centred * centred, axis=-1, keepdims=True)
    return centred * lax.rsqrt(var_val + norm_eps) * gain_vec + shift_vec


def gelu_tanh(values):
    return jax.nn.gelu(values, approximate=True)


def plan_layout(lengths, tok_dev):
    starts = jnp.cumsum(lengths) - lengths
    owner_first = starts // tok_dev
    return (starts, starts, lengths, owner_first)


def to_owners(shard, layout, dev_count, piece_rows):
    starts, owner_start, owner_length, owner_first = layout
    tok_dev = shard.shape[0]
    feat_width = shard.shape[1]
    device = lax.axis_index("dp")
    held_rows = lax.all_to_all(
        shard.reshape(dev_count, piece_rows, feat_width),
        "dp",
        split_axis=0,
        concat_axis=0,
        tiled=True,
    )
    held_rows = held_rows.reshape(dev_count * piece_rows, feat_width)
    slot_ids = jnp.arange(SPAN * piece_rows, dtype=jnp.int32)
    shard_step = slot_ids // piece_rows
    within = slot_ids % piece_rows
    source = owner_first[:, None] + shard_step[None, :]
    global_row = source * tok_dev + device * piece_rows + within[None, :]
    inside = (
        (global_row >= owner_start[:, None])
        & (global_row < (owner_start + owner_length)[:, None])
        & (source < dev_count)
    )
    picked = held_rows[jnp.clip(source, 0, dev_count - 1) * piece_rows + within[None, :]]
    outgoing = jnp.where(inside[:, :, None], picked, jnp.zeros((), picked.dtype))
    arrived = lax.all_to_all(outgoing, "dp", split_axis=0, concat_axis=0, tiled=True)
    arrived = arrived.reshape(dev_count * SPAN * piece_rows, feat_width)
    my_start = owner_start[device]
    my_length = owner_length[device]
    my_first = owner_first[device]
    places = jnp.arange(SEQ_MAX, dtype=jnp.int32)
    global_pos = my_start + places
    shard_of = global_pos // tok_dev
    offset_in = global_pos % tok_dev
    slot_index = (
        offset_in // piece_rows * (SPAN * piece_rows)
        + (shard_of - my_first) * piece_rows
        + offset_in % piece_rows
    )
    valid_rows = places < my_length
    slot_index = jnp.where(valid_rows, slot_index, 0)
    owned = jnp.where(valid_rows[:, None], arrived[slot_index], jnp.zeros((), arrived.dtype))
    return (owned, valid_rows)


def to_order(owned, layout, dev_count, piece_rows, tok_dev):
    starts, owner_start, owner_length, owner_first = layout
    feat_width = owned.shape[1]
    device = lax.axis_index("dp")
    my_start = owner_start[device]
    my_length = owner_length[device]
    my_first = owner_first[device]
    slot_ids = jnp.arange(SPAN * piece_rows, dtype=jnp.int32)
    shard_step = slot_ids // piece_rows
    within = slot_ids % piece_rows
    targets = jnp.arange(dev_count, dtype=jnp.int32)
    global_row = (
        (my_first + shard_step)[None, :] * tok_dev + targets[:, None] * piece_rows + within[None, :]
    )
    place_row = global_row - my_start
    inside = (place_row >= 0) & (place_row < my_length)
    picked = owned[jnp.clip(place_row, 0, owned.shape[0] - 1)]
    outgoing = jnp.where(inside[:, :, None], picked, jnp.zeros((), picked.dtype))
    returned = lax.all_to_all(outgoing, "dp", split_axis=0, concat_axis=0, tiled=True)
    returned = returned.reshape(dev_count * SPAN * piece_rows, feat_width)
    sources = jnp.arange(dev_count, dtype=jnp.int32)
    within_piece = jnp.arange(piece_rows, dtype=jnp.int32)
    row_ids = sources[:, None] * tok_dev + device * piece_rows + within_piece[None, :]
    seq_of = jnp.sum((row_ids[:, :, None] >= starts[None, None, :]).astype(jnp.int32), 2) - 1
    slot_index = (
        seq_of * (SPAN * piece_rows)
        + (sources[:, None] - owner_first[seq_of]) * piece_rows
        + within_piece[None, :]
    )
    pieces = returned[slot_index]
    ordered = lax.all_to_all(pieces, "dp", split_axis=0, concat_axis=0, tiled=True)
    return ordered.reshape(tok_dev, feat_width)


def per_device(
    tokens,
    cotangent,
    lengths,
    wq,
    bq,
    wk,
    wv,
    bv,
    wo,
    bo,
    norm1_gain,
    norm1_bias,
    w1,
    b1,
    w2,
    b2,
    norm2_gain,
    norm2_bias,
):
    f32 = jnp.float32
    bf16 = jnp.bfloat16
    dev_count = lax.axis_size("dp")
    tok_dev = tokens.shape[0]
    feat_width = tokens.shape[1]
    piece_rows = tok_dev // dev_count
    layout = plan_layout(lengths, tok_dev)
    joined, valid_rows = to_owners(
        jnp.concatenate([tokens, cotangent], 1), layout, dev_count, piece_rows
    )
    inputs = joined[:, :feat_width]
    upstream = joined[:, feat_width:].astype(f32)
    slot_count = inputs.shape[0]
    score_scale = HEAD_DIM ** (-0.5)
    full_wq, full_wk, full_wv, full_wo, full_bq, full_bv, full_bo, gain_one, shift_one = (
        lax.all_gather(wq, "dp", axis=0, tiled=True),
        lax.all_gather(wk, "dp", axis=0, tiled=True),
        lax.all_gather(wv, "dp", axis=0, tiled=True),
        lax.all_gather(wo, "dp", axis=0, tiled=True),
        lax.all_gather(bq, "dp", axis=0, tiled=True),
        lax.all_gather(bv, "dp", axis=0, tiled=True),
        lax.all_gather(bo, "dp", axis=0, tiled=True),
        lax.all_gather(norm1_gain, "dp", axis=0, tiled=True),
        lax.all_gather(norm1_bias, "dp", axis=0, tiled=True),
    )
    queries = (
        (jnp.dot(inputs, full_wq, preferred_element_type=f32) + full_bq.astype(f32))
        .astype(bf16)
        .reshape(slot_count, HEADS, HEAD_DIM)
    )
    keys_low = (
        jnp.dot(inputs, full_wk, preferred_element_type=f32)
        .astype(bf16)
        .reshape(slot_count, HEADS, HEAD_DIM)
    )
    values_low = (
        (jnp.dot(inputs, full_wv, preferred_element_type=f32) + full_bv.astype(f32))
        .astype(bf16)
        .reshape(slot_count, HEADS, HEAD_DIM)
    )
    scores = jnp.einsum("qhd,khd->hqk", queries, keys_low, preferred_element_type=f32) * score_scale
    scores = jnp.where(valid_rows[None, None, :], scores, -1e30)
    row_max = jnp.max(scores, -1, keepdims=True)
    row_total = jnp.sum(jnp.exp(scores - row_max), -1, keepdims=True)
    log_total = row_max + jnp.log(row_total)
    attn_probs = jnp.exp(scores - log_total).astype(bf16)
    attended = jnp.einsum("hqk,khd->qhd", attn_probs, values_low, preferred_element_type=f32)
    attended = attended.reshape(slot_count, feat_width).astype(bf16)
    branch = jnp.dot(attended, full_wo, preferred_element_type=f32) + full_bo.astype(f32)
    resid_one = inputs.astype(f32) + branch
    hidden, norm_one_back = jax.vjp(
        layer_norm, resid_one, gain_one.astype(f32), shift_one.astype(f32)
    )
    hidden_low = hidden.astype(bf16)
    full_w1, full_w2, full_b1, full_b2, gain_two, shift_two = (
        lax.all_gather(w1, "dp", axis=0, tiled=True),
        lax.all_gather(w2, "dp", axis=0, tiled=True),
        lax.all_gather(b1, "dp", axis=0, tiled=True),
        lax.all_gather(b2, "dp", axis=0, tiled=True),
        lax.all_gather(norm2_gain, "dp", axis=0, tiled=True),
        lax.all_gather(norm2_bias, "dp", axis=0, tiled=True),
    )
    upward = jnp.dot(hidden_low, full_w1, preferred_element_type=f32) + full_b1.astype(f32)
    activ, gelu_back = jax.vjp(gelu_tanh, upward)
    activ_low = activ.astype(bf16)
    mixed = jnp.dot(activ_low, full_w2, preferred_element_type=f32) + full_b2.astype(f32)
    resid_two = hidden + mixed
    normed, norm_two_back = jax.vjp(
        layer_norm, resid_two, gain_two.astype(f32), shift_two.astype(f32)
    )
    result = jnp.where(valid_rows[:, None], normed, 0.0).astype(bf16)
    output = to_order(result, layout, dev_count, piece_rows, tok_dev)
    back_w1, back_w2 = (
        lax.all_gather(w1, "dp", axis=0, tiled=True),
        lax.all_gather(w2, "dp", axis=0, tiled=True),
    )
    grad_resid_two, grad_gain_two, grad_shift_two = norm_two_back(upstream)
    grad_mixed = grad_resid_two.astype(bf16)
    grad_bias_two = jnp.sum(grad_mixed.astype(f32), 0)
    grad_activ = jnp.einsum("td,fd->tf", grad_mixed, back_w2, preferred_element_type=f32)
    grad_upward = gelu_back(grad_activ)[0].astype(bf16)
    grad_bias_one = jnp.sum(grad_upward.astype(f32), 0)
    grad_hidden = grad_resid_two + jnp.einsum(
        "tf,df->td", grad_upward, back_w1, preferred_element_type=f32
    )
    grad_w2 = jnp.einsum("tf,td->fd", activ_low, grad_mixed, preferred_element_type=f32)
    grad_w1 = jnp.einsum("td,tf->df", hidden_low, grad_upward, preferred_element_type=f32)
    mlp_grads = (
        lax.psum_scatter(grad_w1, "dp", scatter_dimension=0, tiled=True),
        lax.psum_scatter(grad_w2, "dp", scatter_dimension=0, tiled=True),
        lax.psum_scatter(grad_bias_one, "dp", scatter_dimension=0, tiled=True),
        lax.psum_scatter(grad_bias_two, "dp", scatter_dimension=0, tiled=True),
        lax.psum_scatter(grad_gain_two, "dp", scatter_dimension=0, tiled=True),
        lax.psum_scatter(grad_shift_two, "dp", scatter_dimension=0, tiled=True),
    )
    back_wq, back_wk, back_wv, back_wo = (
        lax.all_gather(wq, "dp", axis=0, tiled=True),
        lax.all_gather(wk, "dp", axis=0, tiled=True),
        lax.all_gather(wv, "dp", axis=0, tiled=True),
        lax.all_gather(wo, "dp", axis=0, tiled=True),
    )
    grad_resid_one, grad_gain_one, grad_shift_one = norm_one_back(grad_hidden)
    grad_branch = grad_resid_one.astype(bf16)
    grad_bo = jnp.sum(grad_branch.astype(f32), 0)
    grad_wo = jnp.einsum("tc,td->cd", attended, grad_branch, preferred_element_type=f32)
    grad_attended = jnp.einsum(
        "td,cd->tc", grad_branch, back_wo, preferred_element_type=f32
    ).astype(bf16)
    grad_attended = grad_attended.reshape(slot_count, HEADS, HEAD_DIM)
    re_scores = (
        jnp.einsum("qhd,khd->hqk", queries, keys_low, preferred_element_type=f32) * score_scale
    )
    re_scores = jnp.where(valid_rows[None, None, :], re_scores, -1e30)
    re_probs = jnp.exp(re_scores - log_total)
    re_probs_low = re_probs.astype(bf16)
    grad_values = jnp.einsum(
        "hqk,qhd->khd", re_probs_low, grad_attended, preferred_element_type=f32
    ).astype(bf16)
    grad_probs = jnp.einsum("qhd,khd->hqk", grad_attended, values_low, preferred_element_type=f32)
    grad_scores = re_probs * (grad_probs - jnp.sum(re_probs * grad_probs, -1, keepdims=True))
    grad_scores_low = grad_scores.astype(bf16)
    grad_queries = (
        jnp.einsum("hqk,khd->qhd", grad_scores_low, keys_low, preferred_element_type=f32)
        * score_scale
    ).astype(bf16)
    grad_keys = (
        jnp.einsum("hqk,qhd->khd", grad_scores_low, queries, preferred_element_type=f32)
        * score_scale
    ).astype(bf16)
    grad_queries = grad_queries.reshape(slot_count, feat_width)
    grad_keys = grad_keys.reshape(slot_count, feat_width)
    grad_values = grad_values.reshape(slot_count, feat_width)
    grad_bq = jnp.sum(grad_queries.astype(f32), 0)
    grad_bv = jnp.sum(grad_values.astype(f32), 0)
    grad_wq = jnp.einsum("tc,td->cd", inputs, grad_queries, preferred_element_type=f32)
    grad_wk = jnp.einsum("tc,td->cd", inputs, grad_keys, preferred_element_type=f32)
    grad_wv = jnp.einsum("tc,td->cd", inputs, grad_values, preferred_element_type=f32)
    grad_input = grad_resid_one + jnp.einsum(
        "td,cd->tc", grad_queries, back_wq, preferred_element_type=f32
    )
    grad_input = grad_input + jnp.einsum(
        "td,cd->tc", grad_keys, back_wk, preferred_element_type=f32
    )
    grad_input = grad_input + jnp.einsum(
        "td,cd->tc", grad_values, back_wv, preferred_element_type=f32
    )
    grad_input = jnp.where(valid_rows[:, None], grad_input, 0.0).astype(bf16)
    attn_grads = (
        lax.psum_scatter(grad_wq, "dp", scatter_dimension=0, tiled=True),
        lax.psum_scatter(grad_wk, "dp", scatter_dimension=0, tiled=True),
        lax.psum_scatter(grad_wv, "dp", scatter_dimension=0, tiled=True),
        lax.psum_scatter(grad_wo, "dp", scatter_dimension=0, tiled=True),
        lax.psum_scatter(grad_bq, "dp", scatter_dimension=0, tiled=True),
        lax.psum_scatter(grad_bv, "dp", scatter_dimension=0, tiled=True),
        lax.psum_scatter(grad_bo, "dp", scatter_dimension=0, tiled=True),
        lax.psum_scatter(grad_gain_one, "dp", scatter_dimension=0, tiled=True),
        lax.psum_scatter(grad_shift_one, "dp", scatter_dimension=0, tiled=True),
    )
    sum_w1, sum_w2, sum_b1, sum_b2, sum_g2, sum_s2 = mlp_grads
    sum_wq, sum_wk, sum_wv, sum_wo, sum_bq, sum_bv, sum_bo, sum_g1, sum_s1 = attn_grads
    input_grad = to_order(grad_input, layout, dev_count, piece_rows, tok_dev)
    return (
        output,
        input_grad,
        sum_wq,
        sum_bq,
        sum_wk,
        sum_wv,
        sum_bv,
        sum_wo,
        sum_bo,
        sum_g1,
        sum_s1,
        sum_w1,
        sum_b1,
        sum_w2,
        sum_b2,
        sum_g2,
        sum_s2,
    )


def flip(device, bit):
    step = 1 << bit
    return device + step - 2 * step * ((device // step) % 2)


def chip_bits(device):
    return [(device // 2) % 2, (device // 4) % 2, (device // 8) % 2]


def enter(partners):
    barrier = pltpu.get_barrier_semaphore()
    for partner in partners:
        pl.semaphore_signal(barrier, inc=1, device_id=(partner,), device_id_type=MESH_ID)
    pl.semaphore_wait(barrier, len(partners))


def push(src, dst, send_sem, recv_sem, device):
    return pltpu.make_async_remote_copy(
        src_ref=src,
        dst_ref=dst,
        send_sem=send_sem,
        recv_sem=recv_sem,
        device_id=(device,),
        device_id_type=MESH_ID,
    )


def gather_kernel(x_ref, o_ref, local_sem, send_sem, recv_sem, pair_send, pair_recv):
    device = lax.axis_index("dp")
    core = device % 2
    bits = chip_bits(device)
    partners = [flip(device, 1), flip(device, 2), flip(device, 3)]
    pair = flip(device, 0)
    enter(partners + [pair])

    def at(values, rows):
        return o_ref.at[values[2], values[1], values[0], core, rows, slice(None)]

    own = o_ref.at[bits[2], bits[1], bits[0], core]
    local = pltpu.make_async_copy(x_ref, own, local_sem)
    local.start()
    hops, shares = {}, {}

    def hop(part, step):
        first, count = PORTIONS[part]
        rows = pl.ds(first, count)
        values = list(bits)
        for dim in ORDERS[part][:step]:
            values[dim] = slice(None)
        dst = at(values, rows)
        src = x_ref.at[rows, :] if step == 0 else dst
        copy = push(
            src, dst, send_sem.at[part, step], recv_sem.at[part, step], partners[ORDERS[part][step]]
        )
        copy.start()
        hops[part, step] = copy

    def share(part, step):
        first, count = PORTIONS[part]
        rows = pl.ds(first, count)
        values = list(bits)
        if step:
            for dim in ORDERS[part][: step - 1]:
                values[dim] = slice(None)
            dim = ORDERS[part][step - 1]
            values[dim] = 1 - bits[dim]
        dst = at(values, rows)
        src = dst if step else x_ref.at[rows, :]
        copy = push(src, dst, pair_send.at[part, step], pair_recv.at[part, step], pair)
        copy.start()
        shares[part, step] = copy

    for part in range(3):
        hop(part, 0)
    for part in range(3):
        share(part, 0)
    local.wait()
    for step in (1, 2, 3):
        for part in range(3):
            hops[part, step - 1].wait_recv()
            if step < 3:
                hop(part, step)
            share(part, step)
    for copy in shares.values():
        copy.wait()
    for copy in hops.values():
        copy.wait_send()


def group_gather(rows, name, collective_id):
    count, width = rows.shape
    vmem = pl.BlockSpec(memory_space=pltpu.VMEM)
    sems = pltpu.SemaphoreType.DMA
    out = pl.pallas_call(
        gather_kernel,
        out_shape=jax.ShapeDtypeStruct((2, 2, 2, 2, count, width), rows.dtype),
        in_specs=[vmem],
        out_specs=vmem,
        scratch_shapes=[sems, sems((3, 3)), sems((3, 3)), sems((3, 4)), sems((3, 4))],
        compiler_params=pltpu.CompilerParams(
            collective_id=collective_id, has_side_effects=True, vmem_limit_bytes=VMEM_LIMIT
        ),
        name=name,
    )(rows)
    return out.reshape(GROUP * count, width)


def scatter_kernel(
    x_ref, o_ref, pair_in, sums, in_one, in_two, in_three, send_sem, recv_sem, pair_send, pair_recv
):
    device = lax.axis_index("dp")
    core = device % 2
    bits = chip_bits(device)
    partners = [flip(device, 1), flip(device, 2), flip(device, 3)]
    pair = flip(device, 0)
    width = x_ref.shape[-1]
    f32 = jnp.float32
    incoming = (in_one, in_two, in_three)
    enter(partners + [pair])

    def view(ref, values, rows, with_core=None):
        where = (values[2], values[1], values[0])
        if with_core is not None:
            where = where + (with_core,)
        return ref.at[where + (rows, slice(None))]

    shares, hops = {}, {}
    for half in range(2):
        for part in range(3):
            first, count = PORTIONS[part]
            rows = pl.ds(first, count)
            dim = ORDERS[part][0]
            values = [slice(None)] * 3
            values[dim] = 1 - bits[dim] if half == 0 else bits[dim]
            copy = push(
                view(x_ref, values, rows, 1 - core),
                view(pair_in, values, rows),
                pair_send.at[part, half],
                pair_recv.at[part, half],
                pair,
            )
            copy.start()
            shares[part, half] = copy

    def add_up(part, values, arrived, store):
        first, count = PORTIONS[part]

        def body(index, carry):
            rows = pl.ds(pl.multiple_of(first + index * 16, 16), 16)
            where = (values[2], values[1], values[0])
            total = x_ref[where + (core, rows, slice(None))].astype(f32)
            total = total + pair_in[where + (rows, slice(None))].astype(f32)
            for ref in incoming[:arrived]:
                total = total + ref[where + (rows, slice(None))].astype(f32)
            store(where, rows, total)
            return carry

        lax.fori_loop(0, count // 16, body, 0)

    def keep_sum(where, rows, total):
        sums[where + (rows, slice(None))] = total.astype(sums.dtype)

    def finish(where, rows, total):
        o_ref[rows, :] = total

    def hop(part, step):
        first, count = PORTIONS[part]
        order = ORDERS[part]
        values = list(bits)
        values[order[step]] = 1 - bits[order[step]]
        free = order[step + 1 :]
        for mask in range(1 << len(free)):
            slot = list(values)
            for place, dim in enumerate(free):
                slot[dim] = (mask >> place) & 1
            add_up(part, slot, step, keep_sum)
        for dim in free:
            values[dim] = slice(None)
        rows = pl.ds(first, count)
        copy = push(
            view(sums, values, rows),
            view(incoming[step], values, rows),
            send_sem.at[part, step],
            recv_sem.at[part, step],
            partners[order[step]],
        )
        copy.start()
        hops[part, step] = copy

    for part in range(3):
        shares[part, 0].wait_recv()
        hop(part, 0)
    for part in range(3):
        shares[part, 1].wait_recv()
        hops[part, 0].wait_recv()
        hop(part, 1)
    for part in range(3):
        hops[part, 1].wait_recv()
        hop(part, 2)
    for part in range(3):
        hops[part, 2].wait_recv()
        add_up(part, bits, 3, finish)
    for copy in shares.values():
        copy.wait_send()
    for copy in hops.values():
        copy.wait_send()


def group_scatter(partial, name, collective_id):
    width = partial.shape[-1]
    count = partial.shape[0] // GROUP
    low = partial.dtype
    vmem = pl.BlockSpec(memory_space=pltpu.VMEM)
    sems = pltpu.SemaphoreType.DMA
    slots = pltpu.VMEM((2, 2, 2, count, width), low)
    return pl.pallas_call(
        scatter_kernel,
        out_shape=jax.ShapeDtypeStruct((count, width), jnp.float32),
        in_specs=[vmem],
        out_specs=vmem,
        scratch_shapes=[
            slots, slots, slots, slots, slots,
            sems((3, 3)), sems((3, 3)), sems((3, 2)), sems((3, 2)),
        ],
        compiler_params=pltpu.CompilerParams(
            collective_id=collective_id, has_side_effects=True, vmem_limit_bytes=VMEM_LIMIT
        ),
        name=name,
    )(partial.reshape(2, 2, 2, 2, count, width))


def exchange_blocks(pairs, sems, base, mine, others):
    local_sem, send_sem, recv_sem = sems
    copies = []
    for at, (src, dst) in enumerate(pairs):
        for step, other in enumerate(others):
            copy = push(
                src.at[other - base],
                dst.at[mine],
                send_sem.at[at, step],
                recv_sem.at[at, step],
                other,
            )
            copy.start()
            copies.append(copy)
        local = pltpu.make_async_copy(src.at[mine], dst.at[mine], local_sem.at[at])
        local.start()
        copies.append(local)
    return copies


def group_places():
    device = lax.axis_index("dp")
    base = device // GROUP * GROUP
    mine = device % GROUP
    others = [base + (mine + step) % GROUP for step in range(1, GROUP)]
    across = (device + GROUP) % (2 * GROUP)
    return device // GROUP, base, mine, others, across


def weights_out_kernel(
    qkv_ref, w1_ref, vec_ref, qkv_out, w1_out, vec_out,
    local_sem, send_sem, recv_sem, vec_local, far_send, far_recv, vec_send, vec_recv,
):
    group, base, mine, others, across = group_places()
    enter(others + [across])
    far = push(vec_ref, vec_out.at[group, mine], far_send, far_recv, across)
    far.start()
    local = pltpu.make_async_copy(vec_ref, vec_out.at[group, mine], vec_local)
    local.start()
    copies = exchange_blocks(
        [(qkv_ref, qkv_out), (w1_ref, w1_out)], (local_sem, send_sem, recv_sem), base, mine, others
    )
    local.wait()
    far.wait()
    both = vec_out.at[:, mine]
    for step, other in enumerate(others):
        copy = push(both, both, vec_send.at[step], vec_recv.at[step], other)
        copy.start()
        copies.append(copy)
    for copy in copies:
        copy.wait()


def weights_out(pack_qkv, pack_w1, vector):
    anywhere = pl.BlockSpec(memory_space=pl.ANY)
    vmem = pl.BlockSpec(memory_space=pltpu.VMEM)
    sems = pltpu.SemaphoreType.DMA
    peers = GROUP - 1
    return pl.pallas_call(
        weights_out_kernel,
        out_shape=[
            jax.ShapeDtypeStruct(pack_qkv.shape, pack_qkv.dtype),
            jax.ShapeDtypeStruct(pack_w1.shape, pack_w1.dtype),
            jax.ShapeDtypeStruct((2, GROUP) + vector.shape, vector.dtype),
        ],
        in_specs=[anywhere, anywhere, vmem],
        out_specs=[anywhere, anywhere, vmem],
        scratch_shapes=[
            sems((2,)), sems((2, peers)), sems((2, peers)),
            sems, sems, sems, sems((peers,)), sems((peers,)),
        ],
        compiler_params=pltpu.CompilerParams(
            collective_id=1, has_side_effects=True, vmem_limit_bytes=VMEM_LIMIT
        ),
        name="weights_out",
    )(pack_qkv, pack_w1, vector)


def weights_back_kernel(
    w1_ref, qkv_ref, vec_ref, w1_out, qkv_out, vec_out,
    arrived, theirs, far_in, local_sem, send_sem, recv_sem, vec_sems, vec_send, vec_recv,
    far_send, far_recv,
):
    group, base, mine, others, across = group_places()
    enter(others + [across])
    first = exchange_blocks(
        [(vec_ref, arrived)], (vec_sems, vec_send, vec_recv), base, mine, others
    )
    copies = exchange_blocks(
        [(w1_ref, w1_out), (qkv_ref, qkv_out)], (local_sem, send_sem, recv_sem), base, mine, others
    )
    for copy in first:
        copy.wait()
    total = arrived[0]
    for at in range(1, GROUP):
        total = total + arrived[at]
    rows = total.shape[0] // 2
    low, high = total[:rows], total[rows:]
    theirs[...] = jnp.where(group == 0, high, low)
    far = push(theirs, far_in, far_send, far_recv, across)
    far.start()
    own = jnp.where(group == 0, low, high)
    far.wait()
    vec_out[...] = own + far_in[...]
    for copy in copies:
        copy.wait()


def weights_back(rows_w1, rows_qkv, vectors):
    anywhere = pl.BlockSpec(memory_space=pl.ANY)
    vmem = pl.BlockSpec(memory_space=pltpu.VMEM)
    sems = pltpu.SemaphoreType.DMA
    peers = GROUP - 1
    half = (vectors.shape[1] // 2, vectors.shape[2])
    return pl.pallas_call(
        weights_back_kernel,
        out_shape=[
            jax.ShapeDtypeStruct(rows_w1.shape, rows_w1.dtype),
            jax.ShapeDtypeStruct(rows_qkv.shape, rows_qkv.dtype),
            jax.ShapeDtypeStruct(half, vectors.dtype),
        ],
        in_specs=[anywhere, anywhere, vmem],
        out_specs=[anywhere, anywhere, vmem],
        scratch_shapes=[
            pltpu.VMEM(vectors.shape, vectors.dtype),
            pltpu.VMEM(half, vectors.dtype),
            pltpu.VMEM(half, vectors.dtype),
            sems((2,)), sems((2, peers)), sems((2, peers)),
            sems((1,)), sems((1, peers)), sems((1, peers)), sems, sems,
        ],
        compiler_params=pltpu.CompilerParams(
            collective_id=10, has_side_effects=True, vmem_limit_bytes=VMEM_LIMIT
        ),
        name="weights_back",
    )(rows_w1, rows_qkv, vectors)


def window_start(row, total):
    start = jnp.minimum(jnp.maximum(row - (WINDOW - TILE) // 2, 0), total - WINDOW)
    return pl.multiple_of(start, 64)


def tile_probs(qkv_ref, row, start, seg_q, seg_k):
    f32 = jnp.float32
    queries = qkv_ref[pl.ds(row, TILE), 0:HEAD_DIM]
    keys = qkv_ref[pl.ds(start, WINDOW), HEAD_DIM : 2 * HEAD_DIM]
    scores = lax.dot_general(queries, keys, (((1,), (1,)), ((), ())), preferred_element_type=f32)
    scores = jnp.where(seg_q == seg_k, scores * HEAD_DIM ** (-0.5), -1e30)
    weights = jnp.exp(scores - jnp.max(scores, -1, keepdims=True))
    return queries, keys, weights / jnp.sum(weights, -1, keepdims=True)


def attend_kernel(offset_ref, qkv_ref, seg_q_ref, seg_k_ref, o_ref):
    total = qkv_ref.shape[0]
    offset = offset_ref[0]

    def body(tile, carry):
        row = pl.multiple_of(offset + tile * TILE, TILE)
        start = window_start(row, total)
        _, _, probs = tile_probs(
            qkv_ref, row, start, seg_q_ref[pl.ds(row, TILE), :], seg_k_ref[row // TILE]
        )
        values = qkv_ref[pl.ds(start, WINDOW), 2 * HEAD_DIM : 3 * HEAD_DIM]
        out = jnp.dot(probs.astype(values.dtype), values, preferred_element_type=jnp.float32)
        o_ref[pl.ds(pl.multiple_of(tile * TILE, TILE), TILE), :] = out.astype(o_ref.dtype)
        return carry

    lax.fori_loop(0, o_ref.shape[0] // TILE, body, 0, unroll=2)


def attend_back_kernel(qkv_ref, grad_ref, seg_q_ref, seg_k_ref, o_ref, dq_sum, dk_sum, dv_sum):
    total = qkv_ref.shape[0]
    f32 = jnp.float32
    low = qkv_ref.dtype
    scale = HEAD_DIM ** (-0.5)
    dk_sum[...] = jnp.zeros_like(dk_sum)
    dv_sum[...] = jnp.zeros_like(dv_sum)

    def body(tile, carry):
        row = pl.multiple_of(tile * TILE, TILE)
        start = window_start(row, total)
        queries, keys, probs = tile_probs(
            qkv_ref, row, start, seg_q_ref[pl.ds(row, TILE), :], seg_k_ref[tile]
        )
        window = pl.ds(start, WINDOW)
        values = qkv_ref[window, 2 * HEAD_DIM : 3 * HEAD_DIM]
        grads = grad_ref[pl.ds(row, TILE), :]
        grad_probs = lax.dot_general(
            grads, values, (((1,), (1,)), ((), ())), preferred_element_type=f32
        )
        inner = jnp.sum(probs * grad_probs, -1, keepdims=True)
        grad_scores = (probs * (grad_probs - inner)).astype(low)
        dq_sum[pl.ds(row, TILE), :] = jnp.dot(grad_scores, keys, preferred_element_type=f32)
        dk_sum[window, :] += lax.dot_general(
            grad_scores, queries, (((0,), (0,)), ((), ())), preferred_element_type=f32
        )
        dv_sum[window, :] += lax.dot_general(
            probs.astype(low), grads, (((0,), (0,)), ((), ())), preferred_element_type=f32
        )
        return carry

    lax.fori_loop(0, total // TILE, body, 0, unroll=2)
    o_ref[:, 0:HEAD_DIM] = (dq_sum[...] * scale).astype(low)
    o_ref[:, HEAD_DIM : 2 * HEAD_DIM] = (dk_sum[...] * scale).astype(low)
    o_ref[:, 2 * HEAD_DIM : 3 * HEAD_DIM] = dv_sum[...].astype(low)


def attend(offset, qkv, seg_q, seg_k, rows):
    vmem = pl.BlockSpec(memory_space=pltpu.VMEM)
    return pl.pallas_call(
        attend_kernel,
        out_shape=jax.ShapeDtypeStruct((rows, HEAD_DIM), qkv.dtype),
        in_specs=[pl.BlockSpec(memory_space=pltpu.SMEM), vmem, vmem, vmem],
        out_specs=vmem,
        compiler_params=pltpu.CompilerParams(vmem_limit_bytes=VMEM_LIMIT),
        name="attend",
    )(offset, qkv, seg_q, seg_k)


def attend_back(qkv, grads, seg_q, seg_k):
    vmem = pl.BlockSpec(memory_space=pltpu.VMEM)
    total = qkv.shape[0]
    acc = pltpu.VMEM((total, HEAD_DIM), jnp.float32)
    return pl.pallas_call(
        attend_back_kernel,
        out_shape=jax.ShapeDtypeStruct(qkv.shape, qkv.dtype),
        in_specs=[vmem, vmem, vmem, vmem],
        out_specs=vmem,
        scratch_shapes=[acc, acc, acc],
        compiler_params=pltpu.CompilerParams(vmem_limit_bytes=VMEM_LIMIT),
        name="attend_back",
    )(qkv, grads, seg_q, seg_k)


CHUNKS = 4
COLUMNS = ((0, 768), (768, 640), (1408, 640))
SPLIT = 256


def step_through(flows):
    waiting, alive = list(flows), []
    while waiting or alive:
        if waiting:
            alive.append(waiting.pop(0))
        alive = [flow for flow in alive if next(flow, "done") != "done"]


class Traffic:
    def __init__(self, sems):
        self.hop_send, self.hop_recv, self.pair_send, self.pair_recv = sems
        device = lax.axis_index("dp")
        self.core = device % 2
        self.bits = chip_bits(device)
        self.partners = [flip(device, 1), flip(device, 2), flip(device, 3)]
        self.pair = flip(device, 0)

    def chips(self, ref, values, columns):
        return ref.at[values[2], values[1], values[0], :, columns]

    def push(self, src, dst, stage, chunk, part, step):
        copy = push(
            src, dst,
            self.hop_send.at[stage, chunk, part, step],
            self.hop_recv.at[stage, chunk, part, step],
            self.partners[ORDERS[part][step]],
        )
        copy.start()
        return copy

    def gather(self, slots, stage, chunk):
        mine = slots.at[self.core]
        hops = {}
        for step in range(3):
            for part, (first, count) in enumerate(COLUMNS):
                if step:
                    hops[part, step - 1].wait_recv()
                values = list(self.bits)
                for dim in ORDERS[part][:step]:
                    values[dim] = slice(None)
                view = self.chips(mine, values, pl.ds(first, count))
                hops[part, step] = self.push(view, view, stage, chunk, part, step)
            yield
        for part in range(3):
            hops[part, 2].wait_recv()
        share = push(
            mine, mine, self.pair_send.at[stage, chunk], self.pair_recv.at[stage, chunk], self.pair
        )
        share.start()
        for copy in hops.values():
            copy.wait_send()
        self.share = share

    def scatter(self, own, pair_in, sums, incoming, share, stage, chunk, finish):
        rows = own.shape[-2]
        f32 = jnp.float32
        hops = {}

        share.wait()
        for step in range(4):
            for part, (first, count) in enumerate(COLUMNS):
                order = ORDERS[part]
                columns = pl.ds(first, count)
                if step:
                    hops[part, step - 1].wait_recv()
                values = list(self.bits)
                free = ()
                if step < 3:
                    values[order[step]] = 1 - self.bits[order[step]]
                    free = order[step + 1 :]
                for mask in range(1 << len(free)):
                    slot = list(values)
                    for place, dim in enumerate(free):
                        slot[dim] = (mask >> place) & 1
                    where = (slot[2], slot[1], slot[0])
                    for row in range(0, rows, 16):
                        at = (slice(row, row + 16), columns)
                        total = own[where + at].astype(f32) + pair_in[where + at].astype(f32)
                        for back in range(step):
                            left = [slot[dim] for dim in (2, 1, 0) if dim not in order[: back + 1]]
                            total = total + incoming[back][tuple(left) + at].astype(f32)
                        if step < 3:
                            sums[where + at] = total.astype(sums.dtype)
                        else:
                            finish(row, first, count, total)
                if step == 3:
                    continue
                for dim in free:
                    values[dim] = slice(None)
                left = tuple(slice(None) for _ in free)
                hops[part, step] = self.push(
                    self.chips(sums, values, columns),
                    incoming[step].at[left + (slice(None), columns)],
                    stage, chunk, part, step,
                )
            if step < 3:
                yield
        for copy in hops.values():
            copy.wait_send()


def ff_kernel(
    low_ref, hid_ref, cot_ref, w1_ref, w2_ref, b1_ref, par_ref,
    out_ref, dhid_ref, vec_ref, gb1_ref, gw2_ref, gw1_ref,
    all_h, all_m, own_part, far_part, pair_in, sums, in_one, in_two, in_three,
    up_ref, act_ref, act_t, dup_ref, dup_t, res_ref, stage_ref,
    hop_send, hop_recv, pair_send, pair_recv, out_sems,
):
    f32, low = jnp.float32, low_ref.dtype
    block, width = low_ref.shape
    rows = block // CHUNKS
    half_rows = rows * GROUP // 2
    units = w1_ref.shape[1]
    net = Traffic((hop_send, hop_recv, pair_send, pair_recv))
    core, bits = net.core, net.bits
    own_slot = (core, bits[2], bits[1], bits[0])
    enter(net.partners + [net.pair])
    vec_ref[...] = jnp.zeros_like(vec_ref)
    gb1_ref[...] = jnp.zeros_like(gb1_ref)
    for chunk in range(CHUNKS):
        all_h[(chunk,) + own_slot] = low_ref[chunk * rows : (chunk + 1) * rows, :]

    def row_at(chunk, side):
        return pl.multiple_of((chunk * 2 + side) * half_rows, half_rows)

    def flat(ref, chunk, side, columns=slice(None)):
        return ref[chunk, side, :, :, :, :, columns].reshape(half_rows, -1)

    def tiles(count, body):
        def step(at, carry):
            body(pl.ds(pl.multiple_of(at * SPLIT, SPLIT), SPLIT))
            return carry

        lax.fori_loop(0, count // SPLIT, step, 0)

    def upward(chunk, side):
        here = pl.ds(row_at(chunk, side), half_rows)

        def body(columns):
            up = jnp.dot(flat(all_h, chunk, side), w1_ref[:, columns], preferred_element_type=f32)
            up = up + b1_ref[0:1, columns]
            up_ref[here, columns] = up
            act = gelu_tanh(up)
            act_ref[:, columns] = act.astype(low)
            act_t[columns, here] = act.T.astype(low)

        tiles(units, body)

    def downward(dst):
        def body(columns):
            part = jnp.dot(act_ref[...], w2_ref[:, columns], preferred_element_type=f32)
            dst[:, :, :, :, columns] = part.astype(low).reshape(2, 2, 2, rows, SPLIT)

        tiles(width, body)

    def up_back(chunk, side):
        here = pl.ds(row_at(chunk, side), half_rows)

        def body(columns):
            grad = lax.dot_general(
                flat(all_m, chunk, side), w2_ref[columns, :],
                (((1,), (1,)), ((), ())), preferred_element_type=f32,
            )
            up = up_ref[here, columns]
            inner = 0.7978845608028654 * (up + 0.044715 * (up * up * up))
            tanh = jnp.tanh(inner)
            slope = 0.5 * (1.0 + tanh) + 0.5 * up * (1.0 - tanh * tanh) * (
                0.7978845608028654 * (1.0 + 0.134145 * (up * up))
            )
            grad = (grad * slope).astype(low)
            dup_ref[:, columns] = grad
            wide = grad.astype(f32)
            gb1_ref[0:1, columns] += jnp.sum(wide, 0, keepdims=True)
            dup_t[columns, here] = wide.T.astype(low)

        tiles(units, body)

    def down_back(dst):
        def body(columns):
            part = lax.dot_general(
                dup_ref[...], w1_ref[columns, :],
                (((1,), (1,)), ((), ())), preferred_element_type=f32,
            )
            dst[:, :, :, :, columns] = part.astype(low).reshape(2, 2, 2, rows, SPLIT)

        tiles(width, body)

    def share_part(stage, chunk):
        copy = push(
            far_part.at[chunk % 2], pair_in.at[chunk],
            pair_send.at[stage, chunk], pair_recv.at[stage, chunk], net.pair,
        )
        copy.start()
        return copy

    def keep(chunk):
        def finish(row, first, count, total):
            res_ref[chunk * rows + row : chunk * rows + row + 16, first : first + count] = total

        return finish

    def norms(chunk):
        for row in range(chunk * rows, (chunk + 1) * rows, 16):
            at = slice(row, row + 16)
            res = hid_ref[at, :] + res_ref[at, :] + par_ref[0:1, :]
            mean = jnp.mean(res, -1, keepdims=True)
            res = res - mean
            scale = lax.rsqrt(jnp.mean(res * res, -1, keepdims=True) + norm_eps)
            res = res * scale
            out_ref[at, :] = (res * par_ref[1:2, :] + par_ref[2:3, :]).astype(low)
            grad = cot_ref[at, :].astype(f32)
            vec_ref[2:3, :] += jnp.sum(grad, 0, keepdims=True)
            vec_ref[1:2, :] += jnp.sum(grad * res, 0, keepdims=True)
            grad = grad * par_ref[1:2, :]
            first = jnp.mean(grad, -1, keepdims=True)
            second = jnp.mean(grad * res, -1, keepdims=True)
            grad = (grad - first - res * second) * scale
            dhid_ref[at, :] = grad
            grad_low = grad.astype(low)
            vec_ref[0:1, :] += jnp.sum(grad_low.astype(f32), 0, keepdims=True)
            at_rows = slice(row - chunk * rows, row - chunk * rows + 16)
            all_m[(chunk,) + own_slot + (at_rows, slice(None))] = grad_low

    def flow(chunk):
        incoming = (in_one.at[chunk], in_two.at[chunk], in_three.at[chunk])
        places = (own_part.at[chunk], pair_in.at[chunk], sums.at[chunk], incoming)
        yield from net.gather(all_h.at[chunk], 0, chunk)
        share = net.share
        upward(chunk, core)
        downward(own_part.at[chunk])
        yield
        share.wait()
        upward(chunk, 1 - core)
        downward(far_part.at[chunk % 2])
        share = share_part(1, chunk)
        yield
        yield from net.scatter(*places, share, 1, chunk, keep(chunk))
        norms(chunk)
        yield from net.gather(all_m.at[chunk], 2, chunk)
        share = net.share
        up_back(chunk, core)
        down_back(own_part.at[chunk])
        yield
        share.wait()
        up_back(chunk, 1 - core)
        down_back(far_part.at[chunk % 2])
        share = share_part(3, chunk)
        yield
        yield from net.scatter(*places, share, 3, chunk, keep(chunk))
        here = slice(chunk * rows, (chunk + 1) * rows)
        dhid_ref[here, :] += res_ref[here, :]

    def weight_grads():
        def product(left_t, right, out, columns):
            total = None
            for chunk in range(CHUNKS):
                for side in range(2):
                    here = slice((chunk * 2 + side) * half_rows, (chunk * 2 + side + 1) * half_rows)
                    term = jnp.dot(
                        left_t[:, here], flat(right, chunk, side, columns),
                        preferred_element_type=f32,
                    )
                    total = term if total is None else total + term
            return total

        def run(left_t, right, out):
            def step(at, carry):
                columns = pl.ds(pl.multiple_of(at * SPLIT, SPLIT), SPLIT)
                slot = at % 2

                @pl.when(at >= 2)
                def _():
                    pltpu.make_async_copy(
                        stage_ref.at[slot], out.at[:, columns], out_sems.at[slot]
                    ).wait()

                stage_ref[slot] = product(left_t, right, out, columns)
                pltpu.make_async_copy(
                    stage_ref.at[slot], out.at[:, columns], out_sems.at[slot]
                ).start()
                return carry

            lax.fori_loop(0, width // SPLIT, step, 0)
            for slot in range(2):
                pltpu.make_async_copy(
                    stage_ref.at[slot], out.at[:, pl.ds(0, SPLIT)], out_sems.at[slot]
                ).wait()

        run(act_t, all_m, gw2_ref)
        run(dup_t, all_h, gw1_ref)

    step_through([flow(chunk) for chunk in range(CHUNKS)])
    weight_grads()


def feed_forward(low, hidden, cotangent, w1, w2, b1, params):
    f32, bf16 = jnp.float32, jnp.bfloat16
    block, width = low.shape
    rows = block // CHUNKS
    units = w1.shape[1]
    half_rows = rows * GROUP // 2
    all_rows = GROUP * block
    vmem = pl.BlockSpec(memory_space=pltpu.VMEM)
    anywhere = pl.BlockSpec(memory_space=pl.ANY)
    sems = pltpu.SemaphoreType.DMA

    def slots(*lead):
        return pltpu.VMEM(lead + (rows, width), bf16)

    return pl.pallas_call(
        ff_kernel,
        out_shape=[
            jax.ShapeDtypeStruct((block, width), bf16),
            jax.ShapeDtypeStruct((block, width), f32),
            jax.ShapeDtypeStruct((8, width), f32),
            jax.ShapeDtypeStruct((8, units), f32),
            jax.ShapeDtypeStruct((units, width), f32),
            jax.ShapeDtypeStruct((units, width), f32),
        ],
        in_specs=[vmem] * 7,
        out_specs=[vmem] * 4 + [anywhere] * 2,
        scratch_shapes=[
            slots(CHUNKS, 2, 2, 2, 2), slots(CHUNKS, 2, 2, 2, 2),
            slots(CHUNKS, 2, 2, 2), slots(2, 2, 2, 2), slots(CHUNKS, 2, 2, 2),
            slots(CHUNKS, 2, 2, 2), slots(CHUNKS, 2, 2), slots(CHUNKS, 2), slots(CHUNKS),
            pltpu.VMEM((all_rows, units), f32),
            pltpu.VMEM((half_rows, units), bf16),
            pltpu.VMEM((units, all_rows), bf16),
            pltpu.VMEM((half_rows, units), bf16),
            pltpu.VMEM((units, all_rows), bf16),
            pltpu.VMEM((block, width), f32),
            pltpu.VMEM((2, units, SPLIT), f32),
            sems((4, CHUNKS, 3, 3)), sems((4, CHUNKS, 3, 3)), sems((4, CHUNKS)), sems((4, CHUNKS)),
            sems((2,)),
        ],
        compiler_params=pltpu.CompilerParams(
            collective_id=4, has_side_effects=True, vmem_limit_bytes=63 << 20
        ),
        name="feed_forward",
    )(low, hidden, cotangent, w1, w2, b1, params)


def grouped_device(
    tokens,
    cotangent,
    lengths,
    wq,
    bq,
    wk,
    wv,
    bv,
    wo,
    bo,
    norm1_gain,
    norm1_bias,
    w1,
    b1,
    w2,
    b2,
    norm2_gain,
    norm2_bias,
):
    f32 = jnp.float32
    bf16 = jnp.bfloat16
    devices = lax.axis_size("dp")
    block, width = tokens.shape
    own_rows = GROUP * block
    total_tokens = devices * block
    weight_rows = wq.shape[0]
    unit_rows, units = w2.shape[0], w1.shape[1]
    device = lax.axis_index("dp")
    group, member = device // GROUP, device % GROUP
    chip, core = member // 2, member % 2
    head = core * 8 + chip
    first_group = group == 0
    across = [(at, (at + GROUP) % devices) for at in range(devices)]
    beside = [(at, at + 1 - 2 * (at % 2)) for at in range(devices)]

    def swap(own, other):
        return jnp.where(first_group, own, other), jnp.where(first_group, other, own)

    def in_order(own, other):
        return jnp.concatenate(swap(own, other), 0)

    def by_head(weight):
        return weight.reshape(weight_rows, 2, 8, HEAD_DIM).transpose(2, 1, 0, 3).reshape(
            GROUP, weight_rows, HEAD_DIM
        )

    pack_qkv = jnp.concatenate([by_head(wq), by_head(wk), by_head(wv)], -1)
    pack_w1 = w1.reshape(weight_rows, 2, GROUP, unit_rows).transpose(2, 0, 1, 3).reshape(
        GROUP, weight_rows, 2 * unit_rows
    )
    vectors = [bq, bv, bo, norm1_gain, norm1_bias, b2, norm2_gain, norm2_bias, b1]
    sizes = [item.shape[0] for item in vectors]
    vector = jnp.concatenate(vectors).astype(f32)
    vector = jnp.pad(vector, (0, 1024 - vector.shape[0])).reshape(8, 128)
    own_qkv, own_w1, gathered = weights_out(pack_qkv, pack_w1, vector)
    own_qkv = own_qkv.reshape(GROUP * weight_rows, 3 * HEAD_DIM)
    own_w1 = own_w1.reshape(GROUP * weight_rows, 2 * unit_rows)
    full_qkv = in_order(own_qkv, lax.ppermute(own_qkv, "dp", across))
    wo_pairs = [
        (GROUP * g + 2 * k + g, GROUP * (1 - g) + 2 * k + g) for g in range(2) for k in range(8)
    ]
    gathered = gathered.reshape(devices, -1)
    whole, at = [], 0
    for size in sizes:
        whole.append(gathered[:, at : at + size].reshape(-1))
        at += size
    all_bq, all_bv, all_bo, gain_one, shift_one, all_b2, gain_two, shift_two, all_b1 = whole
    my_b1 = lax.dynamic_index_in_dim(
        all_b1.reshape(2, GROUP, unit_rows), member, 1, keepdims=False
    ).reshape(-1)
    my_bq = lax.dynamic_slice_in_dim(all_bq, head * HEAD_DIM, HEAD_DIM)
    my_bv = lax.dynamic_slice_in_dim(all_bv, head * HEAD_DIM, HEAD_DIM)
    my_bqkv = jnp.concatenate([my_bq, jnp.zeros_like(my_bq), my_bv])

    ext_rows = own_rows + HALO
    ext_first = group * (own_rows - HALO)
    offset = group * HALO
    starts = jnp.cumsum(lengths) - lengths
    ext_ids = ext_first + jnp.arange(ext_rows, dtype=jnp.int32)
    seg = jnp.sum((ext_ids[:, None] >= starts[None, :]).astype(jnp.int32), 1)
    tile_rows = jnp.arange(ext_rows // TILE, dtype=jnp.int32) * TILE
    tile_starts = jnp.clip(tile_rows - (WINDOW - TILE) // 2, 0, ext_rows - WINDOW)
    key_ids = ext_first + tile_starts[:, None] + jnp.arange(WINDOW, dtype=jnp.int32)[None, :]
    seg_k = jnp.sum((key_ids[:, :, None] >= starts[None, None, :]).astype(jnp.int32), 2)
    seg_k = seg_k[:, None, :]
    seg_q = seg[:, None]

    def with_halo(rows):
        edge = jnp.where(first_group, rows[own_rows - HALO :], rows[:HALO])
        halo = lax.ppermute(edge, "dp", across)
        return jnp.where(
            first_group, jnp.concatenate([rows, halo], 0), jnp.concatenate([halo, rows], 0)
        )

    all_tokens = group_gather(tokens, "gather_tokens", 2)
    all_tokens, own_w1, own_wo = lax.optimization_barrier((all_tokens, own_w1, wo))
    wo_beside = lax.ppermute(own_wo, "dp", beside)
    chip_wo = jnp.concatenate(
        [jnp.where(core == 0, own_wo, wo_beside), jnp.where(core == 0, wo_beside, own_wo)], 0
    )
    full_wo = jnp.where(core == group, chip_wo, lax.ppermute(chip_wo, "dp", wo_pairs))
    full_w1 = in_order(own_w1, lax.ppermute(own_w1, "dp", across))
    qkv = (jnp.dot(all_tokens, full_qkv, preferred_element_type=f32) + my_bqkv).astype(bf16)
    qkv_ext = with_halo(qkv)
    attended = attend(offset.reshape(1), qkv_ext, seg_q, seg_k, own_rows)
    attended, own_w2 = lax.optimization_barrier((attended, w2))
    full_w2 = in_order(own_w2, lax.ppermute(own_w2, "dp", across))
    branch_part = jnp.dot(attended, full_wo, preferred_element_type=f32).astype(bf16)
    branch = group_scatter(branch_part, "scatter_branch", 3) + all_bo
    resid_one = tokens.astype(f32) + branch
    hidden, norm_one_back = jax.vjp(layer_norm, resid_one, gain_one, shift_one)

    params = jnp.pad(jnp.stack([all_b2, gain_two, shift_two]), ((0, 5), (0, 0)))
    output, grad_hidden, vec_two, grad_b1, grad_w2, grad_w1_t = feed_forward(
        hidden.astype(bf16), hidden, cotangent, full_w1, full_w2,
        jnp.broadcast_to(my_b1, (8, my_b1.shape[0])), params,
    )
    grad_b2, grad_gain_two, grad_shift_two = vec_two[0], vec_two[1], vec_two[2]
    grad_b1 = grad_b1[0]

    def across_sum(grad):
        halves = grad.reshape((2, grad.shape[0] // 2) + grad.shape[1:])
        mine = jnp.where(first_group, halves[0], halves[1])
        theirs = jnp.where(first_group, halves[1], halves[0]).astype(bf16)
        return mine + lax.ppermute(theirs, "dp", across).astype(f32)

    out_w2 = across_sum(grad_w2)

    grad_resid_one, grad_gain_one, grad_shift_one = norm_one_back(grad_hidden)
    grad_branch = grad_resid_one.astype(bf16)
    grad_bo = jnp.sum(grad_branch.astype(f32), 0)
    all_grad_branch = group_gather(grad_branch, "gather_grad_branch", 8)
    all_grad_branch, grad_w1_t = lax.optimization_barrier((all_grad_branch, grad_w1_t))
    halves_t = jnp.split(grad_w1_t, 2, 1)
    theirs_t = jnp.where(first_group, halves_t[1], halves_t[0]).astype(bf16)
    sum_w1_t = jnp.where(first_group, halves_t[0], halves_t[1])
    sum_w1_t = sum_w1_t + lax.ppermute(theirs_t, "dp", across).astype(f32)
    sum_w1 = sum_w1_t.astype(bf16).T
    grad_attended = jnp.einsum(
        "td,cd->tc", all_grad_branch, full_wo, preferred_element_type=f32
    ).astype(bf16)
    grad_wo = jnp.einsum("tc,td->cd", attended, all_grad_branch, preferred_element_type=f32)
    grad_qkv_ext = attend_back(qkv_ext, with_halo(grad_attended), seg_q, seg_k)
    grad_qkv = lax.dynamic_slice_in_dim(grad_qkv_ext, offset, own_rows, 0)
    grad_bqkv = jnp.sum(grad_qkv.astype(f32), 0)
    input_part = jnp.einsum("tf,df->td", grad_qkv, full_qkv, preferred_element_type=f32)
    grad_wqkv = jnp.einsum("td,tf->df", all_tokens, grad_qkv, preferred_element_type=f32)
    sum_qkv = across_sum(grad_wqkv)
    input_sum = group_scatter(input_part.astype(bf16), "scatter_input", 9)
    input_grad = (grad_resid_one + input_sum).astype(bf16)

    back_pairs = [(dst, src) for src, dst in wo_pairs]
    sum_wo = grad_wo + lax.ppermute(grad_wo.astype(bf16), "dp", back_pairs).astype(f32)
    halves = sum_wo.reshape(2, weight_rows, width)
    mine_wo = jnp.where(core == 0, halves[0], halves[1])
    theirs_wo = jnp.where(core == 0, halves[1], halves[0])
    out_wo = jnp.where(core == group, mine_wo, lax.ppermute(theirs_wo, "dp", beside))
    def place_head(vector):
        return lax.dynamic_update_slice_in_dim(
            jnp.zeros((width,), f32), vector, head * HEAD_DIM, 0
        )

    spread_b1 = lax.dynamic_update_slice_in_dim(
        jnp.zeros((2, GROUP, unit_rows), f32), grad_b1.reshape(2, 1, unit_rows), member, 1
    )
    items = [
        place_head(grad_bqkv[:HEAD_DIM]), place_head(grad_bqkv[2 * HEAD_DIM :]), grad_bo,
        grad_gain_one, grad_shift_one, grad_b2, grad_gain_two, grad_shift_two, spread_b1,
    ]
    parts = jnp.concatenate([item.reshape(2, GROUP, -1) for item in items], 2)
    parts = jnp.pad(parts, ((0, 0), (0, 0), (0, 1024 - parts.shape[2])))
    parts = parts.transpose(1, 0, 2).reshape(GROUP, 16, 128)
    rows_w1, rows_qkv, sums = weights_back(
        sum_w1.astype(bf16).reshape(GROUP, weight_rows, 2 * unit_rows),
        sum_qkv.astype(bf16).reshape(GROUP, weight_rows, 3 * HEAD_DIM),
        parts,
    )
    sums, at = sums.reshape(-1), 0
    small = []
    for size in sizes:
        small.append(sums[at : at + size])
        at += size
    out_bq, out_bv, out_bo, out_g1, out_s1, out_b2, out_g2, out_s2, out_b1 = small
    out_w1 = (
        rows_w1.reshape(GROUP, weight_rows, 2, unit_rows)
        .transpose(1, 2, 0, 3)
        .reshape(weight_rows, units)
        .astype(f32)
    )
    out_q, out_k, out_v = [
        rows_qkv[:, :, at * HEAD_DIM : (at + 1) * HEAD_DIM]
        .reshape(8, 2, weight_rows, HEAD_DIM)
        .transpose(2, 1, 0, 3)
        .reshape(weight_rows, width)
        .astype(f32)
        for at in range(3)
    ]

    return (
        output, input_grad, out_q, out_bq, out_k, out_v, out_bv, out_wo, out_bo, out_g1, out_s1,
        out_w1, out_b1, out_w2, out_b2, out_g2, out_s2,
    )


def solution(mesh):
    in_specs = (
        P("dp", None),
        P("dp", None),
        P(),
        P("dp", None),
        P("dp"),
        P("dp", None),
        P("dp", None),
        P("dp"),
        P("dp", None),
        P("dp"),
        P("dp"),
        P("dp"),
        P("dp", None),
        P("dp"),
        P("dp", None),
        P("dp"),
        P("dp"),
        P("dp"),
    )
    out_specs = (
        P("dp", None),
        P("dp", None),
        P("dp", None),
        P("dp"),
        P("dp", None),
        P("dp", None),
        P("dp"),
        P("dp", None),
        P("dp"),
        P("dp"),
        P("dp"),
        P("dp", None),
        P("dp"),
        P("dp", None),
        P("dp"),
        P("dp"),
        P("dp"),
    )
    two_groups = mesh.shape["dp"] == 2 * GROUP
    return jax.shard_map(
        grouped_device if two_groups else per_device, mesh=mesh, in_specs=in_specs, out_specs=out_specs, check_vma=False
    )
```

```python
import functools

import jax
import jax.numpy as jnp
from jax import lax
from jax.experimental import pallas as pl
from jax.experimental.pallas import tpu as pltpu
from jax.sharding import PartitionSpec as P

HEADS = 16
HEAD_DIM = 128
SEQ_MAX = 160
SPAN = 3

GROUP = 16
HALO = 256
WINDOW = 512
TILE = 128
MESH_ID = pl.DeviceIdType.MESH
VMEM_LIMIT = 60 << 20
PORTIONS = ((0, 48), (48, 48), (96, 32))
ORDERS = ((0, 1, 2), (1, 2, 0), (2, 0, 1))


norm_eps = 1e-05


def layer_norm(residual, gain_vec, shift_vec):
    mean_val = jnp.mean(residual, axis=-1, keepdims=True)
    centred = residual - mean_val
    var_val = jnp.mean(centred * centred, axis=-1, keepdims=True)
    return centred * lax.rsqrt(var_val + norm_eps) * gain_vec + shift_vec


def gelu_tanh(values):
    return jax.nn.gelu(values, approximate=True)


def plan_layout(lengths, tok_dev):
    starts = jnp.cumsum(lengths) - lengths
    owner_first = starts // tok_dev
    return (starts, starts, lengths, owner_first)


def to_owners(shard, layout, dev_count, piece_rows):
    starts, owner_start, owner_length, owner_first = layout
    tok_dev = shard.shape[0]
    feat_width = shard.shape[1]
    device = lax.axis_index("dp")
    held_rows = lax.all_to_all(
        shard.reshape(dev_count, piece_rows, feat_width),
        "dp",
        split_axis=0,
        concat_axis=0,
        tiled=True,
    )
    held_rows = held_rows.reshape(dev_count * piece_rows, feat_width)
    slot_ids = jnp.arange(SPAN * piece_rows, dtype=jnp.int32)
    shard_step = slot_ids // piece_rows
    within = slot_ids % piece_rows
    source = owner_first[:, None] + shard_step[None, :]
    global_row = source * tok_dev + device * piece_rows + within[None, :]
    inside = (
        (global_row >= owner_start[:, None])
        & (global_row < (owner_start + owner_length)[:, None])
        & (source < dev_count)
    )
    picked = held_rows[jnp.clip(source, 0, dev_count - 1) * piece_rows + within[None, :]]
    outgoing = jnp.where(inside[:, :, None], picked, jnp.zeros((), picked.dtype))
    arrived = lax.all_to_all(outgoing, "dp", split_axis=0, concat_axis=0, tiled=True)
    arrived = arrived.reshape(dev_count * SPAN * piece_rows, feat_width)
    my_start = owner_start[device]
    my_length = owner_length[device]
    my_first = owner_first[device]
    places = jnp.arange(SEQ_MAX, dtype=jnp.int32)
    global_pos = my_start + places
    shard_of = global_pos // tok_dev
    offset_in = global_pos % tok_dev
    slot_index = (
        offset_in // piece_rows * (SPAN * piece_rows)
        + (shard_of - my_first) * piece_rows
        + offset_in % piece_rows
    )
    valid_rows = places < my_length
    slot_index = jnp.where(valid_rows, slot_index, 0)
    owned = jnp.where(valid_rows[:, None], arrived[slot_index], jnp.zeros((), arrived.dtype))
    return (owned, valid_rows)


def to_order(owned, layout, dev_count, piece_rows, tok_dev):
    starts, owner_start, owner_length, owner_first = layout
    feat_width = owned.shape[1]
    device = lax.axis_index("dp")
    my_start = owner_start[device]
    my_length = owner_length[device]
    my_first = owner_first[device]
    slot_ids = jnp.arange(SPAN * piece_rows, dtype=jnp.int32)
    shard_step = slot_ids // piece_rows
    within = slot_ids % piece_rows
    targets = jnp.arange(dev_count, dtype=jnp.int32)
    global_row = (
        (my_first + shard_step)[None, :] * tok_dev + targets[:, None] * piece_rows + within[None, :]
    )
    place_row = global_row - my_start
    inside = (place_row >= 0) & (place_row < my_length)
    picked = owned[jnp.clip(place_row, 0, owned.shape[0] - 1)]
    outgoing = jnp.where(inside[:, :, None], picked, jnp.zeros((), picked.dtype))
    returned = lax.all_to_all(outgoing, "dp", split_axis=0, concat_axis=0, tiled=True)
    returned = returned.reshape(dev_count * SPAN * piece_rows, feat_width)
    sources = jnp.arange(dev_count, dtype=jnp.int32)
    within_piece = jnp.arange(piece_rows, dtype=jnp.int32)
    row_ids = sources[:, None] * tok_dev + device * piece_rows + within_piece[None, :]
    seq_of = jnp.sum((row_ids[:, :, None] >= starts[None, None, :]).astype(jnp.int32), 2) - 1
    slot_index = (
        seq_of * (SPAN * piece_rows)
        + (sources[:, None] - owner_first[seq_of]) * piece_rows
        + within_piece[None, :]
    )
    pieces = returned[slot_index]
    ordered = lax.all_to_all(pieces, "dp", split_axis=0, concat_axis=0, tiled=True)
    return ordered.reshape(tok_dev, feat_width)


def per_device(
    tokens,
    cotangent,
    lengths,
    wq,
    bq,
    wk,
    wv,
    bv,
    wo,
    bo,
    norm1_gain,
    norm1_bias,
    w1,
    b1,
    w2,
    b2,
    norm2_gain,
    norm2_bias,
):
    f32 = jnp.float32
    bf16 = jnp.bfloat16
    dev_count = lax.axis_size("dp")
    tok_dev = tokens.shape[0]
    feat_width = tokens.shape[1]
    piece_rows = tok_dev // dev_count
    layout = plan_layout(lengths, tok_dev)
    joined, valid_rows = to_owners(
        jnp.concatenate([tokens, cotangent], 1), layout, dev_count, piece_rows
    )
    inputs = joined[:, :feat_width]
    upstream = joined[:, feat_width:].astype(f32)
    slot_count = inputs.shape[0]
    score_scale = HEAD_DIM ** (-0.5)
    full_wq, full_wk, full_wv, full_wo, full_bq, full_bv, full_bo, gain_one, shift_one = (
        lax.all_gather(wq, "dp", axis=0, tiled=True),
        lax.all_gather(wk, "dp", axis=0, tiled=True),
        lax.all_gather(wv, "dp", axis=0, tiled=True),
        lax.all_gather(wo, "dp", axis=0, tiled=True),
        lax.all_gather(bq, "dp", axis=0, tiled=True),
        lax.all_gather(bv, "dp", axis=0, tiled=True),
        lax.all_gather(bo, "dp", axis=0, tiled=True),
        lax.all_gather(norm1_gain, "dp", axis=0, tiled=True),
        lax.all_gather(norm1_bias, "dp", axis=0, tiled=True),
    )
    queries = (
        (jnp.dot(inputs, full_wq, preferred_element_type=f32) + full_bq.astype(f32))
        .astype(bf16)
        .reshape(slot_count, HEADS, HEAD_DIM)
    )
    keys_low = (
        jnp.dot(inputs, full_wk, preferred_element_type=f32)
        .astype(bf16)
        .reshape(slot_count, HEADS, HEAD_DIM)
    )
    values_low = (
        (jnp.dot(inputs, full_wv, preferred_element_type=f32) + full_bv.astype(f32))
        .astype(bf16)
        .reshape(slot_count, HEADS, HEAD_DIM)
    )
    scores = jnp.einsum("qhd,khd->hqk", queries, keys_low, preferred_element_type=f32) * score_scale
    scores = jnp.where(valid_rows[None, None, :], scores, -1e30)
    row_max = jnp.max(scores, -1, keepdims=True)
    row_total = jnp.sum(jnp.exp(scores - row_max), -1, keepdims=True)
    log_total = row_max + jnp.log(row_total)
    attn_probs = jnp.exp(scores - log_total).astype(bf16)
    attended = jnp.einsum("hqk,khd->qhd", attn_probs, values_low, preferred_element_type=f32)
    attended = attended.reshape(slot_count, feat_width).astype(bf16)
    branch = jnp.dot(attended, full_wo, preferred_element_type=f32) + full_bo.astype(f32)
    resid_one = inputs.astype(f32) + branch
    hidden, norm_one_back = jax.vjp(
        layer_norm, resid_one, gain_one.astype(f32), shift_one.astype(f32)
    )
    hidden_low = hidden.astype(bf16)
    full_w1, full_w2, full_b1, full_b2, gain_two, shift_two = (
        lax.all_gather(w1, "dp", axis=0, tiled=True),
        lax.all_gather(w2, "dp", axis=0, tiled=True),
        lax.all_gather(b1, "dp", axis=0, tiled=True),
        lax.all_gather(b2, "dp", axis=0, tiled=True),
        lax.all_gather(norm2_gain, "dp", axis=0, tiled=True),
        lax.all_gather(norm2_bias, "dp", axis=0, tiled=True),
    )
    upward = jnp.dot(hidden_low, full_w1, preferred_element_type=f32) + full_b1.astype(f32)
    activ, gelu_back = jax.vjp(gelu_tanh, upward)
    activ_low = activ.astype(bf16)
    mixed = jnp.dot(activ_low, full_w2, preferred_element_type=f32) + full_b2.astype(f32)
    resid_two = hidden + mixed
    normed, norm_two_back = jax.vjp(
        layer_norm, resid_two, gain_two.astype(f32), shift_two.astype(f32)
    )
    result = jnp.where(valid_rows[:, None], normed, 0.0).astype(bf16)
    output = to_order(result, layout, dev_count, piece_rows, tok_dev)
    back_w1, back_w2 = (
        lax.all_gather(w1, "dp", axis=0, tiled=True),
        lax.all_gather(w2, "dp", axis=0, tiled=True),
    )
    grad_resid_two, grad_gain_two, grad_shift_two = norm_two_back(upstream)
    grad_mixed = grad_resid_two.astype(bf16)
    grad_bias_two = jnp.sum(grad_mixed.astype(f32), 0)
    grad_activ = jnp.einsum("td,fd->tf", grad_mixed, back_w2, preferred_element_type=f32)
    grad_upward = gelu_back(grad_activ)[0].astype(bf16)
    grad_bias_one = jnp.sum(grad_upward.astype(f32), 0)
    grad_hidden = grad_resid_two + jnp.einsum(
        "tf,df->td", grad_upward, back_w1, preferred_element_type=f32
    )
    grad_w2 = jnp.einsum("tf,td->fd", activ_low, grad_mixed, preferred_element_type=f32)
    grad_w1 = jnp.einsum("td,tf->df", hidden_low, grad_upward, preferred_element_type=f32)
    mlp_grads = (
        lax.psum_scatter(grad_w1, "dp", scatter_dimension=0, tiled=True),
        lax.psum_scatter(grad_w2, "dp", scatter_dimension=0, tiled=True),
        lax.psum_scatter(grad_bias_one, "dp", scatter_dimension=0, tiled=True),
        lax.psum_scatter(grad_bias_two, "dp", scatter_dimension=0, tiled=True),
        lax.psum_scatter(grad_gain_two, "dp", scatter_dimension=0, tiled=True),
        lax.psum_scatter(grad_shift_two, "dp", scatter_dimension=0, tiled=True),
    )
    back_wq, back_wk, back_wv, back_wo = (
        lax.all_gather(wq, "dp", axis=0, tiled=True),
        lax.all_gather(wk, "dp", axis=0, tiled=True),
        lax.all_gather(wv, "dp", axis=0, tiled=True),
        lax.all_gather(wo, "dp", axis=0, tiled=True),
    )
    grad_resid_one, grad_gain_one, grad_shift_one = norm_one_back(grad_hidden)
    grad_branch = grad_resid_one.astype(bf16)
    grad_bo = jnp.sum(grad_branch.astype(f32), 0)
    grad_wo = jnp.einsum("tc,td->cd", attended, grad_branch, preferred_element_type=f32)
    grad_attended = jnp.einsum(
        "td,cd->tc", grad_branch, back_wo, preferred_element_type=f32
    ).astype(bf16)
    grad_attended = grad_attended.reshape(slot_count, HEADS, HEAD_DIM)
    re_scores = (
        jnp.einsum("qhd,khd->hqk", queries, keys_low, preferred_element_type=f32) * score_scale
    )
    re_scores = jnp.where(valid_rows[None, None, :], re_scores, -1e30)
    re_probs = jnp.exp(re_scores - log_total)
    re_probs_low = re_probs.astype(bf16)
    grad_values = jnp.einsum(
        "hqk,qhd->khd", re_probs_low, grad_attended, preferred_element_type=f32
    ).astype(bf16)
    grad_probs = jnp.einsum("qhd,khd->hqk", grad_attended, values_low, preferred_element_type=f32)
    grad_scores = re_probs * (grad_probs - jnp.sum(re_probs * grad_probs, -1, keepdims=True))
    grad_scores_low = grad_scores.astype(bf16)
    grad_queries = (
        jnp.einsum("hqk,khd->qhd", grad_scores_low, keys_low, preferred_element_type=f32)
        * score_scale
    ).astype(bf16)
    grad_keys = (
        jnp.einsum("hqk,qhd->khd", grad_scores_low, queries, preferred_element_type=f32)
        * score_scale
    ).astype(bf16)
    grad_queries = grad_queries.reshape(slot_count, feat_width)
    grad_keys = grad_keys.reshape(slot_count, feat_width)
    grad_values = grad_values.reshape(slot_count, feat_width)
    grad_bq = jnp.sum(grad_queries.astype(f32), 0)
    grad_bv = jnp.sum(grad_values.astype(f32), 0)
    grad_wq = jnp.einsum("tc,td->cd", inputs, grad_queries, preferred_element_type=f32)
    grad_wk = jnp.einsum("tc,td->cd", inputs, grad_keys, preferred_element_type=f32)
    grad_wv = jnp.einsum("tc,td->cd", inputs, grad_values, preferred_element_type=f32)
    grad_input = grad_resid_one + jnp.einsum(
        "td,cd->tc", grad_queries, back_wq, preferred_element_type=f32
    )
    grad_input = grad_input + jnp.einsum(
        "td,cd->tc", grad_keys, back_wk, preferred_element_type=f32
    )
    grad_input = grad_input + jnp.einsum(
        "td,cd->tc", grad_values, back_wv, preferred_element_type=f32
    )
    grad_input = jnp.where(valid_rows[:, None], grad_input, 0.0).astype(bf16)
    attn_grads = (
        lax.psum_scatter(grad_wq, "dp", scatter_dimension=0, tiled=True),
        lax.psum_scatter(grad_wk, "dp", scatter_dimension=0, tiled=True),
        lax.psum_scatter(grad_wv, "dp", scatter_dimension=0, tiled=True),
        lax.psum_scatter(grad_wo, "dp", scatter_dimension=0, tiled=True),
        lax.psum_scatter(grad_bq, "dp", scatter_dimension=0, tiled=True),
        lax.psum_scatter(grad_bv, "dp", scatter_dimension=0, tiled=True),
        lax.psum_scatter(grad_bo, "dp", scatter_dimension=0, tiled=True),
        lax.psum_scatter(grad_gain_one, "dp", scatter_dimension=0, tiled=True),
        lax.psum_scatter(grad_shift_one, "dp", scatter_dimension=0, tiled=True),
    )
    sum_w1, sum_w2, sum_b1, sum_b2, sum_g2, sum_s2 = mlp_grads
    sum_wq, sum_wk, sum_wv, sum_wo, sum_bq, sum_bv, sum_bo, sum_g1, sum_s1 = attn_grads
    input_grad = to_order(grad_input, layout, dev_count, piece_rows, tok_dev)
    return (
        output,
        input_grad,
        sum_wq,
        sum_bq,
        sum_wk,
        sum_wv,
        sum_bv,
        sum_wo,
        sum_bo,
        sum_g1,
        sum_s1,
        sum_w1,
        sum_b1,
        sum_w2,
        sum_b2,
        sum_g2,
        sum_s2,
    )


def flip(device, bit):
    step = 1 << bit
    return device + step - 2 * step * ((device // step) % 2)


def chip_bits(device):
    return [(device // 2) % 2, (device // 4) % 2, (device // 8) % 2]


def enter(partners):
    barrier = pltpu.get_barrier_semaphore()
    for partner in partners:
        pl.semaphore_signal(barrier, inc=1, device_id=(partner,), device_id_type=MESH_ID)
    pl.semaphore_wait(barrier, len(partners))


def push(src, dst, send_sem, recv_sem, device):
    return pltpu.make_async_remote_copy(
        src_ref=src,
        dst_ref=dst,
        send_sem=send_sem,
        recv_sem=recv_sem,
        device_id=(device,),
        device_id_type=MESH_ID,
    )


def gather_kernel(x_ref, o_ref, local_sem, send_sem, recv_sem, pair_send, pair_recv):
    device = lax.axis_index("dp")
    core = device % 2
    bits = chip_bits(device)
    partners = [flip(device, 1), flip(device, 2), flip(device, 3)]
    pair = flip(device, 0)
    enter(partners + [pair])

    def at(values, rows):
        return o_ref.at[values[2], values[1], values[0], core, rows, slice(None)]

    own = o_ref.at[bits[2], bits[1], bits[0], core]
    local = pltpu.make_async_copy(x_ref, own, local_sem)
    local.start()
    hops, shares = {}, {}

    def hop(part, step):
        first, count = PORTIONS[part]
        rows = pl.ds(first, count)
        values = list(bits)
        for dim in ORDERS[part][:step]:
            values[dim] = slice(None)
        dst = at(values, rows)
        src = x_ref.at[rows, :] if step == 0 else dst
        copy = push(
            src, dst, send_sem.at[part, step], recv_sem.at[part, step], partners[ORDERS[part][step]]
        )
        copy.start()
        hops[part, step] = copy

    def share(part, step):
        first, count = PORTIONS[part]
        rows = pl.ds(first, count)
        values = list(bits)
        if step:
            for dim in ORDERS[part][: step - 1]:
                values[dim] = slice(None)
            dim = ORDERS[part][step - 1]
            values[dim] = 1 - bits[dim]
        dst = at(values, rows)
        src = dst if step else x_ref.at[rows, :]
        copy = push(src, dst, pair_send.at[part, step], pair_recv.at[part, step], pair)
        copy.start()
        shares[part, step] = copy

    for part in range(3):
        hop(part, 0)
    for part in range(3):
        share(part, 0)
    local.wait()
    for step in (1, 2, 3):
        for part in range(3):
            hops[part, step - 1].wait_recv()
            if step < 3:
                hop(part, step)
            share(part, step)
    for copy in shares.values():
        copy.wait()
    for copy in hops.values():
        copy.wait_send()


def group_gather(rows, name, collective_id):
    count, width = rows.shape
    vmem = pl.BlockSpec(memory_space=pltpu.VMEM)
    sems = pltpu.SemaphoreType.DMA
    out = pl.pallas_call(
        gather_kernel,
        out_shape=jax.ShapeDtypeStruct((2, 2, 2, 2, count, width), rows.dtype),
        in_specs=[vmem],
        out_specs=vmem,
        scratch_shapes=[sems, sems((3, 3)), sems((3, 3)), sems((3, 4)), sems((3, 4))],
        compiler_params=pltpu.CompilerParams(
            collective_id=collective_id, has_side_effects=True, vmem_limit_bytes=VMEM_LIMIT
        ),
        name=name,
    )(rows)
    return out.reshape(GROUP * count, width)


def scatter_kernel(
    x_ref, o_ref, pair_in, sums, in_one, in_two, in_three, send_sem, recv_sem, pair_send, pair_recv
):
    device = lax.axis_index("dp")
    core = device % 2
    bits = chip_bits(device)
    partners = [flip(device, 1), flip(device, 2), flip(device, 3)]
    pair = flip(device, 0)
    width = x_ref.shape[-1]
    f32 = jnp.float32
    incoming = (in_one, in_two, in_three)
    enter(partners + [pair])

    def view(ref, values, rows, with_core=None):
        where = (values[2], values[1], values[0])
        if with_core is not None:
            where = where + (with_core,)
        return ref.at[where + (rows, slice(None))]

    shares, hops = {}, {}
    for half in range(2):
        for part in range(3):
            first, count = PORTIONS[part]
            rows = pl.ds(first, count)
            dim = ORDERS[part][0]
            values = [slice(None)] * 3
            values[dim] = 1 - bits[dim] if half == 0 else bits[dim]
            copy = push(
                view(x_ref, values, rows, 1 - core),
                view(pair_in, values, rows),
                pair_send.at[part, half],
                pair_recv.at[part, half],
                pair,
            )
            copy.start()
            shares[part, half] = copy

    def add_up(part, values, arrived, store):
        first, count = PORTIONS[part]

        def body(index, carry):
            rows = pl.ds(pl.multiple_of(first + index * 16, 16), 16)
            where = (values[2], values[1], values[0])
            total = x_ref[where + (core, rows, slice(None))].astype(f32)
            total = total + pair_in[where + (rows, slice(None))].astype(f32)
            for ref in incoming[:arrived]:
                total = total + ref[where + (rows, slice(None))].astype(f32)
            store(where, rows, total)
            return carry

        lax.fori_loop(0, count // 16, body, 0)

    def keep_sum(where, rows, total):
        sums[where + (rows, slice(None))] = total.astype(sums.dtype)

    def finish(where, rows, total):
        o_ref[rows, :] = total

    def hop(part, step):
        first, count = PORTIONS[part]
        order = ORDERS[part]
        values = list(bits)
        values[order[step]] = 1 - bits[order[step]]
        free = order[step + 1 :]
        for mask in range(1 << len(free)):
            slot = list(values)
            for place, dim in enumerate(free):
                slot[dim] = (mask >> place) & 1
            add_up(part, slot, step, keep_sum)
        for dim in free:
            values[dim] = slice(None)
        rows = pl.ds(first, count)
        copy = push(
            view(sums, values, rows),
            view(incoming[step], values, rows),
            send_sem.at[part, step],
            recv_sem.at[part, step],
            partners[order[step]],
        )
        copy.start()
        hops[part, step] = copy

    for part in range(3):
        shares[part, 0].wait_recv()
        hop(part, 0)
    for part in range(3):
        shares[part, 1].wait_recv()
        hops[part, 0].wait_recv()
        hop(part, 1)
    for part in range(3):
        hops[part, 1].wait_recv()
        hop(part, 2)
    for part in range(3):
        hops[part, 2].wait_recv()
        add_up(part, bits, 3, finish)
    for copy in shares.values():
        copy.wait_send()
    for copy in hops.values():
        copy.wait_send()


def group_scatter(partial, name, collective_id):
    width = partial.shape[-1]
    count = partial.shape[0] // GROUP
    low = partial.dtype
    vmem = pl.BlockSpec(memory_space=pltpu.VMEM)
    sems = pltpu.SemaphoreType.DMA
    slots = pltpu.VMEM((2, 2, 2, count, width), low)
    return pl.pallas_call(
        scatter_kernel,
        out_shape=jax.ShapeDtypeStruct((count, width), jnp.float32),
        in_specs=[vmem],
        out_specs=vmem,
        scratch_shapes=[
            slots, slots, slots, slots, slots,
            sems((3, 3)), sems((3, 3)), sems((3, 2)), sems((3, 2)),
        ],
        compiler_params=pltpu.CompilerParams(
            collective_id=collective_id, has_side_effects=True, vmem_limit_bytes=VMEM_LIMIT
        ),
        name=name,
    )(partial.reshape(2, 2, 2, 2, count, width))


def exchange_blocks(pairs, sems, base, mine, others):
    local_sem, send_sem, recv_sem = sems
    copies = []
    for at, (src, dst) in enumerate(pairs):
        for step, other in enumerate(others):
            copy = push(
                src.at[other - base],
                dst.at[mine],
                send_sem.at[at, step],
                recv_sem.at[at, step],
                other,
            )
            copy.start()
            copies.append(copy)
        local = pltpu.make_async_copy(src.at[mine], dst.at[mine], local_sem.at[at])
        local.start()
        copies.append(local)
    return copies


def group_places():
    device = lax.axis_index("dp")
    base = device // GROUP * GROUP
    mine = device % GROUP
    others = [base + (mine + step) % GROUP for step in range(1, GROUP)]
    across = (device + GROUP) % (2 * GROUP)
    return device // GROUP, base, mine, others, across


def weights_out_kernel(
    qkv_ref, w1_ref, vec_ref, qkv_out, w1_out, vec_out,
    local_sem, send_sem, recv_sem, vec_local, far_send, far_recv, vec_send, vec_recv,
):
    group, base, mine, others, across = group_places()
    enter(others + [across])
    far = push(vec_ref, vec_out.at[group, mine], far_send, far_recv, across)
    far.start()
    local = pltpu.make_async_copy(vec_ref, vec_out.at[group, mine], vec_local)
    local.start()
    copies = exchange_blocks(
        [(qkv_ref, qkv_out), (w1_ref, w1_out)], (local_sem, send_sem, recv_sem), base, mine, others
    )
    local.wait()
    far.wait()
    both = vec_out.at[:, mine]
    for step, other in enumerate(others):
        copy = push(both, both, vec_send.at[step], vec_recv.at[step], other)
        copy.start()
        copies.append(copy)
    for copy in copies:
        copy.wait()


def weights_out(pack_qkv, pack_w1, vector):
    anywhere = pl.BlockSpec(memory_space=pl.ANY)
    vmem = pl.BlockSpec(memory_space=pltpu.VMEM)
    sems = pltpu.SemaphoreType.DMA
    peers = GROUP - 1
    return pl.pallas_call(
        weights_out_kernel,
        out_shape=[
            jax.ShapeDtypeStruct(pack_qkv.shape, pack_qkv.dtype),
            jax.ShapeDtypeStruct(pack_w1.shape, pack_w1.dtype),
            jax.ShapeDtypeStruct((2, GROUP) + vector.shape, vector.dtype),
        ],
        in_specs=[anywhere, anywhere, vmem],
        out_specs=[anywhere, anywhere, vmem],
        scratch_shapes=[
            sems((2,)), sems((2, peers)), sems((2, peers)),
            sems, sems, sems, sems((peers,)), sems((peers,)),
        ],
        compiler_params=pltpu.CompilerParams(
            collective_id=1, has_side_effects=True, vmem_limit_bytes=VMEM_LIMIT
        ),
        name="weights_out",
    )(pack_qkv, pack_w1, vector)


def weights_back_kernel(
    w1_ref, qkv_ref, vec_ref, w1_out, qkv_out, vec_out,
    arrived, theirs, far_in, local_sem, send_sem, recv_sem, vec_sems, vec_send, vec_recv,
    far_send, far_recv,
):
    group, base, mine, others, across = group_places()
    enter(others + [across])
    first = exchange_blocks(
        [(vec_ref, arrived)], (vec_sems, vec_send, vec_recv), base, mine, others
    )
    copies = exchange_blocks(
        [(w1_ref, w1_out), (qkv_ref, qkv_out)], (local_sem, send_sem, recv_sem), base, mine, others
    )
    for copy in first:
        copy.wait()
    total = arrived[0]
    for at in range(1, GROUP):
        total = total + arrived[at]
    rows = total.shape[0] // 2
    low, high = total[:rows], total[rows:]
    theirs[...] = jnp.where(group == 0, high, low)
    far = push(theirs, far_in, far_send, far_recv, across)
    far.start()
    own = jnp.where(group == 0, low, high)
    far.wait()
    vec_out[...] = own + far_in[...]
    for copy in copies:
        copy.wait()


def weights_back(rows_w1, rows_qkv, vectors):
    anywhere = pl.BlockSpec(memory_space=pl.ANY)
    vmem = pl.BlockSpec(memory_space=pltpu.VMEM)
    sems = pltpu.SemaphoreType.DMA
    peers = GROUP - 1
    half = (vectors.shape[1] // 2, vectors.shape[2])
    return pl.pallas_call(
        weights_back_kernel,
        out_shape=[
            jax.ShapeDtypeStruct(rows_w1.shape, rows_w1.dtype),
            jax.ShapeDtypeStruct(rows_qkv.shape, rows_qkv.dtype),
            jax.ShapeDtypeStruct(half, vectors.dtype),
        ],
        in_specs=[anywhere, anywhere, vmem],
        out_specs=[anywhere, anywhere, vmem],
        scratch_shapes=[
            pltpu.VMEM(vectors.shape, vectors.dtype),
            pltpu.VMEM(half, vectors.dtype),
            pltpu.VMEM(half, vectors.dtype),
            sems((2,)), sems((2, peers)), sems((2, peers)),
            sems((1,)), sems((1, peers)), sems((1, peers)), sems, sems,
        ],
        compiler_params=pltpu.CompilerParams(
            collective_id=10, has_side_effects=True, vmem_limit_bytes=VMEM_LIMIT
        ),
        name="weights_back",
    )(rows_w1, rows_qkv, vectors)


def tile_probs(qkv_ref, row, start, seg_q, seg_k):
    f32 = jnp.float32
    queries = qkv_ref[pl.ds(row, TILE), 0:HEAD_DIM]
    keys = qkv_ref[pl.ds(start, WINDOW), HEAD_DIM : 2 * HEAD_DIM]
    scores = lax.dot_general(queries, keys, (((1,), (1,)), ((), ())), preferred_element_type=f32)
    scores = jnp.where(seg_q == seg_k, scores * HEAD_DIM ** (-0.5), -1e30)
    weights = jnp.exp(scores - jnp.max(scores, -1, keepdims=True))
    return queries, keys, weights / jnp.sum(weights, -1, keepdims=True)


def attend_back_kernel(qkv_ref, grad_ref, seg_q_ref, seg_k_ref, o_ref, dq_sum, dk_sum, dv_sum):
    total = qkv_ref.shape[0]
    f32 = jnp.float32
    low = qkv_ref.dtype
    scale = HEAD_DIM ** (-0.5)
    dq_sum[...] = jnp.zeros_like(dq_sum)
    dk_sum[...] = jnp.zeros_like(dk_sum)
    dv_sum[...] = jnp.zeros_like(dv_sum)

    def body(tile, carry):
        place = pl.multiple_of(tile * TILE, TILE)
        row = pl.multiple_of(PAD + place, 64)
        start = place
        queries, keys, probs = tile_probs(
            qkv_ref, row, start, seg_q_ref[pl.ds(place, TILE), :], seg_k_ref[tile]
        )
        window = pl.ds(start, WINDOW)
        values = qkv_ref[window, 2 * HEAD_DIM : 3 * HEAD_DIM]
        grads = grad_ref[pl.ds(place, TILE), :]
        grad_probs = lax.dot_general(
            grads, values, (((1,), (1,)), ((), ())), preferred_element_type=f32
        )
        inner = jnp.sum(probs * grad_probs, -1, keepdims=True)
        grad_scores = (probs * (grad_probs - inner)).astype(low)
        dq_sum[pl.ds(row, TILE), :] = jnp.dot(grad_scores, keys, preferred_element_type=f32)
        dk_sum[window, :] += lax.dot_general(
            grad_scores, queries, (((0,), (0,)), ((), ())), preferred_element_type=f32
        )
        dv_sum[window, :] += lax.dot_general(
            probs.astype(low), grads, (((0,), (0,)), ((), ())), preferred_element_type=f32
        )
        return carry

    lax.fori_loop(0, grad_ref.shape[0] // TILE, body, 0, unroll=2)
    o_ref[:, 0:HEAD_DIM] = (dq_sum[...] * scale).astype(low)
    o_ref[:, HEAD_DIM : 2 * HEAD_DIM] = (dk_sum[...] * scale).astype(low)
    o_ref[:, 2 * HEAD_DIM : 3 * HEAD_DIM] = dv_sum[...].astype(low)


def attend_back(qkv, grads, seg_q, seg_k):
    vmem = pl.BlockSpec(memory_space=pltpu.VMEM)
    total = qkv.shape[0]
    acc = pltpu.VMEM((total, HEAD_DIM), jnp.float32)
    return pl.pallas_call(
        attend_back_kernel,
        out_shape=jax.ShapeDtypeStruct(qkv.shape, qkv.dtype),
        in_specs=[vmem, vmem, vmem, vmem],
        out_specs=vmem,
        scratch_shapes=[acc, acc, acc],
        compiler_params=pltpu.CompilerParams(vmem_limit_bytes=VMEM_LIMIT),
        name="attend_back",
    )(qkv, grads, seg_q, seg_k)


CHUNKS = 4
COLUMNS = ((0, 768), (768, 640), (1408, 640))
SPLIT = 256
PAD = (WINDOW - TILE) // 2
STAGES = 7


def step_through(flows, fillers=None):
    waiting, alive = list(flows), []
    while waiting or alive:
        if waiting:
            alive.append(waiting.pop(0))
        alive = [flow for flow in alive if next(flow, "done") != "done"]
        if fillers is not None:
            next(fillers, None)
    if fillers is not None:
        for _ in fillers:
            pass


class Traffic:
    def __init__(self, sems):
        self.hop_send, self.hop_recv, self.pair_send, self.pair_recv = sems
        device = lax.axis_index("dp")
        self.core = device % 2
        self.bits = chip_bits(device)
        self.partners = [flip(device, 1), flip(device, 2), flip(device, 3)]
        self.pair = flip(device, 0)

    def chips(self, ref, values, columns):
        return ref.at[values[2], values[1], values[0], :, columns]

    def push(self, src, dst, stage, chunk, part, step):
        copy = push(
            src, dst,
            self.hop_send.at[stage, chunk, part, step],
            self.hop_recv.at[stage, chunk, part, step],
            self.partners[ORDERS[part][step]],
        )
        copy.start()
        return copy

    def share(self, src, dst, stage, chunk):
        copy = push(
            src, dst, self.pair_send.at[stage, chunk], self.pair_recv.at[stage, chunk], self.pair
        )
        copy.start()
        return copy

    def gather(self, slots, stage, chunk):
        mine = slots.at[self.core]
        hops = {}
        for step in range(3):
            for part, (first, count) in enumerate(COLUMNS):
                if step:
                    hops[part, step - 1].wait_recv()
                values = list(self.bits)
                for dim in ORDERS[part][:step]:
                    values[dim] = slice(None)
                view = self.chips(mine, values, pl.ds(first, count))
                hops[part, step] = self.push(view, view, stage, chunk, part, step)
            yield
        for part in range(3):
            hops[part, 2].wait_recv()
        share = self.share(mine, mine, stage, chunk)
        for copy in hops.values():
            copy.wait_send()
        return share

    def scatter(self, own, pair_in, incoming, share, stage, chunk, finish):
        rows = own.shape[-2]
        f32 = jnp.float32
        hops = {}
        share.wait()
        for step in range(4):
            for part, (first, count) in enumerate(COLUMNS):
                order = ORDERS[part]
                columns = pl.ds(first, count)
                if step:
                    hops[part, step - 1].wait_recv()
                values = list(self.bits)
                free = ()
                if step < 3:
                    values[order[step]] = 1 - self.bits[order[step]]
                    free = order[step + 1 :]
                for mask in range(1 << len(free)):
                    slot = list(values)
                    for place, dim in enumerate(free):
                        slot[dim] = (mask >> place) & 1
                    where = (slot[2], slot[1], slot[0])
                    for row in range(0, rows, 16):
                        at = (slice(row, row + 16), columns)
                        total = own[where + at].astype(f32) + pair_in[where + at].astype(f32)
                        for back in range(step):
                            left = [slot[dim] for dim in (2, 1, 0) if dim not in order[: back + 1]]
                            total = total + incoming[back][tuple(left) + at].astype(f32)
                        if step < 3:
                            own[where + at] = total.astype(own.dtype)
                        else:
                            finish(row, first, count, total)
                if step == 3:
                    continue
                for dim in free:
                    values[dim] = slice(None)
                left = tuple(slice(None) for _ in free)
                hops[part, step] = self.push(
                    self.chips(own, values, columns),
                    incoming[step].at[left + (slice(None), columns)],
                    stage, chunk, part, step,
                )
            if step < 3:
                yield
        for copy in hops.values():
            copy.wait_send()


def gelu_slope(up):
    inner = 0.7978845608028654 * (up + 0.044715 * (up * up * up))
    tanh = jnp.tanh(inner)
    return 0.5 * (1.0 + tanh) + 0.5 * up * (1.0 - tanh * tanh) * (
        0.7978845608028654 * (1.0 + 0.134145 * (up * up))
    )


NT = (((1,), (1,)), ((), ()))


def layer_kernel(
    tok_ref, cot_ref, pack_qkv, pack_w1, w2_ref, wo_ref, vec_ref, seg_q_ref, seg_k_ref,
    out_ref, dres_ref, vecg_ref, gb1_ref, gw2_own, gw2_far, gw1_own, gw1_far, gwo_ref,
    x_all, h_all, qkv_ref, dout_ref, wqkv_ref,
    all_h, all_m, own_part, far_part, pair_in, in_one, in_two, in_three,
    up_ref, act_ref, act_t, dup_ref, dup_t, att_ref, att_t, res_ref, hid_ref, norm_ref, scale_ref,
    w1_all, w2_all, wo_all, vec_all, low_ref, high_ref, b1_ref, stage_ref, stage_low,
    hop_send, hop_recv, pair_send, pair_recv,
    block_local, block_send, block_recv, vec_send, vec_recv, far_send, far_recv,
    local_sems, out_sems, spill_sems,
):
    f32, low = jnp.float32, tok_ref.dtype
    block, width = tok_ref.shape
    rows = block // CHUNKS
    half_rows = rows * GROUP // 2
    own_rows = GROUP * block
    units = w1_all.shape[-1]
    group, base, mine, others, across = group_places()
    net = Traffic((hop_send, hop_recv, pair_send, pair_recv))
    core, bits = net.core, net.bits
    chip = mine // 2
    head = core * 8 + chip
    own_slot = (core, bits[2], bits[1], bits[0])
    ext = PAD + group * HALO
    enter(others + [across, flip(across, 0)])

    def far(src, dst, at, device=across):
        copy = push(src, dst, far_send.at[at], far_recv.at[at], device)
        copy.start()
        return copy

    def local(src, dst, at):
        copy = pltpu.make_async_copy(src, dst, local_sems.at[at])
        copy.start()
        return copy

    early = w2_ref.shape[0] // 4
    far_vec = far(vec_ref, vec_all.at[group, mine], 0)
    near = [
        local(vec_ref, vec_all.at[group, mine], 0),
        local(w2_ref, w2_all.at[group], 1),
        local(wo_ref, wo_all.at[group, core], 2),
    ]
    w2_first, w2_last = pl.ds(0, early), pl.ds(early, w2_ref.shape[0] - early)
    far_w2 = [far(w2_ref.at[w2_first, :], w2_all.at[group, w2_first, :], 1)]
    qkv_blocks = exchange_blocks(
        [(pack_qkv, wqkv_ref.at[group])],
        (block_local.at[0:1], block_send.at[0:1], block_recv.at[0:1]), base, mine, others,
    )
    for chunk in range(CHUNKS):
        all_m[(chunk,) + own_slot] = tok_ref[chunk * rows : (chunk + 1) * rows, :]
    wo_near = push(
        wo_ref, wo_all.at[group, core], far_send.at[2], far_recv.at[2], net.pair
    )
    wo_near.start()

    qkv_ref[0:PAD, :] = jnp.zeros((PAD, qkv_ref.shape[1]), low)
    qkv_ref[qkv_ref.shape[0] - PAD :, :] = jnp.zeros((PAD, qkv_ref.shape[1]), low)
    vecg_ref[...] = jnp.zeros_like(vecg_ref)
    gb1_ref[...] = jnp.zeros_like(gb1_ref)

    def row_at(chunk, side):
        return pl.multiple_of((chunk * 2 + side) * half_rows, half_rows)

    def flat(ref, chunk, side, columns=slice(None)):
        return ref[chunk, side, :, :, :, :, columns].reshape(half_rows, -1)

    def tiles(count, body):
        def step(at, carry):
            body(at, pl.ds(pl.multiple_of(at * SPLIT, SPLIT), SPLIT))
            return carry

        lax.fori_loop(0, count // SPLIT, step, 0)

    def pieces(chunk, side):
        return [
            pl.multiple_of((slot * 2 + side) * block + chunk * rows, rows)
            for slot in range(GROUP // 2)
        ]

    def project_half(chunk, side, which):
        columns = pl.ds(pl.multiple_of(which * (width // 2), width // 2), width // 2)
        weight = wqkv_ref[which].reshape(width // 2, -1)
        return jnp.dot(flat(all_m, chunk, side, columns), weight, preferred_element_type=f32)

    def spill(src, dst, chunk, at):
        copy = pltpu.make_async_copy(src.at[chunk], dst.at[chunk], spill_sems.at[at, chunk])
        copy.start()
        return copy

    wide = slice(0, 3 * HEAD_DIM)
    spills = {}

    def token_flow(chunk):
        share = yield from net.gather(all_m.at[chunk], 0, chunk)
        up_ref[pl.ds(row_at(chunk, core), half_rows), wide] = project_half(chunk, core, group)
        yield
        share.wait()
        up_ref[pl.ds(row_at(chunk, 1 - core), half_rows), wide] = project_half(
            chunk, 1 - core, group
        )
        spills[0, chunk] = spill(all_m, x_all, chunk, 0)

    def weight_flow():
        yield
        for copy in qkv_blocks:
            copy.wait()
        state["far_qkv"] = far(wqkv_ref.at[group], wqkv_ref.at[group], 3)
        state["w1_blocks"] = exchange_blocks(
            [(pack_w1, w1_all.at[group])],
            (block_local.at[1:2], block_send.at[1:2], block_recv.at[1:2]), base, mine, others,
        )
        yield
        for copy in near:
            copy.wait()
        far_vec.wait()
        both = vec_all.at[:, mine]
        state["vec"] = []
        for step, other in enumerate(others):
            copy = push(both, both, vec_send.at[step], vec_recv.at[step], other)
            copy.start()
            state["vec"].append(copy)
        yield

    state = {"backs": 0}
    flows = [token_flow(chunk) for chunk in range(CHUNKS)]
    step_through([flows[0], weight_flow()] + flows[1:])

    for copy in state["vec"]:
        copy.wait()
    lane = lax.broadcasted_iota(jnp.int32, (8, 128), 1)
    for at in range(GROUP):
        first = vec_all[at // 8, at % 8 * 2]
        second = vec_all[at // 8, at % 8 * 2 + 1]
        here = slice(at * 128, at * 128 + 128)
        low_ref[:, here] = jnp.where(lane < 64, first, pltpu.roll(second, 64, 1))
        high_ref[:, here] = jnp.where(lane < 64, pltpu.roll(first, 64, 1), second)
    for half in range(2):
        for part in range(2):
            b1_ref[0:1, half * 256 + part * 128 : half * 256 + part * 128 + 128] = vec_all[
                half, mine, 4 + part : 5 + part, :
            ]
    head_at = pl.ds(pl.multiple_of(head * HEAD_DIM, HEAD_DIM), HEAD_DIM)
    bias_q, bias_v = low_ref[0:1, head_at], high_ref[0:1, head_at]
    bias_qkv = jnp.concatenate([bias_q, jnp.zeros_like(bias_q), bias_v], 1)
    bo, shift_one, gain_two = low_ref[1:2, :], low_ref[2:3, :], low_ref[3:4, :]
    gain_one, b2, shift_two = high_ref[1:2, :], high_ref[2:3, :], high_ref[3:4, :]

    state["far_qkv"].wait()
    far_wo_to = (1 - group) * GROUP + 2 * chip + group
    far_wo = push(
        wo_ref, wo_all.at[group, core], far_send.at[4 + core], far_recv.at[4 + core], far_wo_to
    )
    far_wo.start()
    for chunk in range(CHUNKS):
        for side in range(2):
            here = pl.ds((chunk * 2 + side) * half_rows, half_rows)
            total = up_ref[here, wide] + project_half(chunk, side, 1 - group) + bias_qkv
            total = total.astype(low)
            for slot, place in enumerate(pieces(chunk, side)):
                qkv_ref[pl.ds(pl.multiple_of(ext + place, rows), rows), :] = total[
                    slot * rows : (slot + 1) * rows
                ]
    halo_src = pl.ds(pl.multiple_of(PAD + 1792 - group * 1536, 64), HALO)
    halo_dst = pl.ds(pl.multiple_of(PAD + 2048 * group, 64), HALO)
    far_halo = far(qkv_ref.at[halo_src, :], qkv_ref.at[halo_dst, :], 6)
    for copy in state["w1_blocks"]:
        copy.wait()
    far_w1 = far(w1_all.at[group], w1_all.at[group], 7)

    def attend_tile(at):
        tile = at + group * (GROUP - 1 - 2 * at)
        row = pl.multiple_of(ext + tile * TILE, 64)
        start = pl.multiple_of(ext - PAD + tile * TILE, 64)
        place = pl.multiple_of(group * HALO + tile * TILE, TILE)
        _, _, probs = tile_probs(
            qkv_ref, row, start, seg_q_ref[pl.ds(place, TILE), :],
            seg_k_ref[group * (HALO // TILE) + tile],
        )
        values = qkv_ref[pl.ds(start, WINDOW), 2 * HEAD_DIM : 3 * HEAD_DIM]
        out = jnp.dot(probs.astype(low), values, preferred_element_type=f32)
        att_ref[pl.ds(pl.multiple_of(tile * TILE, TILE), TILE), :] = out.astype(low)

    def attend_two(at, carry):
        attend_tile(2 * at)
        attend_tile(2 * at + 1)
        return carry

    lax.fori_loop(0, own_rows // TILE // 2 - 1, attend_two, 0)
    far_halo.wait()
    attend_tile(own_rows // TILE - 2)
    attend_tile(own_rows // TILE - 1)
    for chunk in range(CHUNKS):
        spills[0, chunk].wait()
    wo_near.wait()
    far_wo.wait_send()

    @pl.when(core != group)
    def _():
        for at in range(2):
            push(
                wo_ref, wo_all.at[1 - group, at], far_send.at[4 + at], far_recv.at[4 + at],
                far_wo_to,
            ).wait_recv()

    far_w2.append(far(w2_ref.at[w2_last, :], w2_all.at[group, w2_last, :], 8))

    def branch_part(chunk, side, dst):
        rows_in = jnp.concatenate([att_ref[pl.ds(at, rows), :] for at in pieces(chunk, side)], 0)
        att_t[:, pl.ds(row_at(chunk, side), half_rows)] = rows_in.astype(f32).T.astype(low)

        def body(at, columns):
            weight = wo_all[core, :, :, columns].reshape(HEAD_DIM, SPLIT)
            part = jnp.dot(rows_in, weight, preferred_element_type=f32)
            dst[:, :, :, :, columns] = part.astype(low).reshape(2, 2, 2, rows, SPLIT)

        tiles(width, body)

    def upward(chunk, side):
        here = pl.ds(row_at(chunk, side), half_rows)

        def body(at, columns):
            weight = w1_all[:, :, :, columns].reshape(width, SPLIT)
            up = jnp.dot(flat(all_h, chunk, side), weight, preferred_element_type=f32)
            up = up + b1_ref[0:1, columns]
            up_ref[here, columns] = up
            act = gelu_tanh(up)
            act_ref[:, columns] = act.astype(low)
            act_t[columns, here] = act.T.astype(low)

        tiles(units, body)

    def downward(dst):
        def body(at, columns):
            weight = w2_all[:, :, columns].reshape(units, SPLIT)
            part = jnp.dot(act_ref[...], weight, preferred_element_type=f32)
            dst[:, :, :, :, columns] = part.astype(low).reshape(2, 2, 2, rows, SPLIT)

        tiles(width, body)

    def up_back(chunk, side):
        here = pl.ds(row_at(chunk, side), half_rows)

        def body(at, columns):
            grad = lax.dot_general(
                flat(all_m, chunk, side), w2_all[at], NT, preferred_element_type=f32
            )
            grad = (grad * gelu_slope(up_ref[here, columns])).astype(low)
            dup_ref[:, columns] = grad
            grad = grad.astype(f32)
            gb1_ref[0:1, columns] += jnp.sum(grad, 0, keepdims=True)
            dup_t[columns, here] = grad.T.astype(low)

        tiles(units, body)

    def down_back(dst):
        def body(at, columns):
            weight = w1_all[at // 4, pl.ds(at % 4 * 4, 4)].reshape(SPLIT, units)
            part = lax.dot_general(dup_ref[...], weight, NT, preferred_element_type=f32)
            dst[:, :, :, :, columns] = part.astype(low).reshape(2, 2, 2, rows, SPLIT)

        tiles(width, body)

    def out_back(chunk, side):
        weight = wo_all[core].reshape(HEAD_DIM, width)
        grad = lax.dot_general(flat(all_h, chunk, side), weight, NT, preferred_element_type=f32)
        grad = grad.astype(low)
        for slot, place in enumerate(pieces(chunk, side)):
            dout_ref[pl.ds(pl.multiple_of(group * HALO + place, rows), rows), :] = grad[
                slot * rows : (slot + 1) * rows
            ]

    def keep(chunk):
        def finish(row, first, count, total):
            res_ref[chunk * rows + row : chunk * rows + row + 16, first : first + count] = total

        return finish

    def row_sets(chunk):
        for row in range(0, rows, 16):
            yield slice(chunk * rows + row, chunk * rows + row + 16), slice(row, row + 16)

    def normal(res):
        res = res - jnp.mean(res, -1, keepdims=True)
        scale = lax.rsqrt(jnp.mean(res * res, -1, keepdims=True) + norm_eps)
        return res * scale, scale

    def normal_back(grad, res, gain, scale, at):
        vecg_ref[at + 2 : at + 3, :] += jnp.sum(grad, 0, keepdims=True)
        vecg_ref[at + 1 : at + 2, :] += jnp.sum(grad * res, 0, keepdims=True)
        grad = grad * gain
        first = jnp.mean(grad, -1, keepdims=True)
        second = jnp.mean(grad * res, -1, keepdims=True)
        grad = (grad - first - res * second) * scale
        grad_low = grad.astype(low)
        vecg_ref[at : at + 1, :] += jnp.sum(grad_low.astype(f32), 0, keepdims=True)
        return grad, grad_low

    def norm_one(chunk):
        for at, place in row_sets(chunk):
            res, scale = normal(tok_ref[at, :].astype(f32) + res_ref[at, :] + bo)
            norm_ref[at, :] = res
            scale_ref[at, :] = jnp.broadcast_to(scale, (16, 128))
            hidden = res * gain_one + shift_one
            hid_ref[at, :] = hidden
            all_h[(chunk,) + own_slot + (place, slice(None))] = hidden.astype(low)

    def norm_two(chunk):
        for at, place in row_sets(chunk):
            res, scale = normal(hid_ref[at, :] + res_ref[at, :] + b2)
            out_ref[at, :] = (res * gain_two + shift_two).astype(low)
            grad, grad_low = normal_back(cot_ref[at, :].astype(f32), res, gain_two, scale, 0)
            dres_ref[at, :] = grad
            all_m[(chunk,) + own_slot + (place, slice(None))] = grad_low

    def norm_one_back(chunk):
        for at, place in row_sets(chunk):
            grad, grad_low = normal_back(
                dres_ref[at, :] + res_ref[at, :], norm_ref[at, :], gain_one,
                scale_ref[at, 0:1], 3,
            )
            dres_ref[at, :] = grad
            all_h[(chunk,) + own_slot + (place, slice(None))] = grad_low

    def flow(chunk):
        incoming = (in_one.at[chunk], in_two.at[chunk], in_three.at[chunk])
        own, other = own_part.at[chunk], far_part.at[chunk % 2]
        arrived = pair_in.at[chunk]
        branch_part(chunk, 1 - core, other)
        share = net.share(other, arrived, 1, chunk)
        branch_part(chunk, core, own)
        yield
        yield from net.scatter(own, arrived, incoming, share, 1, chunk, keep(chunk))
        norm_one(chunk)
        share = yield from net.gather(all_h.at[chunk], 2, chunk)
        if chunk == 0:
            far_w1.wait()
        upward(chunk, core)
        if chunk == 0:
            for copy in far_w2:
                copy.wait()
        downward(own)
        yield
        share.wait()
        spills[1, chunk] = spill(all_h, h_all, chunk, 1)
        upward(chunk, 1 - core)
        downward(other)
        share = net.share(other, arrived, 3, chunk)
        yield
        yield from net.scatter(own, arrived, incoming, share, 3, chunk, keep(chunk))
        norm_two(chunk)
        spills[1, chunk].wait()
        share = yield from net.gather(all_m.at[chunk], 4, chunk)
        up_back(chunk, core)
        down_back(own)
        yield
        share.wait()
        up_back(chunk, 1 - core)
        down_back(other)
        share = net.share(other, arrived, 5, chunk)
        state["backs"] += 1
        yield
        yield from net.scatter(own, arrived, incoming, share, 5, chunk, keep(chunk))
        norm_one_back(chunk)
        share = yield from net.gather(all_h.at[chunk], 6, chunk)
        out_back(chunk, core)
        yield
        share.wait()
        out_back(chunk, 1 - core)

    def product(left_t, right, columns):
        total = None
        for chunk in range(CHUNKS):
            for side in range(2):
                here = slice((chunk * 2 + side) * half_rows, (chunk * 2 + side + 1) * half_rows)
                term = jnp.dot(
                    left_t[:, here], flat(right, chunk, side, columns), preferred_element_type=f32
                )
                total = term if total is None else total + term
        return total

    def run(first, last, write):
        def step(at, carry):
            write(at, at % 2, at >= 2)
            return carry

        lax.fori_loop(first, last, step, 0)

    def emit(src, dst, sem, again):
        copy = pltpu.make_async_copy(src, dst, sem)

        @pl.when(again)
        def _():
            copy.wait()

        return copy

    def columns_at(at):
        return pl.ds(pl.multiple_of(at * SPLIT, SPLIT), SPLIT)

    def write_w2(at, slot, again):
        own = emit(stage_ref.at[slot, 0:256, :], gw2_own.at[:, columns_at(at)], out_sems.at[0, slot], again)
        there = emit(stage_low.at[slot, 0:256, :], gw2_far.at[:, columns_at(at)], out_sems.at[1, slot], again)
        total = product(act_t, all_m, columns_at(at))
        first = group == 0
        stage_ref[slot, 0:256, :] = jnp.where(first, total[:256], total[256:])
        stage_low[slot, 0:256, :] = jnp.where(first, total[256:], total[:256]).astype(low)
        own.start()
        there.start()

    def write_w1_own(at, slot, again):
        own = emit(stage_ref.at[slot], gw1_own.at[:, columns_at(at)], out_sems.at[2, slot], again)
        stage_ref[slot] = product(dup_t, all_m, columns_at(group * 4 + at))
        own.start()

    def write_w1_far(at, slot, again):
        there = emit(stage_low.at[slot], gw1_far.at[:, columns_at(at)], out_sems.at[3, slot], again)
        stage_low[slot] = product(dup_t, all_m, columns_at((1 - group) * 4 + at)).astype(low)
        there.start()

    def write_wo(at, slot, again):
        own = emit(stage_ref.at[slot, 0:HEAD_DIM, :], gwo_ref.at[:, columns_at(at)], out_sems.at[4, slot], again)
        stage_ref[slot, 0:HEAD_DIM, :] = product(att_t, all_h, columns_at(at))
        own.start()

    def fill():
        while state["backs"] < CHUNKS:
            yield
        run(0, width // SPLIT // 2, write_w2)
        yield
        run(width // SPLIT // 2, width // SPLIT, write_w2)
        for slot in range(2):
            emit(stage_ref.at[slot, 0:256, :], gw2_own.at[:, columns_at(0)], out_sems.at[0, slot], True)
            emit(stage_low.at[slot, 0:256, :], gw2_far.at[:, columns_at(0)], out_sems.at[1, slot], True)
        back = [pltpu.make_async_copy(h_all.at[at], all_m.at[at], spill_sems.at[2, at]) for at in range(CHUNKS)]
        for copy in back:
            copy.start()
        yield
        for copy in back:
            copy.wait()
        run(0, width // SPLIT // 2, write_w1_own)
        for slot in range(2):
            emit(stage_ref.at[slot], gw1_own.at[:, columns_at(0)], out_sems.at[2, slot], True)
        yield
        run(0, width // SPLIT // 2, write_w1_far)
        for slot in range(2):
            emit(stage_low.at[slot], gw1_far.at[:, columns_at(0)], out_sems.at[3, slot], True)

    step_through([flow(chunk) for chunk in range(CHUNKS)], fill())
    halo_src = pl.ds(pl.multiple_of(1792 - group * 1536, 64), HALO)
    halo_dst = pl.ds(pl.multiple_of(2048 * group, 64), HALO)
    far_dout = far(dout_ref.at[halo_src, :], dout_ref.at[halo_dst, :], 9)
    run(0, width // SPLIT, write_wo)
    for slot in range(2):
        emit(stage_ref.at[slot, 0:HEAD_DIM, :], gwo_ref.at[:, columns_at(0)], out_sems.at[4, slot], True)
    far_dout.wait()


def layer(tokens, cotangent, pack_qkv, pack_w1, w2, wo, vector, seg_q, seg_k):
    f32, bf16 = jnp.float32, jnp.bfloat16
    block, width = tokens.shape
    rows = block // CHUNKS
    unit_rows = w2.shape[0]
    units = 2 * unit_rows
    half_rows = rows * GROUP // 2
    own_rows = GROUP * block
    weight_rows = wo.shape[0]
    peers = GROUP - 1
    vmem = pl.BlockSpec(memory_space=pltpu.VMEM)
    anywhere = pl.BlockSpec(memory_space=pl.ANY)
    sems = pltpu.SemaphoreType.DMA
    shape = jax.ShapeDtypeStruct

    def slots(*lead):
        return pltpu.VMEM(lead + (rows, width), bf16)

    return pl.pallas_call(
        layer_kernel,
        out_shape=[
            shape((block, width), bf16),
            shape((block, width), f32),
            shape((8, width), f32),
            shape((8, units), f32),
            shape((unit_rows, width), f32),
            shape((unit_rows, width), bf16),
            shape((units, width // 2), f32),
            shape((units, width // 2), bf16),
            shape((HEAD_DIM, width), f32),
            shape((CHUNKS, 2, 2, 2, 2, rows, width), bf16),
            shape((CHUNKS, 2, 2, 2, 2, rows, width), bf16),
            shape((own_rows + HALO + 2 * PAD, 3 * HEAD_DIM), bf16),
            shape((own_rows + HALO, HEAD_DIM), bf16),
            shape((2, GROUP, weight_rows, 3 * HEAD_DIM), bf16),
        ],
        in_specs=[vmem, vmem, anywhere, anywhere, anywhere, anywhere, vmem, vmem, vmem],
        out_specs=[vmem] * 4 + [anywhere] * 7 + [vmem] * 3,
        scratch_shapes=[
            slots(CHUNKS, 2, 2, 2, 2), slots(CHUNKS, 2, 2, 2, 2),
            slots(CHUNKS, 2, 2, 2), slots(2, 2, 2, 2), slots(CHUNKS, 2, 2, 2),
            slots(CHUNKS, 2, 2), slots(CHUNKS, 2), slots(CHUNKS),
            pltpu.VMEM((own_rows, units), f32),
            pltpu.VMEM((half_rows, units), bf16),
            pltpu.VMEM((units, own_rows), bf16),
            pltpu.VMEM((half_rows, units), bf16),
            pltpu.VMEM((units, own_rows), bf16),
            pltpu.VMEM((own_rows, HEAD_DIM), bf16),
            pltpu.VMEM((HEAD_DIM, own_rows), bf16),
            pltpu.VMEM((block, width), f32),
            pltpu.VMEM((block, width), f32),
            pltpu.VMEM((block, width), f32),
            pltpu.VMEM((block, 128), f32),
            pltpu.VMEM((2, GROUP, weight_rows, units), bf16),
            pltpu.VMEM((2, unit_rows, width), bf16),
            pltpu.VMEM((2, 2, weight_rows, width), bf16),
            pltpu.VMEM((2, GROUP, 8, 128), f32),
            pltpu.VMEM((8, width), f32),
            pltpu.VMEM((8, width), f32),
            pltpu.VMEM((8, units), f32),
            pltpu.VMEM((2, units, SPLIT), f32),
            pltpu.VMEM((2, units, SPLIT), bf16),
            sems((STAGES, CHUNKS, 3, 3)), sems((STAGES, CHUNKS, 3, 3)),
            sems((STAGES, CHUNKS)), sems((STAGES, CHUNKS)),
            sems((2,)), sems((2, peers)), sems((2, peers)), sems((peers,)), sems((peers,)),
            sems((10,)), sems((10,)), sems((3,)), sems((5, 2)), sems((3, CHUNKS)),
        ],
        compiler_params=pltpu.CompilerParams(
            collective_id=4, has_side_effects=True, vmem_limit_bytes=63 << 20
        ),
        name="layer",
    )(tokens, cotangent, pack_qkv, pack_w1, w2, wo, vector, seg_q, seg_k)


def grouped_device(
    tokens,
    cotangent,
    lengths,
    wq,
    bq,
    wk,
    wv,
    bv,
    wo,
    bo,
    norm1_gain,
    norm1_bias,
    w1,
    b1,
    w2,
    b2,
    norm2_gain,
    norm2_bias,
):
    f32 = jnp.float32
    bf16 = jnp.bfloat16
    devices = lax.axis_size("dp")
    block, width = tokens.shape
    own_rows = GROUP * block
    total_tokens = devices * block
    weight_rows = wq.shape[0]
    unit_rows, units = w2.shape[0], w1.shape[1]
    device = lax.axis_index("dp")
    group, member = device // GROUP, device % GROUP
    chip, core = member // 2, member % 2
    head = core * 8 + chip
    first_group = group == 0
    across = [(at, (at + GROUP) % devices) for at in range(devices)]
    beside = [(at, at + 1 - 2 * (at % 2)) for at in range(devices)]

    def swap(own, other):
        return jnp.where(first_group, own, other), jnp.where(first_group, other, own)

    def in_order(own, other):
        return jnp.concatenate(swap(own, other), 0)

    def by_head(weight):
        return weight.reshape(weight_rows, 2, 8, HEAD_DIM).transpose(2, 1, 0, 3).reshape(
            GROUP, weight_rows, HEAD_DIM
        )

    pack_qkv = jnp.concatenate([by_head(wq), by_head(wk), by_head(wv)], -1)
    pack_w1 = w1.reshape(weight_rows, 2, GROUP, unit_rows).transpose(2, 0, 1, 3).reshape(
        GROUP, weight_rows, 2 * unit_rows
    )
    vectors = [bq, bv, bo, norm1_gain, norm1_bias, b2, norm2_gain, norm2_bias, b1]
    sizes = [item.shape[0] for item in vectors]
    vector = jnp.concatenate(vectors).astype(f32)
    vector = jnp.pad(vector, (0, 1024 - vector.shape[0])).reshape(8, 128)

    ext_rows = own_rows + HALO
    ext_first = group * (own_rows - HALO)
    offset = group * HALO
    starts = jnp.cumsum(lengths) - lengths
    ext_ids = ext_first + jnp.arange(ext_rows, dtype=jnp.int32)
    seg = jnp.sum((ext_ids[:, None] >= starts[None, :]).astype(jnp.int32), 1)
    tile_rows = jnp.arange(ext_rows // TILE, dtype=jnp.int32) * TILE - PAD
    key_rows = tile_rows[:, None] + jnp.arange(WINDOW, dtype=jnp.int32)[None, :]
    key_ids = ext_first + key_rows
    seg_k = jnp.sum((key_ids[:, :, None] >= starts[None, None, :]).astype(jnp.int32), 2)
    seg_k = jnp.where((key_rows >= 0) & (key_rows < ext_rows), seg_k, -1)[:, None, :]
    seg_q = seg[:, None]

    (
        output, grad_resid_one, vec_grads, grad_b1, w2_own, w2_far, w1_own, w1_far, grad_wo,
        all_tokens, _, qkv, grad_out, full_qkv,
    ) = layer(tokens, cotangent, pack_qkv, pack_w1, w2, wo, vector, seg_q, seg_k)
    grad_b2, grad_gain_two, grad_shift_two, grad_bo, grad_gain_one, grad_shift_one = [
        vec_grads[at] for at in range(6)
    ]
    grad_b1 = grad_b1[0]
    out_w2 = w2_own + lax.ppermute(w2_far, "dp", across).astype(f32)

    def across_sum(grad):
        halves = grad.reshape((2, grad.shape[0] // 2) + grad.shape[1:])
        mine = jnp.where(first_group, halves[0], halves[1])
        theirs = jnp.where(first_group, halves[1], halves[0]).astype(bf16)
        return mine + lax.ppermute(theirs, "dp", across).astype(f32)

    grad_qkv_ext = attend_back(qkv, grad_out, seg_q, seg_k)
    grad_qkv = lax.dynamic_slice_in_dim(grad_qkv_ext, PAD + offset, own_rows, 0)
    grad_qkv, w1_far = lax.optimization_barrier((grad_qkv, w1_far))
    sum_w1 = (w1_own + lax.ppermute(w1_far, "dp", across).astype(f32)).astype(bf16).T
    grad_bqkv = jnp.sum(grad_qkv.astype(f32), 0)
    full_qkv = full_qkv.reshape(width, 3 * HEAD_DIM)
    input_part = jnp.einsum("tf,df->td", grad_qkv, full_qkv, preferred_element_type=f32)
    grad_by_chunk = (
        grad_qkv.reshape(8, 2, CHUNKS, block // CHUNKS, 3 * HEAD_DIM)
        .transpose(2, 1, 0, 3, 4)
        .reshape(own_rows, 3 * HEAD_DIM)
    )
    grad_wqkv = jnp.einsum(
        "td,tf->df", all_tokens.reshape(own_rows, width), grad_by_chunk, preferred_element_type=f32
    )
    sum_qkv = across_sum(grad_wqkv)
    input_sum = group_scatter(input_part.astype(bf16), "scatter_input", 9)
    input_grad = (grad_resid_one + input_sum).astype(bf16)

    back_pairs = [
        (GROUP * (1 - g) + 2 * k + g, GROUP * g + 2 * k + g) for g in range(2) for k in range(8)
    ]
    sum_wo = grad_wo + lax.ppermute(grad_wo.astype(bf16), "dp", back_pairs).astype(f32)
    halves = sum_wo.reshape(2, weight_rows, width)
    mine_wo = jnp.where(core == 0, halves[0], halves[1])
    theirs_wo = jnp.where(core == 0, halves[1], halves[0])
    out_wo = jnp.where(core == group, mine_wo, lax.ppermute(theirs_wo, "dp", beside))
    def place_head(vector):
        return lax.dynamic_update_slice_in_dim(
            jnp.zeros((width,), f32), vector, head * HEAD_DIM, 0
        )

    spread_b1 = lax.dynamic_update_slice_in_dim(
        jnp.zeros((2, GROUP, unit_rows), f32), grad_b1.reshape(2, 1, unit_rows), member, 1
    )
    items = [
        place_head(grad_bqkv[:HEAD_DIM]), place_head(grad_bqkv[2 * HEAD_DIM :]), grad_bo,
        grad_gain_one, grad_shift_one, grad_b2, grad_gain_two, grad_shift_two, spread_b1,
    ]
    parts = jnp.concatenate([item.reshape(2, GROUP, -1) for item in items], 2)
    parts = jnp.pad(parts, ((0, 0), (0, 0), (0, 1024 - parts.shape[2])))
    parts = parts.transpose(1, 0, 2).reshape(GROUP, 16, 128)
    rows_w1, rows_qkv, sums = weights_back(
        sum_w1.astype(bf16).reshape(GROUP, weight_rows, 2 * unit_rows),
        sum_qkv.astype(bf16).reshape(GROUP, weight_rows, 3 * HEAD_DIM),
        parts,
    )
    sums, at = sums.reshape(-1), 0
    small = []
    for size in sizes:
        small.append(sums[at : at + size])
        at += size
    out_bq, out_bv, out_bo, out_g1, out_s1, out_b2, out_g2, out_s2, out_b1 = small
    out_w1 = (
        rows_w1.reshape(GROUP, weight_rows, 2, unit_rows)
        .transpose(1, 2, 0, 3)
        .reshape(weight_rows, units)
        .astype(f32)
    )
    out_q, out_k, out_v = [
        rows_qkv[:, :, at * HEAD_DIM : (at + 1) * HEAD_DIM]
        .reshape(8, 2, weight_rows, HEAD_DIM)
        .transpose(2, 1, 0, 3)
        .reshape(weight_rows, width)
        .astype(f32)
        for at in range(3)
    ]

    return (
        output, input_grad, out_q, out_bq, out_k, out_v, out_bv, out_wo, out_bo, out_g1, out_s1,
        out_w1, out_b1, out_w2, out_b2, out_g2, out_s2,
    )


def solution(mesh):
    in_specs = (
        P("dp", None),
        P("dp", None),
        P(),
        P("dp", None),
        P("dp"),
        P("dp", None),
        P("dp", None),
        P("dp"),
        P("dp", None),
        P("dp"),
        P("dp"),
        P("dp"),
        P("dp", None),
        P("dp"),
        P("dp", None),
        P("dp"),
        P("dp"),
        P("dp"),
    )
    out_specs = (
        P("dp", None),
        P("dp", None),
        P("dp", None),
        P("dp"),
        P("dp", None),
        P("dp", None),
        P("dp"),
        P("dp", None),
        P("dp"),
        P("dp"),
        P("dp"),
        P("dp", None),
        P("dp"),
        P("dp", None),
        P("dp"),
        P("dp"),
        P("dp"),
    )
    two_groups = mesh.shape["dp"] == 2 * GROUP
    return jax.shard_map(
        grouped_device if two_groups else per_device, mesh=mesh, in_specs=in_specs, out_specs=out_specs, check_vma=False
    )
```

```python
import functools

import jax
import jax.numpy as jnp
from jax import lax
from jax.experimental import pallas as pl
from jax.experimental.pallas import tpu as pltpu
from jax.sharding import PartitionSpec as P

HEADS = 16
HEAD_DIM = 128
SEQ_MAX = 160
SPAN = 3

GROUP = 16
HALO = 256
WINDOW = 512
TILE = 128
MESH_ID = pl.DeviceIdType.MESH
VMEM_LIMIT = 60 << 20
PORTIONS = ((0, 48), (48, 48), (96, 32))
ORDERS = ((0, 1, 2), (1, 2, 0), (2, 0, 1))


norm_eps = 1e-05


def layer_norm(residual, gain_vec, shift_vec):
    mean_val = jnp.mean(residual, axis=-1, keepdims=True)
    centred = residual - mean_val
    var_val = jnp.mean(centred * centred, axis=-1, keepdims=True)
    return centred * lax.rsqrt(var_val + norm_eps) * gain_vec + shift_vec


def gelu_tanh(values):
    return jax.nn.gelu(values, approximate=True)


def plan_layout(lengths, tok_dev):
    starts = jnp.cumsum(lengths) - lengths
    owner_first = starts // tok_dev
    return (starts, starts, lengths, owner_first)


def to_owners(shard, layout, dev_count, piece_rows):
    starts, owner_start, owner_length, owner_first = layout
    tok_dev = shard.shape[0]
    feat_width = shard.shape[1]
    device = lax.axis_index("dp")
    held_rows = lax.all_to_all(
        shard.reshape(dev_count, piece_rows, feat_width),
        "dp",
        split_axis=0,
        concat_axis=0,
        tiled=True,
    )
    held_rows = held_rows.reshape(dev_count * piece_rows, feat_width)
    slot_ids = jnp.arange(SPAN * piece_rows, dtype=jnp.int32)
    shard_step = slot_ids // piece_rows
    within = slot_ids % piece_rows
    source = owner_first[:, None] + shard_step[None, :]
    global_row = source * tok_dev + device * piece_rows + within[None, :]
    inside = (
        (global_row >= owner_start[:, None])
        & (global_row < (owner_start + owner_length)[:, None])
        & (source < dev_count)
    )
    picked = held_rows[jnp.clip(source, 0, dev_count - 1) * piece_rows + within[None, :]]
    outgoing = jnp.where(inside[:, :, None], picked, jnp.zeros((), picked.dtype))
    arrived = lax.all_to_all(outgoing, "dp", split_axis=0, concat_axis=0, tiled=True)
    arrived = arrived.reshape(dev_count * SPAN * piece_rows, feat_width)
    my_start = owner_start[device]
    my_length = owner_length[device]
    my_first = owner_first[device]
    places = jnp.arange(SEQ_MAX, dtype=jnp.int32)
    global_pos = my_start + places
    shard_of = global_pos // tok_dev
    offset_in = global_pos % tok_dev
    slot_index = (
        offset_in // piece_rows * (SPAN * piece_rows)
        + (shard_of - my_first) * piece_rows
        + offset_in % piece_rows
    )
    valid_rows = places < my_length
    slot_index = jnp.where(valid_rows, slot_index, 0)
    owned = jnp.where(valid_rows[:, None], arrived[slot_index], jnp.zeros((), arrived.dtype))
    return (owned, valid_rows)


def to_order(owned, layout, dev_count, piece_rows, tok_dev):
    starts, owner_start, owner_length, owner_first = layout
    feat_width = owned.shape[1]
    device = lax.axis_index("dp")
    my_start = owner_start[device]
    my_length = owner_length[device]
    my_first = owner_first[device]
    slot_ids = jnp.arange(SPAN * piece_rows, dtype=jnp.int32)
    shard_step = slot_ids // piece_rows
    within = slot_ids % piece_rows
    targets = jnp.arange(dev_count, dtype=jnp.int32)
    global_row = (
        (my_first + shard_step)[None, :] * tok_dev + targets[:, None] * piece_rows + within[None, :]
    )
    place_row = global_row - my_start
    inside = (place_row >= 0) & (place_row < my_length)
    picked = owned[jnp.clip(place_row, 0, owned.shape[0] - 1)]
    outgoing = jnp.where(inside[:, :, None], picked, jnp.zeros((), picked.dtype))
    returned = lax.all_to_all(outgoing, "dp", split_axis=0, concat_axis=0, tiled=True)
    returned = returned.reshape(dev_count * SPAN * piece_rows, feat_width)
    sources = jnp.arange(dev_count, dtype=jnp.int32)
    within_piece = jnp.arange(piece_rows, dtype=jnp.int32)
    row_ids = sources[:, None] * tok_dev + device * piece_rows + within_piece[None, :]
    seq_of = jnp.sum((row_ids[:, :, None] >= starts[None, None, :]).astype(jnp.int32), 2) - 1
    slot_index = (
        seq_of * (SPAN * piece_rows)
        + (sources[:, None] - owner_first[seq_of]) * piece_rows
        + within_piece[None, :]
    )
    pieces = returned[slot_index]
    ordered = lax.all_to_all(pieces, "dp", split_axis=0, concat_axis=0, tiled=True)
    return ordered.reshape(tok_dev, feat_width)


def per_device(
    tokens,
    cotangent,
    lengths,
    wq,
    bq,
    wk,
    wv,
    bv,
    wo,
    bo,
    norm1_gain,
    norm1_bias,
    w1,
    b1,
    w2,
    b2,
    norm2_gain,
    norm2_bias,
):
    f32 = jnp.float32
    bf16 = jnp.bfloat16
    dev_count = lax.axis_size("dp")
    tok_dev = tokens.shape[0]
    feat_width = tokens.shape[1]
    piece_rows = tok_dev // dev_count
    layout = plan_layout(lengths, tok_dev)
    joined, valid_rows = to_owners(
        jnp.concatenate([tokens, cotangent], 1), layout, dev_count, piece_rows
    )
    inputs = joined[:, :feat_width]
    upstream = joined[:, feat_width:].astype(f32)
    slot_count = inputs.shape[0]
    score_scale = HEAD_DIM ** (-0.5)
    full_wq, full_wk, full_wv, full_wo, full_bq, full_bv, full_bo, gain_one, shift_one = (
        lax.all_gather(wq, "dp", axis=0, tiled=True),
        lax.all_gather(wk, "dp", axis=0, tiled=True),
        lax.all_gather(wv, "dp", axis=0, tiled=True),
        lax.all_gather(wo, "dp", axis=0, tiled=True),
        lax.all_gather(bq, "dp", axis=0, tiled=True),
        lax.all_gather(bv, "dp", axis=0, tiled=True),
        lax.all_gather(bo, "dp", axis=0, tiled=True),
        lax.all_gather(norm1_gain, "dp", axis=0, tiled=True),
        lax.all_gather(norm1_bias, "dp", axis=0, tiled=True),
    )
    queries = (
        (jnp.dot(inputs, full_wq, preferred_element_type=f32) + full_bq.astype(f32))
        .astype(bf16)
        .reshape(slot_count, HEADS, HEAD_DIM)
    )
    keys_low = (
        jnp.dot(inputs, full_wk, preferred_element_type=f32)
        .astype(bf16)
        .reshape(slot_count, HEADS, HEAD_DIM)
    )
    values_low = (
        (jnp.dot(inputs, full_wv, preferred_element_type=f32) + full_bv.astype(f32))
        .astype(bf16)
        .reshape(slot_count, HEADS, HEAD_DIM)
    )
    scores = jnp.einsum("qhd,khd->hqk", queries, keys_low, preferred_element_type=f32) * score_scale
    scores = jnp.where(valid_rows[None, None, :], scores, -1e30)
    row_max = jnp.max(scores, -1, keepdims=True)
    row_total = jnp.sum(jnp.exp(scores - row_max), -1, keepdims=True)
    log_total = row_max + jnp.log(row_total)
    attn_probs = jnp.exp(scores - log_total).astype(bf16)
    attended = jnp.einsum("hqk,khd->qhd", attn_probs, values_low, preferred_element_type=f32)
    attended = attended.reshape(slot_count, feat_width).astype(bf16)
    branch = jnp.dot(attended, full_wo, preferred_element_type=f32) + full_bo.astype(f32)
    resid_one = inputs.astype(f32) + branch
    hidden, norm_one_back = jax.vjp(
        layer_norm, resid_one, gain_one.astype(f32), shift_one.astype(f32)
    )
    hidden_low = hidden.astype(bf16)
    full_w1, full_w2, full_b1, full_b2, gain_two, shift_two = (
        lax.all_gather(w1, "dp", axis=0, tiled=True),
        lax.all_gather(w2, "dp", axis=0, tiled=True),
        lax.all_gather(b1, "dp", axis=0, tiled=True),
        lax.all_gather(b2, "dp", axis=0, tiled=True),
        lax.all_gather(norm2_gain, "dp", axis=0, tiled=True),
        lax.all_gather(norm2_bias, "dp", axis=0, tiled=True),
    )
    upward = jnp.dot(hidden_low, full_w1, preferred_element_type=f32) + full_b1.astype(f32)
    activ, gelu_back = jax.vjp(gelu_tanh, upward)
    activ_low = activ.astype(bf16)
    mixed = jnp.dot(activ_low, full_w2, preferred_element_type=f32) + full_b2.astype(f32)
    resid_two = hidden + mixed
    normed, norm_two_back = jax.vjp(
        layer_norm, resid_two, gain_two.astype(f32), shift_two.astype(f32)
    )
    result = jnp.where(valid_rows[:, None], normed, 0.0).astype(bf16)
    output = to_order(result, layout, dev_count, piece_rows, tok_dev)
    back_w1, back_w2 = (
        lax.all_gather(w1, "dp", axis=0, tiled=True),
        lax.all_gather(w2, "dp", axis=0, tiled=True),
    )
    grad_resid_two, grad_gain_two, grad_shift_two = norm_two_back(upstream)
    grad_mixed = grad_resid_two.astype(bf16)
    grad_bias_two = jnp.sum(grad_mixed.astype(f32), 0)
    grad_activ = jnp.einsum("td,fd->tf", grad_mixed, back_w2, preferred_element_type=f32)
    grad_upward = gelu_back(grad_activ)[0].astype(bf16)
    grad_bias_one = jnp.sum(grad_upward.astype(f32), 0)
    grad_hidden = grad_resid_two + jnp.einsum(
        "tf,df->td", grad_upward, back_w1, preferred_element_type=f32
    )
    grad_w2 = jnp.einsum("tf,td->fd", activ_low, grad_mixed, preferred_element_type=f32)
    grad_w1 = jnp.einsum("td,tf->df", hidden_low, grad_upward, preferred_element_type=f32)
    mlp_grads = (
        lax.psum_scatter(grad_w1, "dp", scatter_dimension=0, tiled=True),
        lax.psum_scatter(grad_w2, "dp", scatter_dimension=0, tiled=True),
        lax.psum_scatter(grad_bias_one, "dp", scatter_dimension=0, tiled=True),
        lax.psum_scatter(grad_bias_two, "dp", scatter_dimension=0, tiled=True),
        lax.psum_scatter(grad_gain_two, "dp", scatter_dimension=0, tiled=True),
        lax.psum_scatter(grad_shift_two, "dp", scatter_dimension=0, tiled=True),
    )
    back_wq, back_wk, back_wv, back_wo = (
        lax.all_gather(wq, "dp", axis=0, tiled=True),
        lax.all_gather(wk, "dp", axis=0, tiled=True),
        lax.all_gather(wv, "dp", axis=0, tiled=True),
        lax.all_gather(wo, "dp", axis=0, tiled=True),
    )
    grad_resid_one, grad_gain_one, grad_shift_one = norm_one_back(grad_hidden)
    grad_branch = grad_resid_one.astype(bf16)
    grad_bo = jnp.sum(grad_branch.astype(f32), 0)
    grad_wo = jnp.einsum("tc,td->cd", attended, grad_branch, preferred_element_type=f32)
    grad_attended = jnp.einsum(
        "td,cd->tc", grad_branch, back_wo, preferred_element_type=f32
    ).astype(bf16)
    grad_attended = grad_attended.reshape(slot_count, HEADS, HEAD_DIM)
    re_scores = (
        jnp.einsum("qhd,khd->hqk", queries, keys_low, preferred_element_type=f32) * score_scale
    )
    re_scores = jnp.where(valid_rows[None, None, :], re_scores, -1e30)
    re_probs = jnp.exp(re_scores - log_total)
    re_probs_low = re_probs.astype(bf16)
    grad_values = jnp.einsum(
        "hqk,qhd->khd", re_probs_low, grad_attended, preferred_element_type=f32
    ).astype(bf16)
    grad_probs = jnp.einsum("qhd,khd->hqk", grad_attended, values_low, preferred_element_type=f32)
    grad_scores = re_probs * (grad_probs - jnp.sum(re_probs * grad_probs, -1, keepdims=True))
    grad_scores_low = grad_scores.astype(bf16)
    grad_queries = (
        jnp.einsum("hqk,khd->qhd", grad_scores_low, keys_low, preferred_element_type=f32)
        * score_scale
    ).astype(bf16)
    grad_keys = (
        jnp.einsum("hqk,qhd->khd", grad_scores_low, queries, preferred_element_type=f32)
        * score_scale
    ).astype(bf16)
    grad_queries = grad_queries.reshape(slot_count, feat_width)
    grad_keys = grad_keys.reshape(slot_count, feat_width)
    grad_values = grad_values.reshape(slot_count, feat_width)
    grad_bq = jnp.sum(grad_queries.astype(f32), 0)
    grad_bv = jnp.sum(grad_values.astype(f32), 0)
    grad_wq = jnp.einsum("tc,td->cd", inputs, grad_queries, preferred_element_type=f32)
    grad_wk = jnp.einsum("tc,td->cd", inputs, grad_keys, preferred_element_type=f32)
    grad_wv = jnp.einsum("tc,td->cd", inputs, grad_values, preferred_element_type=f32)
    grad_input = grad_resid_one + jnp.einsum(
        "td,cd->tc", grad_queries, back_wq, preferred_element_type=f32
    )
    grad_input = grad_input + jnp.einsum(
        "td,cd->tc", grad_keys, back_wk, preferred_element_type=f32
    )
    grad_input = grad_input + jnp.einsum(
        "td,cd->tc", grad_values, back_wv, preferred_element_type=f32
    )
    grad_input = jnp.where(valid_rows[:, None], grad_input, 0.0).astype(bf16)
    attn_grads = (
        lax.psum_scatter(grad_wq, "dp", scatter_dimension=0, tiled=True),
        lax.psum_scatter(grad_wk, "dp", scatter_dimension=0, tiled=True),
        lax.psum_scatter(grad_wv, "dp", scatter_dimension=0, tiled=True),
        lax.psum_scatter(grad_wo, "dp", scatter_dimension=0, tiled=True),
        lax.psum_scatter(grad_bq, "dp", scatter_dimension=0, tiled=True),
        lax.psum_scatter(grad_bv, "dp", scatter_dimension=0, tiled=True),
        lax.psum_scatter(grad_bo, "dp", scatter_dimension=0, tiled=True),
        lax.psum_scatter(grad_gain_one, "dp", scatter_dimension=0, tiled=True),
        lax.psum_scatter(grad_shift_one, "dp", scatter_dimension=0, tiled=True),
    )
    sum_w1, sum_w2, sum_b1, sum_b2, sum_g2, sum_s2 = mlp_grads
    sum_wq, sum_wk, sum_wv, sum_wo, sum_bq, sum_bv, sum_bo, sum_g1, sum_s1 = attn_grads
    input_grad = to_order(grad_input, layout, dev_count, piece_rows, tok_dev)
    return (
        output,
        input_grad,
        sum_wq,
        sum_bq,
        sum_wk,
        sum_wv,
        sum_bv,
        sum_wo,
        sum_bo,
        sum_g1,
        sum_s1,
        sum_w1,
        sum_b1,
        sum_w2,
        sum_b2,
        sum_g2,
        sum_s2,
    )


def flip(device, bit):
    step = 1 << bit
    return device + step - 2 * step * ((device // step) % 2)


def chip_bits(device):
    return [(device // 2) % 2, (device // 4) % 2, (device // 8) % 2]


def enter(partners):
    barrier = pltpu.get_barrier_semaphore()
    for partner in partners:
        pl.semaphore_signal(barrier, inc=1, device_id=(partner,), device_id_type=MESH_ID)
    pl.semaphore_wait(barrier, len(partners))


def push(src, dst, send_sem, recv_sem, device):
    return pltpu.make_async_remote_copy(
        src_ref=src,
        dst_ref=dst,
        send_sem=send_sem,
        recv_sem=recv_sem,
        device_id=(device,),
        device_id_type=MESH_ID,
    )


def exchange_blocks(pairs, sems, base, mine, others):
    local_sem, send_sem, recv_sem = sems
    copies = []
    for at, (src, dst) in enumerate(pairs):
        for step, other in enumerate(others):
            copy = push(
                src.at[other - base],
                dst.at[mine],
                send_sem.at[at, step],
                recv_sem.at[at, step],
                other,
            )
            copy.start()
            copies.append(copy)
        local = pltpu.make_async_copy(src.at[mine], dst.at[mine], local_sem.at[at])
        local.start()
        copies.append(local)
    return copies


def group_places():
    device = lax.axis_index("dp")
    base = device // GROUP * GROUP
    mine = device % GROUP
    others = [base + (mine + step) % GROUP for step in range(1, GROUP)]
    across = (device + GROUP) % (2 * GROUP)
    return device // GROUP, base, mine, others, across


def tile_probs(qkv_ref, row, start, seg_q, seg_k):
    f32 = jnp.float32
    queries = qkv_ref[pl.ds(row, TILE), 0:HEAD_DIM]
    keys = qkv_ref[pl.ds(start, WINDOW), HEAD_DIM : 2 * HEAD_DIM]
    scores = lax.dot_general(queries, keys, (((1,), (1,)), ((), ())), preferred_element_type=f32)
    scores = jnp.where(seg_q == seg_k, scores * HEAD_DIM ** (-0.5), -1e30)
    weights = jnp.exp(scores - jnp.max(scores, -1, keepdims=True))
    return queries, keys, weights / jnp.sum(weights, -1, keepdims=True)


CHUNKS = 4
THIRDS = (((0, 768), (0, 1, 2)), ((768, 640), (1, 2, 0)), ((1408, 640), (2, 0, 1)))
LIGHT = (
    ((0, 512), (1, 2, 0)), ((512, 512), (0, 2, 1)), ((1024, 512), (1, 0, 2)), ((1536, 512), (0, 1, 2)),
)
PLANS = (THIRDS, LIGHT) + (THIRDS,) * 5
TAIL_PLANS = (LIGHT,)
SPLIT = 256
PAD = (WINDOW - TILE) // 2
STAGES = 7


def step_through(flows, fillers=None):
    waiting, alive = list(flows), []
    while waiting or alive:
        if waiting:
            alive.append(waiting.pop(0))
        alive = [flow for flow in alive if next(flow, "done") != "done"]
        if fillers is not None:
            next(fillers, None)
    if fillers is not None:
        for _ in fillers:
            pass


class Traffic:
    def __init__(self, sems, plans):
        self.plans = plans
        self.hop_send, self.hop_recv, self.pair_send, self.pair_recv = sems
        device = lax.axis_index("dp")
        self.core = device % 2
        self.bits = chip_bits(device)
        self.partners = [flip(device, 1), flip(device, 2), flip(device, 3)]
        self.pair = flip(device, 0)

    def chips(self, ref, values, columns):
        return ref.at[values[2], values[1], values[0], :, columns]

    def push(self, src, dst, stage, chunk, part, step):
        copy = push(
            src, dst,
            self.hop_send.at[stage, chunk, part, step],
            self.hop_recv.at[stage, chunk, part, step],
            self.partners[self.plans[stage][part][1][step]],
        )
        copy.start()
        return copy

    def share(self, src, dst, stage, chunk):
        copy = push(
            src, dst, self.pair_send.at[stage, chunk], self.pair_recv.at[stage, chunk], self.pair
        )
        copy.start()
        return copy

    def gather(self, slots, stage, chunk):
        mine = slots.at[self.core]
        hops = {}
        for step in range(3):
            for part, ((first, count), order) in enumerate(self.plans[stage]):
                if step:
                    hops[part, step - 1].wait_recv()
                values = list(self.bits)
                for dim in order[:step]:
                    values[dim] = slice(None)
                view = self.chips(mine, values, pl.ds(first, count))
                hops[part, step] = self.push(view, view, stage, chunk, part, step)
            yield
        for part in range(len(self.plans[stage])):
            hops[part, 2].wait_recv()
        share = self.share(mine, mine, stage, chunk)
        for copy in hops.values():
            copy.wait_send()
        return share

    def scatter(self, own, pair_in, incoming, share, stage, chunk, finish):
        rows = own.shape[-2]
        f32 = jnp.float32
        hops = {}
        share.wait()
        for step in range(4):
            for part, ((first, count), order) in enumerate(self.plans[stage]):
                columns = pl.ds(first, count)
                if step:
                    hops[part, step - 1].wait_recv()
                values = list(self.bits)
                free = ()
                if step < 3:
                    values[order[step]] = 1 - self.bits[order[step]]
                    free = order[step + 1 :]
                for mask in range(1 << len(free)):
                    slot = list(values)
                    for place, dim in enumerate(free):
                        slot[dim] = (mask >> place) & 1
                    where = (slot[2], slot[1], slot[0])
                    for row in range(0, rows, 16):
                        at = (slice(row, row + 16), columns)
                        total = own[where + at].astype(f32) + pair_in[where + at].astype(f32)
                        for back in range(step):
                            left = [slot[dim] for dim in (2, 1, 0) if dim not in order[: back + 1]]
                            total = total + incoming[back][tuple(left) + at].astype(f32)
                        if step < 3:
                            own[where + at] = total.astype(own.dtype)
                        else:
                            finish(row, first, count, total)
                if step == 3:
                    continue
                for dim in free:
                    values[dim] = slice(None)
                left = tuple(slice(None) for _ in free)
                hops[part, step] = self.push(
                    self.chips(own, values, columns),
                    incoming[step].at[left + (slice(None), columns)],
                    stage, chunk, part, step,
                )
            if step < 3:
                yield
        for copy in hops.values():
            copy.wait_send()


def gelu_slope(up):
    inner = 0.7978845608028654 * (up + 0.044715 * (up * up * up))
    tanh = jnp.tanh(inner)
    return 0.5 * (1.0 + tanh) + 0.5 * up * (1.0 - tanh * tanh) * (
        0.7978845608028654 * (1.0 + 0.134145 * (up * up))
    )


NT = (((1,), (1,)), ((), ()))
TN = (((0,), (0,)), ((), ()))


def layer_kernel(
    tok_ref, cot_ref, pack_qkv, pack_w1, w2_ref, wo_ref, vec_ref, seg_q_ref, seg_k_ref,
    out_ref, dres_ref, vecg_ref, gb1_ref, gw2_own, gw2_far, gw2_in, gw1_own, gw1_far, gw1_in, gwo_ref,
    x_all, h_all, qkv_ref, dout_ref, wqkv_ref,
    all_h, all_m, own_part, far_part, pair_in, in_one, in_two, in_three,
    up_ref, act_ref, act_t, dup_ref, dup_t, att_ref, att_t, res_ref, hid_ref, norm_ref, scale_ref,
    w1_all, w2_all, wo_all, vec_all, low_ref, high_ref, b1_ref, stage_ref, stage_low, stage_w1, stage_w1_low,
    hop_send, hop_recv, pair_send, pair_recv,
    block_local, block_send, block_recv, vec_send, vec_recv, far_send, far_recv,
    local_sems, out_sems, spill_sems,
):
    f32, low = jnp.float32, tok_ref.dtype
    block, width = tok_ref.shape
    rows = block // CHUNKS
    half_rows = rows * GROUP // 2
    own_rows = GROUP * block
    units = w1_all.shape[-1]
    group, base, mine, others, across = group_places()
    net = Traffic((hop_send, hop_recv, pair_send, pair_recv), PLANS)
    core, bits = net.core, net.bits
    chip = mine // 2
    head = core * 8 + chip
    own_slot = (core, bits[2], bits[1], bits[0])
    ext = PAD + group * HALO
    enter(others + [across, flip(across, 0)])

    def far(src, dst, at, device=across):
        copy = push(src, dst, far_send.at[at], far_recv.at[at], device)
        copy.start()
        return copy

    def local(src, dst, at):
        copy = pltpu.make_async_copy(src, dst, local_sems.at[at])
        copy.start()
        return copy

    early = w2_ref.shape[0] // 2
    far_vec = far(vec_ref, vec_all.at[group, mine], 0)
    near = [
        local(vec_ref, vec_all.at[group, mine], 0),
        local(w2_ref, w2_all.at[group], 1),
        local(wo_ref, wo_all.at[group, core], 2),
    ]
    w2_first, w2_last = pl.ds(0, early), pl.ds(early, w2_ref.shape[0] - early)
    far_w2 = [far(w2_ref.at[w2_first, :], w2_all.at[group, w2_first, :], 1)]
    qkv_blocks = exchange_blocks(
        [(pack_qkv, wqkv_ref.at[group])],
        (block_local.at[0:1], block_send.at[0:1], block_recv.at[0:1]), base, mine, others,
    )
    for chunk in range(CHUNKS):
        all_m[(chunk,) + own_slot] = tok_ref[chunk * rows : (chunk + 1) * rows, :]
    wo_near = push(
        wo_ref, wo_all.at[group, core], far_send.at[2], far_recv.at[2], net.pair
    )
    wo_near.start()

    qkv_ref[0:PAD, :] = jnp.zeros((PAD, qkv_ref.shape[1]), low)
    qkv_ref[qkv_ref.shape[0] - PAD :, :] = jnp.zeros((PAD, qkv_ref.shape[1]), low)
    vecg_ref[...] = jnp.zeros_like(vecg_ref)
    gb1_ref[...] = jnp.zeros_like(gb1_ref)

    def row_at(chunk, side):
        return pl.multiple_of((chunk * 2 + side) * half_rows, half_rows)

    def flat(ref, chunk, side, columns=slice(None)):
        return ref[chunk, side, :, :, :, :, columns].reshape(half_rows, -1)

    def tiles(count, body):
        def step(at, carry):
            body(at, pl.ds(pl.multiple_of(at * SPLIT, SPLIT), SPLIT))
            return carry

        lax.fori_loop(0, count // SPLIT, step, 0)

    def pieces(chunk, side):
        return [
            pl.multiple_of((slot * 2 + side) * block + chunk * rows, rows)
            for slot in range(GROUP // 2)
        ]

    def project_half(chunk, side, which):
        columns = pl.ds(pl.multiple_of(which * (width // 2), width // 2), width // 2)
        weight = wqkv_ref[which].reshape(width // 2, -1)
        return jnp.dot(flat(all_m, chunk, side, columns), weight, preferred_element_type=f32)

    def spill(src, dst, chunk, at):
        copy = pltpu.make_async_copy(src.at[chunk], dst.at[chunk], spill_sems.at[at, chunk])
        copy.start()
        return copy

    wide = slice(0, 3 * HEAD_DIM)
    spills = {}

    def token_flow(chunk):
        share = yield from net.gather(all_m.at[chunk], 0, chunk)
        up_ref[pl.ds(row_at(chunk, core), half_rows), wide] = project_half(chunk, core, group)
        yield
        share.wait()
        up_ref[pl.ds(row_at(chunk, 1 - core), half_rows), wide] = project_half(
            chunk, 1 - core, group
        )
        spills[0, chunk] = spill(all_m, x_all, chunk, 0)

    def weight_flow():
        yield
        for copy in qkv_blocks:
            copy.wait()
        state["far_qkv"] = far(wqkv_ref.at[group], wqkv_ref.at[group], 3)
        state["w1_blocks"] = exchange_blocks(
            [(pack_w1, w1_all.at[group])],
            (block_local.at[1:2], block_send.at[1:2], block_recv.at[1:2]), base, mine, others,
        )
        yield
        for copy in near:
            copy.wait()
        far_vec.wait()
        both = vec_all.at[:, mine]
        state["vec"] = []
        for step, other in enumerate(others):
            copy = push(both, both, vec_send.at[step], vec_recv.at[step], other)
            copy.start()
            state["vec"].append(copy)
        yield

    state = {"backs": 0}
    flows = [token_flow(chunk) for chunk in range(CHUNKS)]
    step_through([flows[0], weight_flow()] + flows[1:])

    for copy in state["vec"]:
        copy.wait()
    lane = lax.broadcasted_iota(jnp.int32, (8, 128), 1)
    for at in range(GROUP):
        first = vec_all[at // 8, at % 8 * 2]
        second = vec_all[at // 8, at % 8 * 2 + 1]
        here = slice(at * 128, at * 128 + 128)
        low_ref[:, here] = jnp.where(lane < 64, first, pltpu.roll(second, 64, 1))
        high_ref[:, here] = jnp.where(lane < 64, pltpu.roll(first, 64, 1), second)
    for half in range(2):
        for part in range(2):
            b1_ref[0:1, half * 256 + part * 128 : half * 256 + part * 128 + 128] = vec_all[
                half, mine, 4 + part : 5 + part, :
            ]
    head_at = pl.ds(pl.multiple_of(head * HEAD_DIM, HEAD_DIM), HEAD_DIM)
    bias_q, bias_v = low_ref[0:1, head_at], high_ref[0:1, head_at]
    bias_qkv = jnp.concatenate([bias_q, jnp.zeros_like(bias_q), bias_v], 1)
    bo, shift_one, gain_two = low_ref[1:2, :], low_ref[2:3, :], low_ref[3:4, :]
    gain_one, b2, shift_two = high_ref[1:2, :], high_ref[2:3, :], high_ref[3:4, :]

    state["far_qkv"].wait()
    far_wo_to = (1 - group) * GROUP + 2 * chip + group
    far_wo = push(
        wo_ref, wo_all.at[group, core], far_send.at[4 + core], far_recv.at[4 + core], far_wo_to
    )
    far_wo.start()
    for chunk in range(CHUNKS):
        for side in range(2):
            here = pl.ds((chunk * 2 + side) * half_rows, half_rows)
            total = up_ref[here, wide] + project_half(chunk, side, 1 - group) + bias_qkv
            total = total.astype(low)
            for slot, place in enumerate(pieces(chunk, side)):
                qkv_ref[pl.ds(pl.multiple_of(ext + place, rows), rows), :] = total[
                    slot * rows : (slot + 1) * rows
                ]
    halo_src = pl.ds(pl.multiple_of(PAD + 1792 - group * 1536, 64), HALO)
    halo_dst = pl.ds(pl.multiple_of(PAD + 2048 * group, 64), HALO)
    far_halo = far(qkv_ref.at[halo_src, :], qkv_ref.at[halo_dst, :], 6)
    for copy in state["w1_blocks"]:
        copy.wait()
    far_w1 = far(w1_all.at[group], w1_all.at[group], 7)
    far_w2.append(far(w2_ref.at[w2_last, :], w2_all.at[group, w2_last, :], 8))

    def attend_tile(at):
        tile = at + group * (GROUP - 1 - 2 * at)
        row = pl.multiple_of(ext + tile * TILE, 64)
        start = pl.multiple_of(ext - PAD + tile * TILE, 64)
        place = pl.multiple_of(group * HALO + tile * TILE, TILE)
        _, _, probs = tile_probs(
            qkv_ref, row, start, seg_q_ref[pl.ds(place, TILE), :],
            seg_k_ref[group * (HALO // TILE) + tile],
        )
        values = qkv_ref[pl.ds(start, WINDOW), 2 * HEAD_DIM : 3 * HEAD_DIM]
        out = jnp.dot(probs.astype(low), values, preferred_element_type=f32)
        att_ref[pl.ds(pl.multiple_of(tile * TILE, TILE), TILE), :] = out.astype(low)

    def attend_two(at, carry):
        attend_tile(2 * at)
        attend_tile(2 * at + 1)
        return carry

    lax.fori_loop(0, own_rows // TILE // 2 - 1, attend_two, 0)
    far_halo.wait()
    attend_tile(own_rows // TILE - 2)
    attend_tile(own_rows // TILE - 1)
    for chunk in range(CHUNKS):
        spills[0, chunk].wait()
    wo_near.wait()
    far_wo.wait_send()

    @pl.when(core != group)
    def _():
        for at in range(2):
            push(
                wo_ref, wo_all.at[1 - group, at], far_send.at[4 + at], far_recv.at[4 + at],
                far_wo_to,
            ).wait_recv()

    def branch_part(chunk, side, dst):
        rows_in = jnp.concatenate([att_ref[pl.ds(at, rows), :] for at in pieces(chunk, side)], 0)
        att_t[:, pl.ds(row_at(chunk, side), half_rows)] = rows_in.astype(f32).T.astype(low)

        def body(at, columns):
            weight = wo_all[core, :, :, columns].reshape(HEAD_DIM, SPLIT)
            part = jnp.dot(rows_in, weight, preferred_element_type=f32)
            dst[:, :, :, :, columns] = part.astype(low).reshape(2, 2, 2, rows, SPLIT)

        tiles(width, body)

    def upward(chunk, side):
        here = pl.ds(row_at(chunk, side), half_rows)

        def body(at, columns):
            weight = w1_all[:, :, :, columns].reshape(width, SPLIT)
            up = jnp.dot(flat(all_h, chunk, side), weight, preferred_element_type=f32)
            up = up + b1_ref[0:1, columns]
            up_ref[here, columns] = up
            act = gelu_tanh(up)
            act_ref[:, columns] = act.astype(low)
            act_t[columns, here] = act.T.astype(low)

        tiles(units, body)

    def downward(dst):
        def body(at, columns):
            weight = w2_all[:, :, columns].reshape(units, SPLIT)
            part = jnp.dot(act_ref[...], weight, preferred_element_type=f32)
            dst[:, :, :, :, columns] = part.astype(low).reshape(2, 2, 2, rows, SPLIT)

        tiles(width, body)

    def up_back(chunk, side):
        here = pl.ds(row_at(chunk, side), half_rows)

        def body(at, columns):
            grad = lax.dot_general(
                flat(all_m, chunk, side), w2_all[at], NT, preferred_element_type=f32
            )
            grad = (grad * gelu_slope(up_ref[here, columns])).astype(low)
            dup_ref[:, columns] = grad
            grad = grad.astype(f32)
            gb1_ref[0:1, columns] += jnp.sum(grad, 0, keepdims=True)
            dup_t[columns, here] = grad.T.astype(low)

        tiles(units, body)

    def down_back(dst):
        def body(at, columns):
            weight = w1_all[at // 4, pl.ds(at % 4 * 4, 4)].reshape(SPLIT, units)
            part = lax.dot_general(dup_ref[...], weight, NT, preferred_element_type=f32)
            dst[:, :, :, :, columns] = part.astype(low).reshape(2, 2, 2, rows, SPLIT)

        tiles(width, body)

    def out_back(chunk, side):
        weight = wo_all[core].reshape(HEAD_DIM, width)
        grad = lax.dot_general(flat(all_h, chunk, side), weight, NT, preferred_element_type=f32)
        grad = grad.astype(low)
        for slot, place in enumerate(pieces(chunk, side)):
            dout_ref[pl.ds(pl.multiple_of(group * HALO + place, rows), rows), :] = grad[
                slot * rows : (slot + 1) * rows
            ]

    def keep(chunk):
        def finish(row, first, count, total):
            res_ref[chunk * rows + row : chunk * rows + row + 16, first : first + count] = total

        return finish

    def row_sets(chunk):
        for row in range(0, rows, 16):
            yield slice(chunk * rows + row, chunk * rows + row + 16), slice(row, row + 16)

    def normal(res):
        res = res - jnp.mean(res, -1, keepdims=True)
        scale = lax.rsqrt(jnp.mean(res * res, -1, keepdims=True) + norm_eps)
        return res * scale, scale

    def normal_back(grad, res, gain, scale, at):
        vecg_ref[at + 2 : at + 3, :] += jnp.sum(grad, 0, keepdims=True)
        vecg_ref[at + 1 : at + 2, :] += jnp.sum(grad * res, 0, keepdims=True)
        grad = grad * gain
        first = jnp.mean(grad, -1, keepdims=True)
        second = jnp.mean(grad * res, -1, keepdims=True)
        grad = (grad - first - res * second) * scale
        grad_low = grad.astype(low)
        vecg_ref[at : at + 1, :] += jnp.sum(grad_low.astype(f32), 0, keepdims=True)
        return grad, grad_low

    def norm_one(chunk):
        for at, place in row_sets(chunk):
            res, scale = normal(tok_ref[at, :].astype(f32) + res_ref[at, :] + bo)
            norm_ref[at, :] = res
            scale_ref[at, :] = jnp.broadcast_to(scale, (16, 128))
            hidden = res * gain_one + shift_one
            hid_ref[at, :] = hidden
            all_h[(chunk,) + own_slot + (place, slice(None))] = hidden.astype(low)

    def norm_two(chunk):
        for at, place in row_sets(chunk):
            res, scale = normal(hid_ref[at, :] + res_ref[at, :] + b2)
            out_ref[at, :] = (res * gain_two + shift_two).astype(low)
            grad, grad_low = normal_back(cot_ref[at, :].astype(f32), res, gain_two, scale, 0)
            dres_ref[at, :] = grad
            all_m[(chunk,) + own_slot + (place, slice(None))] = grad_low

    def norm_one_back(chunk):
        for at, place in row_sets(chunk):
            grad, grad_low = normal_back(
                dres_ref[at, :] + res_ref[at, :], norm_ref[at, :], gain_one,
                scale_ref[at, 0:1], 3,
            )
            dres_ref[at, :] = grad
            all_h[(chunk,) + own_slot + (place, slice(None))] = grad_low

    def flow(chunk):
        incoming = (in_one.at[chunk], in_two.at[chunk], in_three.at[chunk])
        own, other = own_part.at[chunk], far_part.at[chunk % 2]
        arrived = pair_in.at[chunk]
        branch_part(chunk, 1 - core, other)
        share = net.share(other, arrived, 1, chunk)
        branch_part(chunk, core, own)
        yield
        yield from net.scatter(own, arrived, incoming, share, 1, chunk, keep(chunk))
        norm_one(chunk)
        share = yield from net.gather(all_h.at[chunk], 2, chunk)
        if chunk == 0:
            far_w1.wait()
        upward(chunk, core)
        if chunk == 0:
            for copy in far_w2:
                copy.wait()
        downward(own)
        yield
        share.wait()
        spills[1, chunk] = spill(all_h, h_all, chunk, 1)
        upward(chunk, 1 - core)
        downward(other)
        share = net.share(other, arrived, 3, chunk)
        yield
        yield from net.scatter(own, arrived, incoming, share, 3, chunk, keep(chunk))
        norm_two(chunk)
        spills[1, chunk].wait()
        share = yield from net.gather(all_m.at[chunk], 4, chunk)
        up_back(chunk, core)
        down_back(own)
        yield
        share.wait()
        up_back(chunk, 1 - core)
        down_back(other)
        share = net.share(other, arrived, 5, chunk)
        state["backs"] += 1
        yield
        yield from net.scatter(own, arrived, incoming, share, 5, chunk, keep(chunk))
        norm_one_back(chunk)
        share = yield from net.gather(all_h.at[chunk], 6, chunk)
        out_back(chunk, core)
        yield
        share.wait()
        out_back(chunk, 1 - core)

    def product(left_t, right, columns):
        total = None
        for chunk in range(CHUNKS):
            for side in range(2):
                here = slice((chunk * 2 + side) * half_rows, (chunk * 2 + side + 1) * half_rows)
                term = jnp.dot(
                    left_t[:, here], flat(right, chunk, side, columns), preferred_element_type=f32
                )
                total = term if total is None else total + term
        return total

    def run(first, last, write):
        def step(at, carry):
            write(at, at % 2, at >= 2)
            return carry

        lax.fori_loop(first, last, step, 0)

    def emit(src, dst, sem, again):
        copy = pltpu.make_async_copy(src, dst, sem)

        @pl.when(again)
        def _():
            copy.wait()

        return copy

    def columns_at(at):
        return pl.ds(pl.multiple_of(at * SPLIT, SPLIT), SPLIT)

    def write_w2(at, slot, again):
        own = emit(stage_ref.at[slot], gw2_own.at[:, columns_at(at)], out_sems.at[0, slot], again)
        there = emit(stage_low.at[slot], gw2_far.at[:, columns_at(at)], out_sems.at[1, slot], again)
        total = product(act_t, all_m, columns_at(at))
        first = group == 0
        stage_ref[slot] = jnp.where(first, total[:256], total[256:])
        stage_low[slot] = jnp.where(first, total[256:], total[:256]).astype(low)
        own.start()
        there.start()

    def write_w1_own(at, slot, again):
        own = emit(stage_w1.at[slot], gw1_own.at[columns_at(at), :], out_sems.at[2, slot], again)
        stage_w1[slot] = product(dup_t, all_m, columns_at(group * 4 + at)).T
        own.start()

    def write_w1_far(at, slot, again):
        there = emit(stage_w1_low.at[slot], gw1_far.at[columns_at(at), :], out_sems.at[3, slot], again)
        stage_w1_low[slot] = product(dup_t, all_m, columns_at((1 - group) * 4 + at)).T.astype(low)
        there.start()

    def write_wo(at, slot, again):
        own = emit(stage_ref.at[slot, 0:HEAD_DIM, :], gwo_ref.at[:, columns_at(at)], out_sems.at[4, slot], again)
        stage_ref[slot, 0:HEAD_DIM, :] = product(att_t, all_h, columns_at(at))
        own.start()

    def fill():
        while state["backs"] < CHUNKS:
            yield
        run(0, width // SPLIT // 2, write_w2)
        yield
        run(width // SPLIT // 2, width // SPLIT, write_w2)
        for slot in range(2):
            emit(stage_ref.at[slot], gw2_own.at[:, columns_at(0)], out_sems.at[0, slot], True)
            emit(stage_low.at[slot], gw2_far.at[:, columns_at(0)], out_sems.at[1, slot], True)
        swaps.append(far(gw2_far, gw2_in, 10))
        back = [pltpu.make_async_copy(h_all.at[at], all_m.at[at], spill_sems.at[2, at]) for at in range(CHUNKS)]
        for copy in back:
            copy.start()
        yield
        for copy in back:
            copy.wait()
        run(0, width // SPLIT // 2, write_w1_far)
        for slot in range(2):
            emit(stage_w1_low.at[slot], gw1_far.at[columns_at(0), :], out_sems.at[3, slot], True)
        early_w1 = gw1_far.at[pl.ds(0, width // 4), :]
        swaps.append(far(early_w1, gw1_in, 11))
        yield
        run(0, width // SPLIT // 2, write_w1_own)
        for slot in range(2):
            emit(stage_w1.at[slot], gw1_own.at[columns_at(0), :], out_sems.at[2, slot], True)

    swaps = []
    step_through([flow(chunk) for chunk in range(CHUNKS)], fill())
    halo_src = pl.ds(pl.multiple_of(1792 - group * 1536, 64), HALO)
    halo_dst = pl.ds(pl.multiple_of(2048 * group, 64), HALO)
    far_dout = far(dout_ref.at[halo_src, :], dout_ref.at[halo_dst, :], 9)
    run(0, width // SPLIT, write_wo)
    for slot in range(2):
        emit(stage_ref.at[slot, 0:HEAD_DIM, :], gwo_ref.at[:, columns_at(0)], out_sems.at[4, slot], True)
    far_dout.wait()
    for copy in swaps:
        copy.wait()


def layer(tokens, cotangent, pack_qkv, pack_w1, w2, wo, vector, seg_q, seg_k):
    f32, bf16 = jnp.float32, jnp.bfloat16
    block, width = tokens.shape
    rows = block // CHUNKS
    unit_rows = w2.shape[0]
    units = 2 * unit_rows
    half_rows = rows * GROUP // 2
    own_rows = GROUP * block
    weight_rows = wo.shape[0]
    peers = GROUP - 1
    vmem = pl.BlockSpec(memory_space=pltpu.VMEM)
    anywhere = pl.BlockSpec(memory_space=pl.ANY)
    sems = pltpu.SemaphoreType.DMA
    shape = jax.ShapeDtypeStruct

    def slots(*lead):
        return pltpu.VMEM(lead + (rows, width), bf16)

    return pl.pallas_call(
        layer_kernel,
        out_shape=[
            shape((block, width), bf16),
            shape((block, width), f32),
            shape((8, width), f32),
            shape((8, units), f32),
            shape((unit_rows, width), f32),
            shape((unit_rows, width), bf16),
            shape((unit_rows, width), bf16),
            shape((width // 2, units), f32),
            shape((width // 2, units), bf16),
            shape((width // 4, units), bf16),
            shape((HEAD_DIM, width), f32),
            shape((CHUNKS, 2, 2, 2, 2, rows, width), bf16),
            shape((CHUNKS, 2, 2, 2, 2, rows, width), bf16),
            shape((own_rows + HALO + 2 * PAD, 3 * HEAD_DIM), bf16),
            shape((own_rows + HALO, HEAD_DIM), bf16),
            shape((2, GROUP, weight_rows, 3 * HEAD_DIM), bf16),
        ],
        in_specs=[vmem, vmem, anywhere, anywhere, anywhere, anywhere, vmem, vmem, vmem],
        out_specs=[vmem] * 4 + [anywhere] * 9 + [vmem] * 3,
        scratch_shapes=[
            slots(CHUNKS, 2, 2, 2, 2), slots(CHUNKS, 2, 2, 2, 2),
            slots(CHUNKS, 2, 2, 2), slots(2, 2, 2, 2), slots(CHUNKS, 2, 2, 2),
            slots(CHUNKS, 2, 2), slots(CHUNKS, 2), slots(CHUNKS),
            pltpu.VMEM((own_rows, units), f32),
            pltpu.VMEM((half_rows, units), bf16),
            pltpu.VMEM((units, own_rows), bf16),
            pltpu.VMEM((half_rows, units), bf16),
            pltpu.VMEM((units, own_rows), bf16),
            pltpu.VMEM((own_rows, HEAD_DIM), bf16),
            pltpu.VMEM((HEAD_DIM, own_rows), bf16),
            pltpu.VMEM((block, width), f32),
            pltpu.VMEM((block, width), f32),
            pltpu.VMEM((block, width), f32),
            pltpu.VMEM((block, 128), f32),
            pltpu.VMEM((2, GROUP, weight_rows, units), bf16),
            pltpu.VMEM((2, unit_rows, width), bf16),
            pltpu.VMEM((2, 2, weight_rows, width), bf16),
            pltpu.VMEM((2, GROUP, 8, 128), f32),
            pltpu.VMEM((8, width), f32),
            pltpu.VMEM((8, width), f32),
            pltpu.VMEM((8, units), f32),
            pltpu.VMEM((2, SPLIT, SPLIT), f32),
            pltpu.VMEM((2, SPLIT, SPLIT), bf16),
            pltpu.VMEM((2, SPLIT, units), f32),
            pltpu.VMEM((2, SPLIT, units), bf16),
            sems((STAGES, CHUNKS, 4, 3)), sems((STAGES, CHUNKS, 4, 3)),
            sems((STAGES, CHUNKS)), sems((STAGES, CHUNKS)),
            sems((2,)), sems((2, peers)), sems((2, peers)), sems((peers,)), sems((peers,)),
            sems((12,)), sems((12,)), sems((3,)), sems((5, 2)), sems((3, CHUNKS)),
        ],
        compiler_params=pltpu.CompilerParams(
            collective_id=4, has_side_effects=True, vmem_limit_bytes=63 << 20
        ),
        name="layer",
    )(tokens, cotangent, pack_qkv, pack_w1, w2, wo, vector, seg_q, seg_k)


def tail_kernel(
    qkv_ref, dout_ref, seg_q_ref, seg_k_ref, wqkv_ref, dres_ref, gwo_ref, parts_ref,
    x_all, w1_own, w1_far, w1_early, w2_own, w2_early,
    input_ref, out_q, out_k, out_v, out_wo, out_w1, out_w2, vec_ref,
    xs_ref, own_part, far_part, pair_in, in_one, in_two, in_three, res_ref,
    dqkv_ref, dk_sum, dv_sum, dqkv_t, gq_own, gq_far, gq_in, gq_send, gq_recv,
    w1_sum, w1_in, w1_send, w1_recv, w2_sum, w2_in, wo_low, wo_in, wo_pair, wo_pair_in,
    blocks_ref, arrived, theirs, far_vec_in,
    hop_send, hop_recv, pair_send, pair_recv, load_sems,
    block_local, block_send, block_recv, far_send, far_recv,
):
    f32, low = jnp.float32, qkv_ref.dtype
    block, width = dres_ref.shape
    rows = block // CHUNKS
    half_rows = rows * GROUP // 2
    weight_rows = out_q.shape[0]
    scale = HEAD_DIM ** (-0.5)
    group, base, mine, others, across = group_places()
    net = Traffic((hop_send, hop_recv, pair_send, pair_recv), TAIL_PLANS)
    core, chip = net.core, mine // 2
    enter(others + [across, flip(across, 0)])

    def far(src, dst, at, device=across):
        copy = push(src, dst, far_send.at[at], far_recv.at[at], device)
        copy.start()
        return copy

    def load(src, dst, at):
        copy = pltpu.make_async_copy(src, dst, load_sems.at[at])
        copy.start()
        return copy

    far_wo = push(
        wo_low, wo_in, far_send.at[0], far_recv.at[0], core * GROUP + 2 * chip + core
    )

    @pl.when(core != group)
    def _():
        wo_low[...] = gwo_ref[...].astype(low)
        far_wo.start()

    half = w1_far.shape[0] // 2
    late = pl.ds(half, half)
    far_w1 = far(w1_far.at[late, :], w1_in.at[late, :], 1)
    x_loads = [load(x_all.at[at], xs_ref.at[at], at) for at in range(CHUNKS)]
    loads = [
        load(w1_own, w1_sum, CHUNKS),
        load(w1_early, w1_in.at[pl.ds(0, half), :], CHUNKS + 1),
        load(w2_own, w2_sum, CHUNKS + 2),
        load(w2_early, w2_in, CHUNKS + 3),
    ]
    blocks_ref[...] = parts_ref[...]
    dk_sum[...] = jnp.zeros_like(dk_sum)
    dv_sum[...] = jnp.zeros_like(dv_sum)

    def attend_back_tile(tile):
        place = pl.multiple_of(tile * TILE, TILE)
        row = pl.multiple_of(PAD + place, 64)
        window = pl.ds(place, WINDOW)
        queries, keys, probs = tile_probs(
            qkv_ref, row, place, seg_q_ref[pl.ds(place, TILE), :], seg_k_ref[tile]
        )
        values = qkv_ref[window, 2 * HEAD_DIM : 3 * HEAD_DIM]
        grads = dout_ref[pl.ds(place, TILE), :]
        grad_probs = lax.dot_general(grads, values, NT, preferred_element_type=f32)
        inner = jnp.sum(probs * grad_probs, -1, keepdims=True)
        grad_scores = (probs * (grad_probs - inner)).astype(low)
        grad_q = jnp.dot(grad_scores, keys, preferred_element_type=f32)
        dqkv_ref[pl.ds(place, TILE), 0:HEAD_DIM] = (grad_q * scale).astype(low)
        dk_sum[window, :] += lax.dot_general(grad_scores, queries, TN, preferred_element_type=f32)
        dv_sum[window, :] += lax.dot_general(
            probs.astype(low), grads, TN, preferred_element_type=f32
        )

    def attend_back_two(at, carry):
        attend_back_tile(2 * at)
        attend_back_tile(2 * at + 1)
        return carry

    ext_rows = dout_ref.shape[0]
    lax.fori_loop(0, ext_rows // TILE // 2, attend_back_two, 0)
    inside = slice(PAD, PAD + ext_rows)
    dqkv_ref[:, HEAD_DIM : 2 * HEAD_DIM] = (dk_sum[inside, :] * scale).astype(low)
    dqkv_ref[:, 2 * HEAD_DIM : 3 * HEAD_DIM] = dv_sum[inside, :].astype(low)

    def rows_of(chunk, side):
        return jnp.concatenate(
            [
                dqkv_ref[
                    pl.ds(
                        pl.multiple_of(
                            group * HALO + (slot * 2 + side) * block + chunk * rows, rows
                        ),
                        rows,
                    ),
                    :,
                ]
                for slot in range(GROUP // 2)
            ],
            0,
        )

    bias = jnp.zeros((1, 3 * HEAD_DIM), f32)
    for chunk in range(CHUNKS):
        for side in range(2):
            part = rows_of(chunk, side).astype(f32)
            bias = bias + jnp.sum(part, 0, keepdims=True)
            here = slice((chunk * 2 + side) * half_rows, (chunk * 2 + side + 1) * half_rows)
            dqkv_t[:, here] = part.T.astype(low)

    for copy in x_loads:
        copy.wait()

    def product(at):
        columns = pl.ds(pl.multiple_of(at * SPLIT, SPLIT), SPLIT)
        total = None
        for chunk in range(CHUNKS):
            for side in range(2):
                here = slice((chunk * 2 + side) * half_rows, (chunk * 2 + side + 1) * half_rows)
                right = xs_ref[chunk, side, :, :, :, :, columns].reshape(half_rows, SPLIT)
                term = jnp.dot(dqkv_t[:, here], right, preferred_element_type=f32)
                total = term if total is None else total + term
        return total.T

    quarter = width // SPLIT // 2

    def far_tile(at, carry):
        here = pl.ds(pl.multiple_of(at * SPLIT, SPLIT), SPLIT)
        gq_far[here, :] = product((1 - group) * quarter + at).astype(low)
        return carry

    def own_tile(at, carry):
        here = pl.ds(pl.multiple_of(at * SPLIT, SPLIT), SPLIT)
        gq_own[here, :] = product(group * quarter + at)
        return carry

    lax.fori_loop(0, quarter, far_tile, 0)
    far_qkv = far(gq_far, gq_in, 2)

    bias_q, bias_v = bias[:, 0:HEAD_DIM], bias[:, 2 * HEAD_DIM : 3 * HEAD_DIM]
    lane = lax.broadcasted_iota(jnp.int32, (1, 128), 1)
    blocks_ref[2 * chip, pl.ds(core * 8, 1), :] = jnp.where(
        lane < 64, bias_q, pltpu.roll(bias_v, 64, 1)
    )
    blocks_ref[2 * chip + 1, pl.ds(core * 8, 1), :] = jnp.where(
        lane < 64, pltpu.roll(bias_q, 64, 1), bias_v
    )

    def blocks(pairs, at):
        here = slice(at, at + len(pairs))
        return exchange_blocks(
            pairs, (block_local.at[here], block_send.at[here], block_recv.at[here]),
            base, mine, others,
        )

    vec_blocks = blocks([(blocks_ref, arrived)], 0)

    def input_part(chunk, side, dst):
        left = rows_of(chunk, side)

        def body(at, carry):
            weight = wqkv_ref[at // 4, pl.ds(at % 4 * 4, 4)].reshape(SPLIT, 3 * HEAD_DIM)
            part = lax.dot_general(left, weight, NT, preferred_element_type=f32)
            columns = pl.ds(pl.multiple_of(at * SPLIT, SPLIT), SPLIT)
            dst[:, :, :, :, columns] = part.astype(low).reshape(2, 2, 2, rows, SPLIT)
            return carry

        lax.fori_loop(0, width // SPLIT, body, 0)

    def flow(chunk):
        def finish(row, first, count, total):
            res_ref[chunk * rows + row : chunk * rows + row + 16, first : first + count] = total

        incoming = (in_one.at[chunk], in_two.at[chunk], in_three.at[chunk])
        other = far_part.at[chunk % 2]
        input_part(chunk, 1 - core, other)
        share = net.share(other, pair_in.at[chunk], 0, chunk)
        input_part(chunk, core, own_part.at[chunk])
        yield
        yield from net.scatter(
            own_part.at[chunk], pair_in.at[chunk], incoming, share, 0, chunk, finish
        )
        here = slice(chunk * rows, (chunk + 1) * rows)
        input_ref[here, :] = (dres_ref[here, :] + res_ref[here, :]).astype(low)

    def fill():
        yield
        yield
        for copy in loads:
            copy.wait()
        out_w2[...] = w2_sum[...] + w2_in[...].astype(f32)
        yield
        lax.fori_loop(0, quarter, own_tile, 0)
        yield
        for copy in vec_blocks:
            copy.wait()
        total = arrived[0]
        for at in range(1, GROUP):
            total = total + arrived[at]
        first, second = total[:8], total[8:]
        theirs[...] = jnp.where(group == 0, second, first)
        vec_ref[...] = jnp.where(group == 0, first, second)
        state["vec"] = far(theirs, far_vec_in, 3)

    state = {}
    step_through([flow(chunk) for chunk in range(CHUNKS)], fill())

    share_wo = push(wo_pair, wo_pair_in, far_send.at[4], far_recv.at[4], net.pair)

    @pl.when(core == group)
    def _():
        far_wo.wait_recv()
        total = gwo_ref[...] + wo_in[...].astype(f32)
        first, second = total[:weight_rows], total[weight_rows:]
        out_wo[...] = jnp.where(core == 0, first, second)
        wo_pair[...] = jnp.where(core == 0, second, first)
        share_wo.start()

    far_w1.wait()

    def add_w1(at, carry):
        here = pl.ds(pl.multiple_of(at * weight_rows, weight_rows), weight_rows)
        w1_send[at] = (w1_sum[here, :] + w1_in[here, :].astype(f32)).astype(low)
        return carry

    lax.fori_loop(0, GROUP, add_w1, 0)
    w1_blocks = blocks([(w1_send, w1_recv)], 1)
    state["vec"].wait()
    vec_ref[...] += far_vec_in[...]

    @pl.when(core != group)
    def _():
        far_wo.wait_send()
        share_wo.wait_recv()
        out_wo[...] = wo_pair_in[...]

    @pl.when(core == group)
    def _():
        share_wo.wait_send()

    far_qkv.wait()

    def add_qkv(at, carry):
        here = pl.ds(pl.multiple_of(at * weight_rows, weight_rows), weight_rows)
        gq_send[at] = (gq_own[here, :] + gq_in[here, :].astype(f32)).astype(low)
        return carry

    lax.fori_loop(0, GROUP, add_qkv, 0)
    qkv_blocks = blocks([(gq_send, gq_recv)], 2)
    for copy in w1_blocks:
        copy.wait()
    unit_rows = w1_recv.shape[-1] // 2
    for at in range(GROUP):
        for part in range(2):
            first = (part * GROUP + at) * unit_rows
            out_w1[:, first : first + unit_rows] = w1_recv[
                at, :, part * unit_rows : (part + 1) * unit_rows
            ].astype(f32)
    for copy in qkv_blocks:
        copy.wait()
    for at in range(GROUP):
        first = (at % 2 * 8 + at // 2) * HEAD_DIM
        for part, ref in enumerate((out_q, out_k, out_v)):
            ref[:, first : first + HEAD_DIM] = gq_recv[
                at, :, part * HEAD_DIM : (part + 1) * HEAD_DIM
            ].astype(f32)


def layer_tail(
    qkv, dout, seg_q, seg_k, wqkv, dres, gwo, parts, x_all, w1_own, w1_far, w1_early, w2_own, w2_early
):
    f32, bf16 = jnp.float32, jnp.bfloat16
    block, width = dres.shape
    rows = block // CHUNKS
    weight_rows = wqkv.shape[2]
    units = w1_own.shape[1]
    unit_rows = units // 2
    own_rows = GROUP * block
    half_width = width // 2
    peers = GROUP - 1
    vmem = pl.BlockSpec(memory_space=pltpu.VMEM)
    anywhere = pl.BlockSpec(memory_space=pl.ANY)
    sems = pltpu.SemaphoreType.DMA
    shape, scratch = jax.ShapeDtypeStruct, pltpu.VMEM
    heads = 3 * HEAD_DIM

    def slots(*lead):
        return scratch(lead + (rows, width), bf16)

    return pl.pallas_call(
        tail_kernel,
        out_shape=[
            shape((block, width), bf16),
            shape((weight_rows, width), f32),
            shape((weight_rows, width), f32),
            shape((weight_rows, width), f32),
            shape((weight_rows, width), f32),
            shape((weight_rows, GROUP * units), f32),
            shape((unit_rows, width), f32),
            shape((8, 128), f32),
        ],
        in_specs=[vmem] * 8 + [anywhere] * 6,
        out_specs=[vmem] * 8,
        scratch_shapes=[
            slots(CHUNKS, 2, 2, 2, 2),
            slots(CHUNKS, 2, 2, 2), slots(2, 2, 2, 2), slots(CHUNKS, 2, 2, 2),
            slots(CHUNKS, 2, 2), slots(CHUNKS, 2), slots(CHUNKS),
            scratch((block, width), f32),
            scratch((own_rows + HALO, heads), bf16),
            scratch(qkv.shape[:1] + (HEAD_DIM,), f32),
            scratch(qkv.shape[:1] + (HEAD_DIM,), f32),
            scratch((heads, own_rows), bf16),
            scratch((half_width, heads), f32),
            scratch((half_width, heads), bf16),
            scratch((half_width, heads), bf16),
            scratch((GROUP, weight_rows, heads), bf16),
            scratch((GROUP, weight_rows, heads), bf16),
            scratch((half_width, units), f32),
            scratch((half_width, units), bf16),
            scratch((GROUP, weight_rows, units), bf16),
            scratch((GROUP, weight_rows, units), bf16),
            scratch((unit_rows, width), f32),
            scratch((unit_rows, width), bf16),
            scratch((HEAD_DIM, width), bf16),
            scratch((HEAD_DIM, width), bf16),
            scratch((weight_rows, width), f32),
            scratch((weight_rows, width), f32),
            scratch(parts.shape, f32),
            scratch(parts.shape, f32),
            scratch((8, 128), f32),
            scratch((8, 128), f32),
            sems((1, CHUNKS, 4, 3)), sems((1, CHUNKS, 4, 3)), sems((1, CHUNKS)), sems((1, CHUNKS)),
            sems((CHUNKS + 4,)), sems((3,)), sems((3, peers)), sems((3, peers)), sems((5,)), sems((5,)),
        ],
        compiler_params=pltpu.CompilerParams(
            collective_id=5, has_side_effects=True, vmem_limit_bytes=63 << 20
        ),
        name="layer_tail",
    )(qkv, dout, seg_q, seg_k, wqkv, dres, gwo, parts, x_all, w1_own, w1_far, w1_early, w2_own, w2_early)


def grouped_device(
    tokens,
    cotangent,
    lengths,
    wq,
    bq,
    wk,
    wv,
    bv,
    wo,
    bo,
    norm1_gain,
    norm1_bias,
    w1,
    b1,
    w2,
    b2,
    norm2_gain,
    norm2_bias,
):
    f32 = jnp.float32
    bf16 = jnp.bfloat16
    devices = lax.axis_size("dp")
    block, width = tokens.shape
    own_rows = GROUP * block
    total_tokens = devices * block
    weight_rows = wq.shape[0]
    unit_rows, units = w2.shape[0], w1.shape[1]
    device = lax.axis_index("dp")
    group, member = device // GROUP, device % GROUP
    chip, core = member // 2, member % 2
    head = core * 8 + chip

    def by_head(weight):
        return weight.reshape(weight_rows, 2, 8, HEAD_DIM).transpose(2, 1, 0, 3).reshape(
            GROUP, weight_rows, HEAD_DIM
        )

    pack_qkv = jnp.concatenate([by_head(wq), by_head(wk), by_head(wv)], -1)
    pack_w1 = w1.reshape(weight_rows, 2, GROUP, unit_rows).transpose(2, 0, 1, 3).reshape(
        GROUP, weight_rows, 2 * unit_rows
    )
    vectors = [bq, bv, bo, norm1_gain, norm1_bias, b2, norm2_gain, norm2_bias, b1]
    sizes = [item.shape[0] for item in vectors]
    vector = jnp.concatenate(vectors).astype(f32)
    vector = jnp.pad(vector, (0, 1024 - vector.shape[0])).reshape(8, 128)

    ext_rows = own_rows + HALO
    ext_first = group * (own_rows - HALO)
    offset = group * HALO
    starts = jnp.cumsum(lengths) - lengths
    ext_ids = ext_first + jnp.arange(ext_rows, dtype=jnp.int32)
    seg = jnp.sum((ext_ids[:, None] >= starts[None, :]).astype(jnp.int32), 1)
    tile_rows = jnp.arange(ext_rows // TILE, dtype=jnp.int32) * TILE - PAD
    key_rows = tile_rows[:, None] + jnp.arange(WINDOW, dtype=jnp.int32)[None, :]
    key_ids = ext_first + key_rows
    seg_k = jnp.sum((key_ids[:, :, None] >= starts[None, None, :]).astype(jnp.int32), 2)
    seg_k = jnp.where((key_rows >= 0) & (key_rows < ext_rows), seg_k, -1)[:, None, :]
    seg_q = seg[:, None]

    (
        output, grad_resid_one, vec_grads, grad_b1, w2_own, _, w2_early, w1_own, w1_far, w1_early,
        grad_wo, all_tokens, _, qkv, grad_out, full_qkv,
    ) = layer(tokens, cotangent, pack_qkv, pack_w1, w2, wo, vector, seg_q, seg_k)

    spread_b1 = lax.dynamic_update_slice_in_dim(
        jnp.zeros((2, GROUP, unit_rows), f32), grad_b1[0].reshape(2, 1, unit_rows), member, 1
    )
    grad_b2, grad_gain_two, grad_shift_two, grad_bo, grad_gain_one, grad_shift_one = [
        vec_grads[at] for at in range(6)
    ]
    none = jnp.zeros((width,), f32)
    items = [
        none, none, grad_bo, grad_gain_one, grad_shift_one, grad_b2, grad_gain_two, grad_shift_two,
        spread_b1,
    ]
    parts = jnp.concatenate([item.reshape(2, GROUP, -1) for item in items], 2)
    parts = jnp.pad(parts, ((0, 0), (0, 0), (0, 1024 - parts.shape[2])))
    parts = parts.transpose(1, 0, 2).reshape(GROUP, 16, 128)
    input_grad, out_q, out_k, out_v, out_wo, out_w1, out_w2, sums = layer_tail(
        qkv, grad_out, seg_q, seg_k, full_qkv, grad_resid_one, grad_wo, parts,
        all_tokens, w1_own, w1_far, w1_early, w2_own, w2_early,
    )
    sums, at = sums.reshape(-1), 0
    small = []
    for size in sizes:
        small.append(sums[at : at + size])
        at += size
    out_bq, out_bv, out_bo, out_g1, out_s1, out_b2, out_g2, out_s2, out_b1 = small
    return (
        output, input_grad, out_q, out_bq, out_k, out_v, out_bv, out_wo, out_bo, out_g1, out_s1,
        out_w1, out_b1, out_w2, out_b2, out_g2, out_s2,
    )


def solution(mesh):
    in_specs = (
        P("dp", None),
        P("dp", None),
        P(),
        P("dp", None),
        P("dp"),
        P("dp", None),
        P("dp", None),
        P("dp"),
        P("dp", None),
        P("dp"),
        P("dp"),
        P("dp"),
        P("dp", None),
        P("dp"),
        P("dp", None),
        P("dp"),
        P("dp"),
        P("dp"),
    )
    out_specs = (
        P("dp", None),
        P("dp", None),
        P("dp", None),
        P("dp"),
        P("dp", None),
        P("dp", None),
        P("dp"),
        P("dp", None),
        P("dp"),
        P("dp"),
        P("dp"),
        P("dp", None),
        P("dp"),
        P("dp", None),
        P("dp"),
        P("dp"),
        P("dp"),
    )
    two_groups = mesh.shape["dp"] == 2 * GROUP
    return jax.shard_map(
        grouped_device if two_groups else per_device, mesh=mesh, in_specs=in_specs, out_specs=out_specs, check_vma=False
    )
```

```python
import functools

import jax
import jax.numpy as jnp
from jax import lax
from jax.experimental import pallas as pl
from jax.experimental.pallas import tpu as pltpu
from jax.sharding import PartitionSpec as P

HEADS = 16
HEAD_DIM = 128
SEQ_MAX = 160
SPAN = 3

GROUP = 16
HALO = 256
WINDOW = 512
TILE = 128
MESH_ID = pl.DeviceIdType.MESH
VMEM_LIMIT = 60 << 20
PORTIONS = ((0, 48), (48, 48), (96, 32))
ORDERS = ((0, 1, 2), (1, 2, 0), (2, 0, 1))


norm_eps = 1e-05


def layer_norm(residual, gain_vec, shift_vec):
    mean_val = jnp.mean(residual, axis=-1, keepdims=True)
    centred = residual - mean_val
    var_val = jnp.mean(centred * centred, axis=-1, keepdims=True)
    return centred * lax.rsqrt(var_val + norm_eps) * gain_vec + shift_vec


def gelu_tanh(values):
    return jax.nn.gelu(values, approximate=True)


def plan_layout(lengths, tok_dev):
    starts = jnp.cumsum(lengths) - lengths
    owner_first = starts // tok_dev
    return (starts, starts, lengths, owner_first)


def to_owners(shard, layout, dev_count, piece_rows):
    starts, owner_start, owner_length, owner_first = layout
    tok_dev = shard.shape[0]
    feat_width = shard.shape[1]
    device = lax.axis_index("dp")
    held_rows = lax.all_to_all(
        shard.reshape(dev_count, piece_rows, feat_width),
        "dp",
        split_axis=0,
        concat_axis=0,
        tiled=True,
    )
    held_rows = held_rows.reshape(dev_count * piece_rows, feat_width)
    slot_ids = jnp.arange(SPAN * piece_rows, dtype=jnp.int32)
    shard_step = slot_ids // piece_rows
    within = slot_ids % piece_rows
    source = owner_first[:, None] + shard_step[None, :]
    global_row = source * tok_dev + device * piece_rows + within[None, :]
    inside = (
        (global_row >= owner_start[:, None])
        & (global_row < (owner_start + owner_length)[:, None])
        & (source < dev_count)
    )
    picked = held_rows[jnp.clip(source, 0, dev_count - 1) * piece_rows + within[None, :]]
    outgoing = jnp.where(inside[:, :, None], picked, jnp.zeros((), picked.dtype))
    arrived = lax.all_to_all(outgoing, "dp", split_axis=0, concat_axis=0, tiled=True)
    arrived = arrived.reshape(dev_count * SPAN * piece_rows, feat_width)
    my_start = owner_start[device]
    my_length = owner_length[device]
    my_first = owner_first[device]
    places = jnp.arange(SEQ_MAX, dtype=jnp.int32)
    global_pos = my_start + places
    shard_of = global_pos // tok_dev
    offset_in = global_pos % tok_dev
    slot_index = (
        offset_in // piece_rows * (SPAN * piece_rows)
        + (shard_of - my_first) * piece_rows
        + offset_in % piece_rows
    )
    valid_rows = places < my_length
    slot_index = jnp.where(valid_rows, slot_index, 0)
    owned = jnp.where(valid_rows[:, None], arrived[slot_index], jnp.zeros((), arrived.dtype))
    return (owned, valid_rows)


def to_order(owned, layout, dev_count, piece_rows, tok_dev):
    starts, owner_start, owner_length, owner_first = layout
    feat_width = owned.shape[1]
    device = lax.axis_index("dp")
    my_start = owner_start[device]
    my_length = owner_length[device]
    my_first = owner_first[device]
    slot_ids = jnp.arange(SPAN * piece_rows, dtype=jnp.int32)
    shard_step = slot_ids // piece_rows
    within = slot_ids % piece_rows
    targets = jnp.arange(dev_count, dtype=jnp.int32)
    global_row = (
        (my_first + shard_step)[None, :] * tok_dev + targets[:, None] * piece_rows + within[None, :]
    )
    place_row = global_row - my_start
    inside = (place_row >= 0) & (place_row < my_length)
    picked = owned[jnp.clip(place_row, 0, owned.shape[0] - 1)]
    outgoing = jnp.where(inside[:, :, None], picked, jnp.zeros((), picked.dtype))
    returned = lax.all_to_all(outgoing, "dp", split_axis=0, concat_axis=0, tiled=True)
    returned = returned.reshape(dev_count * SPAN * piece_rows, feat_width)
    sources = jnp.arange(dev_count, dtype=jnp.int32)
    within_piece = jnp.arange(piece_rows, dtype=jnp.int32)
    row_ids = sources[:, None] * tok_dev + device * piece_rows + within_piece[None, :]
    seq_of = jnp.sum((row_ids[:, :, None] >= starts[None, None, :]).astype(jnp.int32), 2) - 1
    slot_index = (
        seq_of * (SPAN * piece_rows)
        + (sources[:, None] - owner_first[seq_of]) * piece_rows
        + within_piece[None, :]
    )
    pieces = returned[slot_index]
    ordered = lax.all_to_all(pieces, "dp", split_axis=0, concat_axis=0, tiled=True)
    return ordered.reshape(tok_dev, feat_width)


def per_device(
    tokens,
    cotangent,
    lengths,
    wq,
    bq,
    wk,
    wv,
    bv,
    wo,
    bo,
    norm1_gain,
    norm1_bias,
    w1,
    b1,
    w2,
    b2,
    norm2_gain,
    norm2_bias,
):
    f32 = jnp.float32
    bf16 = jnp.bfloat16
    dev_count = lax.axis_size("dp")
    tok_dev = tokens.shape[0]
    feat_width = tokens.shape[1]
    piece_rows = tok_dev // dev_count
    layout = plan_layout(lengths, tok_dev)
    joined, valid_rows = to_owners(
        jnp.concatenate([tokens, cotangent], 1), layout, dev_count, piece_rows
    )
    inputs = joined[:, :feat_width]
    upstream = joined[:, feat_width:].astype(f32)
    slot_count = inputs.shape[0]
    score_scale = HEAD_DIM ** (-0.5)
    full_wq, full_wk, full_wv, full_wo, full_bq, full_bv, full_bo, gain_one, shift_one = (
        lax.all_gather(wq, "dp", axis=0, tiled=True),
        lax.all_gather(wk, "dp", axis=0, tiled=True),
        lax.all_gather(wv, "dp", axis=0, tiled=True),
        lax.all_gather(wo, "dp", axis=0, tiled=True),
        lax.all_gather(bq, "dp", axis=0, tiled=True),
        lax.all_gather(bv, "dp", axis=0, tiled=True),
        lax.all_gather(bo, "dp", axis=0, tiled=True),
        lax.all_gather(norm1_gain, "dp", axis=0, tiled=True),
        lax.all_gather(norm1_bias, "dp", axis=0, tiled=True),
    )
    queries = (
        (jnp.dot(inputs, full_wq, preferred_element_type=f32) + full_bq.astype(f32))
        .astype(bf16)
        .reshape(slot_count, HEADS, HEAD_DIM)
    )
    keys_low = (
        jnp.dot(inputs, full_wk, preferred_element_type=f32)
        .astype(bf16)
        .reshape(slot_count, HEADS, HEAD_DIM)
    )
    values_low = (
        (jnp.dot(inputs, full_wv, preferred_element_type=f32) + full_bv.astype(f32))
        .astype(bf16)
        .reshape(slot_count, HEADS, HEAD_DIM)
    )
    scores = jnp.einsum("qhd,khd->hqk", queries, keys_low, preferred_element_type=f32) * score_scale
    scores = jnp.where(valid_rows[None, None, :], scores, -1e30)
    row_max = jnp.max(scores, -1, keepdims=True)
    row_total = jnp.sum(jnp.exp(scores - row_max), -1, keepdims=True)
    log_total = row_max + jnp.log(row_total)
    attn_probs = jnp.exp(scores - log_total).astype(bf16)
    attended = jnp.einsum("hqk,khd->qhd", attn_probs, values_low, preferred_element_type=f32)
    attended = attended.reshape(slot_count, feat_width).astype(bf16)
    branch = jnp.dot(attended, full_wo, preferred_element_type=f32) + full_bo.astype(f32)
    resid_one = inputs.astype(f32) + branch
    hidden, norm_one_back = jax.vjp(
        layer_norm, resid_one, gain_one.astype(f32), shift_one.astype(f32)
    )
    hidden_low = hidden.astype(bf16)
    full_w1, full_w2, full_b1, full_b2, gain_two, shift_two = (
        lax.all_gather(w1, "dp", axis=0, tiled=True),
        lax.all_gather(w2, "dp", axis=0, tiled=True),
        lax.all_gather(b1, "dp", axis=0, tiled=True),
        lax.all_gather(b2, "dp", axis=0, tiled=True),
        lax.all_gather(norm2_gain, "dp", axis=0, tiled=True),
        lax.all_gather(norm2_bias, "dp", axis=0, tiled=True),
    )
    upward = jnp.dot(hidden_low, full_w1, preferred_element_type=f32) + full_b1.astype(f32)
    activ, gelu_back = jax.vjp(gelu_tanh, upward)
    activ_low = activ.astype(bf16)
    mixed = jnp.dot(activ_low, full_w2, preferred_element_type=f32) + full_b2.astype(f32)
    resid_two = hidden + mixed
    normed, norm_two_back = jax.vjp(
        layer_norm, resid_two, gain_two.astype(f32), shift_two.astype(f32)
    )
    result = jnp.where(valid_rows[:, None], normed, 0.0).astype(bf16)
    output = to_order(result, layout, dev_count, piece_rows, tok_dev)
    back_w1, back_w2 = (
        lax.all_gather(w1, "dp", axis=0, tiled=True),
        lax.all_gather(w2, "dp", axis=0, tiled=True),
    )
    grad_resid_two, grad_gain_two, grad_shift_two = norm_two_back(upstream)
    grad_mixed = grad_resid_two.astype(bf16)
    grad_bias_two = jnp.sum(grad_mixed.astype(f32), 0)
    grad_activ = jnp.einsum("td,fd->tf", grad_mixed, back_w2, preferred_element_type=f32)
    grad_upward = gelu_back(grad_activ)[0].astype(bf16)
    grad_bias_one = jnp.sum(grad_upward.astype(f32), 0)
    grad_hidden = grad_resid_two + jnp.einsum(
        "tf,df->td", grad_upward, back_w1, preferred_element_type=f32
    )
    grad_w2 = jnp.einsum("tf,td->fd", activ_low, grad_mixed, preferred_element_type=f32)
    grad_w1 = jnp.einsum("td,tf->df", hidden_low, grad_upward, preferred_element_type=f32)
    mlp_grads = (
        lax.psum_scatter(grad_w1, "dp", scatter_dimension=0, tiled=True),
        lax.psum_scatter(grad_w2, "dp", scatter_dimension=0, tiled=True),
        lax.psum_scatter(grad_bias_one, "dp", scatter_dimension=0, tiled=True),
        lax.psum_scatter(grad_bias_two, "dp", scatter_dimension=0, tiled=True),
        lax.psum_scatter(grad_gain_two, "dp", scatter_dimension=0, tiled=True),
        lax.psum_scatter(grad_shift_two, "dp", scatter_dimension=0, tiled=True),
    )
    back_wq, back_wk, back_wv, back_wo = (
        lax.all_gather(wq, "dp", axis=0, tiled=True),
        lax.all_gather(wk, "dp", axis=0, tiled=True),
        lax.all_gather(wv, "dp", axis=0, tiled=True),
        lax.all_gather(wo, "dp", axis=0, tiled=True),
    )
    grad_resid_one, grad_gain_one, grad_shift_one = norm_one_back(grad_hidden)
    grad_branch = grad_resid_one.astype(bf16)
    grad_bo = jnp.sum(grad_branch.astype(f32), 0)
    grad_wo = jnp.einsum("tc,td->cd", attended, grad_branch, preferred_element_type=f32)
    grad_attended = jnp.einsum(
        "td,cd->tc", grad_branch, back_wo, preferred_element_type=f32
    ).astype(bf16)
    grad_attended = grad_attended.reshape(slot_count, HEADS, HEAD_DIM)
    re_scores = (
        jnp.einsum("qhd,khd->hqk", queries, keys_low, preferred_element_type=f32) * score_scale
    )
    re_scores = jnp.where(valid_rows[None, None, :], re_scores, -1e30)
    re_probs = jnp.exp(re_scores - log_total)
    re_probs_low = re_probs.astype(bf16)
    grad_values = jnp.einsum(
        "hqk,qhd->khd", re_probs_low, grad_attended, preferred_element_type=f32
    ).astype(bf16)
    grad_probs = jnp.einsum("qhd,khd->hqk", grad_attended, values_low, preferred_element_type=f32)
    grad_scores = re_probs * (grad_probs - jnp.sum(re_probs * grad_probs, -1, keepdims=True))
    grad_scores_low = grad_scores.astype(bf16)
    grad_queries = (
        jnp.einsum("hqk,khd->qhd", grad_scores_low, keys_low, preferred_element_type=f32)
        * score_scale
    ).astype(bf16)
    grad_keys = (
        jnp.einsum("hqk,qhd->khd", grad_scores_low, queries, preferred_element_type=f32)
        * score_scale
    ).astype(bf16)
    grad_queries = grad_queries.reshape(slot_count, feat_width)
    grad_keys = grad_keys.reshape(slot_count, feat_width)
    grad_values = grad_values.reshape(slot_count, feat_width)
    grad_bq = jnp.sum(grad_queries.astype(f32), 0)
    grad_bv = jnp.sum(grad_values.astype(f32), 0)
    grad_wq = jnp.einsum("tc,td->cd", inputs, grad_queries, preferred_element_type=f32)
    grad_wk = jnp.einsum("tc,td->cd", inputs, grad_keys, preferred_element_type=f32)
    grad_wv = jnp.einsum("tc,td->cd", inputs, grad_values, preferred_element_type=f32)
    grad_input = grad_resid_one + jnp.einsum(
        "td,cd->tc", grad_queries, back_wq, preferred_element_type=f32
    )
    grad_input = grad_input + jnp.einsum(
        "td,cd->tc", grad_keys, back_wk, preferred_element_type=f32
    )
    grad_input = grad_input + jnp.einsum(
        "td,cd->tc", grad_values, back_wv, preferred_element_type=f32
    )
    grad_input = jnp.where(valid_rows[:, None], grad_input, 0.0).astype(bf16)
    attn_grads = (
        lax.psum_scatter(grad_wq, "dp", scatter_dimension=0, tiled=True),
        lax.psum_scatter(grad_wk, "dp", scatter_dimension=0, tiled=True),
        lax.psum_scatter(grad_wv, "dp", scatter_dimension=0, tiled=True),
        lax.psum_scatter(grad_wo, "dp", scatter_dimension=0, tiled=True),
        lax.psum_scatter(grad_bq, "dp", scatter_dimension=0, tiled=True),
        lax.psum_scatter(grad_bv, "dp", scatter_dimension=0, tiled=True),
        lax.psum_scatter(grad_bo, "dp", scatter_dimension=0, tiled=True),
        lax.psum_scatter(grad_gain_one, "dp", scatter_dimension=0, tiled=True),
        lax.psum_scatter(grad_shift_one, "dp", scatter_dimension=0, tiled=True),
    )
    sum_w1, sum_w2, sum_b1, sum_b2, sum_g2, sum_s2 = mlp_grads
    sum_wq, sum_wk, sum_wv, sum_wo, sum_bq, sum_bv, sum_bo, sum_g1, sum_s1 = attn_grads
    input_grad = to_order(grad_input, layout, dev_count, piece_rows, tok_dev)
    return (
        output,
        input_grad,
        sum_wq,
        sum_bq,
        sum_wk,
        sum_wv,
        sum_bv,
        sum_wo,
        sum_bo,
        sum_g1,
        sum_s1,
        sum_w1,
        sum_b1,
        sum_w2,
        sum_b2,
        sum_g2,
        sum_s2,
    )


def flip(device, bit):
    step = 1 << bit
    return device + step - 2 * step * ((device // step) % 2)


def chip_bits(device):
    return [(device // 2) % 2, (device // 4) % 2, (device // 8) % 2]


def enter(partners):
    barrier = pltpu.get_barrier_semaphore()
    for partner in partners:
        pl.semaphore_signal(barrier, inc=1, device_id=(partner,), device_id_type=MESH_ID)
    pl.semaphore_wait(barrier, len(partners))


def push(src, dst, send_sem, recv_sem, device):
    return pltpu.make_async_remote_copy(
        src_ref=src,
        dst_ref=dst,
        send_sem=send_sem,
        recv_sem=recv_sem,
        device_id=(device,),
        device_id_type=MESH_ID,
    )


def exchange_blocks(pairs, sems, base, mine, others):
    local_sem, send_sem, recv_sem = sems
    copies = []
    for at, (src, dst) in enumerate(pairs):
        for step, other in enumerate(others):
            copy = push(
                src.at[other - base],
                dst.at[mine],
                send_sem.at[at, step],
                recv_sem.at[at, step],
                other,
            )
            copy.start()
            copies.append(copy)
        local = pltpu.make_async_copy(src.at[mine], dst.at[mine], local_sem.at[at])
        local.start()
        copies.append(local)
    return copies


def far_blocks(src, dst, send_sem, recv_sem, group, mine):
    copies = []
    for step in range(GROUP):
        member = (mine + step) % GROUP
        copy = push(
            src.at[member],
            dst.at[mine],
            send_sem.at[step],
            recv_sem.at[step],
            (1 - group) * GROUP + member,
        )
        copy.start()
        copies.append(copy)
    return copies


def group_places():
    device = lax.axis_index("dp")
    base = device // GROUP * GROUP
    mine = device % GROUP
    others = [base + (mine + step) % GROUP for step in range(1, GROUP)]
    across = (device + GROUP) % (2 * GROUP)
    there = [GROUP - base + (mine + step) % GROUP for step in range(GROUP)]
    return device // GROUP, base, mine, others, across, there


def tile_probs(qkv_ref, row, start, seg_q, seg_k):
    f32 = jnp.float32
    queries = qkv_ref[pl.ds(row, TILE), 0:HEAD_DIM]
    keys = qkv_ref[pl.ds(start, WINDOW), HEAD_DIM : 2 * HEAD_DIM]
    scores = lax.dot_general(queries, keys, (((1,), (1,)), ((), ())), preferred_element_type=f32)
    scores = jnp.where(seg_q == seg_k, scores * HEAD_DIM ** (-0.5), -1e30)
    weights = jnp.exp(scores - jnp.max(scores, -1, keepdims=True))
    return queries, keys, weights / jnp.sum(weights, -1, keepdims=True)


CHUNKS = 4
TAIL_CHUNKS = 2
THIRDS = (((0, 768), (0, 1, 2)), ((768, 640), (1, 2, 0)), ((1408, 640), (2, 0, 1)))
LIGHT = (
    ((0, 512), (1, 2, 0)), ((512, 512), (0, 2, 1)), ((1024, 512), (1, 0, 2)), ((1536, 512), (0, 1, 2)),
)
PLANS = (THIRDS, LIGHT) + (THIRDS,) * 5
TAIL_PLANS = (LIGHT,)
SPLIT = 256
PAD = (WINDOW - TILE) // 2
REACH = SEQ_MAX
STAGES = 7


def step_through(flows, fillers=None):
    waiting, alive = list(flows), []
    while waiting or alive:
        if waiting:
            alive.append(waiting.pop(0))
        alive = [flow for flow in alive if next(flow, "done") != "done"]
        if fillers is not None:
            next(fillers, None)
    if fillers is not None:
        for _ in fillers:
            pass


class Traffic:
    def __init__(self, sems, plans):
        self.plans = plans
        self.hop_send, self.hop_recv, self.pair_send, self.pair_recv = sems
        device = lax.axis_index("dp")
        self.core = device % 2
        self.bits = chip_bits(device)
        self.partners = [flip(device, 1), flip(device, 2), flip(device, 3)]
        self.pair = flip(device, 0)

    def chips(self, ref, values, columns):
        return ref.at[values[2], values[1], values[0], :, columns]

    def push(self, src, dst, stage, chunk, part, step):
        copy = push(
            src, dst,
            self.hop_send.at[stage, chunk, part, step],
            self.hop_recv.at[stage, chunk, part, step],
            self.partners[self.plans[stage][part][1][step]],
        )
        copy.start()
        return copy

    def share(self, src, dst, stage, chunk):
        copy = push(
            src, dst, self.pair_send.at[stage, chunk], self.pair_recv.at[stage, chunk], self.pair
        )
        copy.start()
        return copy

    def gather(self, slots, stage, chunk):
        mine = slots.at[self.core]
        hops = {}
        for step in range(3):
            for part, ((first, count), order) in enumerate(self.plans[stage]):
                if step:
                    hops[part, step - 1].wait_recv()
                values = list(self.bits)
                for dim in order[:step]:
                    values[dim] = slice(None)
                view = self.chips(mine, values, pl.ds(first, count))
                hops[part, step] = self.push(view, view, stage, chunk, part, step)
            yield
        for part in range(len(self.plans[stage])):
            hops[part, 2].wait_recv()
        share = self.share(mine, mine, stage, chunk)
        for copy in hops.values():
            copy.wait_send()
        return share

    def scatter(self, own, pair_in, incoming, share, stage, chunk, finish):
        rows = own.shape[-2]
        f32 = jnp.float32
        hops = {}
        share.wait()
        for step in range(4):
            for part, ((first, count), order) in enumerate(self.plans[stage]):
                columns = pl.ds(first, count)
                if step:
                    hops[part, step - 1].wait_recv()
                values = list(self.bits)
                free = ()
                if step < 3:
                    values[order[step]] = 1 - self.bits[order[step]]
                    free = order[step + 1 :]
                for mask in range(1 << len(free)):
                    slot = list(values)
                    for place, dim in enumerate(free):
                        slot[dim] = (mask >> place) & 1
                    where = (slot[2], slot[1], slot[0])
                    for row in range(0, rows, 16):
                        at = (slice(row, row + 16), columns)
                        total = own[where + at].astype(f32) + pair_in[where + at].astype(f32)
                        for back in range(step):
                            left = [slot[dim] for dim in (2, 1, 0) if dim not in order[: back + 1]]
                            total = total + incoming[back][tuple(left) + at].astype(f32)
                        if step < 3:
                            own[where + at] = total.astype(own.dtype)
                        else:
                            finish(row, first, count, total)
                if step == 3:
                    continue
                for dim in free:
                    values[dim] = slice(None)
                left = tuple(slice(None) for _ in free)
                hops[part, step] = self.push(
                    self.chips(own, values, columns),
                    incoming[step].at[left + (slice(None), columns)],
                    stage, chunk, part, step,
                )
            if step < 3:
                yield
        for copy in hops.values():
            copy.wait_send()


def gelu_slope(up):
    inner = 0.7978845608028654 * (up + 0.044715 * (up * up * up))
    tanh = jnp.tanh(inner)
    return 0.5 * (1.0 + tanh) + 0.5 * up * (1.0 - tanh * tanh) * (
        0.7978845608028654 * (1.0 + 0.134145 * (up * up))
    )


NT = (((1,), (1,)), ((), ()))
TN = (((0,), (0,)), ((), ()))


def layer_kernel(
    tok_ref, cot_ref, pack_qkv, pack_w1, w2_ref, wo_ref, vec_ref, seg_q_ref, seg_k_ref,
    out_ref, dres_ref, vecg_ref, gb1_ref, gw2_own, gw2_far, gw2_in, gw1_ref, gw1_in, gwo_ref,
    x_all, h_all, qkv_ref, dout_ref, wqkv_ref,
    all_h, all_m, own_part, far_part, pair_in, in_one, in_two, in_three,
    up_ref, act_ref, act_t, dup_ref, dup_t, att_ref, att_t, res_ref, hid_ref, norm_ref, scale_ref,
    w1_all, w2_all, wo_all, vec_all, low_ref, high_ref, b1_ref, stage_ref, stage_low, stage_w1,
    hop_send, hop_recv, pair_send, pair_recv,
    block_local, block_send, block_recv, there_send, there_recv, vec_send, vec_recv, far_send, far_recv,
    local_sems, out_sems, spill_sems,
):
    f32, low = jnp.float32, tok_ref.dtype
    block, width = tok_ref.shape
    rows = block // CHUNKS
    half_rows = rows * GROUP // 2
    own_rows = GROUP * block
    units = w1_all.shape[-1]
    group, base, mine, others, across, there = group_places()
    net = Traffic((hop_send, hop_recv, pair_send, pair_recv), PLANS)
    core, bits = net.core, net.bits
    chip = mine // 2
    head = core * 8 + chip
    own_slot = (core, bits[2], bits[1], bits[0])
    ext = PAD + group * HALO
    enter(others + there)

    def far(src, dst, at, device=across):
        copy = push(src, dst, far_send.at[at], far_recv.at[at], device)
        copy.start()
        return copy

    def local(src, dst, at):
        copy = pltpu.make_async_copy(src, dst, local_sems.at[at])
        copy.start()
        return copy

    early = w2_ref.shape[0] // 2
    far_vec = far(vec_ref, vec_all.at[group, mine], 0)
    near = [
        local(vec_ref, vec_all.at[group, mine], 0),
        local(w2_ref, w2_all.at[group], 1),
        local(wo_ref, wo_all.at[group, core], 2),
    ]
    w2_first, w2_last = pl.ds(0, early), pl.ds(early, w2_ref.shape[0] - early)
    far_w2 = [far(w2_ref.at[w2_first, :], w2_all.at[group, w2_first, :], 1)]
    qkv_blocks = exchange_blocks(
        [(pack_qkv, wqkv_ref.at[group])],
        (block_local.at[0:1], block_send.at[0:1], block_recv.at[0:1]), base, mine, others,
    )
    for chunk in range(CHUNKS):
        all_m[(chunk,) + own_slot] = tok_ref[chunk * rows : (chunk + 1) * rows, :]
    wo_near = push(
        wo_ref, wo_all.at[group, core], far_send.at[2], far_recv.at[2], net.pair
    )
    wo_near.start()

    unsent = own_rows + REACH - group * (own_rows + REACH)
    for first in (0, qkv_ref.shape[0] - PAD):
        qkv_ref[first : first + PAD, :] = jnp.zeros((PAD, qkv_ref.shape[1]), low)
    qkv_ref[pl.ds(pl.multiple_of(PAD + unsent, 32), HALO - REACH), :] = jnp.zeros(
        (HALO - REACH, qkv_ref.shape[1]), low
    )
    dout_ref[pl.ds(pl.multiple_of(unsent, 32), HALO - REACH), :] = jnp.zeros(
        (HALO - REACH, HEAD_DIM), low
    )
    vecg_ref[...] = jnp.zeros_like(vecg_ref)
    gb1_ref[...] = jnp.zeros_like(gb1_ref)

    def row_at(chunk, side):
        return pl.multiple_of((chunk * 2 + side) * half_rows, half_rows)

    def flat(ref, chunk, side, columns=slice(None)):
        return ref[chunk, side, :, :, :, :, columns].reshape(half_rows, -1)

    def tiles(count, body):
        def step(at, carry):
            body(at, pl.ds(pl.multiple_of(at * SPLIT, SPLIT), SPLIT))
            return carry

        lax.fori_loop(0, count // SPLIT, step, 0)

    def pieces(chunk, side):
        return [
            pl.multiple_of((slot * 2 + side) * block + chunk * rows, rows)
            for slot in range(GROUP // 2)
        ]

    def project_half(chunk, side, which):
        columns = pl.ds(pl.multiple_of(which * (width // 2), width // 2), width // 2)
        weight = wqkv_ref[which].reshape(width // 2, -1)
        return jnp.dot(flat(all_m, chunk, side, columns), weight, preferred_element_type=f32)

    def spill(src, dst, chunk, at):
        copy = pltpu.make_async_copy(src.at[chunk], dst.at[chunk], spill_sems.at[at, chunk])
        copy.start()
        return copy

    wide = slice(0, 3 * HEAD_DIM)
    spills = {}

    def token_flow(chunk):
        share = yield from net.gather(all_m.at[chunk], 0, chunk)
        up_ref[pl.ds(row_at(chunk, core), half_rows), wide] = project_half(chunk, core, group)
        yield
        share.wait()
        up_ref[pl.ds(row_at(chunk, 1 - core), half_rows), wide] = project_half(
            chunk, 1 - core, group
        )
        spills[0, chunk] = spill(all_m, x_all, chunk, 0)

    def weight_flow():
        yield
        for copy in qkv_blocks:
            copy.wait()
        state["far_qkv"] = far(wqkv_ref.at[group], wqkv_ref.at[group], 3)
        yield
        for copy in near:
            copy.wait()
        far_vec.wait()
        both = vec_all.at[:, mine]
        state["vec"] = []
        for step, other in enumerate(others):
            copy = push(both, both, vec_send.at[step], vec_recv.at[step], other)
            copy.start()
            state["vec"].append(copy)
        yield

    state = {"backs": 0}
    flows = [token_flow(chunk) for chunk in range(CHUNKS)]
    step_through([flows[0], weight_flow()] + flows[1:])

    for copy in state["vec"]:
        copy.wait()
    lane = lax.broadcasted_iota(jnp.int32, (8, 128), 1)
    for at in range(GROUP):
        first = vec_all[at // 8, at % 8 * 2]
        second = vec_all[at // 8, at % 8 * 2 + 1]
        here = slice(at * 128, at * 128 + 128)
        low_ref[:, here] = jnp.where(lane < 64, first, pltpu.roll(second, 64, 1))
        high_ref[:, here] = jnp.where(lane < 64, pltpu.roll(first, 64, 1), second)
    for half in range(2):
        for part in range(2):
            b1_ref[0:1, half * 256 + part * 128 : half * 256 + part * 128 + 128] = vec_all[
                half, mine, 4 + part : 5 + part, :
            ]
    head_at = pl.ds(pl.multiple_of(head * HEAD_DIM, HEAD_DIM), HEAD_DIM)
    bias_q, bias_v = low_ref[0:1, head_at], high_ref[0:1, head_at]
    bias_qkv = jnp.concatenate([bias_q, jnp.zeros_like(bias_q), bias_v], 1)
    bo, shift_one, gain_two = low_ref[1:2, :], low_ref[2:3, :], low_ref[3:4, :]
    gain_one, b2, shift_two = high_ref[1:2, :], high_ref[2:3, :], high_ref[3:4, :]

    state["far_qkv"].wait()
    for chunk in range(CHUNKS):
        for side in range(2):
            here = pl.ds((chunk * 2 + side) * half_rows, half_rows)
            total = up_ref[here, wide] + project_half(chunk, side, 1 - group) + bias_qkv
            total = total.astype(low)
            for slot, place in enumerate(pieces(chunk, side)):
                qkv_ref[pl.ds(pl.multiple_of(ext + place, rows), rows), :] = total[
                    slot * rows : (slot + 1) * rows
                ]
    near_edge = own_rows - REACH - group * (own_rows - REACH - HALO)
    far_edge = HALO - REACH + group * (own_rows - HALO + REACH)
    halo_src = pl.ds(pl.multiple_of(PAD + near_edge, 32), REACH)
    halo_dst = pl.ds(pl.multiple_of(PAD + far_edge, 32), REACH)
    key_value = pl.ds(HEAD_DIM, 2 * HEAD_DIM)
    far_halo = far(qkv_ref.at[halo_src, key_value], qkv_ref.at[halo_dst, key_value], 6)
    far_wo_to = (1 - group) * GROUP + 2 * chip + group
    far_wo = push(
        wo_ref, wo_all.at[group, core], far_send.at[4 + core], far_recv.at[4 + core], far_wo_to
    )
    far_wo.start()
    far_w2.append(far(w2_ref.at[w2_last, :], w2_all.at[group, w2_last, :], 8))
    w1_blocks = exchange_blocks(
        [(pack_w1, w1_all.at[group])],
        (block_local.at[1:2], block_send.at[1:2], block_recv.at[1:2]), base, mine, others,
    )

    def attend_tile(at):
        tile = at + group * (GROUP - 1 - 2 * at)
        row = pl.multiple_of(ext + tile * TILE, 64)
        start = pl.multiple_of(ext - PAD + tile * TILE, 64)
        place = pl.multiple_of(group * HALO + tile * TILE, TILE)
        _, _, probs = tile_probs(
            qkv_ref, row, start, seg_q_ref[pl.ds(place, TILE), :],
            seg_k_ref[group * (HALO // TILE) + tile],
        )
        values = qkv_ref[pl.ds(start, WINDOW), 2 * HEAD_DIM : 3 * HEAD_DIM]
        out = jnp.dot(probs.astype(low), values, preferred_element_type=f32)
        att_ref[pl.ds(pl.multiple_of(tile * TILE, TILE), TILE), :] = out.astype(low)

    def attend_two(at, carry):
        attend_tile(2 * at)
        attend_tile(2 * at + 1)
        return carry

    lax.fori_loop(0, own_rows // TILE // 2 - 1, attend_two, 0)
    far_halo.wait()
    for copy in w1_blocks:
        copy.wait()
    far_w1 = far(w1_all.at[group], w1_all.at[group], 7)
    attend_tile(own_rows // TILE - 2)
    attend_tile(own_rows // TILE - 1)
    for chunk in range(CHUNKS):
        spills[0, chunk].wait()
    wo_near.wait()
    far_wo.wait_send()

    @pl.when(core != group)
    def _():
        for at in range(2):
            push(
                wo_ref, wo_all.at[1 - group, at], far_send.at[4 + at], far_recv.at[4 + at],
                far_wo_to,
            ).wait_recv()

    def branch_part(chunk, side, dst):
        rows_in = jnp.concatenate([att_ref[pl.ds(at, rows), :] for at in pieces(chunk, side)], 0)
        att_t[:, pl.ds(row_at(chunk, side), half_rows)] = rows_in.astype(f32).T.astype(low)

        def body(at, columns):
            weight = wo_all[core, :, :, columns].reshape(HEAD_DIM, SPLIT)
            part = jnp.dot(rows_in, weight, preferred_element_type=f32)
            dst[:, :, :, :, columns] = part.astype(low).reshape(2, 2, 2, rows, SPLIT)

        tiles(width, body)

    def upward(chunk, side):
        here = pl.ds(row_at(chunk, side), half_rows)

        def body(at, columns):
            weight = w1_all[:, :, :, columns].reshape(width, SPLIT)
            up = jnp.dot(flat(all_h, chunk, side), weight, preferred_element_type=f32)
            up = up + b1_ref[0:1, columns]
            up_ref[here, columns] = up
            act = gelu_tanh(up)
            act_ref[:, columns] = act.astype(low)
            act_t[columns, here] = act.T.astype(low)

        tiles(units, body)

    def downward(dst):
        def body(at, columns):
            weight = w2_all[:, :, columns].reshape(units, SPLIT)
            part = jnp.dot(act_ref[...], weight, preferred_element_type=f32)
            dst[:, :, :, :, columns] = part.astype(low).reshape(2, 2, 2, rows, SPLIT)

        tiles(width, body)

    def up_back(chunk, side):
        here = pl.ds(row_at(chunk, side), half_rows)

        def body(at, columns):
            grad = lax.dot_general(
                flat(all_m, chunk, side), w2_all[at], NT, preferred_element_type=f32
            )
            grad = (grad * gelu_slope(up_ref[here, columns])).astype(low)
            dup_ref[:, columns] = grad
            grad = grad.astype(f32)
            gb1_ref[0:1, columns] += jnp.sum(grad, 0, keepdims=True)
            dup_t[columns, here] = grad.T.astype(low)

        tiles(units, body)

    def down_back(dst):
        def body(at, columns):
            weight = w1_all[at // 4, pl.ds(at % 4 * 4, 4)].reshape(SPLIT, units)
            part = lax.dot_general(dup_ref[...], weight, NT, preferred_element_type=f32)
            dst[:, :, :, :, columns] = part.astype(low).reshape(2, 2, 2, rows, SPLIT)

        tiles(width, body)

    def out_back(chunk, side):
        weight = wo_all[core].reshape(HEAD_DIM, width)
        grad = lax.dot_general(flat(all_h, chunk, side), weight, NT, preferred_element_type=f32)
        grad = grad.astype(low)
        for slot, place in enumerate(pieces(chunk, side)):
            dout_ref[pl.ds(pl.multiple_of(group * HALO + place, rows), rows), :] = grad[
                slot * rows : (slot + 1) * rows
            ]

    def keep(chunk):
        def finish(row, first, count, total):
            res_ref[chunk * rows + row : chunk * rows + row + 16, first : first + count] = total

        return finish

    def row_sets(chunk):
        for row in range(0, rows, 16):
            yield slice(chunk * rows + row, chunk * rows + row + 16), slice(row, row + 16)

    def normal(res):
        res = res - jnp.mean(res, -1, keepdims=True)
        scale = lax.rsqrt(jnp.mean(res * res, -1, keepdims=True) + norm_eps)
        return res * scale, scale

    def normal_back(grad, res, gain, scale, at):
        vecg_ref[at + 2 : at + 3, :] += jnp.sum(grad, 0, keepdims=True)
        vecg_ref[at + 1 : at + 2, :] += jnp.sum(grad * res, 0, keepdims=True)
        grad = grad * gain
        first = jnp.mean(grad, -1, keepdims=True)
        second = jnp.mean(grad * res, -1, keepdims=True)
        grad = (grad - first - res * second) * scale
        grad_low = grad.astype(low)
        vecg_ref[at : at + 1, :] += jnp.sum(grad_low.astype(f32), 0, keepdims=True)
        return grad, grad_low

    def norm_one(chunk):
        for at, place in row_sets(chunk):
            res, scale = normal(tok_ref[at, :].astype(f32) + res_ref[at, :] + bo)
            norm_ref[at, :] = res
            scale_ref[at, :] = jnp.broadcast_to(scale, (16, 128))
            hidden = res * gain_one + shift_one
            hid_ref[at, :] = hidden
            all_h[(chunk,) + own_slot + (place, slice(None))] = hidden.astype(low)

    def norm_two(chunk):
        for at, place in row_sets(chunk):
            res, scale = normal(hid_ref[at, :] + res_ref[at, :] + b2)
            out_ref[at, :] = (res * gain_two + shift_two).astype(low)
            grad, grad_low = normal_back(cot_ref[at, :].astype(f32), res, gain_two, scale, 0)
            dres_ref[at, :] = grad
            all_m[(chunk,) + own_slot + (place, slice(None))] = grad_low

    def norm_one_back(chunk):
        for at, place in row_sets(chunk):
            grad, grad_low = normal_back(
                dres_ref[at, :] + res_ref[at, :], norm_ref[at, :], gain_one,
                scale_ref[at, 0:1], 3,
            )
            dres_ref[at, :] = grad
            all_h[(chunk,) + own_slot + (place, slice(None))] = grad_low

    def flow(chunk):
        incoming = (in_one.at[chunk], in_two.at[chunk], in_three.at[chunk])
        own, other = own_part.at[chunk], far_part.at[chunk % 2]
        arrived = pair_in.at[chunk]
        branch_part(chunk, 1 - core, other)
        share = net.share(other, arrived, 1, chunk)
        branch_part(chunk, core, own)
        yield
        yield from net.scatter(own, arrived, incoming, share, 1, chunk, keep(chunk))
        norm_one(chunk)
        share = yield from net.gather(all_h.at[chunk], 2, chunk)
        if chunk == 0:
            far_w1.wait()
        upward(chunk, core)
        if chunk == 0:
            for copy in far_w2:
                copy.wait()
        downward(own)
        yield
        share.wait()
        spills[1, chunk] = spill(all_h, h_all, chunk, 1)
        upward(chunk, 1 - core)
        downward(other)
        share = net.share(other, arrived, 3, chunk)
        yield
        yield from net.scatter(own, arrived, incoming, share, 3, chunk, keep(chunk))
        norm_two(chunk)
        spills[1, chunk].wait()
        share = yield from net.gather(all_m.at[chunk], 4, chunk)
        up_back(chunk, core)
        down_back(own)
        yield
        share.wait()
        up_back(chunk, 1 - core)
        down_back(other)
        share = net.share(other, arrived, 5, chunk)
        state["backs"] += 1
        yield
        yield from net.scatter(own, arrived, incoming, share, 5, chunk, keep(chunk))
        norm_one_back(chunk)
        share = yield from net.gather(all_h.at[chunk], 6, chunk)
        out_back(chunk, core)
        yield
        share.wait()
        out_back(chunk, 1 - core)

    def product(left_t, right, columns):
        total = None
        for chunk in range(CHUNKS):
            for side in range(2):
                here = slice((chunk * 2 + side) * half_rows, (chunk * 2 + side + 1) * half_rows)
                term = jnp.dot(
                    left_t[:, here], flat(right, chunk, side, columns), preferred_element_type=f32
                )
                total = term if total is None else total + term
        return total

    def run(first, last, write):
        def step(at, carry):
            write(at, at % 2, at >= 2)
            return carry

        lax.fori_loop(first, last, step, 0)

    def emit(src, dst, sem, again):
        copy = pltpu.make_async_copy(src, dst, sem)

        @pl.when(again)
        def _():
            copy.wait()

        return copy

    def columns_at(at):
        return pl.ds(pl.multiple_of(at * SPLIT, SPLIT), SPLIT)

    def write_w2(at, slot, again):
        own = emit(stage_ref.at[slot], gw2_own.at[:, columns_at(at)], out_sems.at[0, slot], again)
        there = emit(stage_low.at[slot], gw2_far.at[:, columns_at(at)], out_sems.at[1, slot], again)
        total = product(act_t, all_m, columns_at(at))
        first = group == 0
        stage_ref[slot] = jnp.where(first, total[:256], total[256:])
        stage_low[slot] = jnp.where(first, total[256:], total[:256]).astype(low)
        own.start()
        there.start()

    def write_w1(first):
        def write(at, slot, again):
            tile = first + at
            here = gw1_ref.at[pl.ds(pl.multiple_of(tile * 4, 4), 4)]
            copy = emit(stage_w1.at[slot], here, out_sems.at[2, slot], again)
            total = product(dup_t, all_m, columns_at(tile)).T.astype(low)
            stage_w1[slot] = total.reshape(4, SPLIT // 4, units)
            copy.start()

        return write

    def write_wo(at, slot, again):
        own = emit(stage_ref.at[slot, 0:HEAD_DIM, :], gwo_ref.at[:, columns_at(at)], out_sems.at[4, slot], again)
        stage_ref[slot, 0:HEAD_DIM, :] = product(att_t, all_h, columns_at(at))
        own.start()

    def fill():
        while state["backs"] < CHUNKS:
            yield
        run(0, width // SPLIT // 2, write_w2)
        yield
        run(width // SPLIT // 2, width // SPLIT, write_w2)
        for slot in range(2):
            emit(stage_ref.at[slot], gw2_own.at[:, columns_at(0)], out_sems.at[0, slot], True)
            emit(stage_low.at[slot], gw2_far.at[:, columns_at(0)], out_sems.at[1, slot], True)
        swaps.append(far(gw2_far, gw2_in, 10))
        back = [pltpu.make_async_copy(h_all.at[at], all_m.at[at], spill_sems.at[2, at]) for at in range(CHUNKS)]
        for copy in back:
            copy.start()
        yield
        for copy in back:
            copy.wait()
        run(0, width // SPLIT // 2, write_w1((1 - group) * 4))
        for slot in range(2):
            emit(stage_w1.at[slot], gw1_ref.at[pl.ds(0, 4)], out_sems.at[2, slot], True)
        first = pl.ds(pl.multiple_of((1 - group) * GROUP, GROUP), GROUP)
        swaps.extend(
            far_blocks(
                gw1_ref.at[first, :, pl.ds(0, units // 2)], gw1_in,
                there_send, there_recv, group, mine,
            )
        )
        yield
        run(0, width // SPLIT // 2, write_w1(group * 4))
        for slot in range(2):
            emit(stage_w1.at[slot], gw1_ref.at[pl.ds(0, 4)], out_sems.at[2, slot], True)

    swaps = []
    step_through([flow(chunk) for chunk in range(CHUNKS)], fill())
    query = pl.ds(0, HEAD_DIM)
    far_query = far(qkv_ref.at[halo_src, query], qkv_ref.at[halo_dst, query], 12)
    dout_src = pl.ds(pl.multiple_of(near_edge, 32), REACH)
    dout_dst = pl.ds(pl.multiple_of(far_edge, 32), REACH)
    far_dout = far(dout_ref.at[dout_src, :], dout_ref.at[dout_dst, :], 9)
    run(0, width // SPLIT, write_wo)
    for slot in range(2):
        emit(stage_ref.at[slot, 0:HEAD_DIM, :], gwo_ref.at[:, columns_at(0)], out_sems.at[4, slot], True)
    far_dout.wait()
    far_query.wait()
    for copy in swaps:
        copy.wait()


def layer(tokens, cotangent, pack_qkv, pack_w1, w2, wo, vector, seg_q, seg_k):
    f32, bf16 = jnp.float32, jnp.bfloat16
    block, width = tokens.shape
    rows = block // CHUNKS
    unit_rows = w2.shape[0]
    units = 2 * unit_rows
    half_rows = rows * GROUP // 2
    own_rows = GROUP * block
    weight_rows = wo.shape[0]
    peers = GROUP - 1
    vmem = pl.BlockSpec(memory_space=pltpu.VMEM)
    anywhere = pl.BlockSpec(memory_space=pl.ANY)
    sems = pltpu.SemaphoreType.DMA
    shape = jax.ShapeDtypeStruct

    def slots(*lead):
        return pltpu.VMEM(lead + (rows, width), bf16)

    return pl.pallas_call(
        layer_kernel,
        out_shape=[
            shape((block, width), bf16),
            shape((block, width), f32),
            shape((8, width), f32),
            shape((8, units), f32),
            shape((unit_rows, width), f32),
            shape((unit_rows, width), bf16),
            shape((unit_rows, width), bf16),
            shape((2 * GROUP, weight_rows, units), bf16),
            shape((GROUP, weight_rows, unit_rows), bf16),
            shape((HEAD_DIM, width), f32),
            shape((CHUNKS, 2, 2, 2, 2, rows, width), bf16),
            shape((CHUNKS, 2, 2, 2, 2, rows, width), bf16),
            shape((own_rows + HALO + 2 * PAD, 3 * HEAD_DIM), bf16),
            shape((own_rows + HALO, HEAD_DIM), bf16),
            shape((2, GROUP, weight_rows, 3 * HEAD_DIM), bf16),
        ],
        in_specs=[vmem, vmem, anywhere, anywhere, anywhere, anywhere, vmem, vmem, vmem],
        out_specs=[vmem] * 4 + [anywhere] * 8 + [vmem] * 3,
        scratch_shapes=[
            slots(CHUNKS, 2, 2, 2, 2), slots(CHUNKS, 2, 2, 2, 2),
            slots(CHUNKS, 2, 2, 2), slots(2, 2, 2, 2), slots(CHUNKS, 2, 2, 2),
            slots(CHUNKS, 2, 2), slots(CHUNKS, 2), slots(CHUNKS),
            pltpu.VMEM((own_rows, units), f32),
            pltpu.VMEM((half_rows, units), bf16),
            pltpu.VMEM((units, own_rows), bf16),
            pltpu.VMEM((half_rows, units), bf16),
            pltpu.VMEM((units, own_rows), bf16),
            pltpu.VMEM((own_rows, HEAD_DIM), bf16),
            pltpu.VMEM((HEAD_DIM, own_rows), bf16),
            pltpu.VMEM((block, width), f32),
            pltpu.VMEM((block, width), f32),
            pltpu.VMEM((block, width), f32),
            pltpu.VMEM((block, 128), f32),
            pltpu.VMEM((2, GROUP, weight_rows, units), bf16),
            pltpu.VMEM((2, unit_rows, width), bf16),
            pltpu.VMEM((2, 2, weight_rows, width), bf16),
            pltpu.VMEM((2, GROUP, 8, 128), f32),
            pltpu.VMEM((8, width), f32),
            pltpu.VMEM((8, width), f32),
            pltpu.VMEM((8, units), f32),
            pltpu.VMEM((2, SPLIT, SPLIT), f32),
            pltpu.VMEM((2, SPLIT, SPLIT), bf16),
            pltpu.VMEM((2, 4, SPLIT // 4, units), bf16),
            sems((STAGES, CHUNKS, 4, 3)), sems((STAGES, CHUNKS, 4, 3)),
            sems((STAGES, CHUNKS)), sems((STAGES, CHUNKS)),
            sems((2,)), sems((2, peers)), sems((2, peers)), sems((GROUP,)), sems((GROUP,)),
            sems((peers,)), sems((peers,)),
            sems((13,)), sems((13,)), sems((3,)), sems((5, 2)), sems((3, CHUNKS)),
        ],
        compiler_params=pltpu.CompilerParams(
            collective_id=4, has_side_effects=True, vmem_limit_bytes=63 << 20
        ),
        name="layer",
    )(tokens, cotangent, pack_qkv, pack_w1, w2, wo, vector, seg_q, seg_k)


def tail_kernel(
    qkv_ref, dout_ref, seg_q_ref, seg_k_ref, wqkv_ref, dres_ref, gwo_ref, parts_ref,
    x_all, gw1_ref, w1_early, w2_own, w2_early,
    input_ref, out_q, out_k, out_v, out_wo, out_w1, out_w2, vec_ref,
    xs_ref, own_part, far_part, pair_in, in_one, in_two, in_three, res_ref,
    dqkv_ref, dk_sum, dv_sum, dqkv_t, gq_own, gq_far, gq_here, gq_there,
    w1_here, w1_there, w2_sum, w2_in, wo_low, wo_in, wo_pair, wo_pair_in,
    blocks_ref, arrived, theirs, far_vec_in,
    hop_send, hop_recv, pair_send, pair_recv, load_sems,
    block_local, block_send, block_recv, there_send, there_recv, far_send, far_recv,
):
    f32, low = jnp.float32, qkv_ref.dtype
    block, width = dres_ref.shape
    rows = block // TAIL_CHUNKS
    weight_rows = out_q.shape[0]
    scale = HEAD_DIM ** (-0.5)
    group, base, mine, others, across, there = group_places()
    net = Traffic((hop_send, hop_recv, pair_send, pair_recv), TAIL_PLANS)
    core, chip = net.core, mine // 2
    enter(others + there)

    def far(src, dst, at, device=across):
        copy = push(src, dst, far_send.at[at], far_recv.at[at], device)
        copy.start()
        return copy

    def load(src, dst, at):
        copy = pltpu.make_async_copy(src, dst, load_sems.at[at])
        copy.start()
        return copy

    far_wo = push(
        wo_low, wo_in, far_send.at[0], far_recv.at[0], core * GROUP + 2 * chip + core
    )

    @pl.when(core != group)
    def _():
        wo_low[...] = gwo_ref[...].astype(low)
        far_wo.start()

    def blocks(pairs, at):
        here = slice(at, at + len(pairs))
        return exchange_blocks(
            pairs, (block_local.at[here], block_send.at[here], block_recv.at[here]),
            base, mine, others,
        )

    unit_rows = w1_early.shape[-1]
    early, late = pl.ds(0, unit_rows), pl.ds(unit_rows, unit_rows)
    first = pl.ds(pl.multiple_of((1 - group) * GROUP, GROUP), GROUP)
    w1_far = far_blocks(
        gw1_ref.at[first, :, late], w1_there.at[:, :, late],
        there_send.at[0], there_recv.at[0], group, mine,
    )
    x_loads = [load(x_all.at[at], xs_ref.at[at], at) for at in range(CHUNKS)]
    loads = [
        load(w1_early, w1_there.at[:, :, early], CHUNKS),
        load(w2_own, w2_sum, CHUNKS + 1),
        load(w2_early, w2_in, CHUNKS + 2),
    ]
    blocks_ref[...] = parts_ref[...]
    dk_sum[...] = jnp.zeros_like(dk_sum)
    dv_sum[...] = jnp.zeros_like(dv_sum)

    def attend_back_tile(tile):
        place = pl.multiple_of(tile * TILE, TILE)
        row = pl.multiple_of(PAD + place, 64)
        window = pl.ds(place, WINDOW)
        queries, keys, probs = tile_probs(
            qkv_ref, row, place, seg_q_ref[pl.ds(place, TILE), :], seg_k_ref[tile]
        )
        values = qkv_ref[window, 2 * HEAD_DIM : 3 * HEAD_DIM]
        grads = dout_ref[pl.ds(place, TILE), :]
        grad_probs = lax.dot_general(grads, values, NT, preferred_element_type=f32)
        inner = jnp.sum(probs * grad_probs, -1, keepdims=True)
        grad_scores = (probs * (grad_probs - inner)).astype(low)
        grad_q = jnp.dot(grad_scores, keys, preferred_element_type=f32)
        dqkv_ref[pl.ds(place, TILE), 0:HEAD_DIM] = (grad_q * scale).astype(low)
        dk_sum[window, :] += lax.dot_general(grad_scores, queries, TN, preferred_element_type=f32)
        dv_sum[window, :] += lax.dot_general(
            probs.astype(low), grads, TN, preferred_element_type=f32
        )

    def attend_back_two(at, carry):
        attend_back_tile(2 * at)
        attend_back_tile(2 * at + 1)
        return carry

    ext_rows = dout_ref.shape[0]
    lax.fori_loop(0, ext_rows // TILE // 2, attend_back_two, 0)
    inside = slice(PAD, PAD + ext_rows)
    dqkv_ref[:, HEAD_DIM : 2 * HEAD_DIM] = (dk_sum[inside, :] * scale).astype(low)
    dqkv_ref[:, 2 * HEAD_DIM : 3 * HEAD_DIM] = dv_sum[inside, :].astype(low)

    def rows_of(chunk, side, rows):
        places = [
            group * HALO + (slot * 2 + side) * block + chunk * rows for slot in range(GROUP // 2)
        ]
        return jnp.concatenate(
            [dqkv_ref[pl.ds(pl.multiple_of(place, rows), rows), :] for place in places], 0
        )

    x_rows = block // CHUNKS
    x_half = x_rows * GROUP // 2
    bias = jnp.zeros((1, 3 * HEAD_DIM), f32)
    for chunk in range(CHUNKS):
        for side in range(2):
            part = rows_of(chunk, side, x_rows).astype(f32)
            bias = bias + jnp.sum(part, 0, keepdims=True)
            here = slice((chunk * 2 + side) * x_half, (chunk * 2 + side + 1) * x_half)
            dqkv_t[:, here] = part.T.astype(low)

    for copy in x_loads:
        copy.wait()

    def product(at):
        columns = pl.ds(pl.multiple_of(at * SPLIT, SPLIT), SPLIT)
        total = None
        for chunk in range(CHUNKS):
            for side in range(2):
                here = slice((chunk * 2 + side) * x_half, (chunk * 2 + side + 1) * x_half)
                right = xs_ref[chunk, side, :, :, :, :, columns].reshape(x_half, SPLIT)
                term = jnp.dot(dqkv_t[:, here], right, preferred_element_type=f32)
                total = term if total is None else total + term
        return total.T

    quarter = width // SPLIT // 2

    def tile_of(ref, first):
        def body(at, carry):
            total = product(first + at).astype(low)
            ref[pl.ds(pl.multiple_of(at * 4, 4), 4)] = total.reshape(4, SPLIT // 4, 3 * HEAD_DIM)
            return carry

        lax.fori_loop(0, quarter, body, 0)

    tile_of(gq_far, (1 - group) * quarter)
    qkv_far = far_blocks(gq_far, gq_there, there_send.at[1], there_recv.at[1], group, mine)

    bias_q, bias_v = bias[:, 0:HEAD_DIM], bias[:, 2 * HEAD_DIM : 3 * HEAD_DIM]
    lane = lax.broadcasted_iota(jnp.int32, (1, 128), 1)
    blocks_ref[2 * chip, pl.ds(core * 8, 1), :] = jnp.where(
        lane < 64, bias_q, pltpu.roll(bias_v, 64, 1)
    )
    blocks_ref[2 * chip + 1, pl.ds(core * 8, 1), :] = jnp.where(
        lane < 64, pltpu.roll(bias_q, 64, 1), bias_v
    )

    vec_blocks = blocks([(blocks_ref, arrived)], 0)

    def input_part(chunk, side, dst):
        left = rows_of(chunk, side, rows)

        def body(at, carry):
            weight = wqkv_ref[at // 4, pl.ds(at % 4 * 4, 4)].reshape(SPLIT, 3 * HEAD_DIM)
            part = lax.dot_general(left, weight, NT, preferred_element_type=f32)
            columns = pl.ds(pl.multiple_of(at * SPLIT, SPLIT), SPLIT)
            dst[:, :, :, :, columns] = part.astype(low).reshape(2, 2, 2, rows, SPLIT)
            return carry

        lax.fori_loop(0, width // SPLIT, body, 0)

    def flow(chunk):
        def finish(row, first, count, total):
            res_ref[chunk * rows + row : chunk * rows + row + 16, first : first + count] = total

        incoming = (in_one.at[chunk], in_two.at[chunk], in_three.at[chunk])
        other = far_part.at[chunk % 2]
        input_part(chunk, 1 - core, other)
        share = net.share(other, pair_in.at[chunk], 0, chunk)
        input_part(chunk, core, own_part.at[chunk])
        yield
        yield from net.scatter(
            own_part.at[chunk], pair_in.at[chunk], incoming, share, 0, chunk, finish
        )
        here = slice(chunk * rows, (chunk + 1) * rows)
        input_ref[here, :] = (dres_ref[here, :] + res_ref[here, :]).astype(low)

    def fill():
        yield
        yield
        for copy in loads:
            copy.wait()
        out_w2[...] = w2_sum[...] + w2_in[...].astype(f32)
        yield
        tile_of(gq_own, group * quarter)
        state["qkv"] = blocks([(gq_own, gq_here)], 2)
        yield
        for copy in vec_blocks:
            copy.wait()
        total = arrived[0]
        for at in range(1, GROUP):
            total = total + arrived[at]
        first, second = total[:8], total[8:]
        theirs[...] = jnp.where(group == 0, second, first)
        vec_ref[...] = jnp.where(group == 0, first, second)
        state["vec"] = far(theirs, far_vec_in, 3)

    state = {}
    step_through([flow(chunk) for chunk in range(TAIL_CHUNKS)], fill())

    share_wo = push(wo_pair, wo_pair_in, far_send.at[4], far_recv.at[4], net.pair)

    @pl.when(core == group)
    def _():
        far_wo.wait_recv()
        total = gwo_ref[...] + wo_in[...].astype(f32)
        first, second = total[:weight_rows], total[weight_rows:]
        out_wo[...] = jnp.where(core == 0, first, second)
        wo_pair[...] = jnp.where(core == 0, second, first)
        share_wo.start()

    own_first = pl.ds(pl.multiple_of(group * GROUP, GROUP), GROUP)
    w1_blocks = blocks([(gw1_ref.at[own_first], w1_here)], 1)
    state["vec"].wait()
    vec_ref[...] += far_vec_in[...]

    @pl.when(core != group)
    def _():
        far_wo.wait_send()
        share_wo.wait_recv()
        out_wo[...] = wo_pair_in[...]

    @pl.when(core == group)
    def _():
        share_wo.wait_send()

    for copy in w1_blocks + w1_far:
        copy.wait()
    for at in range(GROUP):
        for part in range(2):
            here = slice(part * unit_rows, (part + 1) * unit_rows)
            to = (part * GROUP + at) * unit_rows
            out_w1[:, to : to + unit_rows] = w1_here[at, :, here].astype(f32) + w1_there[
                at, :, here
            ].astype(f32)
    for copy in state["qkv"] + qkv_far:
        copy.wait()
    for at in range(GROUP):
        to = (at % 2 * 8 + at // 2) * HEAD_DIM
        for part, ref in enumerate((out_q, out_k, out_v)):
            here = slice(part * HEAD_DIM, (part + 1) * HEAD_DIM)
            ref[:, to : to + HEAD_DIM] = gq_here[at, :, here].astype(f32) + gq_there[
                at, :, here
            ].astype(f32)


def layer_tail(
    qkv, dout, seg_q, seg_k, wqkv, dres, gwo, parts, x_all, gw1, w1_early, w2_own, w2_early
):
    f32, bf16 = jnp.float32, jnp.bfloat16
    block, width = dres.shape
    rows = block // TAIL_CHUNKS
    weight_rows = wqkv.shape[2]
    units = gw1.shape[2]
    unit_rows = units // 2
    own_rows = GROUP * block
    peers = GROUP - 1
    vmem = pl.BlockSpec(memory_space=pltpu.VMEM)
    anywhere = pl.BlockSpec(memory_space=pl.ANY)
    sems = pltpu.SemaphoreType.DMA
    shape, scratch = jax.ShapeDtypeStruct, pltpu.VMEM
    heads = 3 * HEAD_DIM

    def slots(*lead):
        return scratch(lead + (rows, width), bf16)

    return pl.pallas_call(
        tail_kernel,
        out_shape=[
            shape((block, width), bf16),
            shape((weight_rows, width), f32),
            shape((weight_rows, width), f32),
            shape((weight_rows, width), f32),
            shape((weight_rows, width), f32),
            shape((weight_rows, GROUP * units), f32),
            shape((unit_rows, width), f32),
            shape((8, 128), f32),
        ],
        in_specs=[vmem] * 8 + [anywhere] * 5,
        out_specs=[vmem] * 8,
        scratch_shapes=[
            scratch(x_all.shape, bf16),
            slots(TAIL_CHUNKS, 2, 2, 2), slots(2, 2, 2, 2), slots(TAIL_CHUNKS, 2, 2, 2),
            slots(TAIL_CHUNKS, 2, 2), slots(TAIL_CHUNKS, 2), slots(TAIL_CHUNKS),
            scratch((block, width), f32),
            scratch((own_rows + HALO, heads), bf16),
            scratch(qkv.shape[:1] + (HEAD_DIM,), f32),
            scratch(qkv.shape[:1] + (HEAD_DIM,), f32),
            scratch((heads, own_rows), bf16),
            scratch((GROUP, weight_rows, heads), bf16),
            scratch((GROUP, weight_rows, heads), bf16),
            scratch((GROUP, weight_rows, heads), bf16),
            scratch((GROUP, weight_rows, heads), bf16),
            scratch((GROUP, weight_rows, units), bf16),
            scratch((GROUP, weight_rows, units), bf16),
            scratch((unit_rows, width), f32),
            scratch((unit_rows, width), bf16),
            scratch((HEAD_DIM, width), bf16),
            scratch((HEAD_DIM, width), bf16),
            scratch((weight_rows, width), f32),
            scratch((weight_rows, width), f32),
            scratch(parts.shape, f32),
            scratch(parts.shape, f32),
            scratch((8, 128), f32),
            scratch((8, 128), f32),
            sems((1, TAIL_CHUNKS, 4, 3)), sems((1, TAIL_CHUNKS, 4, 3)),
            sems((1, TAIL_CHUNKS)), sems((1, TAIL_CHUNKS)),
            sems((CHUNKS + 3,)), sems((3,)), sems((3, peers)), sems((3, peers)),
            sems((2, GROUP)), sems((2, GROUP)), sems((5,)), sems((5,)),
        ],
        compiler_params=pltpu.CompilerParams(
            collective_id=5, has_side_effects=True, vmem_limit_bytes=63 << 20
        ),
        name="layer_tail",
    )(qkv, dout, seg_q, seg_k, wqkv, dres, gwo, parts, x_all, gw1, w1_early, w2_own, w2_early)


def grouped_device(
    tokens,
    cotangent,
    lengths,
    wq,
    bq,
    wk,
    wv,
    bv,
    wo,
    bo,
    norm1_gain,
    norm1_bias,
    w1,
    b1,
    w2,
    b2,
    norm2_gain,
    norm2_bias,
):
    f32 = jnp.float32
    bf16 = jnp.bfloat16
    devices = lax.axis_size("dp")
    block, width = tokens.shape
    own_rows = GROUP * block
    total_tokens = devices * block
    weight_rows = wq.shape[0]
    unit_rows, units = w2.shape[0], w1.shape[1]
    device = lax.axis_index("dp")
    group, member = device // GROUP, device % GROUP
    chip, core = member // 2, member % 2
    head = core * 8 + chip

    def by_head(weight):
        return weight.reshape(weight_rows, 2, 8, HEAD_DIM).transpose(2, 1, 0, 3).reshape(
            GROUP, weight_rows, HEAD_DIM
        )

    pack_qkv = jnp.concatenate([by_head(wq), by_head(wk), by_head(wv)], -1)
    pack_w1 = w1.reshape(weight_rows, 2, GROUP, unit_rows).transpose(2, 0, 1, 3).reshape(
        GROUP, weight_rows, 2 * unit_rows
    )
    vectors = [bq, bv, bo, norm1_gain, norm1_bias, b2, norm2_gain, norm2_bias, b1]
    sizes = [item.shape[0] for item in vectors]
    vector = jnp.concatenate(vectors).astype(f32)
    vector = jnp.pad(vector, (0, 1024 - vector.shape[0])).reshape(8, 128)

    ext_rows = own_rows + HALO
    ext_first = group * (own_rows - HALO)
    offset = group * HALO
    starts = jnp.cumsum(lengths) - lengths
    ext_ids = ext_first + jnp.arange(ext_rows, dtype=jnp.int32)
    seg = jnp.sum((ext_ids[:, None] >= starts[None, :]).astype(jnp.int32), 1)
    tile_rows = jnp.arange(ext_rows // TILE, dtype=jnp.int32) * TILE - PAD
    key_rows = tile_rows[:, None] + jnp.arange(WINDOW, dtype=jnp.int32)[None, :]
    key_ids = ext_first + key_rows
    seg_k = jnp.sum((key_ids[:, :, None] >= starts[None, None, :]).astype(jnp.int32), 2)
    seg_k = jnp.where((key_rows >= 0) & (key_rows < ext_rows), seg_k, -1)[:, None, :]
    seg_q = seg[:, None]

    (
        output, grad_resid_one, vec_grads, grad_b1, w2_own, _, w2_early, grad_w1, w1_early, grad_wo,
        all_tokens, _, qkv, grad_out, full_qkv,
    ) = layer(tokens, cotangent, pack_qkv, pack_w1, w2, wo, vector, seg_q, seg_k)

    spread_b1 = lax.dynamic_update_slice_in_dim(
        jnp.zeros((2, GROUP, unit_rows), f32), grad_b1[0].reshape(2, 1, unit_rows), member, 1
    )
    grad_b2, grad_gain_two, grad_shift_two, grad_bo, grad_gain_one, grad_shift_one = [
        vec_grads[at] for at in range(6)
    ]
    none = jnp.zeros((width,), f32)
    items = [
        none, none, grad_bo, grad_gain_one, grad_shift_one, grad_b2, grad_gain_two, grad_shift_two,
        spread_b1,
    ]
    parts = jnp.concatenate([item.reshape(2, GROUP, -1) for item in items], 2)
    parts = jnp.pad(parts, ((0, 0), (0, 0), (0, 1024 - parts.shape[2])))
    parts = parts.transpose(1, 0, 2).reshape(GROUP, 16, 128)
    input_grad, out_q, out_k, out_v, out_wo, out_w1, out_w2, sums = layer_tail(
        qkv, grad_out, seg_q, seg_k, full_qkv, grad_resid_one, grad_wo, parts,
        all_tokens, grad_w1, w1_early, w2_own, w2_early,
    )
    sums, at = sums.reshape(-1), 0
    small = []
    for size in sizes:
        small.append(sums[at : at + size])
        at += size
    out_bq, out_bv, out_bo, out_g1, out_s1, out_b2, out_g2, out_s2, out_b1 = small
    return (
        output, input_grad, out_q, out_bq, out_k, out_v, out_bv, out_wo, out_bo, out_g1, out_s1,
        out_w1, out_b1, out_w2, out_b2, out_g2, out_s2,
    )


def solution(mesh):
    in_specs = (
        P("dp", None),
        P("dp", None),
        P(),
        P("dp", None),
        P("dp"),
        P("dp", None),
        P("dp", None),
        P("dp"),
        P("dp", None),
        P("dp"),
        P("dp"),
        P("dp"),
        P("dp", None),
        P("dp"),
        P("dp", None),
        P("dp"),
        P("dp"),
        P("dp"),
    )
    out_specs = (
        P("dp", None),
        P("dp", None),
        P("dp", None),
        P("dp"),
        P("dp", None),
        P("dp", None),
        P("dp"),
        P("dp", None),
        P("dp"),
        P("dp"),
        P("dp"),
        P("dp", None),
        P("dp"),
        P("dp", None),
        P("dp"),
        P("dp"),
        P("dp"),
    )
    two_groups = mesh.shape["dp"] == 2 * GROUP
    return jax.shard_map(
        grouped_device if two_groups else per_device, mesh=mesh, in_specs=in_specs, out_specs=out_specs, check_vma=False
    )
```

```python
import functools

import jax
import jax.numpy as jnp
from jax import lax
from jax.experimental import pallas as pl
from jax.experimental.pallas import tpu as pltpu
from jax.sharding import PartitionSpec as P

HEADS = 16
HEAD_DIM = 128
SEQ_MAX = 160
SPAN = 3

GROUP = 16
HALO = 256
WINDOW = 512
TILE = 128
MESH_ID = pl.DeviceIdType.MESH
VMEM_LIMIT = 60 << 20
PORTIONS = ((0, 48), (48, 48), (96, 32))
ORDERS = ((0, 1, 2), (1, 2, 0), (2, 0, 1))


norm_eps = 1e-05


def layer_norm(residual, gain_vec, shift_vec):
    mean_val = jnp.mean(residual, axis=-1, keepdims=True)
    centred = residual - mean_val
    var_val = jnp.mean(centred * centred, axis=-1, keepdims=True)
    return centred * lax.rsqrt(var_val + norm_eps) * gain_vec + shift_vec


def gelu_tanh(values):
    return jax.nn.gelu(values, approximate=True)


def plan_layout(lengths, tok_dev):
    starts = jnp.cumsum(lengths) - lengths
    owner_first = starts // tok_dev
    return (starts, starts, lengths, owner_first)


def to_owners(shard, layout, dev_count, piece_rows):
    starts, owner_start, owner_length, owner_first = layout
    tok_dev = shard.shape[0]
    feat_width = shard.shape[1]
    device = lax.axis_index("dp")
    held_rows = lax.all_to_all(
        shard.reshape(dev_count, piece_rows, feat_width),
        "dp",
        split_axis=0,
        concat_axis=0,
        tiled=True,
    )
    held_rows = held_rows.reshape(dev_count * piece_rows, feat_width)
    slot_ids = jnp.arange(SPAN * piece_rows, dtype=jnp.int32)
    shard_step = slot_ids // piece_rows
    within = slot_ids % piece_rows
    source = owner_first[:, None] + shard_step[None, :]
    global_row = source * tok_dev + device * piece_rows + within[None, :]
    inside = (
        (global_row >= owner_start[:, None])
        & (global_row < (owner_start + owner_length)[:, None])
        & (source < dev_count)
    )
    picked = held_rows[jnp.clip(source, 0, dev_count - 1) * piece_rows + within[None, :]]
    outgoing = jnp.where(inside[:, :, None], picked, jnp.zeros((), picked.dtype))
    arrived = lax.all_to_all(outgoing, "dp", split_axis=0, concat_axis=0, tiled=True)
    arrived = arrived.reshape(dev_count * SPAN * piece_rows, feat_width)
    my_start = owner_start[device]
    my_length = owner_length[device]
    my_first = owner_first[device]
    places = jnp.arange(SEQ_MAX, dtype=jnp.int32)
    global_pos = my_start + places
    shard_of = global_pos // tok_dev
    offset_in = global_pos % tok_dev
    slot_index = (
        offset_in // piece_rows * (SPAN * piece_rows)
        + (shard_of - my_first) * piece_rows
        + offset_in % piece_rows
    )
    valid_rows = places < my_length
    slot_index = jnp.where(valid_rows, slot_index, 0)
    owned = jnp.where(valid_rows[:, None], arrived[slot_index], jnp.zeros((), arrived.dtype))
    return (owned, valid_rows)


def to_order(owned, layout, dev_count, piece_rows, tok_dev):
    starts, owner_start, owner_length, owner_first = layout
    feat_width = owned.shape[1]
    device = lax.axis_index("dp")
    my_start = owner_start[device]
    my_length = owner_length[device]
    my_first = owner_first[device]
    slot_ids = jnp.arange(SPAN * piece_rows, dtype=jnp.int32)
    shard_step = slot_ids // piece_rows
    within = slot_ids % piece_rows
    targets = jnp.arange(dev_count, dtype=jnp.int32)
    global_row = (
        (my_first + shard_step)[None, :] * tok_dev + targets[:, None] * piece_rows + within[None, :]
    )
    place_row = global_row - my_start
    inside = (place_row >= 0) & (place_row < my_length)
    picked = owned[jnp.clip(place_row, 0, owned.shape[0] - 1)]
    outgoing = jnp.where(inside[:, :, None], picked, jnp.zeros((), picked.dtype))
    returned = lax.all_to_all(outgoing, "dp", split_axis=0, concat_axis=0, tiled=True)
    returned = returned.reshape(dev_count * SPAN * piece_rows, feat_width)
    sources = jnp.arange(dev_count, dtype=jnp.int32)
    within_piece = jnp.arange(piece_rows, dtype=jnp.int32)
    row_ids = sources[:, None] * tok_dev + device * piece_rows + within_piece[None, :]
    seq_of = jnp.sum((row_ids[:, :, None] >= starts[None, None, :]).astype(jnp.int32), 2) - 1
    slot_index = (
        seq_of * (SPAN * piece_rows)
        + (sources[:, None] - owner_first[seq_of]) * piece_rows
        + within_piece[None, :]
    )
    pieces = returned[slot_index]
    ordered = lax.all_to_all(pieces, "dp", split_axis=0, concat_axis=0, tiled=True)
    return ordered.reshape(tok_dev, feat_width)


def per_device(
    tokens,
    cotangent,
    lengths,
    wq,
    bq,
    wk,
    wv,
    bv,
    wo,
    bo,
    norm1_gain,
    norm1_bias,
    w1,
    b1,
    w2,
    b2,
    norm2_gain,
    norm2_bias,
):
    f32 = jnp.float32
    bf16 = jnp.bfloat16
    dev_count = lax.axis_size("dp")
    tok_dev = tokens.shape[0]
    feat_width = tokens.shape[1]
    piece_rows = tok_dev // dev_count
    layout = plan_layout(lengths, tok_dev)
    joined, valid_rows = to_owners(
        jnp.concatenate([tokens, cotangent], 1), layout, dev_count, piece_rows
    )
    inputs = joined[:, :feat_width]
    upstream = joined[:, feat_width:].astype(f32)
    slot_count = inputs.shape[0]
    score_scale = HEAD_DIM ** (-0.5)
    full_wq, full_wk, full_wv, full_wo, full_bq, full_bv, full_bo, gain_one, shift_one = (
        lax.all_gather(wq, "dp", axis=0, tiled=True),
        lax.all_gather(wk, "dp", axis=0, tiled=True),
        lax.all_gather(wv, "dp", axis=0, tiled=True),
        lax.all_gather(wo, "dp", axis=0, tiled=True),
        lax.all_gather(bq, "dp", axis=0, tiled=True),
        lax.all_gather(bv, "dp", axis=0, tiled=True),
        lax.all_gather(bo, "dp", axis=0, tiled=True),
        lax.all_gather(norm1_gain, "dp", axis=0, tiled=True),
        lax.all_gather(norm1_bias, "dp", axis=0, tiled=True),
    )
    queries = (
        (jnp.dot(inputs, full_wq, preferred_element_type=f32) + full_bq.astype(f32))
        .astype(bf16)
        .reshape(slot_count, HEADS, HEAD_DIM)
    )
    keys_low = (
        jnp.dot(inputs, full_wk, preferred_element_type=f32)
        .astype(bf16)
        .reshape(slot_count, HEADS, HEAD_DIM)
    )
    values_low = (
        (jnp.dot(inputs, full_wv, preferred_element_type=f32) + full_bv.astype(f32))
        .astype(bf16)
        .reshape(slot_count, HEADS, HEAD_DIM)
    )
    scores = jnp.einsum("qhd,khd->hqk", queries, keys_low, preferred_element_type=f32) * score_scale
    scores = jnp.where(valid_rows[None, None, :], scores, -1e30)
    row_max = jnp.max(scores, -1, keepdims=True)
    row_total = jnp.sum(jnp.exp(scores - row_max), -1, keepdims=True)
    log_total = row_max + jnp.log(row_total)
    attn_probs = jnp.exp(scores - log_total).astype(bf16)
    attended = jnp.einsum("hqk,khd->qhd", attn_probs, values_low, preferred_element_type=f32)
    attended = attended.reshape(slot_count, feat_width).astype(bf16)
    branch = jnp.dot(attended, full_wo, preferred_element_type=f32) + full_bo.astype(f32)
    resid_one = inputs.astype(f32) + branch
    hidden, norm_one_back = jax.vjp(
        layer_norm, resid_one, gain_one.astype(f32), shift_one.astype(f32)
    )
    hidden_low = hidden.astype(bf16)
    full_w1, full_w2, full_b1, full_b2, gain_two, shift_two = (
        lax.all_gather(w1, "dp", axis=0, tiled=True),
        lax.all_gather(w2, "dp", axis=0, tiled=True),
        lax.all_gather(b1, "dp", axis=0, tiled=True),
        lax.all_gather(b2, "dp", axis=0, tiled=True),
        lax.all_gather(norm2_gain, "dp", axis=0, tiled=True),
        lax.all_gather(norm2_bias, "dp", axis=0, tiled=True),
    )
    upward = jnp.dot(hidden_low, full_w1, preferred_element_type=f32) + full_b1.astype(f32)
    activ, gelu_back = jax.vjp(gelu_tanh, upward)
    activ_low = activ.astype(bf16)
    mixed = jnp.dot(activ_low, full_w2, preferred_element_type=f32) + full_b2.astype(f32)
    resid_two = hidden + mixed
    normed, norm_two_back = jax.vjp(
        layer_norm, resid_two, gain_two.astype(f32), shift_two.astype(f32)
    )
    result = jnp.where(valid_rows[:, None], normed, 0.0).astype(bf16)
    output = to_order(result, layout, dev_count, piece_rows, tok_dev)
    back_w1, back_w2 = (
        lax.all_gather(w1, "dp", axis=0, tiled=True),
        lax.all_gather(w2, "dp", axis=0, tiled=True),
    )
    grad_resid_two, grad_gain_two, grad_shift_two = norm_two_back(upstream)
    grad_mixed = grad_resid_two.astype(bf16)
    grad_bias_two = jnp.sum(grad_mixed.astype(f32), 0)
    grad_activ = jnp.einsum("td,fd->tf", grad_mixed, back_w2, preferred_element_type=f32)
    grad_upward = gelu_back(grad_activ)[0].astype(bf16)
    grad_bias_one = jnp.sum(grad_upward.astype(f32), 0)
    grad_hidden = grad_resid_two + jnp.einsum(
        "tf,df->td", grad_upward, back_w1, preferred_element_type=f32
    )
    grad_w2 = jnp.einsum("tf,td->fd", activ_low, grad_mixed, preferred_element_type=f32)
    grad_w1 = jnp.einsum("td,tf->df", hidden_low, grad_upward, preferred_element_type=f32)
    mlp_grads = (
        lax.psum_scatter(grad_w1, "dp", scatter_dimension=0, tiled=True),
        lax.psum_scatter(grad_w2, "dp", scatter_dimension=0, tiled=True),
        lax.psum_scatter(grad_bias_one, "dp", scatter_dimension=0, tiled=True),
        lax.psum_scatter(grad_bias_two, "dp", scatter_dimension=0, tiled=True),
        lax.psum_scatter(grad_gain_two, "dp", scatter_dimension=0, tiled=True),
        lax.psum_scatter(grad_shift_two, "dp", scatter_dimension=0, tiled=True),
    )
    back_wq, back_wk, back_wv, back_wo = (
        lax.all_gather(wq, "dp", axis=0, tiled=True),
        lax.all_gather(wk, "dp", axis=0, tiled=True),
        lax.all_gather(wv, "dp", axis=0, tiled=True),
        lax.all_gather(wo, "dp", axis=0, tiled=True),
    )
    grad_resid_one, grad_gain_one, grad_shift_one = norm_one_back(grad_hidden)
    grad_branch = grad_resid_one.astype(bf16)
    grad_bo = jnp.sum(grad_branch.astype(f32), 0)
    grad_wo = jnp.einsum("tc,td->cd", attended, grad_branch, preferred_element_type=f32)
    grad_attended = jnp.einsum(
        "td,cd->tc", grad_branch, back_wo, preferred_element_type=f32
    ).astype(bf16)
    grad_attended = grad_attended.reshape(slot_count, HEADS, HEAD_DIM)
    re_scores = (
        jnp.einsum("qhd,khd->hqk", queries, keys_low, preferred_element_type=f32) * score_scale
    )
    re_scores = jnp.where(valid_rows[None, None, :], re_scores, -1e30)
    re_probs = jnp.exp(re_scores - log_total)
    re_probs_low = re_probs.astype(bf16)
    grad_values = jnp.einsum(
        "hqk,qhd->khd", re_probs_low, grad_attended, preferred_element_type=f32
    ).astype(bf16)
    grad_probs = jnp.einsum("qhd,khd->hqk", grad_attended, values_low, preferred_element_type=f32)
    grad_scores = re_probs * (grad_probs - jnp.sum(re_probs * grad_probs, -1, keepdims=True))
    grad_scores_low = grad_scores.astype(bf16)
    grad_queries = (
        jnp.einsum("hqk,khd->qhd", grad_scores_low, keys_low, preferred_element_type=f32)
        * score_scale
    ).astype(bf16)
    grad_keys = (
        jnp.einsum("hqk,qhd->khd", grad_scores_low, queries, preferred_element_type=f32)
        * score_scale
    ).astype(bf16)
    grad_queries = grad_queries.reshape(slot_count, feat_width)
    grad_keys = grad_keys.reshape(slot_count, feat_width)
    grad_values = grad_values.reshape(slot_count, feat_width)
    grad_bq = jnp.sum(grad_queries.astype(f32), 0)
    grad_bv = jnp.sum(grad_values.astype(f32), 0)
    grad_wq = jnp.einsum("tc,td->cd", inputs, grad_queries, preferred_element_type=f32)
    grad_wk = jnp.einsum("tc,td->cd", inputs, grad_keys, preferred_element_type=f32)
    grad_wv = jnp.einsum("tc,td->cd", inputs, grad_values, preferred_element_type=f32)
    grad_input = grad_resid_one + jnp.einsum(
        "td,cd->tc", grad_queries, back_wq, preferred_element_type=f32
    )
    grad_input = grad_input + jnp.einsum(
        "td,cd->tc", grad_keys, back_wk, preferred_element_type=f32
    )
    grad_input = grad_input + jnp.einsum(
        "td,cd->tc", grad_values, back_wv, preferred_element_type=f32
    )
    grad_input = jnp.where(valid_rows[:, None], grad_input, 0.0).astype(bf16)
    attn_grads = (
        lax.psum_scatter(grad_wq, "dp", scatter_dimension=0, tiled=True),
        lax.psum_scatter(grad_wk, "dp", scatter_dimension=0, tiled=True),
        lax.psum_scatter(grad_wv, "dp", scatter_dimension=0, tiled=True),
        lax.psum_scatter(grad_wo, "dp", scatter_dimension=0, tiled=True),
        lax.psum_scatter(grad_bq, "dp", scatter_dimension=0, tiled=True),
        lax.psum_scatter(grad_bv, "dp", scatter_dimension=0, tiled=True),
        lax.psum_scatter(grad_bo, "dp", scatter_dimension=0, tiled=True),
        lax.psum_scatter(grad_gain_one, "dp", scatter_dimension=0, tiled=True),
        lax.psum_scatter(grad_shift_one, "dp", scatter_dimension=0, tiled=True),
    )
    sum_w1, sum_w2, sum_b1, sum_b2, sum_g2, sum_s2 = mlp_grads
    sum_wq, sum_wk, sum_wv, sum_wo, sum_bq, sum_bv, sum_bo, sum_g1, sum_s1 = attn_grads
    input_grad = to_order(grad_input, layout, dev_count, piece_rows, tok_dev)
    return (
        output,
        input_grad,
        sum_wq,
        sum_bq,
        sum_wk,
        sum_wv,
        sum_bv,
        sum_wo,
        sum_bo,
        sum_g1,
        sum_s1,
        sum_w1,
        sum_b1,
        sum_w2,
        sum_b2,
        sum_g2,
        sum_s2,
    )


def flip(device, bit):
    step = 1 << bit
    return device + step - 2 * step * ((device // step) % 2)


def chip_bits(device):
    return [(device // 2) % 2, (device // 4) % 2, (device // 8) % 2]


def enter(partners):
    barrier = pltpu.get_barrier_semaphore()
    for partner in partners:
        pl.semaphore_signal(barrier, inc=1, device_id=(partner,), device_id_type=MESH_ID)
    pl.semaphore_wait(barrier, len(partners))


def push(src, dst, send_sem, recv_sem, device):
    return pltpu.make_async_remote_copy(
        src_ref=src,
        dst_ref=dst,
        send_sem=send_sem,
        recv_sem=recv_sem,
        device_id=(device,),
        device_id_type=MESH_ID,
    )


def exchange_blocks(pairs, sems, base, mine, others):
    local_sem, send_sem, recv_sem = sems
    copies = []
    for at, (src, dst) in enumerate(pairs):
        for step, other in enumerate(others):
            copy = push(
                src.at[other - base],
                dst.at[mine],
                send_sem.at[at, step],
                recv_sem.at[at, step],
                other,
            )
            copy.start()
            copies.append(copy)
        local = pltpu.make_async_copy(src.at[mine], dst.at[mine], local_sem.at[at])
        local.start()
        copies.append(local)
    return copies


def exchange_columns(source, to, sems, base, mine, others):
    local_sem, send_sem, recv_sem = sems
    copies = []
    for step, other in enumerate(others):
        copy = push(source(other - base), to, send_sem.at[step], recv_sem.at[step], other)
        copy.start()
        copies.append(copy)
    copy = pltpu.make_async_copy(source(mine), to, local_sem)
    copy.start()
    return copies + [copy]


def far_blocks(src, dst, send_sem, recv_sem, group, mine):
    copies = []
    for step in range(GROUP):
        member = (mine + step) % GROUP
        copy = push(
            src.at[member],
            dst.at[mine],
            send_sem.at[step],
            recv_sem.at[step],
            (1 - group) * GROUP + member,
        )
        copy.start()
        copies.append(copy)
    return copies


def group_places():
    device = lax.axis_index("dp")
    base = device // GROUP * GROUP
    mine = device % GROUP
    others = [base + (mine + step) % GROUP for step in range(1, GROUP)]
    across = (device + GROUP) % (2 * GROUP)
    there = [GROUP - base + (mine + step) % GROUP for step in range(GROUP)]
    return device // GROUP, base, mine, others, across, there


def write_segments(lengths_ref, first, keys_ref, queries_ref):
    f32 = jnp.float32
    rows = queries_ref.shape[1]

    def numbers(ref, ahead):
        ids = first - ahead + lax.broadcasted_iota(jnp.int32, ref.shape, 1)
        total = jnp.zeros(ref.shape, jnp.int32)
        start = jnp.int32(0)
        for at in range(lengths_ref.shape[0]):
            total = total + (ids >= start).astype(jnp.int32)
            start = start + lengths_ref[at]
        return total.astype(f32)

    queries_ref[...] = numbers(queries_ref, 0)
    place = lax.broadcasted_iota(jnp.int32, keys_ref.shape, 1)
    inside = (place >= PAD) & (place < PAD + rows)
    keys_ref[...] = jnp.where(inside, numbers(keys_ref, PAD), -1.0)


def tile_probs(qkv_ref, queries_ref, keys_ref, tile):
    f32 = jnp.float32
    place = pl.multiple_of(tile * TILE, TILE)
    row = pl.multiple_of(PAD + place, 64)
    window = pl.ds(place, WINDOW)
    queries = qkv_ref[pl.ds(row, TILE), 0:HEAD_DIM]
    keys = qkv_ref[window, HEAD_DIM : 2 * HEAD_DIM]
    scores = lax.dot_general(queries, keys, NT, preferred_element_type=f32)
    own = jnp.broadcast_to(queries_ref[0:1, pl.ds(place, TILE)], (TILE, TILE)).T[:, 0:1]
    scores = jnp.where(own == keys_ref[0:1, window], scores * HEAD_DIM ** (-0.5), -1e30)
    weights = jnp.exp(scores - jnp.max(scores, -1, keepdims=True))
    return queries, keys, weights * (1.0 / jnp.sum(weights, -1, keepdims=True))


CHUNKS = 4
TAIL_CHUNKS = 2
THIRDS = (((0, 768), (0, 1, 2)), ((768, 640), (1, 2, 0)), ((1408, 640), (2, 0, 1)))
LIGHT = (
    ((0, 512), (1, 2, 0)), ((512, 512), (0, 2, 1)), ((1024, 512), (1, 0, 2)), ((1536, 512), (0, 1, 2)),
)
PLANS = (THIRDS, LIGHT) + (THIRDS,) * 5
TAIL_PLANS = (LIGHT,)
SPLIT = 256
PAD = (WINDOW - TILE) // 2
REACH = SEQ_MAX
STAGES = 7


def step_through(flows, fillers=None):
    waiting, alive = list(flows), []
    while waiting or alive:
        if waiting:
            alive.append(waiting.pop(0))
        alive = [flow for flow in alive if next(flow, "done") != "done"]
        if fillers is not None:
            next(fillers, None)
    if fillers is not None:
        for _ in fillers:
            pass


class Traffic:
    def __init__(self, sems, plans):
        self.plans = plans
        self.hop_send, self.hop_recv, self.pair_send, self.pair_recv = sems
        device = lax.axis_index("dp")
        self.core = device % 2
        self.bits = chip_bits(device)
        self.partners = [flip(device, 1), flip(device, 2), flip(device, 3)]
        self.pair = flip(device, 0)

    def chips(self, ref, values, columns):
        return ref.at[values[2], values[1], values[0], :, columns]

    def push(self, src, dst, stage, chunk, part, step):
        copy = push(
            src, dst,
            self.hop_send.at[stage, chunk, part, step],
            self.hop_recv.at[stage, chunk, part, step],
            self.partners[self.plans[stage][part][1][step]],
        )
        copy.start()
        return copy

    def share(self, src, dst, stage, chunk):
        copy = push(
            src, dst, self.pair_send.at[stage, chunk], self.pair_recv.at[stage, chunk], self.pair
        )
        copy.start()
        return copy

    def gather(self, slots, stage, chunk):
        mine = slots.at[self.core]
        hops = {}
        for step in range(3):
            for part, ((first, count), order) in enumerate(self.plans[stage]):
                if step:
                    hops[part, step - 1].wait_recv()
                values = list(self.bits)
                for dim in order[:step]:
                    values[dim] = slice(None)
                view = self.chips(mine, values, pl.ds(first, count))
                hops[part, step] = self.push(view, view, stage, chunk, part, step)
            yield
        for part in range(len(self.plans[stage])):
            hops[part, 2].wait_recv()
        share = self.share(mine, mine, stage, chunk)
        for copy in hops.values():
            copy.wait_send()
        return share

    def scatter(self, own, pair_in, incoming, share, stage, chunk, finish):
        rows = own.shape[-2]
        f32 = jnp.float32
        hops = {}
        share.wait()
        for step in range(4):
            for part, ((first, count), order) in enumerate(self.plans[stage]):
                columns = pl.ds(first, count)
                if step:
                    hops[part, step - 1].wait_recv()
                values = list(self.bits)
                free = ()
                if step < 3:
                    values[order[step]] = 1 - self.bits[order[step]]
                    free = order[step + 1 :]
                for mask in range(1 << len(free)):
                    slot = list(values)
                    for place, dim in enumerate(free):
                        slot[dim] = (mask >> place) & 1
                    where = (slot[2], slot[1], slot[0])
                    lefts = [
                        tuple(slot[dim] for dim in (2, 1, 0) if dim not in order[: back + 1])
                        for back in range(step)
                    ]

                    def add(index, carry, step=step, where=where, lefts=lefts, columns=columns):
                        row = pl.multiple_of(index * 16, 16)
                        at = (pl.ds(row, 16), columns)
                        total = own[where + at].astype(f32) + pair_in[where + at].astype(f32)
                        for back in range(step):
                            total = total + incoming[back][lefts[back] + at].astype(f32)
                        if step < 3:
                            own[where + at] = total.astype(own.dtype)
                        else:
                            finish(row, columns, total)
                        return carry

                    lax.fori_loop(0, rows // 16, add, 0)
                if step == 3:
                    continue
                for dim in free:
                    values[dim] = slice(None)
                left = tuple(slice(None) for _ in free)
                hops[part, step] = self.push(
                    self.chips(own, values, columns),
                    incoming[step].at[left + (slice(None), columns)],
                    stage, chunk, part, step,
                )
            if step < 3:
                yield
        for copy in hops.values():
            copy.wait_send()


def gelu_slope(up):
    inner = 0.7978845608028654 * (up + 0.044715 * (up * up * up))
    tanh = jnp.tanh(inner)
    return 0.5 * (1.0 + tanh) + 0.5 * up * (1.0 - tanh * tanh) * (
        0.7978845608028654 * (1.0 + 0.134145 * (up * up))
    )


NT = (((1,), (1,)), ((), ()))
TN = (((0,), (0,)), ((), ()))


def layer_kernel(
    tok_ref, cot_ref, wq_ref, wk_ref, wv_ref, w1_ref, w2_ref, wo_ref, vec_ref, lengths_ref,
    out_ref, dres_ref, vecg_ref, gb1_ref, gw2_own, gw2_far, gw2_in, gw1_ref, gwo_ref,
    x_all, h_all, qkv_ref, dout_ref, wqkv_ref,
    all_h, all_m, own_part, far_part, pair_in, in_one, in_two, in_three,
    up_ref, act_ref, act_t, dup_ref, dup_t, att_ref, att_t, res_ref, hid_ref, norm_ref, scale_ref,
    w1_all, w2_all, wo_all, vec_all, low_ref, high_ref, b1_ref, stage_ref, stage_low, stage_w1,
    queries_ref, keys_ref,
    hop_send, hop_recv, pair_send, pair_recv,
    block_local, block_send, block_recv, vec_send, vec_recv, far_send, far_recv,
    local_sems, out_sems, spill_sems,
):
    f32, low = jnp.float32, tok_ref.dtype
    block, width = tok_ref.shape
    rows = block // CHUNKS
    half_rows = rows * GROUP // 2
    own_rows = GROUP * block
    units = w1_all.shape[-1]
    group, base, mine, others, across, there = group_places()
    net = Traffic((hop_send, hop_recv, pair_send, pair_recv), PLANS)
    core, bits = net.core, net.bits
    chip = mine // 2
    head = core * 8 + chip
    own_slot = (core, bits[2], bits[1], bits[0])
    ext = PAD + group * HALO
    enter(others + there)

    def far(src, dst, at, device=across):
        copy = push(src, dst, far_send.at[at], far_recv.at[at], device)
        copy.start()
        return copy

    def local(src, dst, at):
        copy = pltpu.make_async_copy(src, dst, local_sems.at[at])
        copy.start()
        return copy

    early = w2_ref.shape[0] // 4 * 3
    far_vec = far(vec_ref, vec_all.at[group, mine], 0)
    near = [
        local(vec_ref, vec_all.at[group, mine], 0),
        local(w2_ref, w2_all.at[group], 1),
        local(wo_ref, wo_all.at[group, core], 2),
    ]
    w2_first, w2_last = pl.ds(0, early), pl.ds(early, w2_ref.shape[0] - early)
    far_w2 = [far(w2_ref.at[w2_first, :], w2_all.at[group, w2_first, :], 1)]

    def block_sems(at):
        return block_local.at[at], block_send.at[at], block_recv.at[at]

    qkv_blocks = []
    for part, ref in enumerate((wq_ref, wk_ref, wv_ref)):

        def head_columns(member, ref=ref):
            first = pl.multiple_of((member % 2 * 8 + member // 2) * HEAD_DIM, HEAD_DIM)
            return ref.at[:, pl.ds(first, HEAD_DIM)]

        qkv_blocks += exchange_columns(
            head_columns, wqkv_ref.at[group, mine, :, pl.ds(part * HEAD_DIM, HEAD_DIM)],
            block_sems(part), base, mine, others,
        )
    for chunk in range(CHUNKS):
        all_m[(chunk,) + own_slot] = tok_ref[chunk * rows : (chunk + 1) * rows, :]
    wo_near = push(
        wo_ref, wo_all.at[group, core], far_send.at[2], far_recv.at[2], net.pair
    )
    wo_near.start()

    unsent = own_rows + REACH - group * (own_rows + REACH)
    for first in (0, qkv_ref.shape[0] - PAD):
        qkv_ref[first : first + PAD, :] = jnp.zeros((PAD, qkv_ref.shape[1]), low)
    qkv_ref[pl.ds(pl.multiple_of(PAD + unsent, 32), HALO - REACH), :] = jnp.zeros(
        (HALO - REACH, qkv_ref.shape[1]), low
    )
    dout_ref[pl.ds(pl.multiple_of(unsent, 32), HALO - REACH), :] = jnp.zeros(
        (HALO - REACH, HEAD_DIM), low
    )
    vecg_ref[...] = jnp.zeros_like(vecg_ref)
    gb1_ref[...] = jnp.zeros_like(gb1_ref)

    write_segments(lengths_ref, group * (own_rows - HALO), keys_ref, queries_ref)

    def row_at(chunk, side):
        return pl.multiple_of((chunk * 2 + side) * half_rows, half_rows)

    def flat(ref, chunk, side, columns=slice(None)):
        return ref[chunk, side, :, :, :, :, columns].reshape(half_rows, -1)

    def tiles(count, body):
        def step(at, carry):
            body(at, pl.ds(pl.multiple_of(at * SPLIT, SPLIT), SPLIT))
            return carry

        lax.fori_loop(0, count // SPLIT, step, 0)

    def pieces(chunk, side):
        return [
            pl.multiple_of((slot * 2 + side) * block + chunk * rows, rows)
            for slot in range(GROUP // 2)
        ]

    def project_half(chunk, side, which):
        columns = pl.ds(pl.multiple_of(which * (width // 2), width // 2), width // 2)
        weight = wqkv_ref[which].reshape(width // 2, -1)
        return jnp.dot(flat(all_m, chunk, side, columns), weight, preferred_element_type=f32)

    def spill(src, dst, chunk, at):
        copy = pltpu.make_async_copy(src.at[chunk], dst.at[chunk], spill_sems.at[at, chunk])
        copy.start()
        return copy

    wide = slice(0, 3 * HEAD_DIM)
    spills = {}

    def token_flow(chunk):
        share = yield from net.gather(all_m.at[chunk], 0, chunk)
        up_ref[pl.ds(row_at(chunk, core), half_rows), wide] = project_half(chunk, core, group)
        yield
        share.wait()
        up_ref[pl.ds(row_at(chunk, 1 - core), half_rows), wide] = project_half(
            chunk, 1 - core, group
        )
        spills[0, chunk] = spill(all_m, x_all, chunk, 0)

    def weight_flow():
        yield
        for copy in qkv_blocks:
            copy.wait()
        state["far_qkv"] = far(wqkv_ref.at[group], wqkv_ref.at[group], 3)
        yield
        for copy in near:
            copy.wait()
        far_vec.wait()
        both = vec_all.at[:, mine]
        state["vec"] = []
        for step, other in enumerate(others):
            copy = push(both, both, vec_send.at[step], vec_recv.at[step], other)
            copy.start()
            state["vec"].append(copy)
        yield

    state = {"backs": 0}
    flows = [token_flow(chunk) for chunk in range(CHUNKS)]
    step_through([flows[0], weight_flow()] + flows[1:])

    for copy in state["vec"]:
        copy.wait()
    lane = lax.broadcasted_iota(jnp.int32, (8, 128), 1)
    for at in range(GROUP):
        first = vec_all[at // 8, at % 8 * 2]
        second = vec_all[at // 8, at % 8 * 2 + 1]
        here = slice(at * 128, at * 128 + 128)
        low_ref[:, here] = jnp.where(lane < 64, first, pltpu.roll(second, 64, 1))
        high_ref[:, here] = jnp.where(lane < 64, pltpu.roll(first, 64, 1), second)
    for half in range(2):
        for part in range(2):
            b1_ref[0:1, half * 256 + part * 128 : half * 256 + part * 128 + 128] = vec_all[
                half, mine, 4 + part : 5 + part, :
            ]
    head_at = pl.ds(pl.multiple_of(head * HEAD_DIM, HEAD_DIM), HEAD_DIM)
    bias_q, bias_v = low_ref[0:1, head_at], high_ref[0:1, head_at]
    bias_qkv = jnp.concatenate([bias_q, jnp.zeros_like(bias_q), bias_v], 1)
    bo, shift_one, gain_two = low_ref[1:2, :], low_ref[2:3, :], low_ref[3:4, :]
    gain_one, b2, shift_two = high_ref[1:2, :], high_ref[2:3, :], high_ref[3:4, :]

    state["far_qkv"].wait()
    for chunk in range(CHUNKS):
        for side in range(2):
            here = pl.ds((chunk * 2 + side) * half_rows, half_rows)
            total = up_ref[here, wide] + project_half(chunk, side, 1 - group) + bias_qkv
            total = total.astype(low)
            for slot, place in enumerate(pieces(chunk, side)):
                qkv_ref[pl.ds(pl.multiple_of(ext + place, rows), rows), :] = total[
                    slot * rows : (slot + 1) * rows
                ]
    near_edge = own_rows - REACH - group * (own_rows - REACH - HALO)
    far_edge = HALO - REACH + group * (own_rows - HALO + REACH)
    halo_src = pl.ds(pl.multiple_of(PAD + near_edge, 32), REACH)
    halo_dst = pl.ds(pl.multiple_of(PAD + far_edge, 32), REACH)
    key_value = pl.ds(HEAD_DIM, 2 * HEAD_DIM)
    far_halo = far(qkv_ref.at[halo_src, key_value], qkv_ref.at[halo_dst, key_value], 6)
    far_wo_to = (1 - group) * GROUP + 2 * chip + group
    far_wo = push(
        wo_ref, wo_all.at[group, core], far_send.at[4 + core], far_recv.at[4 + core], far_wo_to
    )
    far_wo.start()
    far_w2.append(far(w2_ref.at[w2_last, :], w2_all.at[group, w2_last, :], 8))
    w1_blocks = []
    for part in range(2):

        def w1_columns(member, part=part):
            first = pl.multiple_of((part * GROUP + member) * SPLIT, SPLIT)
            return w1_ref.at[:, pl.ds(first, SPLIT)]

        w1_blocks += exchange_columns(
            w1_columns, w1_all.at[group, mine, :, pl.ds(part * SPLIT, SPLIT)],
            block_sems(3 + part), base, mine, others,
        )

    def attend_tile(at):
        tile = at + group * (GROUP - 1 - 2 * at)
        inner = group * (HALO // TILE) + tile
        _, _, probs = tile_probs(qkv_ref, queries_ref, keys_ref, inner)
        window = pl.ds(pl.multiple_of(inner * TILE, TILE), WINDOW)
        values = qkv_ref[window, 2 * HEAD_DIM : 3 * HEAD_DIM]
        out = jnp.dot(probs.astype(low), values, preferred_element_type=f32)
        att_ref[pl.ds(pl.multiple_of(tile * TILE, TILE), TILE), :] = out.astype(low)

    def attend_two(at, carry):
        attend_tile(2 * at)
        attend_tile(2 * at + 1)
        return carry

    lax.fori_loop(0, own_rows // TILE // 2 - 1, attend_two, 0)
    far_halo.wait()
    for copy in w1_blocks:
        copy.wait()
    far_w1 = far(w1_all.at[group], w1_all.at[group], 7)
    attend_tile(own_rows // TILE - 2)
    attend_tile(own_rows // TILE - 1)
    for chunk in range(CHUNKS):
        spills[0, chunk].wait()
    wo_near.wait()
    far_wo.wait_send()

    @pl.when(core != group)
    def _():
        for at in range(2):
            push(
                wo_ref, wo_all.at[1 - group, at], far_send.at[4 + at], far_recv.at[4 + at],
                far_wo_to,
            ).wait_recv()

    def branch_part(chunk, side, dst):
        rows_in = jnp.concatenate([att_ref[pl.ds(at, rows), :] for at in pieces(chunk, side)], 0)
        att_t[:, pl.ds(row_at(chunk, side), half_rows)] = rows_in.astype(f32).T.astype(low)

        def body(at, columns):
            weight = wo_all[core, :, :, columns].reshape(HEAD_DIM, SPLIT)
            part = jnp.dot(rows_in, weight, preferred_element_type=f32)
            dst[:, :, :, :, columns] = part.astype(low).reshape(2, 2, 2, rows, SPLIT)

        tiles(width, body)

    def upward(chunk, side):
        here = pl.ds(row_at(chunk, side), half_rows)

        def body(at, columns):
            weight = w1_all[:, :, :, columns].reshape(width, SPLIT)
            up = jnp.dot(flat(all_h, chunk, side), weight, preferred_element_type=f32)
            up = up + b1_ref[0:1, columns]
            up_ref[here, columns] = up
            act = gelu_tanh(up)
            act_ref[:, columns] = act.astype(low)
            act_t[columns, here] = act.T.astype(low)

        tiles(units, body)

    def downward(dst):
        def body(at, columns):
            weight = w2_all[:, :, columns].reshape(units, SPLIT)
            part = jnp.dot(act_ref[...], weight, preferred_element_type=f32)
            dst[:, :, :, :, columns] = part.astype(low).reshape(2, 2, 2, rows, SPLIT)

        tiles(width, body)

    def up_back(chunk, side):
        here = pl.ds(row_at(chunk, side), half_rows)

        def body(at, columns):
            grad = lax.dot_general(
                flat(all_m, chunk, side), w2_all[at], NT, preferred_element_type=f32
            )
            grad = (grad * gelu_slope(up_ref[here, columns])).astype(low)
            dup_ref[:, columns] = grad
            grad = grad.astype(f32)
            gb1_ref[0:1, columns] += jnp.sum(grad, 0, keepdims=True)
            dup_t[columns, here] = grad.T.astype(low)

        tiles(units, body)

    def down_back(dst):
        def body(at, columns):
            weight = w1_all[at // 4, pl.ds(at % 4 * 4, 4)].reshape(SPLIT, units)
            part = lax.dot_general(dup_ref[...], weight, NT, preferred_element_type=f32)
            dst[:, :, :, :, columns] = part.astype(low).reshape(2, 2, 2, rows, SPLIT)

        tiles(width, body)

    def out_back(chunk, side):
        weight = wo_all[core].reshape(HEAD_DIM, width)
        grad = lax.dot_general(flat(all_h, chunk, side), weight, NT, preferred_element_type=f32)
        grad = grad.astype(low)
        for slot, place in enumerate(pieces(chunk, side)):
            dout_ref[pl.ds(pl.multiple_of(group * HALO + place, rows), rows), :] = grad[
                slot * rows : (slot + 1) * rows
            ]

    def keep(chunk):
        def finish(row, columns, total):
            res_ref[pl.ds(pl.multiple_of(chunk * rows + row, 16), 16), columns] = total

        return finish

    def row_sets(chunk, body):
        def step(index, carry):
            row = pl.multiple_of(index * 16, 16)
            body(pl.ds(pl.multiple_of(chunk * rows + row, 16), 16), pl.ds(row, 16))
            return carry

        lax.fori_loop(0, rows // 16, step, 0)

    def normal(res):
        res = res - jnp.mean(res, -1, keepdims=True)
        scale = lax.rsqrt(jnp.mean(res * res, -1, keepdims=True) + norm_eps)
        return res * scale, scale

    def normal_back(grad, res, gain, scale, at):
        vecg_ref[at + 2 : at + 3, :] += jnp.sum(grad, 0, keepdims=True)
        vecg_ref[at + 1 : at + 2, :] += jnp.sum(grad * res, 0, keepdims=True)
        grad = grad * gain
        first = jnp.mean(grad, -1, keepdims=True)
        second = jnp.mean(grad * res, -1, keepdims=True)
        grad = (grad - first - res * second) * scale
        grad_low = grad.astype(low)
        vecg_ref[at : at + 1, :] += jnp.sum(grad_low.astype(f32), 0, keepdims=True)
        return grad, grad_low

    def norm_one(chunk):
        def body(at, place):
            res, scale = normal(tok_ref[at, :].astype(f32) + res_ref[at, :] + bo)
            norm_ref[at, :] = res
            scale_ref[at, :] = jnp.broadcast_to(scale, (16, 128))
            hidden = res * gain_one + shift_one
            hid_ref[at, :] = hidden
            all_h[(chunk,) + own_slot + (place, slice(None))] = hidden.astype(low)

        row_sets(chunk, body)

    def norm_two(chunk):
        def body(at, place):
            res, scale = normal(hid_ref[at, :] + res_ref[at, :] + b2)
            out_ref[at, :] = (res * gain_two + shift_two).astype(low)
            grad, grad_low = normal_back(cot_ref[at, :].astype(f32), res, gain_two, scale, 0)
            dres_ref[at, :] = grad
            all_m[(chunk,) + own_slot + (place, slice(None))] = grad_low

        row_sets(chunk, body)

    def norm_one_back(chunk):
        def body(at, place):
            grad, grad_low = normal_back(
                dres_ref[at, :] + res_ref[at, :], norm_ref[at, :], gain_one,
                scale_ref[at, 0:1], 3,
            )
            dres_ref[at, :] = grad
            all_h[(chunk,) + own_slot + (place, slice(None))] = grad_low

        row_sets(chunk, body)

    def flow(chunk):
        incoming = (in_one.at[chunk], in_two.at[chunk], in_three.at[chunk])
        own, other = own_part.at[chunk], far_part.at[chunk % 2]
        arrived = pair_in.at[chunk]
        branch_part(chunk, 1 - core, other)
        share = net.share(other, arrived, 1, chunk)
        branch_part(chunk, core, own)
        yield
        yield from net.scatter(own, arrived, incoming, share, 1, chunk, keep(chunk))
        norm_one(chunk)
        share = yield from net.gather(all_h.at[chunk], 2, chunk)
        if chunk == 0:
            far_w1.wait()
        upward(chunk, core)
        if chunk == 0:
            for copy in far_w2:
                copy.wait()
        downward(own)
        yield
        share.wait()
        spills[1, chunk] = spill(all_h, h_all, chunk, 1)
        upward(chunk, 1 - core)
        downward(other)
        share = net.share(other, arrived, 3, chunk)
        yield
        yield from net.scatter(own, arrived, incoming, share, 3, chunk, keep(chunk))
        norm_two(chunk)
        spills[1, chunk].wait()
        share = yield from net.gather(all_m.at[chunk], 4, chunk)
        up_back(chunk, core)
        down_back(own)
        yield
        share.wait()
        up_back(chunk, 1 - core)
        down_back(other)
        share = net.share(other, arrived, 5, chunk)
        state["backs"] += 1
        yield
        yield from net.scatter(own, arrived, incoming, share, 5, chunk, keep(chunk))
        norm_one_back(chunk)
        share = yield from net.gather(all_h.at[chunk], 6, chunk)
        out_back(chunk, core)
        yield
        share.wait()
        out_back(chunk, 1 - core)

    def product(left_t, right, columns):
        total = None
        for chunk in range(CHUNKS):
            for side in range(2):
                here = slice((chunk * 2 + side) * half_rows, (chunk * 2 + side + 1) * half_rows)
                term = jnp.dot(
                    left_t[:, here], flat(right, chunk, side, columns), preferred_element_type=f32
                )
                total = term if total is None else total + term
        return total

    def run(first, last, write):
        def step(at, carry):
            write(at, at % 2, at >= 2)
            return carry

        lax.fori_loop(first, last, step, 0)

    def emit(src, dst, sem, again):
        copy = pltpu.make_async_copy(src, dst, sem)

        @pl.when(again)
        def _():
            copy.wait()

        return copy

    def columns_at(at):
        return pl.ds(pl.multiple_of(at * SPLIT, SPLIT), SPLIT)

    def write_w2(at, slot, again):
        own = emit(stage_ref.at[slot], gw2_own.at[:, columns_at(at)], out_sems.at[0, slot], again)
        there = emit(stage_low.at[slot], gw2_far.at[:, columns_at(at)], out_sems.at[1, slot], again)
        total = product(act_t, all_m, columns_at(at))
        first = group == 0
        stage_ref[slot] = jnp.where(first, total[:256], total[256:])
        stage_low[slot] = jnp.where(first, total[256:], total[:256]).astype(low)
        own.start()
        there.start()

    def write_w1(first):
        def write(at, slot, again):
            tile = first + at
            here = gw1_ref.at[pl.ds(pl.multiple_of(tile * 4, 4), 4)]
            copy = emit(stage_w1.at[slot], here, out_sems.at[2, slot], again)
            total = product(dup_t, all_m, columns_at(tile)).T.astype(low)
            stage_w1[slot] = total.reshape(4, SPLIT // 4, units)
            copy.start()

        return write

    def write_wo(at, slot, again):
        own = emit(stage_ref.at[slot, 0:HEAD_DIM, :], gwo_ref.at[:, columns_at(at)], out_sems.at[4, slot], again)
        stage_ref[slot, 0:HEAD_DIM, :] = product(att_t, all_h, columns_at(at))
        own.start()

    def fill():
        while state["backs"] < CHUNKS:
            yield
        run(0, width // SPLIT // 2, write_w2)
        yield
        run(width // SPLIT // 2, width // SPLIT, write_w2)
        for slot in range(2):
            emit(stage_ref.at[slot], gw2_own.at[:, columns_at(0)], out_sems.at[0, slot], True)
            emit(stage_low.at[slot], gw2_far.at[:, columns_at(0)], out_sems.at[1, slot], True)
        swaps.append(far(gw2_far, gw2_in, 10))
        back = [pltpu.make_async_copy(h_all.at[at], all_m.at[at], spill_sems.at[2, at]) for at in range(CHUNKS)]
        for copy in back:
            copy.start()
        yield
        for copy in back:
            copy.wait()
        run(0, width // SPLIT // 2, write_w1((1 - group) * 4))
        for slot in range(2):
            emit(stage_w1.at[slot], gw1_ref.at[pl.ds(0, 4)], out_sems.at[2, slot], True)
        yield
        run(0, width // SPLIT // 2, write_w1(group * 4))
        for slot in range(2):
            emit(stage_w1.at[slot], gw1_ref.at[pl.ds(0, 4)], out_sems.at[2, slot], True)

    swaps = []
    step_through([flow(chunk) for chunk in range(CHUNKS)], fill())
    query = pl.ds(0, HEAD_DIM)
    far_query = far(qkv_ref.at[halo_src, query], qkv_ref.at[halo_dst, query], 12)
    dout_src = pl.ds(pl.multiple_of(near_edge, 32), REACH)
    dout_dst = pl.ds(pl.multiple_of(far_edge, 32), REACH)
    far_dout = far(dout_ref.at[dout_src, :], dout_ref.at[dout_dst, :], 9)
    run(0, width // SPLIT, write_wo)
    for slot in range(2):
        emit(stage_ref.at[slot, 0:HEAD_DIM, :], gwo_ref.at[:, columns_at(0)], out_sems.at[4, slot], True)
    far_dout.wait()
    far_query.wait()
    for copy in swaps:
        copy.wait()


def layer(tokens, cotangent, wq, wk, wv, w1, w2, wo, vector, lengths):
    f32, bf16 = jnp.float32, jnp.bfloat16
    block, width = tokens.shape
    rows = block // CHUNKS
    unit_rows = w2.shape[0]
    units = 2 * unit_rows
    half_rows = rows * GROUP // 2
    own_rows = GROUP * block
    weight_rows = wo.shape[0]
    peers = GROUP - 1
    vmem = pl.BlockSpec(memory_space=pltpu.VMEM)
    anywhere = pl.BlockSpec(memory_space=pl.ANY)
    smem = pl.BlockSpec(memory_space=pltpu.SMEM)
    sems = pltpu.SemaphoreType.DMA
    shape = jax.ShapeDtypeStruct

    def slots(*lead):
        return pltpu.VMEM(lead + (rows, width), bf16)

    return pl.pallas_call(
        layer_kernel,
        out_shape=[
            shape((block, width), bf16),
            shape((block, width), f32),
            shape((8, width), f32),
            shape((8, units), f32),
            shape((unit_rows, width), f32),
            shape((unit_rows, width), bf16),
            shape((unit_rows, width), bf16),
            shape((2 * GROUP, weight_rows, units), bf16),
            shape((HEAD_DIM, width), f32),
            shape((CHUNKS, 2, 2, 2, 2, rows, width), bf16),
            shape((CHUNKS, 2, 2, 2, 2, rows, width), bf16),
            shape((own_rows + HALO + 2 * PAD, 3 * HEAD_DIM), bf16),
            shape((own_rows + HALO, HEAD_DIM), bf16),
            shape((2, GROUP, weight_rows, 3 * HEAD_DIM), bf16),
        ],
        in_specs=[vmem] * 2 + [anywhere] * 6 + [vmem, smem],
        out_specs=[vmem] * 4 + [anywhere] * 7 + [vmem] * 3,
        scratch_shapes=[
            slots(CHUNKS, 2, 2, 2, 2), slots(CHUNKS, 2, 2, 2, 2),
            slots(CHUNKS, 2, 2, 2), slots(2, 2, 2, 2), slots(CHUNKS, 2, 2, 2),
            slots(CHUNKS, 2, 2), slots(CHUNKS, 2), slots(CHUNKS),
            pltpu.VMEM((own_rows, units), f32),
            pltpu.VMEM((half_rows, units), bf16),
            pltpu.VMEM((units, own_rows), bf16),
            pltpu.VMEM((half_rows, units), bf16),
            pltpu.VMEM((units, own_rows), bf16),
            pltpu.VMEM((own_rows, HEAD_DIM), bf16),
            pltpu.VMEM((HEAD_DIM, own_rows), bf16),
            pltpu.VMEM((block, width), f32),
            pltpu.VMEM((block, width), f32),
            pltpu.VMEM((block, width), f32),
            pltpu.VMEM((block, 128), f32),
            pltpu.VMEM((2, GROUP, weight_rows, units), bf16),
            pltpu.VMEM((2, unit_rows, width), bf16),
            pltpu.VMEM((2, 2, weight_rows, width), bf16),
            pltpu.VMEM((2, GROUP, 8, 128), f32),
            pltpu.VMEM((8, width), f32),
            pltpu.VMEM((8, width), f32),
            pltpu.VMEM((8, units), f32),
            pltpu.VMEM((2, SPLIT, SPLIT), f32),
            pltpu.VMEM((2, SPLIT, SPLIT), bf16),
            pltpu.VMEM((2, 4, SPLIT // 4, units), bf16),
            pltpu.VMEM((1, own_rows + HALO), f32),
            pltpu.VMEM((1, own_rows + HALO + 2 * PAD), f32),
            sems((STAGES, CHUNKS, 4, 3)), sems((STAGES, CHUNKS, 4, 3)),
            sems((STAGES, CHUNKS)), sems((STAGES, CHUNKS)),
            sems((5,)), sems((5, peers)), sems((5, peers)),
            sems((peers,)), sems((peers,)),
            sems((13,)), sems((13,)), sems((3,)), sems((5, 2)), sems((3, CHUNKS)),
        ],
        compiler_params=pltpu.CompilerParams(
            collective_id=4, has_side_effects=True, vmem_limit_bytes=63 << 20
        ),
        name="layer",
    )(tokens, cotangent, wq, wk, wv, w1, w2, wo, vector, lengths)


def tail_kernel(
    qkv_ref, dout_ref, wqkv_ref, dres_ref, gwo_ref, vecg_ref, gb1_ref, lengths_ref,
    x_all, gw1_ref, w2_own, w2_early,
    input_ref, out_q, out_k, out_v, out_wo, out_w1, out_w2, vec_ref,
    xs_ref, own_part, far_part, pair_in, in_one, in_two, in_three, res_ref,
    dqkv_ref, dk_sum, dv_sum, dqkv_t, gq_own, gq_far, gq_here, gq_there,
    w1_here, w1_there, w2_sum, w2_in, wo_low, wo_in, wo_pair, wo_pair_in,
    blocks_ref, arrived, theirs, far_vec_in,
    queries_ref, keys_ref,
    hop_send, hop_recv, pair_send, pair_recv, load_sems,
    block_local, block_send, block_recv, there_send, there_recv, far_send, far_recv,
):
    f32, low = jnp.float32, qkv_ref.dtype
    block, width = dres_ref.shape
    rows = block // TAIL_CHUNKS
    weight_rows = out_q.shape[0]
    scale = HEAD_DIM ** (-0.5)
    group, base, mine, others, across, there = group_places()
    net = Traffic((hop_send, hop_recv, pair_send, pair_recv), TAIL_PLANS)
    core, chip = net.core, mine // 2
    enter(others + there)

    def far(src, dst, at, device=across):
        copy = push(src, dst, far_send.at[at], far_recv.at[at], device)
        copy.start()
        return copy

    def load(src, dst, at):
        copy = pltpu.make_async_copy(src, dst, load_sems.at[at])
        copy.start()
        return copy

    far_wo = push(
        wo_low, wo_in, far_send.at[0], far_recv.at[0], core * GROUP + 2 * chip + core
    )

    @pl.when(core != group)
    def _():
        wo_low[...] = gwo_ref[...].astype(low)
        far_wo.start()

    def blocks(pairs, at):
        here = slice(at, at + len(pairs))
        return exchange_blocks(
            pairs, (block_local.at[here], block_send.at[here], block_recv.at[here]),
            base, mine, others,
        )

    first = pl.ds(pl.multiple_of((1 - group) * GROUP, GROUP), GROUP)
    w1_far = far_blocks(
        gw1_ref.at[first], w1_there, there_send.at[0], there_recv.at[0], group, mine
    )
    x_loads = [load(x_all.at[at], xs_ref.at[at], at) for at in range(CHUNKS)]
    loads = [
        load(w2_own, w2_sum, CHUNKS),
        load(w2_early, w2_in, CHUNKS + 1),
    ]
    own_rows = GROUP * block
    write_segments(lengths_ref, group * (own_rows - HALO), keys_ref, queries_ref)
    dk_sum[...] = jnp.zeros_like(dk_sum)
    dv_sum[...] = jnp.zeros_like(dv_sum)

    def attend_back_tile(tile):
        place = pl.multiple_of(tile * TILE, TILE)
        window = pl.ds(place, WINDOW)
        queries, keys, probs = tile_probs(qkv_ref, queries_ref, keys_ref, tile)
        values = qkv_ref[window, 2 * HEAD_DIM : 3 * HEAD_DIM]
        grads = dout_ref[pl.ds(place, TILE), :]
        grad_probs = lax.dot_general(grads, values, NT, preferred_element_type=f32)
        inner = jnp.sum(probs * grad_probs, -1, keepdims=True)
        grad_scores = (probs * (grad_probs - inner)).astype(low)
        grad_q = jnp.dot(grad_scores, keys, preferred_element_type=f32)
        dqkv_ref[pl.ds(place, TILE), 0:HEAD_DIM] = (grad_q * scale).astype(low)
        dk_sum[window, :] += lax.dot_general(grad_scores, queries, TN, preferred_element_type=f32)
        dv_sum[window, :] += lax.dot_general(
            probs.astype(low), grads, TN, preferred_element_type=f32
        )

    def attend_back_two(at, carry):
        attend_back_tile(2 * at)
        attend_back_tile(2 * at + 1)
        return carry

    ext_rows = dout_ref.shape[0]
    lax.fori_loop(0, ext_rows // TILE // 2, attend_back_two, 0)
    inside = slice(PAD, PAD + ext_rows)
    dqkv_ref[:, HEAD_DIM : 2 * HEAD_DIM] = (dk_sum[inside, :] * scale).astype(low)
    dqkv_ref[:, 2 * HEAD_DIM : 3 * HEAD_DIM] = dv_sum[inside, :].astype(low)

    def rows_of(chunk, side, rows):
        places = [
            group * HALO + (slot * 2 + side) * block + chunk * rows for slot in range(GROUP // 2)
        ]
        return jnp.concatenate(
            [dqkv_ref[pl.ds(pl.multiple_of(place, rows), rows), :] for place in places], 0
        )

    x_rows = block // CHUNKS
    x_half = x_rows * GROUP // 2
    bias = jnp.zeros((1, 3 * HEAD_DIM), f32)
    for chunk in range(CHUNKS):
        for side in range(2):
            part = rows_of(chunk, side, x_rows).astype(f32)
            bias = bias + jnp.sum(part, 0, keepdims=True)
            here = slice((chunk * 2 + side) * x_half, (chunk * 2 + side + 1) * x_half)
            dqkv_t[:, here] = part.T.astype(low)

    for copy in x_loads:
        copy.wait()

    def product(at):
        columns = pl.ds(pl.multiple_of(at * SPLIT, SPLIT), SPLIT)
        total = None
        for chunk in range(CHUNKS):
            for side in range(2):
                here = slice((chunk * 2 + side) * x_half, (chunk * 2 + side + 1) * x_half)
                right = xs_ref[chunk, side, :, :, :, :, columns].reshape(x_half, SPLIT)
                term = jnp.dot(dqkv_t[:, here], right, preferred_element_type=f32)
                total = term if total is None else total + term
        return total.T

    quarter = width // SPLIT // 2

    def tile_of(ref, first):
        def body(at, carry):
            total = product(first + at).astype(low)
            ref[pl.ds(pl.multiple_of(at * 4, 4), 4)] = total.reshape(4, SPLIT // 4, 3 * HEAD_DIM)
            return carry

        lax.fori_loop(0, quarter, body, 0)

    tile_of(gq_far, (1 - group) * quarter)
    qkv_far = far_blocks(gq_far, gq_there, there_send.at[1], there_recv.at[1], group, mine)

    blocks_ref[...] = jnp.zeros_like(blocks_ref)
    lane = lax.broadcasted_iota(jnp.int32, (1, 128), 1)

    def pieces_of(low_row, high_row):
        return (
            jnp.where(lane < 64, low_row, pltpu.roll(high_row, 64, 1)),
            jnp.where(lane < 64, pltpu.roll(low_row, 64, 1), high_row),
        )

    for tile in range(GROUP):
        here = slice(tile * 128, tile * 128 + 128)
        for at, (low_row, high_row) in enumerate(((3, 4), (5, 0), (1, 2))):
            to = tile // 8 * 8 + 1 + at
            both = pieces_of(vecg_ref[low_row : low_row + 1, here], vecg_ref[high_row : high_row + 1, here])
            for odd in range(2):
                blocks_ref[tile % 8 * 2 + odd, to : to + 1, :] = both[odd]
    for half in range(2):
        for part in range(2):
            to = half * 8 + 4 + part
            here = slice((half * 2 + part) * 128, (half * 2 + part + 1) * 128)
            blocks_ref[mine, to : to + 1, :] = gb1_ref[0:1, here]
    bias_q, bias_v = bias[:, 0:HEAD_DIM], bias[:, 2 * HEAD_DIM : 3 * HEAD_DIM]
    both = pieces_of(bias_q, bias_v)
    for odd in range(2):
        blocks_ref[2 * chip + odd, pl.ds(core * 8, 1), :] = both[odd]

    vec_blocks = blocks([(blocks_ref, arrived)], 0)

    def input_part(chunk, side, dst):
        left = rows_of(chunk, side, rows)

        def body(at, carry):
            weight = wqkv_ref[at // 4, pl.ds(at % 4 * 4, 4)].reshape(SPLIT, 3 * HEAD_DIM)
            part = lax.dot_general(left, weight, NT, preferred_element_type=f32)
            columns = pl.ds(pl.multiple_of(at * SPLIT, SPLIT), SPLIT)
            dst[:, :, :, :, columns] = part.astype(low).reshape(2, 2, 2, rows, SPLIT)
            return carry

        lax.fori_loop(0, width // SPLIT, body, 0)

    def flow(chunk):
        def finish(row, columns, total):
            res_ref[pl.ds(pl.multiple_of(chunk * rows + row, 16), 16), columns] = total

        incoming = (in_one.at[chunk], in_two.at[chunk], in_three.at[chunk])
        other = far_part.at[chunk % 2]
        input_part(chunk, 1 - core, other)
        share = net.share(other, pair_in.at[chunk], 0, chunk)
        input_part(chunk, core, own_part.at[chunk])
        yield
        yield from net.scatter(
            own_part.at[chunk], pair_in.at[chunk], incoming, share, 0, chunk, finish
        )
        here = slice(chunk * rows, (chunk + 1) * rows)
        input_ref[here, :] = (dres_ref[here, :] + res_ref[here, :]).astype(low)

    def fill():
        yield
        yield
        for copy in loads:
            copy.wait()
        out_w2[...] = w2_sum[...] + w2_in[...].astype(f32)
        yield
        tile_of(gq_own, group * quarter)
        state["qkv"] = blocks([(gq_own, gq_here)], 2)
        yield
        for copy in vec_blocks:
            copy.wait()
        total = arrived[0]
        for at in range(1, GROUP):
            total = total + arrived[at]
        first, second = total[:8], total[8:]
        theirs[...] = jnp.where(group == 0, second, first)
        vec_ref[...] = jnp.where(group == 0, first, second)
        state["vec"] = far(theirs, far_vec_in, 3)

    state = {}
    step_through([flow(chunk) for chunk in range(TAIL_CHUNKS)], fill())

    share_wo = push(wo_pair, wo_pair_in, far_send.at[4], far_recv.at[4], net.pair)

    @pl.when(core == group)
    def _():
        far_wo.wait_recv()
        total = gwo_ref[...] + wo_in[...].astype(f32)
        first, second = total[:weight_rows], total[weight_rows:]
        out_wo[...] = jnp.where(core == 0, first, second)
        wo_pair[...] = jnp.where(core == 0, second, first)
        share_wo.start()

    own_first = pl.ds(pl.multiple_of(group * GROUP, GROUP), GROUP)
    w1_blocks = blocks([(gw1_ref.at[own_first], w1_here)], 1)
    state["vec"].wait()
    vec_ref[...] += far_vec_in[...]

    @pl.when(core != group)
    def _():
        far_wo.wait_send()
        share_wo.wait_recv()
        out_wo[...] = wo_pair_in[...]

    @pl.when(core == group)
    def _():
        share_wo.wait_send()

    for copy in w1_blocks + w1_far:
        copy.wait()
    unit_rows = out_w2.shape[0]
    for at in range(GROUP):
        for part in range(2):
            here = slice(part * unit_rows, (part + 1) * unit_rows)
            to = (part * GROUP + at) * unit_rows
            out_w1[:, to : to + unit_rows] = w1_here[at, :, here].astype(f32) + w1_there[
                at, :, here
            ].astype(f32)
    for copy in state["qkv"] + qkv_far:
        copy.wait()
    for at in range(GROUP):
        to = (at % 2 * 8 + at // 2) * HEAD_DIM
        for part, ref in enumerate((out_q, out_k, out_v)):
            here = slice(part * HEAD_DIM, (part + 1) * HEAD_DIM)
            ref[:, to : to + HEAD_DIM] = gq_here[at, :, here].astype(f32) + gq_there[
                at, :, here
            ].astype(f32)


def layer_tail(
    qkv, dout, wqkv, dres, gwo, vecg, gb1, lengths, x_all, gw1, w2_own, w2_early
):
    f32, bf16 = jnp.float32, jnp.bfloat16
    block, width = dres.shape
    rows = block // TAIL_CHUNKS
    weight_rows = wqkv.shape[2]
    units = gw1.shape[2]
    unit_rows = units // 2
    own_rows = GROUP * block
    peers = GROUP - 1
    vmem = pl.BlockSpec(memory_space=pltpu.VMEM)
    anywhere = pl.BlockSpec(memory_space=pl.ANY)
    smem = pl.BlockSpec(memory_space=pltpu.SMEM)
    sems = pltpu.SemaphoreType.DMA
    shape, scratch = jax.ShapeDtypeStruct, pltpu.VMEM
    heads = 3 * HEAD_DIM

    def slots(*lead):
        return scratch(lead + (rows, width), bf16)

    return pl.pallas_call(
        tail_kernel,
        out_shape=[
            shape((block, width), bf16),
            shape((weight_rows, width), f32),
            shape((weight_rows, width), f32),
            shape((weight_rows, width), f32),
            shape((weight_rows, width), f32),
            shape((weight_rows, GROUP * units), f32),
            shape((unit_rows, width), f32),
            shape((8, 128), f32),
        ],
        in_specs=[vmem] * 7 + [smem] + [anywhere] * 4,
        out_specs=[vmem] * 8,
        scratch_shapes=[
            scratch(x_all.shape, bf16),
            slots(TAIL_CHUNKS, 2, 2, 2), slots(2, 2, 2, 2), slots(TAIL_CHUNKS, 2, 2, 2),
            slots(TAIL_CHUNKS, 2, 2), slots(TAIL_CHUNKS, 2), slots(TAIL_CHUNKS),
            scratch((block, width), f32),
            scratch((own_rows + HALO, heads), bf16),
            scratch(qkv.shape[:1] + (HEAD_DIM,), f32),
            scratch(qkv.shape[:1] + (HEAD_DIM,), f32),
            scratch((heads, own_rows), bf16),
            scratch((GROUP, weight_rows, heads), bf16),
            scratch((GROUP, weight_rows, heads), bf16),
            scratch((GROUP, weight_rows, heads), bf16),
            scratch((GROUP, weight_rows, heads), bf16),
            scratch((GROUP, weight_rows, units), bf16),
            scratch((GROUP, weight_rows, units), bf16),
            scratch((unit_rows, width), f32),
            scratch((unit_rows, width), bf16),
            scratch((HEAD_DIM, width), bf16),
            scratch((HEAD_DIM, width), bf16),
            scratch((weight_rows, width), f32),
            scratch((weight_rows, width), f32),
            scratch((GROUP, 16, 128), f32),
            scratch((GROUP, 16, 128), f32),
            scratch((8, 128), f32),
            scratch((8, 128), f32),
            pltpu.VMEM((1, own_rows + HALO), f32),
            pltpu.VMEM((1, own_rows + HALO + 2 * PAD), f32),
            sems((1, TAIL_CHUNKS, 4, 3)), sems((1, TAIL_CHUNKS, 4, 3)),
            sems((1, TAIL_CHUNKS)), sems((1, TAIL_CHUNKS)),
            sems((CHUNKS + 2,)), sems((3,)), sems((3, peers)), sems((3, peers)),
            sems((2, GROUP)), sems((2, GROUP)), sems((5,)), sems((5,)),
        ],
        compiler_params=pltpu.CompilerParams(
            collective_id=5, has_side_effects=True, vmem_limit_bytes=63 << 20
        ),
        name="layer_tail",
    )(qkv, dout, wqkv, dres, gwo, vecg, gb1, lengths, x_all, gw1, w2_own, w2_early)


def grouped_device(
    tokens,
    cotangent,
    lengths,
    wq,
    bq,
    wk,
    wv,
    bv,
    wo,
    bo,
    norm1_gain,
    norm1_bias,
    w1,
    b1,
    w2,
    b2,
    norm2_gain,
    norm2_bias,
):
    f32 = jnp.float32
    vectors = [bq, bv, bo, norm1_gain, norm1_bias, b2, norm2_gain, norm2_bias, b1]
    sizes = [item.shape[0] for item in vectors]
    vector, at = jnp.zeros((1024,), f32), 0
    for item, size in zip(vectors, sizes):
        vector = vector + jnp.pad(item.astype(f32), (at, 1024 - at - size))
        at += size
    vector = vector.reshape(8, 128)

    (
        output, grad_resid_one, vec_grads, grad_b1, w2_own, _, w2_early, grad_w1, grad_wo,
        all_tokens, _, qkv, grad_out, full_qkv,
    ) = layer(tokens, cotangent, wq, wk, wv, w1, w2, wo, vector, lengths)

    input_grad, out_q, out_k, out_v, out_wo, out_w1, out_w2, sums = layer_tail(
        qkv, grad_out, full_qkv, grad_resid_one, grad_wo, vec_grads, grad_b1, lengths,
        all_tokens, grad_w1, w2_own, w2_early,
    )
    sums, at = sums.reshape(-1), 0
    small = []
    for size in sizes:
        small.append(sums[at : at + size])
        at += size
    out_bq, out_bv, out_bo, out_g1, out_s1, out_b2, out_g2, out_s2, out_b1 = small
    return (
        output, input_grad, out_q, out_bq, out_k, out_v, out_bv, out_wo, out_bo, out_g1, out_s1,
        out_w1, out_b1, out_w2, out_b2, out_g2, out_s2,
    )


def solution(mesh):
    in_specs = (
        P("dp", None),
        P("dp", None),
        P(),
        P("dp", None),
        P("dp"),
        P("dp", None),
        P("dp", None),
        P("dp"),
        P("dp", None),
        P("dp"),
        P("dp"),
        P("dp"),
        P("dp", None),
        P("dp"),
        P("dp", None),
        P("dp"),
        P("dp"),
        P("dp"),
    )
    out_specs = (
        P("dp", None),
        P("dp", None),
        P("dp", None),
        P("dp"),
        P("dp", None),
        P("dp", None),
        P("dp"),
        P("dp", None),
        P("dp"),
        P("dp"),
        P("dp"),
        P("dp", None),
        P("dp"),
        P("dp", None),
        P("dp"),
        P("dp"),
        P("dp"),
    )
    two_groups = mesh.shape["dp"] == 2 * GROUP
    return jax.shard_map(
        grouped_device if two_groups else per_device, mesh=mesh, in_specs=in_specs, out_specs=out_specs, check_vma=False
    )
```

```python
import functools

import jax
import jax.numpy as jnp
from jax import lax
from jax.experimental import pallas as pl
from jax.experimental.pallas import tpu as pltpu
from jax.sharding import PartitionSpec as P

HEADS = 16
HEAD_DIM = 128
SEQ_MAX = 160
SPAN = 3

GROUP = 16
HALO = 256
WINDOW = 512
TILE = 128
MESH_ID = pl.DeviceIdType.MESH
VMEM_LIMIT = 60 << 20


norm_eps = 1e-05


def layer_norm(residual, gain_vec, shift_vec):
    mean_val = jnp.mean(residual, axis=-1, keepdims=True)
    centred = residual - mean_val
    var_val = jnp.mean(centred * centred, axis=-1, keepdims=True)
    return centred * lax.rsqrt(var_val + norm_eps) * gain_vec + shift_vec


def gelu_tanh(values):
    return jax.nn.gelu(values, approximate=True)


def plan_layout(lengths, tok_dev):
    starts = jnp.cumsum(lengths) - lengths
    owner_first = starts // tok_dev
    return (starts, starts, lengths, owner_first)


def to_owners(shard, layout, dev_count, piece_rows):
    starts, owner_start, owner_length, owner_first = layout
    tok_dev = shard.shape[0]
    feat_width = shard.shape[1]
    device = lax.axis_index("dp")
    held_rows = lax.all_to_all(
        shard.reshape(dev_count, piece_rows, feat_width),
        "dp",
        split_axis=0,
        concat_axis=0,
        tiled=True,
    )
    held_rows = held_rows.reshape(dev_count * piece_rows, feat_width)
    slot_ids = jnp.arange(SPAN * piece_rows, dtype=jnp.int32)
    shard_step = slot_ids // piece_rows
    within = slot_ids % piece_rows
    source = owner_first[:, None] + shard_step[None, :]
    global_row = source * tok_dev + device * piece_rows + within[None, :]
    inside = (
        (global_row >= owner_start[:, None])
        & (global_row < (owner_start + owner_length)[:, None])
        & (source < dev_count)
    )
    picked = held_rows[jnp.clip(source, 0, dev_count - 1) * piece_rows + within[None, :]]
    outgoing = jnp.where(inside[:, :, None], picked, jnp.zeros((), picked.dtype))
    arrived = lax.all_to_all(outgoing, "dp", split_axis=0, concat_axis=0, tiled=True)
    arrived = arrived.reshape(dev_count * SPAN * piece_rows, feat_width)
    my_start = owner_start[device]
    my_length = owner_length[device]
    my_first = owner_first[device]
    places = jnp.arange(SEQ_MAX, dtype=jnp.int32)
    global_pos = my_start + places
    shard_of = global_pos // tok_dev
    offset_in = global_pos % tok_dev
    slot_index = (
        offset_in // piece_rows * (SPAN * piece_rows)
        + (shard_of - my_first) * piece_rows
        + offset_in % piece_rows
    )
    valid_rows = places < my_length
    slot_index = jnp.where(valid_rows, slot_index, 0)
    owned = jnp.where(valid_rows[:, None], arrived[slot_index], jnp.zeros((), arrived.dtype))
    return (owned, valid_rows)


def to_order(owned, layout, dev_count, piece_rows, tok_dev):
    starts, owner_start, owner_length, owner_first = layout
    feat_width = owned.shape[1]
    device = lax.axis_index("dp")
    my_start = owner_start[device]
    my_length = owner_length[device]
    my_first = owner_first[device]
    slot_ids = jnp.arange(SPAN * piece_rows, dtype=jnp.int32)
    shard_step = slot_ids // piece_rows
    within = slot_ids % piece_rows
    targets = jnp.arange(dev_count, dtype=jnp.int32)
    global_row = (
        (my_first + shard_step)[None, :] * tok_dev + targets[:, None] * piece_rows + within[None, :]
    )
    place_row = global_row - my_start
    inside = (place_row >= 0) & (place_row < my_length)
    picked = owned[jnp.clip(place_row, 0, owned.shape[0] - 1)]
    outgoing = jnp.where(inside[:, :, None], picked, jnp.zeros((), picked.dtype))
    returned = lax.all_to_all(outgoing, "dp", split_axis=0, concat_axis=0, tiled=True)
    returned = returned.reshape(dev_count * SPAN * piece_rows, feat_width)
    sources = jnp.arange(dev_count, dtype=jnp.int32)
    within_piece = jnp.arange(piece_rows, dtype=jnp.int32)
    row_ids = sources[:, None] * tok_dev + device * piece_rows + within_piece[None, :]
    seq_of = jnp.sum((row_ids[:, :, None] >= starts[None, None, :]).astype(jnp.int32), 2) - 1
    slot_index = (
        seq_of * (SPAN * piece_rows)
        + (sources[:, None] - owner_first[seq_of]) * piece_rows
        + within_piece[None, :]
    )
    pieces = returned[slot_index]
    ordered = lax.all_to_all(pieces, "dp", split_axis=0, concat_axis=0, tiled=True)
    return ordered.reshape(tok_dev, feat_width)


def per_device(
    tokens,
    cotangent,
    lengths,
    wq,
    bq,
    wk,
    wv,
    bv,
    wo,
    bo,
    norm1_gain,
    norm1_bias,
    w1,
    b1,
    w2,
    b2,
    norm2_gain,
    norm2_bias,
):
    f32 = jnp.float32
    bf16 = jnp.bfloat16
    dev_count = lax.axis_size("dp")
    tok_dev = tokens.shape[0]
    feat_width = tokens.shape[1]
    piece_rows = tok_dev // dev_count
    layout = plan_layout(lengths, tok_dev)
    joined, valid_rows = to_owners(
        jnp.concatenate([tokens, cotangent], 1), layout, dev_count, piece_rows
    )
    inputs = joined[:, :feat_width]
    upstream = joined[:, feat_width:].astype(f32)
    slot_count = inputs.shape[0]
    score_scale = HEAD_DIM ** (-0.5)
    full_wq, full_wk, full_wv, full_wo, full_bq, full_bv, full_bo, gain_one, shift_one = (
        lax.all_gather(wq, "dp", axis=0, tiled=True),
        lax.all_gather(wk, "dp", axis=0, tiled=True),
        lax.all_gather(wv, "dp", axis=0, tiled=True),
        lax.all_gather(wo, "dp", axis=0, tiled=True),
        lax.all_gather(bq, "dp", axis=0, tiled=True),
        lax.all_gather(bv, "dp", axis=0, tiled=True),
        lax.all_gather(bo, "dp", axis=0, tiled=True),
        lax.all_gather(norm1_gain, "dp", axis=0, tiled=True),
        lax.all_gather(norm1_bias, "dp", axis=0, tiled=True),
    )
    queries = (
        (jnp.dot(inputs, full_wq, preferred_element_type=f32) + full_bq.astype(f32))
        .astype(bf16)
        .reshape(slot_count, HEADS, HEAD_DIM)
    )
    keys_low = (
        jnp.dot(inputs, full_wk, preferred_element_type=f32)
        .astype(bf16)
        .reshape(slot_count, HEADS, HEAD_DIM)
    )
    values_low = (
        (jnp.dot(inputs, full_wv, preferred_element_type=f32) + full_bv.astype(f32))
        .astype(bf16)
        .reshape(slot_count, HEADS, HEAD_DIM)
    )
    scores = jnp.einsum("qhd,khd->hqk", queries, keys_low, preferred_element_type=f32) * score_scale
    scores = jnp.where(valid_rows[None, None, :], scores, -1e30)
    row_max = jnp.max(scores, -1, keepdims=True)
    row_total = jnp.sum(jnp.exp(scores - row_max), -1, keepdims=True)
    log_total = row_max + jnp.log(row_total)
    attn_probs = jnp.exp(scores - log_total).astype(bf16)
    attended = jnp.einsum("hqk,khd->qhd", attn_probs, values_low, preferred_element_type=f32)
    attended = attended.reshape(slot_count, feat_width).astype(bf16)
    branch = jnp.dot(attended, full_wo, preferred_element_type=f32) + full_bo.astype(f32)
    resid_one = inputs.astype(f32) + branch
    hidden, norm_one_back = jax.vjp(
        layer_norm, resid_one, gain_one.astype(f32), shift_one.astype(f32)
    )
    hidden_low = hidden.astype(bf16)
    full_w1, full_w2, full_b1, full_b2, gain_two, shift_two = (
        lax.all_gather(w1, "dp", axis=0, tiled=True),
        lax.all_gather(w2, "dp", axis=0, tiled=True),
        lax.all_gather(b1, "dp", axis=0, tiled=True),
        lax.all_gather(b2, "dp", axis=0, tiled=True),
        lax.all_gather(norm2_gain, "dp", axis=0, tiled=True),
        lax.all_gather(norm2_bias, "dp", axis=0, tiled=True),
    )
    upward = jnp.dot(hidden_low, full_w1, preferred_element_type=f32) + full_b1.astype(f32)
    activ, gelu_back = jax.vjp(gelu_tanh, upward)
    activ_low = activ.astype(bf16)
    mixed = jnp.dot(activ_low, full_w2, preferred_element_type=f32) + full_b2.astype(f32)
    resid_two = hidden + mixed
    normed, norm_two_back = jax.vjp(
        layer_norm, resid_two, gain_two.astype(f32), shift_two.astype(f32)
    )
    result = jnp.where(valid_rows[:, None], normed, 0.0).astype(bf16)
    output = to_order(result, layout, dev_count, piece_rows, tok_dev)
    back_w1, back_w2 = (
        lax.all_gather(w1, "dp", axis=0, tiled=True),
        lax.all_gather(w2, "dp", axis=0, tiled=True),
    )
    grad_resid_two, grad_gain_two, grad_shift_two = norm_two_back(upstream)
    grad_mixed = grad_resid_two.astype(bf16)
    grad_bias_two = jnp.sum(grad_mixed.astype(f32), 0)
    grad_activ = jnp.einsum("td,fd->tf", grad_mixed, back_w2, preferred_element_type=f32)
    grad_upward = gelu_back(grad_activ)[0].astype(bf16)
    grad_bias_one = jnp.sum(grad_upward.astype(f32), 0)
    grad_hidden = grad_resid_two + jnp.einsum(
        "tf,df->td", grad_upward, back_w1, preferred_element_type=f32
    )
    grad_w2 = jnp.einsum("tf,td->fd", activ_low, grad_mixed, preferred_element_type=f32)
    grad_w1 = jnp.einsum("td,tf->df", hidden_low, grad_upward, preferred_element_type=f32)
    mlp_grads = (
        lax.psum_scatter(grad_w1, "dp", scatter_dimension=0, tiled=True),
        lax.psum_scatter(grad_w2, "dp", scatter_dimension=0, tiled=True),
        lax.psum_scatter(grad_bias_one, "dp", scatter_dimension=0, tiled=True),
        lax.psum_scatter(grad_bias_two, "dp", scatter_dimension=0, tiled=True),
        lax.psum_scatter(grad_gain_two, "dp", scatter_dimension=0, tiled=True),
        lax.psum_scatter(grad_shift_two, "dp", scatter_dimension=0, tiled=True),
    )
    back_wq, back_wk, back_wv, back_wo = (
        lax.all_gather(wq, "dp", axis=0, tiled=True),
        lax.all_gather(wk, "dp", axis=0, tiled=True),
        lax.all_gather(wv, "dp", axis=0, tiled=True),
        lax.all_gather(wo, "dp", axis=0, tiled=True),
    )
    grad_resid_one, grad_gain_one, grad_shift_one = norm_one_back(grad_hidden)
    grad_branch = grad_resid_one.astype(bf16)
    grad_bo = jnp.sum(grad_branch.astype(f32), 0)
    grad_wo = jnp.einsum("tc,td->cd", attended, grad_branch, preferred_element_type=f32)
    grad_attended = jnp.einsum(
        "td,cd->tc", grad_branch, back_wo, preferred_element_type=f32
    ).astype(bf16)
    grad_attended = grad_attended.reshape(slot_count, HEADS, HEAD_DIM)
    re_scores = (
        jnp.einsum("qhd,khd->hqk", queries, keys_low, preferred_element_type=f32) * score_scale
    )
    re_scores = jnp.where(valid_rows[None, None, :], re_scores, -1e30)
    re_probs = jnp.exp(re_scores - log_total)
    re_probs_low = re_probs.astype(bf16)
    grad_values = jnp.einsum(
        "hqk,qhd->khd", re_probs_low, grad_attended, preferred_element_type=f32
    ).astype(bf16)
    grad_probs = jnp.einsum("qhd,khd->hqk", grad_attended, values_low, preferred_element_type=f32)
    grad_scores = re_probs * (grad_probs - jnp.sum(re_probs * grad_probs, -1, keepdims=True))
    grad_scores_low = grad_scores.astype(bf16)
    grad_queries = (
        jnp.einsum("hqk,khd->qhd", grad_scores_low, keys_low, preferred_element_type=f32)
        * score_scale
    ).astype(bf16)
    grad_keys = (
        jnp.einsum("hqk,qhd->khd", grad_scores_low, queries, preferred_element_type=f32)
        * score_scale
    ).astype(bf16)
    grad_queries = grad_queries.reshape(slot_count, feat_width)
    grad_keys = grad_keys.reshape(slot_count, feat_width)
    grad_values = grad_values.reshape(slot_count, feat_width)
    grad_bq = jnp.sum(grad_queries.astype(f32), 0)
    grad_bv = jnp.sum(grad_values.astype(f32), 0)
    grad_wq = jnp.einsum("tc,td->cd", inputs, grad_queries, preferred_element_type=f32)
    grad_wk = jnp.einsum("tc,td->cd", inputs, grad_keys, preferred_element_type=f32)
    grad_wv = jnp.einsum("tc,td->cd", inputs, grad_values, preferred_element_type=f32)
    grad_input = grad_resid_one + jnp.einsum(
        "td,cd->tc", grad_queries, back_wq, preferred_element_type=f32
    )
    grad_input = grad_input + jnp.einsum(
        "td,cd->tc", grad_keys, back_wk, preferred_element_type=f32
    )
    grad_input = grad_input + jnp.einsum(
        "td,cd->tc", grad_values, back_wv, preferred_element_type=f32
    )
    grad_input = jnp.where(valid_rows[:, None], grad_input, 0.0).astype(bf16)
    attn_grads = (
        lax.psum_scatter(grad_wq, "dp", scatter_dimension=0, tiled=True),
        lax.psum_scatter(grad_wk, "dp", scatter_dimension=0, tiled=True),
        lax.psum_scatter(grad_wv, "dp", scatter_dimension=0, tiled=True),
        lax.psum_scatter(grad_wo, "dp", scatter_dimension=0, tiled=True),
        lax.psum_scatter(grad_bq, "dp", scatter_dimension=0, tiled=True),
        lax.psum_scatter(grad_bv, "dp", scatter_dimension=0, tiled=True),
        lax.psum_scatter(grad_bo, "dp", scatter_dimension=0, tiled=True),
        lax.psum_scatter(grad_gain_one, "dp", scatter_dimension=0, tiled=True),
        lax.psum_scatter(grad_shift_one, "dp", scatter_dimension=0, tiled=True),
    )
    sum_w1, sum_w2, sum_b1, sum_b2, sum_g2, sum_s2 = mlp_grads
    sum_wq, sum_wk, sum_wv, sum_wo, sum_bq, sum_bv, sum_bo, sum_g1, sum_s1 = attn_grads
    input_grad = to_order(grad_input, layout, dev_count, piece_rows, tok_dev)
    return (
        output,
        input_grad,
        sum_wq,
        sum_bq,
        sum_wk,
        sum_wv,
        sum_bv,
        sum_wo,
        sum_bo,
        sum_g1,
        sum_s1,
        sum_w1,
        sum_b1,
        sum_w2,
        sum_b2,
        sum_g2,
        sum_s2,
    )


def flip(device, bit):
    step = 1 << bit
    return device + step - 2 * step * ((device // step) % 2)


def chip_bits(device):
    return [(device // 2) % 2, (device // 4) % 2, (device // 8) % 2]


def enter(partners):
    barrier = pltpu.get_barrier_semaphore()
    for partner in partners:
        pl.semaphore_signal(barrier, inc=1, device_id=(partner,), device_id_type=MESH_ID)
    pl.semaphore_wait(barrier, len(partners))


def push(src, dst, send_sem, recv_sem, device):
    return pltpu.make_async_remote_copy(
        src_ref=src,
        dst_ref=dst,
        send_sem=send_sem,
        recv_sem=recv_sem,
        device_id=(device,),
        device_id_type=MESH_ID,
    )


def exchange_blocks(pairs, sems, base, mine, others):
    local_sem, send_sem, recv_sem = sems
    copies = []
    for at, (src, dst) in enumerate(pairs):
        for step, other in enumerate(others):
            copy = push(
                src.at[other - base],
                dst.at[mine],
                send_sem.at[at, step],
                recv_sem.at[at, step],
                other,
            )
            copy.start()
            copies.append(copy)
        local = pltpu.make_async_copy(src.at[mine], dst.at[mine], local_sem.at[at])
        local.start()
        copies.append(local)
    return copies


def exchange_columns(source, to, sems, base, mine, others):
    local_sem, send_sem, recv_sem = sems
    copies = []
    for step, other in enumerate(others):
        copy = push(source(other - base), to, send_sem.at[step], recv_sem.at[step], other)
        copy.start()
        copies.append(copy)
    copy = pltpu.make_async_copy(source(mine), to, local_sem)
    copy.start()
    return copies + [copy]


def far_blocks(src, dst, send_sem, recv_sem, group, mine):
    copies = []
    for step in range(GROUP):
        member = (mine + step) % GROUP
        copy = push(
            src.at[member],
            dst.at[mine],
            send_sem.at[step],
            recv_sem.at[step],
            (1 - group) * GROUP + member,
        )
        copy.start()
        copies.append(copy)
    return copies


def group_places():
    device = lax.axis_index("dp")
    base = device // GROUP * GROUP
    mine = device % GROUP
    others = [base + (mine + step) % GROUP for step in range(1, GROUP)]
    across = (device + GROUP) % (2 * GROUP)
    there = [GROUP - base + (mine + step) % GROUP for step in range(GROUP)]
    return device // GROUP, base, mine, others, across, there


def write_segments(lengths_ref, first, keys_ref, queries_ref):
    f32 = jnp.float32
    rows = queries_ref.shape[1]

    def numbers(ref, ahead):
        ids = first - ahead + lax.broadcasted_iota(jnp.int32, ref.shape, 1)
        total = jnp.zeros(ref.shape, jnp.int32)
        start = jnp.int32(0)
        for at in range(lengths_ref.shape[0]):
            total = total + (ids >= start).astype(jnp.int32)
            start = start + lengths_ref[at]
        return total.astype(f32)

    queries_ref[...] = numbers(queries_ref, 0)
    place = lax.broadcasted_iota(jnp.int32, keys_ref.shape, 1)
    inside = (place >= PAD) & (place < PAD + rows)
    keys_ref[...] = jnp.where(inside, numbers(keys_ref, PAD), -1.0)


def tile_probs(qkv_ref, queries_ref, keys_ref, tile):
    f32 = jnp.float32
    place = pl.multiple_of(tile * TILE, TILE)
    row = pl.multiple_of(PAD + place, 64)
    window = pl.ds(place, WINDOW)
    queries = qkv_ref[pl.ds(row, TILE), 0:HEAD_DIM]
    keys = qkv_ref[window, HEAD_DIM : 2 * HEAD_DIM]
    scores = lax.dot_general(queries, keys, NT, preferred_element_type=f32)
    own = jnp.broadcast_to(queries_ref[0:1, pl.ds(place, TILE)], (TILE, TILE)).T[:, 0:1]
    scores = jnp.where(own == keys_ref[0:1, window], scores * HEAD_DIM ** (-0.5), -1e30)
    weights = jnp.exp(scores - jnp.max(scores, -1, keepdims=True))
    return queries, keys, weights * (1.0 / jnp.sum(weights, -1, keepdims=True))


CHUNKS = 2
TAIL_CHUNKS = 2
THIRDS = (((0, 768), (0, 1, 2)), ((768, 640), (1, 2, 0)), ((1408, 640), (2, 0, 1)))
LIGHT = (
    ((0, 512), (1, 2, 0)), ((512, 512), (0, 2, 1)), ((1024, 512), (1, 0, 2)), ((1536, 512), (0, 1, 2)),
)
PLANS = (THIRDS, LIGHT) + (THIRDS,) * 5
TAIL_PLANS = (LIGHT,)
SPLIT = 256
PAD = (WINDOW - TILE) // 2
REACH = SEQ_MAX
STAGES = 7


def step_through(flows, fillers=None):
    waiting, alive = list(flows), []
    while waiting or alive:
        if waiting:
            alive.append(waiting.pop(0))
        alive = [flow for flow in alive if next(flow, "done") != "done"]
        if fillers is not None:
            next(fillers, None)
    if fillers is not None:
        for _ in fillers:
            pass


class Traffic:
    def __init__(self, sems, plans):
        self.plans = plans
        self.hop_send, self.hop_recv, self.pair_send, self.pair_recv = sems
        device = lax.axis_index("dp")
        self.core = device % 2
        self.bits = chip_bits(device)
        self.partners = [flip(device, 1), flip(device, 2), flip(device, 3)]
        self.pair = flip(device, 0)

    def chips(self, ref, values, columns):
        return ref.at[values[2], values[1], values[0], :, columns]

    def push(self, src, dst, stage, chunk, part, step):
        copy = push(
            src, dst,
            self.hop_send.at[stage, chunk, part, step],
            self.hop_recv.at[stage, chunk, part, step],
            self.partners[self.plans[stage][part][1][step]],
        )
        copy.start()
        return copy

    def share(self, src, dst, stage, chunk):
        copy = push(
            src, dst, self.pair_send.at[stage, chunk], self.pair_recv.at[stage, chunk], self.pair
        )
        copy.start()
        return copy

    def gather(self, slots, stage, chunk):
        mine = slots.at[self.core]
        hops = {}
        for step in range(3):
            for part, ((first, count), order) in enumerate(self.plans[stage]):
                if step:
                    hops[part, step - 1].wait_recv()
                values = list(self.bits)
                for dim in order[:step]:
                    values[dim] = slice(None)
                view = self.chips(mine, values, pl.ds(first, count))
                hops[part, step] = self.push(view, view, stage, chunk, part, step)
            yield
        for part in range(len(self.plans[stage])):
            hops[part, 2].wait_recv()
        share = self.share(mine, mine, stage, chunk)
        for copy in hops.values():
            copy.wait_send()
        return share

    def scatter(self, own, pair_in, incoming, share, stage, chunk, finish):
        rows = own.shape[-2]
        f32 = jnp.float32
        hops = {}
        share.wait()
        for step in range(4):
            for part, ((first, count), order) in enumerate(self.plans[stage]):
                columns = pl.ds(first, count)
                if step:
                    hops[part, step - 1].wait_recv()
                values = list(self.bits)
                free = ()
                if step < 3:
                    values[order[step]] = 1 - self.bits[order[step]]
                    free = order[step + 1 :]
                for mask in range(1 << len(free)):
                    slot = list(values)
                    for place, dim in enumerate(free):
                        slot[dim] = (mask >> place) & 1
                    where = (slot[2], slot[1], slot[0])
                    lefts = [
                        tuple(slot[dim] for dim in (2, 1, 0) if dim not in order[: back + 1])
                        for back in range(step)
                    ]

                    def add(index, carry, step=step, where=where, lefts=lefts, columns=columns):
                        row = pl.multiple_of(index * 16, 16)
                        at = (pl.ds(row, 16), columns)
                        total = own[where + at].astype(f32) + pair_in[where + at].astype(f32)
                        for back in range(step):
                            total = total + incoming[back][lefts[back] + at].astype(f32)
                        if step < 3:
                            own[where + at] = total.astype(own.dtype)
                        else:
                            finish(row, columns, total)
                        return carry

                    lax.fori_loop(0, rows // 16, add, 0)
                if step == 3:
                    continue
                for dim in free:
                    values[dim] = slice(None)
                left = tuple(slice(None) for _ in free)
                hops[part, step] = self.push(
                    self.chips(own, values, columns),
                    incoming[step].at[left + (slice(None), columns)],
                    stage, chunk, part, step,
                )
            if step < 3:
                yield
        for copy in hops.values():
            copy.wait_send()


def gelu_slope(up):
    inner = 0.7978845608028654 * (up + 0.044715 * (up * up * up))
    tanh = jnp.tanh(inner)
    return 0.5 * (1.0 + tanh) + 0.5 * up * (1.0 - tanh * tanh) * (
        0.7978845608028654 * (1.0 + 0.134145 * (up * up))
    )


NT = (((1,), (1,)), ((), ()))
TN = (((0,), (0,)), ((), ()))


def layer_kernel(
    tok_ref, cot_ref, wq_ref, wk_ref, wv_ref, w1_ref, w2_ref, wo_ref, vec_ref, lengths_ref,
    out_ref, dres_ref, vecg_ref, gb1_ref, gw2_own, gw2_far, gw2_in, gw1_ref, gwo_ref,
    x_all, h_all, qkv_ref, dout_ref, wqkv_ref,
    all_h, all_m, own_part, far_part, pair_in, in_one, in_two, in_three,
    up_ref, act_ref, act_t, dup_ref, dup_t, att_ref, att_t, res_ref, hid_ref, norm_ref, scale_ref,
    w1_all, w2_all, wo_all, vec_all, low_ref, high_ref, b1_ref, stage_ref, stage_low, stage_w1,
    queries_ref, keys_ref,
    hop_send, hop_recv, pair_send, pair_recv,
    block_local, block_send, block_recv, vec_send, vec_recv, far_send, far_recv,
    local_sems, out_sems, spill_sems,
):
    f32, low = jnp.float32, tok_ref.dtype
    block, width = tok_ref.shape
    rows = block // CHUNKS
    half_rows = rows * GROUP // 2
    own_rows = GROUP * block
    units = w1_all.shape[-1]
    group, base, mine, others, across, there = group_places()
    net = Traffic((hop_send, hop_recv, pair_send, pair_recv), PLANS)
    core, bits = net.core, net.bits
    chip = mine // 2
    head = core * 8 + chip
    own_slot = (core, bits[2], bits[1], bits[0])
    ext = PAD + group * HALO
    enter(others + there)

    def far(src, dst, at, device=across):
        copy = push(src, dst, far_send.at[at], far_recv.at[at], device)
        copy.start()
        return copy

    def local(src, dst, at):
        copy = pltpu.make_async_copy(src, dst, local_sems.at[at])
        copy.start()
        return copy

    early = w2_ref.shape[0] // 4 * 3
    far_vec = far(vec_ref, vec_all.at[group, mine], 0)
    near = [
        local(vec_ref, vec_all.at[group, mine], 0),
        local(w2_ref, w2_all.at[group], 1),
        local(wo_ref, wo_all.at[group, core], 2),
    ]
    w2_first, w2_last = pl.ds(0, early), pl.ds(early, w2_ref.shape[0] - early)
    far_w2 = [far(w2_ref.at[w2_first, :], w2_all.at[group, w2_first, :], 1)]

    def block_sems(at):
        return block_local.at[at], block_send.at[at], block_recv.at[at]

    qkv_blocks = []
    for part, ref in enumerate((wq_ref, wk_ref, wv_ref)):

        def head_columns(member, ref=ref):
            first = pl.multiple_of((member % 2 * 8 + member // 2) * HEAD_DIM, HEAD_DIM)
            return ref.at[:, pl.ds(first, HEAD_DIM)]

        qkv_blocks += exchange_columns(
            head_columns, wqkv_ref.at[group, mine, :, pl.ds(part * HEAD_DIM, HEAD_DIM)],
            block_sems(part), base, mine, others,
        )
    for chunk in range(CHUNKS):
        all_m[(chunk,) + own_slot] = tok_ref[chunk * rows : (chunk + 1) * rows, :]
    wo_near = push(
        wo_ref, wo_all.at[group, core], far_send.at[2], far_recv.at[2], net.pair
    )
    wo_near.start()

    unsent = own_rows + REACH - group * (own_rows + REACH)
    for first in (0, qkv_ref.shape[0] - PAD):
        qkv_ref[first : first + PAD, :] = jnp.zeros((PAD, qkv_ref.shape[1]), low)
    qkv_ref[pl.ds(pl.multiple_of(PAD + unsent, 32), HALO - REACH), :] = jnp.zeros(
        (HALO - REACH, qkv_ref.shape[1]), low
    )
    dout_ref[pl.ds(pl.multiple_of(unsent, 32), HALO - REACH), :] = jnp.zeros(
        (HALO - REACH, HEAD_DIM), low
    )
    vecg_ref[...] = jnp.zeros_like(vecg_ref)
    gb1_ref[...] = jnp.zeros_like(gb1_ref)

    write_segments(lengths_ref, group * (own_rows - HALO), keys_ref, queries_ref)

    def row_at(chunk, side):
        return pl.multiple_of((chunk * 2 + side) * half_rows, half_rows)

    def flat(ref, chunk, side, columns=slice(None)):
        return ref[chunk, side, :, :, :, :, columns].reshape(half_rows, -1)

    def tiles(count, body):
        def step(at, carry):
            body(at, pl.ds(pl.multiple_of(at * SPLIT, SPLIT), SPLIT))
            return carry

        lax.fori_loop(0, count // SPLIT, step, 0)

    def pieces(chunk, side):
        return [
            pl.multiple_of((slot * 2 + side) * block + chunk * rows, rows)
            for slot in range(GROUP // 2)
        ]

    def project_half(chunk, side, which):
        columns = pl.ds(pl.multiple_of(which * (width // 2), width // 2), width // 2)
        weight = wqkv_ref[which].reshape(width // 2, -1)
        return jnp.dot(flat(all_m, chunk, side, columns), weight, preferred_element_type=f32)

    def spill(src, dst, chunk, at):
        copy = pltpu.make_async_copy(src.at[chunk], dst.at[chunk], spill_sems.at[at, chunk])
        copy.start()
        return copy

    wide = slice(0, 3 * HEAD_DIM)
    spills = {}

    def token_flow(chunk):
        share = yield from net.gather(all_m.at[chunk], 0, chunk)
        up_ref[pl.ds(row_at(chunk, core), half_rows), wide] = project_half(chunk, core, group)
        yield
        share.wait()
        up_ref[pl.ds(row_at(chunk, 1 - core), half_rows), wide] = project_half(
            chunk, 1 - core, group
        )
        spills[0, chunk] = spill(all_m, x_all, chunk, 0)

    def weight_flow():
        yield
        for copy in qkv_blocks:
            copy.wait()
        state["far_qkv"] = far(wqkv_ref.at[group], wqkv_ref.at[group], 3)
        yield
        for copy in near:
            copy.wait()
        far_vec.wait()
        both = vec_all.at[:, mine]
        state["vec"] = []
        for step, other in enumerate(others):
            copy = push(both, both, vec_send.at[step], vec_recv.at[step], other)
            copy.start()
            state["vec"].append(copy)
        yield

    state = {"backs": 0}
    flows = [token_flow(chunk) for chunk in range(CHUNKS)]
    step_through([flows[0], weight_flow()] + flows[1:])

    for copy in state["vec"]:
        copy.wait()
    lane = lax.broadcasted_iota(jnp.int32, (8, 128), 1)
    for at in range(GROUP):
        first = vec_all[at // 8, at % 8 * 2]
        second = vec_all[at // 8, at % 8 * 2 + 1]
        here = slice(at * 128, at * 128 + 128)
        low_ref[:, here] = jnp.where(lane < 64, first, pltpu.roll(second, 64, 1))
        high_ref[:, here] = jnp.where(lane < 64, pltpu.roll(first, 64, 1), second)
    for half in range(2):
        for part in range(2):
            b1_ref[0:1, half * 256 + part * 128 : half * 256 + part * 128 + 128] = vec_all[
                half, mine, 4 + part : 5 + part, :
            ]
    head_at = pl.ds(pl.multiple_of(head * HEAD_DIM, HEAD_DIM), HEAD_DIM)
    bias_q, bias_v = low_ref[0:1, head_at], high_ref[0:1, head_at]
    bias_qkv = jnp.concatenate([bias_q, jnp.zeros_like(bias_q), bias_v], 1)
    bo, shift_one, gain_two = low_ref[1:2, :], low_ref[2:3, :], low_ref[3:4, :]
    gain_one, b2, shift_two = high_ref[1:2, :], high_ref[2:3, :], high_ref[3:4, :]

    state["far_qkv"].wait()
    for chunk in range(CHUNKS):
        for side in range(2):
            here = pl.ds((chunk * 2 + side) * half_rows, half_rows)
            total = up_ref[here, wide] + project_half(chunk, side, 1 - group) + bias_qkv
            total = total.astype(low)
            for slot, place in enumerate(pieces(chunk, side)):
                qkv_ref[pl.ds(pl.multiple_of(ext + place, rows), rows), :] = total[
                    slot * rows : (slot + 1) * rows
                ]
    near_edge = own_rows - REACH - group * (own_rows - REACH - HALO)
    far_edge = HALO - REACH + group * (own_rows - HALO + REACH)
    halo_src = pl.ds(pl.multiple_of(PAD + near_edge, 32), REACH)
    halo_dst = pl.ds(pl.multiple_of(PAD + far_edge, 32), REACH)
    key_value = pl.ds(HEAD_DIM, 2 * HEAD_DIM)
    far_halo = far(qkv_ref.at[halo_src, key_value], qkv_ref.at[halo_dst, key_value], 6)
    far_wo_to = (1 - group) * GROUP + 2 * chip + group
    far_wo = push(
        wo_ref, wo_all.at[group, core], far_send.at[4 + core], far_recv.at[4 + core], far_wo_to
    )
    far_wo.start()
    far_w2.append(far(w2_ref.at[w2_last, :], w2_all.at[group, w2_last, :], 8))
    w1_blocks = []
    for part in range(2):

        def w1_columns(member, part=part):
            first = pl.multiple_of((part * GROUP + member) * SPLIT, SPLIT)
            return w1_ref.at[:, pl.ds(first, SPLIT)]

        w1_blocks += exchange_columns(
            w1_columns, w1_all.at[group, mine, :, pl.ds(part * SPLIT, SPLIT)],
            block_sems(3 + part), base, mine, others,
        )

    def attend_tile(at):
        tile = at + group * (GROUP - 1 - 2 * at)
        inner = group * (HALO // TILE) + tile
        _, _, probs = tile_probs(qkv_ref, queries_ref, keys_ref, inner)
        window = pl.ds(pl.multiple_of(inner * TILE, TILE), WINDOW)
        values = qkv_ref[window, 2 * HEAD_DIM : 3 * HEAD_DIM]
        out = jnp.dot(probs.astype(low), values, preferred_element_type=f32)
        att_ref[pl.ds(pl.multiple_of(tile * TILE, TILE), TILE), :] = out.astype(low)

    def attend_two(at, carry):
        attend_tile(2 * at)
        attend_tile(2 * at + 1)
        return carry

    lax.fori_loop(0, own_rows // TILE // 2 - 1, attend_two, 0)
    far_halo.wait()
    for copy in w1_blocks:
        copy.wait()
    far_w1 = far(w1_all.at[group], w1_all.at[group], 7)
    attend_tile(own_rows // TILE - 2)
    attend_tile(own_rows // TILE - 1)
    for chunk in range(CHUNKS):
        spills[0, chunk].wait()
    wo_near.wait()
    far_wo.wait_send()

    @pl.when(core != group)
    def _():
        for at in range(2):
            push(
                wo_ref, wo_all.at[1 - group, at], far_send.at[4 + at], far_recv.at[4 + at],
                far_wo_to,
            ).wait_recv()

    def branch_part(chunk, side, dst):
        rows_in = jnp.concatenate([att_ref[pl.ds(at, rows), :] for at in pieces(chunk, side)], 0)
        att_t[:, pl.ds(row_at(chunk, side), half_rows)] = rows_in.astype(f32).T.astype(low)

        def body(at, columns):
            weight = wo_all[core, :, :, columns].reshape(HEAD_DIM, SPLIT)
            part = jnp.dot(rows_in, weight, preferred_element_type=f32)
            dst[:, :, :, :, columns] = part.astype(low).reshape(2, 2, 2, rows, SPLIT)

        tiles(width, body)

    def upward(chunk, side):
        here = pl.ds(row_at(chunk, side), half_rows)

        def body(at, columns):
            weight = w1_all[:, :, :, columns].reshape(width, SPLIT)
            up = jnp.dot(flat(all_h, chunk, side), weight, preferred_element_type=f32)
            up = up + b1_ref[0:1, columns]
            up_ref[here, columns] = up
            act = gelu_tanh(up)
            act_ref[:, columns] = act.astype(low)
            act_t[columns, here] = act.T.astype(low)

        tiles(units, body)

    def downward(dst):
        def body(at, columns):
            weight = w2_all[:, :, columns].reshape(units, SPLIT)
            part = jnp.dot(act_ref[...], weight, preferred_element_type=f32)
            dst[:, :, :, :, columns] = part.astype(low).reshape(2, 2, 2, rows, SPLIT)

        tiles(width, body)

    def up_back(chunk, side):
        here = pl.ds(row_at(chunk, side), half_rows)

        def body(at, columns):
            grad = lax.dot_general(
                flat(all_m, chunk, side), w2_all[at], NT, preferred_element_type=f32
            )
            grad = (grad * gelu_slope(up_ref[here, columns])).astype(low)
            dup_ref[:, columns] = grad
            grad = grad.astype(f32)
            gb1_ref[0:1, columns] += jnp.sum(grad, 0, keepdims=True)
            dup_t[columns, here] = grad.T.astype(low)

        tiles(units, body)

    def down_back(dst):
        def body(at, columns):
            weight = w1_all[at // 4, pl.ds(at % 4 * 4, 4)].reshape(SPLIT, units)
            part = lax.dot_general(dup_ref[...], weight, NT, preferred_element_type=f32)
            dst[:, :, :, :, columns] = part.astype(low).reshape(2, 2, 2, rows, SPLIT)

        tiles(width, body)

    def out_back(chunk, side):
        weight = wo_all[core].reshape(HEAD_DIM, width)
        grad = lax.dot_general(flat(all_h, chunk, side), weight, NT, preferred_element_type=f32)
        grad = grad.astype(low)
        for slot, place in enumerate(pieces(chunk, side)):
            dout_ref[pl.ds(pl.multiple_of(group * HALO + place, rows), rows), :] = grad[
                slot * rows : (slot + 1) * rows
            ]

    def keep(chunk):
        def finish(row, columns, total):
            res_ref[pl.ds(pl.multiple_of(chunk * rows + row, 16), 16), columns] = total

        return finish

    def row_sets(chunk, body):
        def step(index, carry):
            row = pl.multiple_of(index * 16, 16)
            body(pl.ds(pl.multiple_of(chunk * rows + row, 16), 16), pl.ds(row, 16))
            return carry

        lax.fori_loop(0, rows // 16, step, 0)

    def normal(res):
        res = res - jnp.mean(res, -1, keepdims=True)
        scale = lax.rsqrt(jnp.mean(res * res, -1, keepdims=True) + norm_eps)
        return res * scale, scale

    def normal_back(grad, res, gain, scale, at):
        vecg_ref[at + 2 : at + 3, :] += jnp.sum(grad, 0, keepdims=True)
        vecg_ref[at + 1 : at + 2, :] += jnp.sum(grad * res, 0, keepdims=True)
        grad = grad * gain
        first = jnp.mean(grad, -1, keepdims=True)
        second = jnp.mean(grad * res, -1, keepdims=True)
        grad = (grad - first - res * second) * scale
        grad_low = grad.astype(low)
        vecg_ref[at : at + 1, :] += jnp.sum(grad_low.astype(f32), 0, keepdims=True)
        return grad, grad_low

    def norm_one(chunk):
        def body(at, place):
            res, scale = normal(tok_ref[at, :].astype(f32) + res_ref[at, :] + bo)
            norm_ref[at, :] = res
            scale_ref[at, :] = jnp.broadcast_to(scale, (16, 128))
            hidden = res * gain_one + shift_one
            hid_ref[at, :] = hidden
            all_h[(chunk,) + own_slot + (place, slice(None))] = hidden.astype(low)

        row_sets(chunk, body)

    def norm_two(chunk):
        def body(at, place):
            res, scale = normal(hid_ref[at, :] + res_ref[at, :] + b2)
            out_ref[at, :] = (res * gain_two + shift_two).astype(low)
            grad, grad_low = normal_back(cot_ref[at, :].astype(f32), res, gain_two, scale, 0)
            dres_ref[at, :] = grad
            all_m[(chunk,) + own_slot + (place, slice(None))] = grad_low

        row_sets(chunk, body)

    def norm_one_back(chunk):
        def body(at, place):
            grad, grad_low = normal_back(
                dres_ref[at, :] + res_ref[at, :], norm_ref[at, :], gain_one,
                scale_ref[at, 0:1], 3,
            )
            dres_ref[at, :] = grad
            all_h[(chunk,) + own_slot + (place, slice(None))] = grad_low

        row_sets(chunk, body)

    def flow(chunk):
        incoming = (in_one.at[chunk], in_two.at[chunk], in_three.at[chunk])
        own, other = own_part.at[chunk], far_part.at[chunk % 2]
        arrived = pair_in.at[chunk]
        branch_part(chunk, 1 - core, other)
        share = net.share(other, arrived, 1, chunk)
        branch_part(chunk, core, own)
        yield
        yield from net.scatter(own, arrived, incoming, share, 1, chunk, keep(chunk))
        norm_one(chunk)
        share = yield from net.gather(all_h.at[chunk], 2, chunk)
        if chunk == 0:
            far_w1.wait()
        upward(chunk, core)
        if chunk == 0:
            for copy in far_w2:
                copy.wait()
        downward(own)
        yield
        share.wait()
        spills[1, chunk] = spill(all_h, h_all, chunk, 1)
        upward(chunk, 1 - core)
        downward(other)
        share = net.share(other, arrived, 3, chunk)
        yield
        yield from net.scatter(own, arrived, incoming, share, 3, chunk, keep(chunk))
        norm_two(chunk)
        spills[1, chunk].wait()
        share = yield from net.gather(all_m.at[chunk], 4, chunk)
        up_back(chunk, core)
        down_back(own)
        yield
        share.wait()
        up_back(chunk, 1 - core)
        down_back(other)
        share = net.share(other, arrived, 5, chunk)
        state["backs"] += 1
        yield
        yield from net.scatter(own, arrived, incoming, share, 5, chunk, keep(chunk))
        norm_one_back(chunk)
        share = yield from net.gather(all_h.at[chunk], 6, chunk)
        out_back(chunk, core)
        yield
        share.wait()
        out_back(chunk, 1 - core)

    def product(left_t, right, columns):
        total = None
        for chunk in range(CHUNKS):
            for side in range(2):
                here = slice((chunk * 2 + side) * half_rows, (chunk * 2 + side + 1) * half_rows)
                term = jnp.dot(
                    left_t[:, here], flat(right, chunk, side, columns), preferred_element_type=f32
                )
                total = term if total is None else total + term
        return total

    def run(first, last, write):
        def step(at, carry):
            write(at, at % 2, at >= 2)
            return carry

        lax.fori_loop(first, last, step, 0)

    def emit(src, dst, sem, again):
        copy = pltpu.make_async_copy(src, dst, sem)

        @pl.when(again)
        def _():
            copy.wait()

        return copy

    def columns_at(at):
        return pl.ds(pl.multiple_of(at * SPLIT, SPLIT), SPLIT)

    def write_w2(at, slot, again):
        own = emit(stage_ref.at[slot], gw2_own.at[:, columns_at(at)], out_sems.at[0, slot], again)
        there = emit(stage_low.at[slot], gw2_far.at[:, columns_at(at)], out_sems.at[1, slot], again)
        total = product(act_t, all_m, columns_at(at))
        first = group == 0
        stage_ref[slot] = jnp.where(first, total[:256], total[256:])
        stage_low[slot] = jnp.where(first, total[256:], total[:256]).astype(low)
        own.start()
        there.start()

    def write_w1(first):
        def write(at, slot, again):
            tile = first + at
            here = gw1_ref.at[pl.ds(pl.multiple_of(tile * 4, 4), 4)]
            copy = emit(stage_w1.at[slot], here, out_sems.at[2, slot], again)
            total = product(dup_t, all_m, columns_at(tile)).T.astype(low)
            stage_w1[slot] = total.reshape(4, SPLIT // 4, units)
            copy.start()

        return write

    def write_wo(at, slot, again):
        own = emit(stage_ref.at[slot, 0:HEAD_DIM, :], gwo_ref.at[:, columns_at(at)], out_sems.at[4, slot], again)
        stage_ref[slot, 0:HEAD_DIM, :] = product(att_t, all_h, columns_at(at))
        own.start()

    def fill():
        while state["backs"] < CHUNKS:
            yield
        run(0, width // SPLIT // 2, write_w2)
        yield
        run(width // SPLIT // 2, width // SPLIT, write_w2)
        for slot in range(2):
            emit(stage_ref.at[slot], gw2_own.at[:, columns_at(0)], out_sems.at[0, slot], True)
            emit(stage_low.at[slot], gw2_far.at[:, columns_at(0)], out_sems.at[1, slot], True)
        swaps.append(far(gw2_far, gw2_in, 10))
        back = [pltpu.make_async_copy(h_all.at[at], all_m.at[at], spill_sems.at[2, at]) for at in range(CHUNKS)]
        for copy in back:
            copy.start()
        yield
        for copy in back:
            copy.wait()
        run(0, width // SPLIT // 2, write_w1((1 - group) * 4))
        for slot in range(2):
            emit(stage_w1.at[slot], gw1_ref.at[pl.ds(0, 4)], out_sems.at[2, slot], True)
        yield
        run(0, width // SPLIT // 2, write_w1(group * 4))
        for slot in range(2):
            emit(stage_w1.at[slot], gw1_ref.at[pl.ds(0, 4)], out_sems.at[2, slot], True)

    swaps = []
    step_through([flow(chunk) for chunk in range(CHUNKS)], fill())
    query = pl.ds(0, HEAD_DIM)
    far_query = far(qkv_ref.at[halo_src, query], qkv_ref.at[halo_dst, query], 12)
    dout_src = pl.ds(pl.multiple_of(near_edge, 32), REACH)
    dout_dst = pl.ds(pl.multiple_of(far_edge, 32), REACH)
    far_dout = far(dout_ref.at[dout_src, :], dout_ref.at[dout_dst, :], 9)
    run(0, width // SPLIT, write_wo)
    for slot in range(2):
        emit(stage_ref.at[slot, 0:HEAD_DIM, :], gwo_ref.at[:, columns_at(0)], out_sems.at[4, slot], True)
    far_dout.wait()
    far_query.wait()
    for copy in swaps:
        copy.wait()


def layer(tokens, cotangent, wq, wk, wv, w1, w2, wo, vector, lengths):
    f32, bf16 = jnp.float32, jnp.bfloat16
    block, width = tokens.shape
    rows = block // CHUNKS
    unit_rows = w2.shape[0]
    units = 2 * unit_rows
    half_rows = rows * GROUP // 2
    own_rows = GROUP * block
    weight_rows = wo.shape[0]
    peers = GROUP - 1
    vmem = pl.BlockSpec(memory_space=pltpu.VMEM)
    anywhere = pl.BlockSpec(memory_space=pl.ANY)
    smem = pl.BlockSpec(memory_space=pltpu.SMEM)
    sems = pltpu.SemaphoreType.DMA
    shape = jax.ShapeDtypeStruct

    def slots(*lead):
        return pltpu.VMEM(lead + (rows, width), bf16)

    return pl.pallas_call(
        layer_kernel,
        out_shape=[
            shape((block, width), bf16),
            shape((block, width), f32),
            shape((8, width), f32),
            shape((8, units), f32),
            shape((unit_rows, width), f32),
            shape((unit_rows, width), bf16),
            shape((unit_rows, width), bf16),
            shape((2 * GROUP, weight_rows, units), bf16),
            shape((HEAD_DIM, width), f32),
            shape((CHUNKS, 2, 2, 2, 2, rows, width), bf16),
            shape((CHUNKS, 2, 2, 2, 2, rows, width), bf16),
            shape((own_rows + HALO + 2 * PAD, 3 * HEAD_DIM), bf16),
            shape((own_rows + HALO, HEAD_DIM), bf16),
            shape((2, GROUP, weight_rows, 3 * HEAD_DIM), bf16),
        ],
        in_specs=[vmem] * 2 + [anywhere] * 6 + [vmem, smem],
        out_specs=[vmem] * 4 + [anywhere] * 7 + [vmem] * 3,
        scratch_shapes=[
            slots(CHUNKS, 2, 2, 2, 2), slots(CHUNKS, 2, 2, 2, 2),
            slots(CHUNKS, 2, 2, 2), slots(2, 2, 2, 2), slots(CHUNKS, 2, 2, 2),
            slots(CHUNKS, 2, 2), slots(CHUNKS, 2), slots(CHUNKS),
            pltpu.VMEM((own_rows, units), f32),
            pltpu.VMEM((half_rows, units), bf16),
            pltpu.VMEM((units, own_rows), bf16),
            pltpu.VMEM((half_rows, units), bf16),
            pltpu.VMEM((units, own_rows), bf16),
            pltpu.VMEM((own_rows, HEAD_DIM), bf16),
            pltpu.VMEM((HEAD_DIM, own_rows), bf16),
            pltpu.VMEM((block, width), f32),
            pltpu.VMEM((block, width), f32),
            pltpu.VMEM((block, width), f32),
            pltpu.VMEM((block, 128), f32),
            pltpu.VMEM((2, GROUP, weight_rows, units), bf16),
            pltpu.VMEM((2, unit_rows, width), bf16),
            pltpu.VMEM((2, 2, weight_rows, width), bf16),
            pltpu.VMEM((2, GROUP, 8, 128), f32),
            pltpu.VMEM((8, width), f32),
            pltpu.VMEM((8, width), f32),
            pltpu.VMEM((8, units), f32),
            pltpu.VMEM((2, SPLIT, SPLIT), f32),
            pltpu.VMEM((2, SPLIT, SPLIT), bf16),
            pltpu.VMEM((2, 4, SPLIT // 4, units), bf16),
            pltpu.VMEM((1, own_rows + HALO), f32),
            pltpu.VMEM((1, own_rows + HALO + 2 * PAD), f32),
            sems((STAGES, CHUNKS, 4, 3)), sems((STAGES, CHUNKS, 4, 3)),
            sems((STAGES, CHUNKS)), sems((STAGES, CHUNKS)),
            sems((5,)), sems((5, peers)), sems((5, peers)),
            sems((peers,)), sems((peers,)),
            sems((13,)), sems((13,)), sems((3,)), sems((5, 2)), sems((3, CHUNKS)),
        ],
        compiler_params=pltpu.CompilerParams(
            collective_id=4, has_side_effects=True, vmem_limit_bytes=63 << 20
        ),
        name="layer",
    )(tokens, cotangent, wq, wk, wv, w1, w2, wo, vector, lengths)


def tail_kernel(
    qkv_ref, dout_ref, wqkv_ref, dres_ref, gwo_ref, vecg_ref, gb1_ref, lengths_ref,
    x_all, gw1_ref, w2_own, w2_early,
    input_ref, out_q, out_k, out_v, out_wo, out_w1, out_w2, vec_ref,
    xs_ref, own_part, far_part, pair_in, in_one, in_two, in_three, res_ref,
    dqkv_ref, dk_sum, dv_sum, dqkv_t, gq_own, gq_far, gq_here, gq_there,
    w1_here, w1_there, w2_sum, w2_in, wo_low, wo_in, wo_pair, wo_pair_in,
    blocks_ref, arrived, theirs, far_vec_in,
    queries_ref, keys_ref,
    hop_send, hop_recv, pair_send, pair_recv, load_sems,
    block_local, block_send, block_recv, there_send, there_recv, far_send, far_recv,
):
    f32, low = jnp.float32, qkv_ref.dtype
    block, width = dres_ref.shape
    rows = block // TAIL_CHUNKS
    weight_rows = out_q.shape[0]
    scale = HEAD_DIM ** (-0.5)
    group, base, mine, others, across, there = group_places()
    net = Traffic((hop_send, hop_recv, pair_send, pair_recv), TAIL_PLANS)
    core, chip = net.core, mine // 2
    enter(others + there)

    def far(src, dst, at, device=across):
        copy = push(src, dst, far_send.at[at], far_recv.at[at], device)
        copy.start()
        return copy

    def load(src, dst, at):
        copy = pltpu.make_async_copy(src, dst, load_sems.at[at])
        copy.start()
        return copy

    far_wo = push(
        wo_low, wo_in, far_send.at[0], far_recv.at[0], core * GROUP + 2 * chip + core
    )

    @pl.when(core != group)
    def _():
        wo_low[...] = gwo_ref[...].astype(low)
        far_wo.start()

    def blocks(pairs, at):
        here = slice(at, at + len(pairs))
        return exchange_blocks(
            pairs, (block_local.at[here], block_send.at[here], block_recv.at[here]),
            base, mine, others,
        )

    first = pl.ds(pl.multiple_of((1 - group) * GROUP, GROUP), GROUP)
    w1_far = far_blocks(
        gw1_ref.at[first], w1_there, there_send.at[0], there_recv.at[0], group, mine
    )
    x_loads = [load(x_all.at[at], xs_ref.at[at], at) for at in range(CHUNKS)]
    loads = [
        load(w2_own, w2_sum, CHUNKS),
        load(w2_early, w2_in, CHUNKS + 1),
    ]
    own_rows = GROUP * block
    write_segments(lengths_ref, group * (own_rows - HALO), keys_ref, queries_ref)
    dk_sum[...] = jnp.zeros_like(dk_sum)
    dv_sum[...] = jnp.zeros_like(dv_sum)

    def attend_back_tile(tile):
        place = pl.multiple_of(tile * TILE, TILE)
        window = pl.ds(place, WINDOW)
        queries, keys, probs = tile_probs(qkv_ref, queries_ref, keys_ref, tile)
        values = qkv_ref[window, 2 * HEAD_DIM : 3 * HEAD_DIM]
        grads = dout_ref[pl.ds(place, TILE), :]
        grad_probs = lax.dot_general(grads, values, NT, preferred_element_type=f32)
        inner = jnp.sum(probs * grad_probs, -1, keepdims=True)
        grad_scores = (probs * (grad_probs - inner)).astype(low)
        grad_q = jnp.dot(grad_scores, keys, preferred_element_type=f32)
        dqkv_ref[pl.ds(place, TILE), 0:HEAD_DIM] = (grad_q * scale).astype(low)
        dk_sum[window, :] += lax.dot_general(grad_scores, queries, TN, preferred_element_type=f32)
        dv_sum[window, :] += lax.dot_general(
            probs.astype(low), grads, TN, preferred_element_type=f32
        )

    def attend_back_two(at, carry):
        attend_back_tile(2 * at)
        attend_back_tile(2 * at + 1)
        return carry

    ext_rows = dout_ref.shape[0]
    lax.fori_loop(0, ext_rows // TILE // 2, attend_back_two, 0)
    inside = slice(PAD, PAD + ext_rows)
    dqkv_ref[:, HEAD_DIM : 2 * HEAD_DIM] = (dk_sum[inside, :] * scale).astype(low)
    dqkv_ref[:, 2 * HEAD_DIM : 3 * HEAD_DIM] = dv_sum[inside, :].astype(low)

    def rows_of(chunk, side, rows):
        places = [
            group * HALO + (slot * 2 + side) * block + chunk * rows for slot in range(GROUP // 2)
        ]
        return jnp.concatenate(
            [dqkv_ref[pl.ds(pl.multiple_of(place, rows), rows), :] for place in places], 0
        )

    x_rows = block // CHUNKS
    x_half = x_rows * GROUP // 2
    bias = jnp.zeros((1, 3 * HEAD_DIM), f32)
    for chunk in range(CHUNKS):
        for side in range(2):
            part = rows_of(chunk, side, x_rows).astype(f32)
            bias = bias + jnp.sum(part, 0, keepdims=True)
            here = slice((chunk * 2 + side) * x_half, (chunk * 2 + side + 1) * x_half)
            dqkv_t[:, here] = part.T.astype(low)

    for copy in x_loads:
        copy.wait()

    def product(at):
        columns = pl.ds(pl.multiple_of(at * SPLIT, SPLIT), SPLIT)
        total = None
        for chunk in range(CHUNKS):
            for side in range(2):
                here = slice((chunk * 2 + side) * x_half, (chunk * 2 + side + 1) * x_half)
                right = xs_ref[chunk, side, :, :, :, :, columns].reshape(x_half, SPLIT)
                term = jnp.dot(dqkv_t[:, here], right, preferred_element_type=f32)
                total = term if total is None else total + term
        return total.T

    quarter = width // SPLIT // 2

    def tile_of(ref, first):
        def body(at, carry):
            total = product(first + at).astype(low)
            ref[pl.ds(pl.multiple_of(at * 4, 4), 4)] = total.reshape(4, SPLIT // 4, 3 * HEAD_DIM)
            return carry

        lax.fori_loop(0, quarter, body, 0)

    tile_of(gq_far, (1 - group) * quarter)
    qkv_far = far_blocks(gq_far, gq_there, there_send.at[1], there_recv.at[1], group, mine)

    blocks_ref[...] = jnp.zeros_like(blocks_ref)
    lane = lax.broadcasted_iota(jnp.int32, (1, 128), 1)

    def pieces_of(low_row, high_row):
        return (
            jnp.where(lane < 64, low_row, pltpu.roll(high_row, 64, 1)),
            jnp.where(lane < 64, pltpu.roll(low_row, 64, 1), high_row),
        )

    for tile in range(GROUP):
        here = slice(tile * 128, tile * 128 + 128)
        for at, (low_row, high_row) in enumerate(((3, 4), (5, 0), (1, 2))):
            to = tile // 8 * 8 + 1 + at
            both = pieces_of(vecg_ref[low_row : low_row + 1, here], vecg_ref[high_row : high_row + 1, here])
            for odd in range(2):
                blocks_ref[tile % 8 * 2 + odd, to : to + 1, :] = both[odd]
    for half in range(2):
        for part in range(2):
            to = half * 8 + 4 + part
            here = slice((half * 2 + part) * 128, (half * 2 + part + 1) * 128)
            blocks_ref[mine, to : to + 1, :] = gb1_ref[0:1, here]
    bias_q, bias_v = bias[:, 0:HEAD_DIM], bias[:, 2 * HEAD_DIM : 3 * HEAD_DIM]
    both = pieces_of(bias_q, bias_v)
    for odd in range(2):
        blocks_ref[2 * chip + odd, pl.ds(core * 8, 1), :] = both[odd]

    vec_blocks = blocks([(blocks_ref, arrived)], 0)

    def input_part(chunk, side, dst):
        left = rows_of(chunk, side, rows)

        def body(at, carry):
            weight = wqkv_ref[at // 4, pl.ds(at % 4 * 4, 4)].reshape(SPLIT, 3 * HEAD_DIM)
            part = lax.dot_general(left, weight, NT, preferred_element_type=f32)
            columns = pl.ds(pl.multiple_of(at * SPLIT, SPLIT), SPLIT)
            dst[:, :, :, :, columns] = part.astype(low).reshape(2, 2, 2, rows, SPLIT)
            return carry

        lax.fori_loop(0, width // SPLIT, body, 0)

    def flow(chunk):
        def finish(row, columns, total):
            res_ref[pl.ds(pl.multiple_of(chunk * rows + row, 16), 16), columns] = total

        incoming = (in_one.at[chunk], in_two.at[chunk], in_three.at[chunk])
        other = far_part.at[chunk % 2]
        input_part(chunk, 1 - core, other)
        share = net.share(other, pair_in.at[chunk], 0, chunk)
        input_part(chunk, core, own_part.at[chunk])
        yield
        yield from net.scatter(
            own_part.at[chunk], pair_in.at[chunk], incoming, share, 0, chunk, finish
        )
        here = slice(chunk * rows, (chunk + 1) * rows)
        input_ref[here, :] = (dres_ref[here, :] + res_ref[here, :]).astype(low)

    def fill():
        yield
        yield
        for copy in loads:
            copy.wait()
        out_w2[...] = w2_sum[...] + w2_in[...].astype(f32)
        yield
        tile_of(gq_own, group * quarter)
        state["qkv"] = blocks([(gq_own, gq_here)], 2)
        yield
        for copy in vec_blocks:
            copy.wait()
        total = arrived[0]
        for at in range(1, GROUP):
            total = total + arrived[at]
        first, second = total[:8], total[8:]
        theirs[...] = jnp.where(group == 0, second, first)
        vec_ref[...] = jnp.where(group == 0, first, second)
        state["vec"] = far(theirs, far_vec_in, 3)

    state = {}
    step_through([flow(chunk) for chunk in range(TAIL_CHUNKS)], fill())

    share_wo = push(wo_pair, wo_pair_in, far_send.at[4], far_recv.at[4], net.pair)

    @pl.when(core == group)
    def _():
        far_wo.wait_recv()
        total = gwo_ref[...] + wo_in[...].astype(f32)
        first, second = total[:weight_rows], total[weight_rows:]
        out_wo[...] = jnp.where(core == 0, first, second)
        wo_pair[...] = jnp.where(core == 0, second, first)
        share_wo.start()

    own_first = pl.ds(pl.multiple_of(group * GROUP, GROUP), GROUP)
    w1_blocks = blocks([(gw1_ref.at[own_first], w1_here)], 1)
    state["vec"].wait()
    vec_ref[...] += far_vec_in[...]

    @pl.when(core != group)
    def _():
        far_wo.wait_send()
        share_wo.wait_recv()
        out_wo[...] = wo_pair_in[...]

    @pl.when(core == group)
    def _():
        share_wo.wait_send()

    for copy in w1_blocks + w1_far:
        copy.wait()
    unit_rows = out_w2.shape[0]
    for at in range(GROUP):
        for part in range(2):
            here = slice(part * unit_rows, (part + 1) * unit_rows)
            to = (part * GROUP + at) * unit_rows
            out_w1[:, to : to + unit_rows] = w1_here[at, :, here].astype(f32) + w1_there[
                at, :, here
            ].astype(f32)
    for copy in state["qkv"] + qkv_far:
        copy.wait()
    for at in range(GROUP):
        to = (at % 2 * 8 + at // 2) * HEAD_DIM
        for part, ref in enumerate((out_q, out_k, out_v)):
            here = slice(part * HEAD_DIM, (part + 1) * HEAD_DIM)
            ref[:, to : to + HEAD_DIM] = gq_here[at, :, here].astype(f32) + gq_there[
                at, :, here
            ].astype(f32)


def layer_tail(
    qkv, dout, wqkv, dres, gwo, vecg, gb1, lengths, x_all, gw1, w2_own, w2_early
):
    f32, bf16 = jnp.float32, jnp.bfloat16
    block, width = dres.shape
    rows = block // TAIL_CHUNKS
    weight_rows = wqkv.shape[2]
    units = gw1.shape[2]
    unit_rows = units // 2
    own_rows = GROUP * block
    peers = GROUP - 1
    vmem = pl.BlockSpec(memory_space=pltpu.VMEM)
    anywhere = pl.BlockSpec(memory_space=pl.ANY)
    smem = pl.BlockSpec(memory_space=pltpu.SMEM)
    sems = pltpu.SemaphoreType.DMA
    shape, scratch = jax.ShapeDtypeStruct, pltpu.VMEM
    heads = 3 * HEAD_DIM

    def slots(*lead):
        return scratch(lead + (rows, width), bf16)

    return pl.pallas_call(
        tail_kernel,
        out_shape=[
            shape((block, width), bf16),
            shape((weight_rows, width), f32),
            shape((weight_rows, width), f32),
            shape((weight_rows, width), f32),
            shape((weight_rows, width), f32),
            shape((weight_rows, GROUP * units), f32),
            shape((unit_rows, width), f32),
            shape((8, 128), f32),
        ],
        in_specs=[vmem] * 7 + [smem] + [anywhere] * 4,
        out_specs=[vmem] * 8,
        scratch_shapes=[
            scratch(x_all.shape, bf16),
            slots(TAIL_CHUNKS, 2, 2, 2), slots(2, 2, 2, 2), slots(TAIL_CHUNKS, 2, 2, 2),
            slots(TAIL_CHUNKS, 2, 2), slots(TAIL_CHUNKS, 2), slots(TAIL_CHUNKS),
            scratch((block, width), f32),
            scratch((own_rows + HALO, heads), bf16),
            scratch(qkv.shape[:1] + (HEAD_DIM,), f32),
            scratch(qkv.shape[:1] + (HEAD_DIM,), f32),
            scratch((heads, own_rows), bf16),
            scratch((GROUP, weight_rows, heads), bf16),
            scratch((GROUP, weight_rows, heads), bf16),
            scratch((GROUP, weight_rows, heads), bf16),
            scratch((GROUP, weight_rows, heads), bf16),
            scratch((GROUP, weight_rows, units), bf16),
            scratch((GROUP, weight_rows, units), bf16),
            scratch((unit_rows, width), f32),
            scratch((unit_rows, width), bf16),
            scratch((HEAD_DIM, width), bf16),
            scratch((HEAD_DIM, width), bf16),
            scratch((weight_rows, width), f32),
            scratch((weight_rows, width), f32),
            scratch((GROUP, 16, 128), f32),
            scratch((GROUP, 16, 128), f32),
            scratch((8, 128), f32),
            scratch((8, 128), f32),
            pltpu.VMEM((1, own_rows + HALO), f32),
            pltpu.VMEM((1, own_rows + HALO + 2 * PAD), f32),
            sems((1, TAIL_CHUNKS, 4, 3)), sems((1, TAIL_CHUNKS, 4, 3)),
            sems((1, TAIL_CHUNKS)), sems((1, TAIL_CHUNKS)),
            sems((CHUNKS + 2,)), sems((3,)), sems((3, peers)), sems((3, peers)),
            sems((2, GROUP)), sems((2, GROUP)), sems((5,)), sems((5,)),
        ],
        compiler_params=pltpu.CompilerParams(
            collective_id=5, has_side_effects=True, vmem_limit_bytes=63 << 20
        ),
        name="layer_tail",
    )(qkv, dout, wqkv, dres, gwo, vecg, gb1, lengths, x_all, gw1, w2_own, w2_early)


def grouped_device(
    tokens,
    cotangent,
    lengths,
    wq,
    bq,
    wk,
    wv,
    bv,
    wo,
    bo,
    norm1_gain,
    norm1_bias,
    w1,
    b1,
    w2,
    b2,
    norm2_gain,
    norm2_bias,
):
    f32 = jnp.float32
    vectors = [bq, bv, bo, norm1_gain, norm1_bias, b2, norm2_gain, norm2_bias, b1]
    sizes = [item.shape[0] for item in vectors]
    vector, at = jnp.zeros((1024,), f32), 0
    for item, size in zip(vectors, sizes):
        vector = vector + jnp.pad(item.astype(f32), (at, 1024 - at - size))
        at += size
    vector = vector.reshape(8, 128)

    (
        output, grad_resid_one, vec_grads, grad_b1, w2_own, _, w2_early, grad_w1, grad_wo,
        all_tokens, _, qkv, grad_out, full_qkv,
    ) = layer(tokens, cotangent, wq, wk, wv, w1, w2, wo, vector, lengths)

    input_grad, out_q, out_k, out_v, out_wo, out_w1, out_w2, sums = layer_tail(
        qkv, grad_out, full_qkv, grad_resid_one, grad_wo, vec_grads, grad_b1, lengths,
        all_tokens, grad_w1, w2_own, w2_early,
    )
    sums, at = sums.reshape(-1), 0
    small = []
    for size in sizes:
        small.append(sums[at : at + size])
        at += size
    out_bq, out_bv, out_bo, out_g1, out_s1, out_b2, out_g2, out_s2, out_b1 = small
    return (
        output, input_grad, out_q, out_bq, out_k, out_v, out_bv, out_wo, out_bo, out_g1, out_s1,
        out_w1, out_b1, out_w2, out_b2, out_g2, out_s2,
    )


def solution(mesh):
    in_specs = (
        P("dp", None),
        P("dp", None),
        P(),
        P("dp", None),
        P("dp"),
        P("dp", None),
        P("dp", None),
        P("dp"),
        P("dp", None),
        P("dp"),
        P("dp"),
        P("dp"),
        P("dp", None),
        P("dp"),
        P("dp", None),
        P("dp"),
        P("dp"),
        P("dp"),
    )
    out_specs = (
        P("dp", None),
        P("dp", None),
        P("dp", None),
        P("dp"),
        P("dp", None),
        P("dp", None),
        P("dp"),
        P("dp", None),
        P("dp"),
        P("dp"),
        P("dp"),
        P("dp", None),
        P("dp"),
        P("dp", None),
        P("dp"),
        P("dp"),
        P("dp"),
    )
    two_groups = mesh.shape["dp"] == 2 * GROUP
    return jax.shard_map(
        grouped_device if two_groups else per_device, mesh=mesh, in_specs=in_specs, out_specs=out_specs, check_vma=False
    )
```

```python
import functools

import jax
import jax.numpy as jnp
from jax import lax
from jax.experimental import pallas as pl
from jax.experimental.pallas import tpu as pltpu
from jax.sharding import PartitionSpec as P

HEADS = 16
HEAD_DIM = 128
SEQ_MAX = 160
SPAN = 3

GROUP = 16
HALO = 256
WINDOW = 512
TILE = 128
MESH_ID = pl.DeviceIdType.MESH
VMEM_LIMIT = 60 << 20


norm_eps = 1e-05


def layer_norm(residual, gain_vec, shift_vec):
    mean_val = jnp.mean(residual, axis=-1, keepdims=True)
    centred = residual - mean_val
    var_val = jnp.mean(centred * centred, axis=-1, keepdims=True)
    return centred * lax.rsqrt(var_val + norm_eps) * gain_vec + shift_vec


def gelu_tanh(values):
    return jax.nn.gelu(values, approximate=True)


def plan_layout(lengths, tok_dev):
    starts = jnp.cumsum(lengths) - lengths
    owner_first = starts // tok_dev
    return (starts, starts, lengths, owner_first)


def to_owners(shard, layout, dev_count, piece_rows):
    starts, owner_start, owner_length, owner_first = layout
    tok_dev = shard.shape[0]
    feat_width = shard.shape[1]
    device = lax.axis_index("dp")
    held_rows = lax.all_to_all(
        shard.reshape(dev_count, piece_rows, feat_width),
        "dp",
        split_axis=0,
        concat_axis=0,
        tiled=True,
    )
    held_rows = held_rows.reshape(dev_count * piece_rows, feat_width)
    slot_ids = jnp.arange(SPAN * piece_rows, dtype=jnp.int32)
    shard_step = slot_ids // piece_rows
    within = slot_ids % piece_rows
    source = owner_first[:, None] + shard_step[None, :]
    global_row = source * tok_dev + device * piece_rows + within[None, :]
    inside = (
        (global_row >= owner_start[:, None])
        & (global_row < (owner_start + owner_length)[:, None])
        & (source < dev_count)
    )
    picked = held_rows[jnp.clip(source, 0, dev_count - 1) * piece_rows + within[None, :]]
    outgoing = jnp.where(inside[:, :, None], picked, jnp.zeros((), picked.dtype))
    arrived = lax.all_to_all(outgoing, "dp", split_axis=0, concat_axis=0, tiled=True)
    arrived = arrived.reshape(dev_count * SPAN * piece_rows, feat_width)
    my_start = owner_start[device]
    my_length = owner_length[device]
    my_first = owner_first[device]
    places = jnp.arange(SEQ_MAX, dtype=jnp.int32)
    global_pos = my_start + places
    shard_of = global_pos // tok_dev
    offset_in = global_pos % tok_dev
    slot_index = (
        offset_in // piece_rows * (SPAN * piece_rows)
        + (shard_of - my_first) * piece_rows
        + offset_in % piece_rows
    )
    valid_rows = places < my_length
    slot_index = jnp.where(valid_rows, slot_index, 0)
    owned = jnp.where(valid_rows[:, None], arrived[slot_index], jnp.zeros((), arrived.dtype))
    return (owned, valid_rows)


def to_order(owned, layout, dev_count, piece_rows, tok_dev):
    starts, owner_start, owner_length, owner_first = layout
    feat_width = owned.shape[1]
    device = lax.axis_index("dp")
    my_start = owner_start[device]
    my_length = owner_length[device]
    my_first = owner_first[device]
    slot_ids = jnp.arange(SPAN * piece_rows, dtype=jnp.int32)
    shard_step = slot_ids // piece_rows
    within = slot_ids % piece_rows
    targets = jnp.arange(dev_count, dtype=jnp.int32)
    global_row = (
        (my_first + shard_step)[None, :] * tok_dev + targets[:, None] * piece_rows + within[None, :]
    )
    place_row = global_row - my_start
    inside = (place_row >= 0) & (place_row < my_length)
    picked = owned[jnp.clip(place_row, 0, owned.shape[0] - 1)]
    outgoing = jnp.where(inside[:, :, None], picked, jnp.zeros((), picked.dtype))
    returned = lax.all_to_all(outgoing, "dp", split_axis=0, concat_axis=0, tiled=True)
    returned = returned.reshape(dev_count * SPAN * piece_rows, feat_width)
    sources = jnp.arange(dev_count, dtype=jnp.int32)
    within_piece = jnp.arange(piece_rows, dtype=jnp.int32)
    row_ids = sources[:, None] * tok_dev + device * piece_rows + within_piece[None, :]
    seq_of = jnp.sum((row_ids[:, :, None] >= starts[None, None, :]).astype(jnp.int32), 2) - 1
    slot_index = (
        seq_of * (SPAN * piece_rows)
        + (sources[:, None] - owner_first[seq_of]) * piece_rows
        + within_piece[None, :]
    )
    pieces = returned[slot_index]
    ordered = lax.all_to_all(pieces, "dp", split_axis=0, concat_axis=0, tiled=True)
    return ordered.reshape(tok_dev, feat_width)


def per_device(
    tokens,
    cotangent,
    lengths,
    wq,
    bq,
    wk,
    wv,
    bv,
    wo,
    bo,
    norm1_gain,
    norm1_bias,
    w1,
    b1,
    w2,
    b2,
    norm2_gain,
    norm2_bias,
):
    f32 = jnp.float32
    bf16 = jnp.bfloat16
    dev_count = lax.axis_size("dp")
    tok_dev = tokens.shape[0]
    feat_width = tokens.shape[1]
    piece_rows = tok_dev // dev_count
    layout = plan_layout(lengths, tok_dev)
    joined, valid_rows = to_owners(
        jnp.concatenate([tokens, cotangent], 1), layout, dev_count, piece_rows
    )
    inputs = joined[:, :feat_width]
    upstream = joined[:, feat_width:].astype(f32)
    slot_count = inputs.shape[0]
    score_scale = HEAD_DIM ** (-0.5)
    full_wq, full_wk, full_wv, full_wo, full_bq, full_bv, full_bo, gain_one, shift_one = (
        lax.all_gather(wq, "dp", axis=0, tiled=True),
        lax.all_gather(wk, "dp", axis=0, tiled=True),
        lax.all_gather(wv, "dp", axis=0, tiled=True),
        lax.all_gather(wo, "dp", axis=0, tiled=True),
        lax.all_gather(bq, "dp", axis=0, tiled=True),
        lax.all_gather(bv, "dp", axis=0, tiled=True),
        lax.all_gather(bo, "dp", axis=0, tiled=True),
        lax.all_gather(norm1_gain, "dp", axis=0, tiled=True),
        lax.all_gather(norm1_bias, "dp", axis=0, tiled=True),
    )
    queries = (
        (jnp.dot(inputs, full_wq, preferred_element_type=f32) + full_bq.astype(f32))
        .astype(bf16)
        .reshape(slot_count, HEADS, HEAD_DIM)
    )
    keys_low = (
        jnp.dot(inputs, full_wk, preferred_element_type=f32)
        .astype(bf16)
        .reshape(slot_count, HEADS, HEAD_DIM)
    )
    values_low = (
        (jnp.dot(inputs, full_wv, preferred_element_type=f32) + full_bv.astype(f32))
        .astype(bf16)
        .reshape(slot_count, HEADS, HEAD_DIM)
    )
    scores = jnp.einsum("qhd,khd->hqk", queries, keys_low, preferred_element_type=f32) * score_scale
    scores = jnp.where(valid_rows[None, None, :], scores, -1e30)
    row_max = jnp.max(scores, -1, keepdims=True)
    row_total = jnp.sum(jnp.exp(scores - row_max), -1, keepdims=True)
    log_total = row_max + jnp.log(row_total)
    attn_probs = jnp.exp(scores - log_total).astype(bf16)
    attended = jnp.einsum("hqk,khd->qhd", attn_probs, values_low, preferred_element_type=f32)
    attended = attended.reshape(slot_count, feat_width).astype(bf16)
    branch = jnp.dot(attended, full_wo, preferred_element_type=f32) + full_bo.astype(f32)
    resid_one = inputs.astype(f32) + branch
    hidden, norm_one_back = jax.vjp(
        layer_norm, resid_one, gain_one.astype(f32), shift_one.astype(f32)
    )
    hidden_low = hidden.astype(bf16)
    full_w1, full_w2, full_b1, full_b2, gain_two, shift_two = (
        lax.all_gather(w1, "dp", axis=0, tiled=True),
        lax.all_gather(w2, "dp", axis=0, tiled=True),
        lax.all_gather(b1, "dp", axis=0, tiled=True),
        lax.all_gather(b2, "dp", axis=0, tiled=True),
        lax.all_gather(norm2_gain, "dp", axis=0, tiled=True),
        lax.all_gather(norm2_bias, "dp", axis=0, tiled=True),
    )
    upward = jnp.dot(hidden_low, full_w1, preferred_element_type=f32) + full_b1.astype(f32)
    activ, gelu_back = jax.vjp(gelu_tanh, upward)
    activ_low = activ.astype(bf16)
    mixed = jnp.dot(activ_low, full_w2, preferred_element_type=f32) + full_b2.astype(f32)
    resid_two = hidden + mixed
    normed, norm_two_back = jax.vjp(
        layer_norm, resid_two, gain_two.astype(f32), shift_two.astype(f32)
    )
    result = jnp.where(valid_rows[:, None], normed, 0.0).astype(bf16)
    output = to_order(result, layout, dev_count, piece_rows, tok_dev)
    back_w1, back_w2 = (
        lax.all_gather(w1, "dp", axis=0, tiled=True),
        lax.all_gather(w2, "dp", axis=0, tiled=True),
    )
    grad_resid_two, grad_gain_two, grad_shift_two = norm_two_back(upstream)
    grad_mixed = grad_resid_two.astype(bf16)
    grad_bias_two = jnp.sum(grad_mixed.astype(f32), 0)
    grad_activ = jnp.einsum("td,fd->tf", grad_mixed, back_w2, preferred_element_type=f32)
    grad_upward = gelu_back(grad_activ)[0].astype(bf16)
    grad_bias_one = jnp.sum(grad_upward.astype(f32), 0)
    grad_hidden = grad_resid_two + jnp.einsum(
        "tf,df->td", grad_upward, back_w1, preferred_element_type=f32
    )
    grad_w2 = jnp.einsum("tf,td->fd", activ_low, grad_mixed, preferred_element_type=f32)
    grad_w1 = jnp.einsum("td,tf->df", hidden_low, grad_upward, preferred_element_type=f32)
    mlp_grads = (
        lax.psum_scatter(grad_w1, "dp", scatter_dimension=0, tiled=True),
        lax.psum_scatter(grad_w2, "dp", scatter_dimension=0, tiled=True),
        lax.psum_scatter(grad_bias_one, "dp", scatter_dimension=0, tiled=True),
        lax.psum_scatter(grad_bias_two, "dp", scatter_dimension=0, tiled=True),
        lax.psum_scatter(grad_gain_two, "dp", scatter_dimension=0, tiled=True),
        lax.psum_scatter(grad_shift_two, "dp", scatter_dimension=0, tiled=True),
    )
    back_wq, back_wk, back_wv, back_wo = (
        lax.all_gather(wq, "dp", axis=0, tiled=True),
        lax.all_gather(wk, "dp", axis=0, tiled=True),
        lax.all_gather(wv, "dp", axis=0, tiled=True),
        lax.all_gather(wo, "dp", axis=0, tiled=True),
    )
    grad_resid_one, grad_gain_one, grad_shift_one = norm_one_back(grad_hidden)
    grad_branch = grad_resid_one.astype(bf16)
    grad_bo = jnp.sum(grad_branch.astype(f32), 0)
    grad_wo = jnp.einsum("tc,td->cd", attended, grad_branch, preferred_element_type=f32)
    grad_attended = jnp.einsum(
        "td,cd->tc", grad_branch, back_wo, preferred_element_type=f32
    ).astype(bf16)
    grad_attended = grad_attended.reshape(slot_count, HEADS, HEAD_DIM)
    re_scores = (
        jnp.einsum("qhd,khd->hqk", queries, keys_low, preferred_element_type=f32) * score_scale
    )
    re_scores = jnp.where(valid_rows[None, None, :], re_scores, -1e30)
    re_probs = jnp.exp(re_scores - log_total)
    re_probs_low = re_probs.astype(bf16)
    grad_values = jnp.einsum(
        "hqk,qhd->khd", re_probs_low, grad_attended, preferred_element_type=f32
    ).astype(bf16)
    grad_probs = jnp.einsum("qhd,khd->hqk", grad_attended, values_low, preferred_element_type=f32)
    grad_scores = re_probs * (grad_probs - jnp.sum(re_probs * grad_probs, -1, keepdims=True))
    grad_scores_low = grad_scores.astype(bf16)
    grad_queries = (
        jnp.einsum("hqk,khd->qhd", grad_scores_low, keys_low, preferred_element_type=f32)
        * score_scale
    ).astype(bf16)
    grad_keys = (
        jnp.einsum("hqk,qhd->khd", grad_scores_low, queries, preferred_element_type=f32)
        * score_scale
    ).astype(bf16)
    grad_queries = grad_queries.reshape(slot_count, feat_width)
    grad_keys = grad_keys.reshape(slot_count, feat_width)
    grad_values = grad_values.reshape(slot_count, feat_width)
    grad_bq = jnp.sum(grad_queries.astype(f32), 0)
    grad_bv = jnp.sum(grad_values.astype(f32), 0)
    grad_wq = jnp.einsum("tc,td->cd", inputs, grad_queries, preferred_element_type=f32)
    grad_wk = jnp.einsum("tc,td->cd", inputs, grad_keys, preferred_element_type=f32)
    grad_wv = jnp.einsum("tc,td->cd", inputs, grad_values, preferred_element_type=f32)
    grad_input = grad_resid_one + jnp.einsum(
        "td,cd->tc", grad_queries, back_wq, preferred_element_type=f32
    )
    grad_input = grad_input + jnp.einsum(
        "td,cd->tc", grad_keys, back_wk, preferred_element_type=f32
    )
    grad_input = grad_input + jnp.einsum(
        "td,cd->tc", grad_values, back_wv, preferred_element_type=f32
    )
    grad_input = jnp.where(valid_rows[:, None], grad_input, 0.0).astype(bf16)
    attn_grads = (
        lax.psum_scatter(grad_wq, "dp", scatter_dimension=0, tiled=True),
        lax.psum_scatter(grad_wk, "dp", scatter_dimension=0, tiled=True),
        lax.psum_scatter(grad_wv, "dp", scatter_dimension=0, tiled=True),
        lax.psum_scatter(grad_wo, "dp", scatter_dimension=0, tiled=True),
        lax.psum_scatter(grad_bq, "dp", scatter_dimension=0, tiled=True),
        lax.psum_scatter(grad_bv, "dp", scatter_dimension=0, tiled=True),
        lax.psum_scatter(grad_bo, "dp", scatter_dimension=0, tiled=True),
        lax.psum_scatter(grad_gain_one, "dp", scatter_dimension=0, tiled=True),
        lax.psum_scatter(grad_shift_one, "dp", scatter_dimension=0, tiled=True),
    )
    sum_w1, sum_w2, sum_b1, sum_b2, sum_g2, sum_s2 = mlp_grads
    sum_wq, sum_wk, sum_wv, sum_wo, sum_bq, sum_bv, sum_bo, sum_g1, sum_s1 = attn_grads
    input_grad = to_order(grad_input, layout, dev_count, piece_rows, tok_dev)
    return (
        output,
        input_grad,
        sum_wq,
        sum_bq,
        sum_wk,
        sum_wv,
        sum_bv,
        sum_wo,
        sum_bo,
        sum_g1,
        sum_s1,
        sum_w1,
        sum_b1,
        sum_w2,
        sum_b2,
        sum_g2,
        sum_s2,
    )


def flip(device, bit):
    step = 1 << bit
    return device + step - 2 * step * ((device // step) % 2)


def chip_bits(device):
    return [(device // 2) % 2, (device // 4) % 2, (device // 8) % 2]


def enter(partners):
    barrier = pltpu.get_barrier_semaphore()
    for partner in partners:
        pl.semaphore_signal(barrier, inc=1, device_id=(partner,), device_id_type=MESH_ID)
    pl.semaphore_wait(barrier, len(partners))


def push(src, dst, send_sem, recv_sem, device):
    return pltpu.make_async_remote_copy(
        src_ref=src,
        dst_ref=dst,
        send_sem=send_sem,
        recv_sem=recv_sem,
        device_id=(device,),
        device_id_type=MESH_ID,
    )


def exchange_blocks(pairs, sems, base, mine, others):
    local_sem, send_sem, recv_sem = sems
    copies = []
    for at, (src, dst) in enumerate(pairs):
        for step, other in enumerate(others):
            copy = push(
                src.at[other - base],
                dst.at[mine],
                send_sem.at[at, step],
                recv_sem.at[at, step],
                other,
            )
            copy.start()
            copies.append(copy)
        local = pltpu.make_async_copy(src.at[mine], dst.at[mine], local_sem.at[at])
        local.start()
        copies.append(local)
    return copies


def exchange_columns(source, to, sems, base, mine, others):
    local_sem, send_sem, recv_sem = sems
    copies = []
    for step, other in enumerate(others):
        copy = push(source(other - base), to, send_sem.at[step], recv_sem.at[step], other)
        copy.start()
        copies.append(copy)
    copy = pltpu.make_async_copy(source(mine), to, local_sem)
    copy.start()
    return copies + [copy]


def far_blocks(src, dst, send_sem, recv_sem, group, mine):
    copies = []
    for step in range(GROUP):
        member = (mine + step) % GROUP
        copy = push(
            src.at[member],
            dst.at[mine],
            send_sem.at[step],
            recv_sem.at[step],
            (1 - group) * GROUP + member,
        )
        copy.start()
        copies.append(copy)
    return copies


def group_places():
    device = lax.axis_index("dp")
    base = device // GROUP * GROUP
    mine = device % GROUP
    others = [base + (mine + step) % GROUP for step in range(1, GROUP)]
    across = (device + GROUP) % (2 * GROUP)
    there = [GROUP - base + (mine + step) % GROUP for step in range(GROUP)]
    return device // GROUP, base, mine, others, across, there


def write_segments(lengths_ref, first, keys_ref, queries_ref):
    f32 = jnp.float32
    rows = queries_ref.shape[1]

    def numbers(ref, ahead):
        ids = first - ahead + lax.broadcasted_iota(jnp.int32, ref.shape, 1)
        total = jnp.zeros(ref.shape, jnp.int32)
        start = jnp.int32(0)
        for at in range(lengths_ref.shape[0]):
            total = total + (ids >= start).astype(jnp.int32)
            start = start + lengths_ref[at]
        return total.astype(f32)

    queries_ref[...] = numbers(queries_ref, 0)
    place = lax.broadcasted_iota(jnp.int32, keys_ref.shape, 1)
    inside = (place >= PAD) & (place < PAD + rows)
    keys_ref[...] = jnp.where(inside, numbers(keys_ref, PAD), -1.0)


def tile_probs(qkv_ref, queries_ref, keys_ref, tile):
    f32 = jnp.float32
    place = pl.multiple_of(tile * TILE, TILE)
    row = pl.multiple_of(PAD + place, 64)
    window = pl.ds(place, WINDOW)
    queries = qkv_ref[pl.ds(row, TILE), 0:HEAD_DIM]
    keys = qkv_ref[window, HEAD_DIM : 2 * HEAD_DIM]
    scores = lax.dot_general(queries, keys, NT, preferred_element_type=f32)
    own = jnp.broadcast_to(queries_ref[0:1, pl.ds(place, TILE)], (TILE, TILE)).T[:, 0:1]
    scores = jnp.where(own == keys_ref[0:1, window], scores * HEAD_DIM ** (-0.5), -1e30)
    weights = jnp.exp(scores - jnp.max(scores, -1, keepdims=True))
    return queries, keys, weights * (1.0 / jnp.sum(weights, -1, keepdims=True))


CHUNKS = 2
TAIL_CHUNKS = 2
THIRDS = (((0, 768), (0, 1, 2)), ((768, 640), (1, 2, 0)), ((1408, 640), (2, 0, 1)))
LIGHT = (
    ((0, 512), (1, 2, 0)), ((512, 512), (0, 2, 1)), ((1024, 512), (1, 0, 2)), ((1536, 512), (0, 1, 2)),
)
PLANS = (THIRDS, LIGHT) + (THIRDS,) * 5
TAIL_PLANS = (LIGHT,)
SPLIT = 256
PAD = (WINDOW - TILE) // 2
REACH = SEQ_MAX
STAGES = 7


def step_through(flows, fillers=None):
    waiting, alive = list(flows), []
    while waiting or alive:
        if waiting:
            alive.append(waiting.pop(0))
        alive = [flow for flow in alive if next(flow, "done") != "done"]
        if fillers is not None:
            next(fillers, None)
    if fillers is not None:
        for _ in fillers:
            pass


class Traffic:
    def __init__(self, sems, plans):
        self.plans = plans
        self.hop_send, self.hop_recv, self.pair_send, self.pair_recv = sems
        device = lax.axis_index("dp")
        self.core = device % 2
        self.bits = chip_bits(device)
        self.partners = [flip(device, 1), flip(device, 2), flip(device, 3)]
        self.pair = flip(device, 0)

    def chips(self, ref, values, columns):
        return ref.at[values[2], values[1], values[0], :, columns]

    def push(self, src, dst, stage, chunk, part, step):
        copy = push(
            src, dst,
            self.hop_send.at[stage, chunk, part, step],
            self.hop_recv.at[stage, chunk, part, step],
            self.partners[self.plans[stage][part][1][step]],
        )
        copy.start()
        return copy

    def share(self, src, dst, stage, chunk):
        copy = push(
            src, dst, self.pair_send.at[stage, chunk], self.pair_recv.at[stage, chunk], self.pair
        )
        copy.start()
        return copy

    def gather(self, slots, stage, chunk):
        mine = slots.at[self.core]
        hops = {}
        for step in range(3):
            for part, ((first, count), order) in enumerate(self.plans[stage]):
                if step:
                    hops[part, step - 1].wait_recv()
                values = list(self.bits)
                for dim in order[:step]:
                    values[dim] = slice(None)
                view = self.chips(mine, values, pl.ds(first, count))
                hops[part, step] = self.push(view, view, stage, chunk, part, step)
            yield
        for part in range(len(self.plans[stage])):
            hops[part, 2].wait_recv()
        share = self.share(mine, mine, stage, chunk)
        for copy in hops.values():
            copy.wait_send()
        return share

    def scatter(self, own, pair_in, incoming, share, stage, chunk, finish):
        rows = own.shape[-2]
        f32 = jnp.float32
        hops = {}
        share.wait()
        for step in range(4):
            for part, ((first, count), order) in enumerate(self.plans[stage]):
                columns = pl.ds(first, count)
                if step:
                    hops[part, step - 1].wait_recv()
                values = list(self.bits)
                free = ()
                if step < 3:
                    values[order[step]] = 1 - self.bits[order[step]]
                    free = order[step + 1 :]
                for mask in range(1 << len(free)):
                    slot = list(values)
                    for place, dim in enumerate(free):
                        slot[dim] = (mask >> place) & 1
                    where = (slot[2], slot[1], slot[0])
                    lefts = [
                        tuple(slot[dim] for dim in (2, 1, 0) if dim not in order[: back + 1])
                        for back in range(step)
                    ]

                    def add(index, carry, step=step, where=where, lefts=lefts, columns=columns):
                        row = pl.multiple_of(index * 32, 32)
                        at = (pl.ds(row, 32), columns)
                        total = own[where + at].astype(f32) + pair_in[where + at].astype(f32)
                        for back in range(step):
                            total = total + incoming[back][lefts[back] + at].astype(f32)
                        if step < 3:
                            own[where + at] = total.astype(own.dtype)
                        else:
                            finish(row, columns, total)
                        return carry

                    lax.fori_loop(0, rows // 32, add, 0)
                if step == 3:
                    continue
                for dim in free:
                    values[dim] = slice(None)
                left = tuple(slice(None) for _ in free)
                hops[part, step] = self.push(
                    self.chips(own, values, columns),
                    incoming[step].at[left + (slice(None), columns)],
                    stage, chunk, part, step,
                )
            if step < 3:
                yield
        for copy in hops.values():
            copy.wait_send()


def gelu_slope(up):
    inner = 0.7978845608028654 * (up + 0.044715 * (up * up * up))
    tanh = jnp.tanh(inner)
    return 0.5 * (1.0 + tanh) + 0.5 * up * (1.0 - tanh * tanh) * (
        0.7978845608028654 * (1.0 + 0.134145 * (up * up))
    )


NT = (((1,), (1,)), ((), ()))
TN = (((0,), (0,)), ((), ()))


def layer_kernel(
    tok_ref, cot_ref, wq_ref, wk_ref, wv_ref, w1_ref, w2_ref, wo_ref, vec_ref, lengths_ref,
    out_ref, dres_ref, vecg_ref, gb1_ref, gw2_own, gw2_far, gw2_in, gw1_ref, gwo_ref,
    x_all, h_all, qkv_ref, dout_ref, wqkv_ref,
    all_h, all_m, own_part, far_part, pair_in, in_one, in_two, in_three,
    up_ref, act_ref, act_t, dup_ref, dup_t, att_ref, att_t, res_ref, hid_ref, norm_ref, scale_ref,
    w1_all, w2_all, wo_all, vec_all, low_ref, high_ref, b1_ref, stage_ref, stage_low, stage_w1,
    queries_ref, keys_ref,
    hop_send, hop_recv, pair_send, pair_recv,
    block_local, block_send, block_recv, vec_send, vec_recv, far_send, far_recv,
    local_sems, out_sems, spill_sems,
):
    f32, low = jnp.float32, tok_ref.dtype
    block, width = tok_ref.shape
    rows = block // CHUNKS
    half_rows = rows * GROUP // 2
    own_rows = GROUP * block
    units = w1_all.shape[-1]
    group, base, mine, others, across, there = group_places()
    net = Traffic((hop_send, hop_recv, pair_send, pair_recv), PLANS)
    core, bits = net.core, net.bits
    chip = mine // 2
    head = core * 8 + chip
    own_slot = (core, bits[2], bits[1], bits[0])
    ext = PAD + group * HALO
    enter(others + there)

    def far(src, dst, at, device=across):
        copy = push(src, dst, far_send.at[at], far_recv.at[at], device)
        copy.start()
        return copy

    def local(src, dst, at):
        copy = pltpu.make_async_copy(src, dst, local_sems.at[at])
        copy.start()
        return copy

    early = w2_ref.shape[0] // 4 * 3
    far_vec = far(vec_ref, vec_all.at[group, mine], 0)
    near = [
        local(vec_ref, vec_all.at[group, mine], 0),
        local(w2_ref, w2_all.at[group], 1),
        local(wo_ref, wo_all.at[group, core], 2),
    ]
    w2_first, w2_last = pl.ds(0, early), pl.ds(early, w2_ref.shape[0] - early)
    far_w2 = [far(w2_ref.at[w2_first, :], w2_all.at[group, w2_first, :], 1)]

    def block_sems(at):
        return block_local.at[at], block_send.at[at], block_recv.at[at]

    qkv_blocks = []
    for part, ref in enumerate((wq_ref, wk_ref, wv_ref)):

        def head_columns(member, ref=ref):
            first = pl.multiple_of((member % 2 * 8 + member // 2) * HEAD_DIM, HEAD_DIM)
            return ref.at[:, pl.ds(first, HEAD_DIM)]

        qkv_blocks += exchange_columns(
            head_columns, wqkv_ref.at[group, mine, :, pl.ds(part * HEAD_DIM, HEAD_DIM)],
            block_sems(part), base, mine, others,
        )
    for chunk in range(CHUNKS):
        all_m[(chunk,) + own_slot] = tok_ref[chunk * rows : (chunk + 1) * rows, :]
    wo_near = push(
        wo_ref, wo_all.at[group, core], far_send.at[2], far_recv.at[2], net.pair
    )
    wo_near.start()

    unsent = own_rows + REACH - group * (own_rows + REACH)
    for first in (0, qkv_ref.shape[0] - PAD):
        qkv_ref[first : first + PAD, :] = jnp.zeros((PAD, qkv_ref.shape[1]), low)
    qkv_ref[pl.ds(pl.multiple_of(PAD + unsent, 32), HALO - REACH), :] = jnp.zeros(
        (HALO - REACH, qkv_ref.shape[1]), low
    )
    dout_ref[pl.ds(pl.multiple_of(unsent, 32), HALO - REACH), :] = jnp.zeros(
        (HALO - REACH, HEAD_DIM), low
    )
    vecg_ref[...] = jnp.zeros_like(vecg_ref)
    gb1_ref[...] = jnp.zeros_like(gb1_ref)

    write_segments(lengths_ref, group * (own_rows - HALO), keys_ref, queries_ref)

    def row_at(chunk, side):
        return pl.multiple_of((chunk * 2 + side) * half_rows, half_rows)

    def flat(ref, chunk, side, columns=slice(None)):
        return ref[chunk, side, :, :, :, :, columns].reshape(half_rows, -1)

    def tiles(count, body):
        def step(at, carry):
            body(at, pl.ds(pl.multiple_of(at * SPLIT, SPLIT), SPLIT))
            return carry

        lax.fori_loop(0, count // SPLIT, step, 0)

    def pieces(chunk, side):
        return [
            pl.multiple_of((slot * 2 + side) * block + chunk * rows, rows)
            for slot in range(GROUP // 2)
        ]

    def project_half(chunk, side, which):
        columns = pl.ds(pl.multiple_of(which * (width // 2), width // 2), width // 2)
        weight = wqkv_ref[which].reshape(width // 2, -1)
        return jnp.dot(flat(all_m, chunk, side, columns), weight, preferred_element_type=f32)

    def spill(src, dst, chunk, at):
        copy = pltpu.make_async_copy(src.at[chunk], dst.at[chunk], spill_sems.at[at, chunk])
        copy.start()
        return copy

    wide = slice(0, 3 * HEAD_DIM)
    spills = {}

    def token_flow(chunk):
        share = yield from net.gather(all_m.at[chunk], 0, chunk)
        up_ref[pl.ds(row_at(chunk, core), half_rows), wide] = project_half(chunk, core, group)
        yield
        share.wait()
        up_ref[pl.ds(row_at(chunk, 1 - core), half_rows), wide] = project_half(
            chunk, 1 - core, group
        )
        spills[0, chunk] = spill(all_m, x_all, chunk, 0)

    def weight_flow():
        yield
        for copy in qkv_blocks:
            copy.wait()
        state["far_qkv"] = far(wqkv_ref.at[group], wqkv_ref.at[group], 3)
        yield
        for copy in near:
            copy.wait()
        far_vec.wait()
        both = vec_all.at[:, mine]
        state["vec"] = []
        for step, other in enumerate(others):
            copy = push(both, both, vec_send.at[step], vec_recv.at[step], other)
            copy.start()
            state["vec"].append(copy)
        yield

    state = {"backs": 0}
    flows = [token_flow(chunk) for chunk in range(CHUNKS)]
    step_through([flows[0], weight_flow()] + flows[1:])

    for copy in state["vec"]:
        copy.wait()
    lane = lax.broadcasted_iota(jnp.int32, (8, 128), 1)
    for at in range(GROUP):
        first = vec_all[at // 8, at % 8 * 2]
        second = vec_all[at // 8, at % 8 * 2 + 1]
        here = slice(at * 128, at * 128 + 128)
        low_ref[:, here] = jnp.where(lane < 64, first, pltpu.roll(second, 64, 1))
        high_ref[:, here] = jnp.where(lane < 64, pltpu.roll(first, 64, 1), second)
    for half in range(2):
        for part in range(2):
            b1_ref[0:1, half * 256 + part * 128 : half * 256 + part * 128 + 128] = vec_all[
                half, mine, 4 + part : 5 + part, :
            ]
    head_at = pl.ds(pl.multiple_of(head * HEAD_DIM, HEAD_DIM), HEAD_DIM)
    bias_q, bias_v = low_ref[0:1, head_at], high_ref[0:1, head_at]
    bias_qkv = jnp.concatenate([bias_q, jnp.zeros_like(bias_q), bias_v], 1)
    bo, shift_one, gain_two = low_ref[1:2, :], low_ref[2:3, :], low_ref[3:4, :]
    gain_one, b2, shift_two = high_ref[1:2, :], high_ref[2:3, :], high_ref[3:4, :]

    state["far_qkv"].wait()
    for chunk in range(CHUNKS):
        for side in range(2):
            here = pl.ds((chunk * 2 + side) * half_rows, half_rows)
            total = up_ref[here, wide] + project_half(chunk, side, 1 - group) + bias_qkv
            total = total.astype(low)
            for slot, place in enumerate(pieces(chunk, side)):
                qkv_ref[pl.ds(pl.multiple_of(ext + place, rows), rows), :] = total[
                    slot * rows : (slot + 1) * rows
                ]
    near_edge = own_rows - REACH - group * (own_rows - REACH - HALO)
    far_edge = HALO - REACH + group * (own_rows - HALO + REACH)
    halo_src = pl.ds(pl.multiple_of(PAD + near_edge, 32), REACH)
    halo_dst = pl.ds(pl.multiple_of(PAD + far_edge, 32), REACH)
    key_value = pl.ds(HEAD_DIM, 2 * HEAD_DIM)
    far_halo = far(qkv_ref.at[halo_src, key_value], qkv_ref.at[halo_dst, key_value], 6)
    far_wo_to = (1 - group) * GROUP + 2 * chip + group
    far_wo = push(
        wo_ref, wo_all.at[group, core], far_send.at[4 + core], far_recv.at[4 + core], far_wo_to
    )
    far_wo.start()
    far_w2.append(far(w2_ref.at[w2_last, :], w2_all.at[group, w2_last, :], 8))
    w1_blocks = []
    for part in range(2):

        def w1_columns(member, part=part):
            first = pl.multiple_of((part * GROUP + member) * SPLIT, SPLIT)
            return w1_ref.at[:, pl.ds(first, SPLIT)]

        w1_blocks += exchange_columns(
            w1_columns, w1_all.at[group, mine, :, pl.ds(part * SPLIT, SPLIT)],
            block_sems(3 + part), base, mine, others,
        )

    def attend_tile(at):
        tile = at + group * (GROUP - 1 - 2 * at)
        inner = group * (HALO // TILE) + tile
        _, _, probs = tile_probs(qkv_ref, queries_ref, keys_ref, inner)
        window = pl.ds(pl.multiple_of(inner * TILE, TILE), WINDOW)
        values = qkv_ref[window, 2 * HEAD_DIM : 3 * HEAD_DIM]
        out = jnp.dot(probs.astype(low), values, preferred_element_type=f32)
        att_ref[pl.ds(pl.multiple_of(tile * TILE, TILE), TILE), :] = out.astype(low)

    def attend_two(at, carry):
        attend_tile(2 * at)
        attend_tile(2 * at + 1)
        return carry

    lax.fori_loop(0, own_rows // TILE // 2 - 1, attend_two, 0)
    far_halo.wait()
    for copy in w1_blocks:
        copy.wait()
    far_w1 = far(w1_all.at[group], w1_all.at[group], 7)
    attend_tile(own_rows // TILE - 2)
    attend_tile(own_rows // TILE - 1)
    for chunk in range(CHUNKS):
        spills[0, chunk].wait()
    wo_near.wait()
    far_wo.wait_send()

    @pl.when(core != group)
    def _():
        for at in range(2):
            push(
                wo_ref, wo_all.at[1 - group, at], far_send.at[4 + at], far_recv.at[4 + at],
                far_wo_to,
            ).wait_recv()

    def branch_part(chunk, side, dst):
        rows_in = jnp.concatenate([att_ref[pl.ds(at, rows), :] for at in pieces(chunk, side)], 0)
        att_t[:, pl.ds(row_at(chunk, side), half_rows)] = rows_in.astype(f32).T.astype(low)

        def body(at, columns):
            weight = wo_all[core, :, :, columns].reshape(HEAD_DIM, SPLIT)
            part = jnp.dot(rows_in, weight, preferred_element_type=f32)
            dst[:, :, :, :, columns] = part.astype(low).reshape(2, 2, 2, rows, SPLIT)

        tiles(width, body)

    def upward(chunk, side):
        here = pl.ds(row_at(chunk, side), half_rows)

        def body(at, columns):
            weight = w1_all[:, :, :, columns].reshape(width, SPLIT)
            up = jnp.dot(flat(all_h, chunk, side), weight, preferred_element_type=f32)
            up = up + b1_ref[0:1, columns]
            up_ref[here, columns] = up
            act = gelu_tanh(up)
            act_ref[:, columns] = act.astype(low)
            act_t[columns, here] = act.T.astype(low)

        tiles(units, body)

    def downward(dst):
        def body(at, columns):
            weight = w2_all[:, :, columns].reshape(units, SPLIT)
            part = jnp.dot(act_ref[...], weight, preferred_element_type=f32)
            dst[:, :, :, :, columns] = part.astype(low).reshape(2, 2, 2, rows, SPLIT)

        tiles(width, body)

    def up_back(chunk, side):
        here = pl.ds(row_at(chunk, side), half_rows)

        def body(at, columns):
            grad = lax.dot_general(
                flat(all_m, chunk, side), w2_all[at], NT, preferred_element_type=f32
            )
            grad = (grad * gelu_slope(up_ref[here, columns])).astype(low)
            dup_ref[:, columns] = grad
            grad = grad.astype(f32)
            gb1_ref[0:1, columns] += jnp.sum(grad, 0, keepdims=True)
            dup_t[columns, here] = grad.T.astype(low)

        tiles(units, body)

    def down_back(dst):
        def body(at, columns):
            weight = w1_all[at // 4, pl.ds(at % 4 * 4, 4)].reshape(SPLIT, units)
            part = lax.dot_general(dup_ref[...], weight, NT, preferred_element_type=f32)
            dst[:, :, :, :, columns] = part.astype(low).reshape(2, 2, 2, rows, SPLIT)

        tiles(width, body)

    def out_back(chunk, side):
        weight = wo_all[core].reshape(HEAD_DIM, width)
        grad = lax.dot_general(flat(all_h, chunk, side), weight, NT, preferred_element_type=f32)
        grad = grad.astype(low)
        for slot, place in enumerate(pieces(chunk, side)):
            dout_ref[pl.ds(pl.multiple_of(group * HALO + place, rows), rows), :] = grad[
                slot * rows : (slot + 1) * rows
            ]

    def keep(chunk):
        def finish(row, columns, total):
            res_ref[pl.ds(pl.multiple_of(chunk * rows + row, 32), 32), columns] = total

        return finish

    def row_sets(chunk, body):
        def step(index, carry):
            row = pl.multiple_of(index * 16, 16)
            body(pl.ds(pl.multiple_of(chunk * rows + row, 16), 16), pl.ds(row, 16))
            return carry

        lax.fori_loop(0, rows // 16, step, 0)

    def normal(res):
        res = res - jnp.mean(res, -1, keepdims=True)
        scale = lax.rsqrt(jnp.mean(res * res, -1, keepdims=True) + norm_eps)
        return res * scale, scale

    def normal_back(grad, res, gain, scale, at):
        vecg_ref[at + 2 : at + 3, :] += jnp.sum(grad, 0, keepdims=True)
        vecg_ref[at + 1 : at + 2, :] += jnp.sum(grad * res, 0, keepdims=True)
        grad = grad * gain
        first = jnp.mean(grad, -1, keepdims=True)
        second = jnp.mean(grad * res, -1, keepdims=True)
        grad = (grad - first - res * second) * scale
        grad_low = grad.astype(low)
        vecg_ref[at : at + 1, :] += jnp.sum(grad_low.astype(f32), 0, keepdims=True)
        return grad, grad_low

    def norm_one(chunk):
        def body(at, place):
            res, scale = normal(tok_ref[at, :].astype(f32) + res_ref[at, :] + bo)
            norm_ref[at, :] = res
            scale_ref[at, :] = jnp.broadcast_to(scale, (16, 128))
            hidden = res * gain_one + shift_one
            hid_ref[at, :] = hidden
            all_h[(chunk,) + own_slot + (place, slice(None))] = hidden.astype(low)

        row_sets(chunk, body)

    def norm_two(chunk):
        def body(at, place):
            res, scale = normal(hid_ref[at, :] + res_ref[at, :] + b2)
            out_ref[at, :] = (res * gain_two + shift_two).astype(low)
            grad, grad_low = normal_back(cot_ref[at, :].astype(f32), res, gain_two, scale, 0)
            dres_ref[at, :] = grad
            all_m[(chunk,) + own_slot + (place, slice(None))] = grad_low

        row_sets(chunk, body)

    def norm_one_back(chunk):
        def body(at, place):
            grad, grad_low = normal_back(
                dres_ref[at, :] + res_ref[at, :], norm_ref[at, :], gain_one,
                scale_ref[at, 0:1], 3,
            )
            dres_ref[at, :] = grad
            all_h[(chunk,) + own_slot + (place, slice(None))] = grad_low

        row_sets(chunk, body)

    def flow(chunk):
        incoming = (in_one.at[chunk], in_two.at[chunk], in_three.at[chunk])
        own, other = own_part.at[chunk], far_part.at[chunk % 2]
        arrived = pair_in.at[chunk]
        branch_part(chunk, 1 - core, other)
        share = net.share(other, arrived, 1, chunk)
        branch_part(chunk, core, own)
        yield
        yield from net.scatter(own, arrived, incoming, share, 1, chunk, keep(chunk))
        norm_one(chunk)
        share = yield from net.gather(all_h.at[chunk], 2, chunk)
        if chunk == 0:
            far_w1.wait()
        upward(chunk, core)
        if chunk == 0:
            for copy in far_w2:
                copy.wait()
        downward(own)
        yield
        share.wait()
        spills[1, chunk] = spill(all_h, h_all, chunk, 1)
        upward(chunk, 1 - core)
        downward(other)
        share = net.share(other, arrived, 3, chunk)
        yield
        yield from net.scatter(own, arrived, incoming, share, 3, chunk, keep(chunk))
        norm_two(chunk)
        spills[1, chunk].wait()
        share = yield from net.gather(all_m.at[chunk], 4, chunk)
        up_back(chunk, core)
        down_back(own)
        yield
        share.wait()
        up_back(chunk, 1 - core)
        down_back(other)
        share = net.share(other, arrived, 5, chunk)
        state["backs"] += 1
        yield
        yield from net.scatter(own, arrived, incoming, share, 5, chunk, keep(chunk))
        norm_one_back(chunk)
        share = yield from net.gather(all_h.at[chunk], 6, chunk)
        out_back(chunk, core)
        yield
        share.wait()
        out_back(chunk, 1 - core)

    def product(left_t, right, columns):
        total = None
        for chunk in range(CHUNKS):
            for side in range(2):
                here = slice((chunk * 2 + side) * half_rows, (chunk * 2 + side + 1) * half_rows)
                term = jnp.dot(
                    left_t[:, here], flat(right, chunk, side, columns), preferred_element_type=f32
                )
                total = term if total is None else total + term
        return total

    def run(first, last, write):
        def step(at, carry):
            write(at, at % 2, at >= 2)
            return carry

        lax.fori_loop(first, last, step, 0)

    def emit(src, dst, sem, again):
        copy = pltpu.make_async_copy(src, dst, sem)

        @pl.when(again)
        def _():
            copy.wait()

        return copy

    def columns_at(at):
        return pl.ds(pl.multiple_of(at * SPLIT, SPLIT), SPLIT)

    def write_w2(at, slot, again):
        own = emit(stage_ref.at[slot], gw2_own.at[:, columns_at(at)], out_sems.at[0, slot], again)
        there = emit(stage_low.at[slot], gw2_far.at[:, columns_at(at)], out_sems.at[1, slot], again)
        total = product(act_t, all_m, columns_at(at))
        first = group == 0
        stage_ref[slot] = jnp.where(first, total[:256], total[256:])
        stage_low[slot] = jnp.where(first, total[256:], total[:256]).astype(low)
        own.start()
        there.start()

    def write_w1(first):
        def write(at, slot, again):
            tile = first + at
            here = gw1_ref.at[pl.ds(pl.multiple_of(tile * 4, 4), 4)]
            copy = emit(stage_w1.at[slot], here, out_sems.at[2, slot], again)
            total = product(dup_t, all_m, columns_at(tile)).T.astype(low)
            stage_w1[slot] = total.reshape(4, SPLIT // 4, units)
            copy.start()

        return write

    def write_wo(at, slot, again):
        own = emit(stage_ref.at[slot, 0:HEAD_DIM, :], gwo_ref.at[:, columns_at(at)], out_sems.at[4, slot], again)
        stage_ref[slot, 0:HEAD_DIM, :] = product(att_t, all_h, columns_at(at))
        own.start()

    def fill():
        while state["backs"] < CHUNKS:
            yield
        run(0, width // SPLIT // 2, write_w2)
        yield
        run(width // SPLIT // 2, width // SPLIT, write_w2)
        for slot in range(2):
            emit(stage_ref.at[slot], gw2_own.at[:, columns_at(0)], out_sems.at[0, slot], True)
            emit(stage_low.at[slot], gw2_far.at[:, columns_at(0)], out_sems.at[1, slot], True)
        swaps.append(far(gw2_far, gw2_in, 10))
        back = [pltpu.make_async_copy(h_all.at[at], all_m.at[at], spill_sems.at[2, at]) for at in range(CHUNKS)]
        for copy in back:
            copy.start()
        yield
        for copy in back:
            copy.wait()
        run(0, width // SPLIT // 2, write_w1((1 - group) * 4))
        for slot in range(2):
            emit(stage_w1.at[slot], gw1_ref.at[pl.ds(0, 4)], out_sems.at[2, slot], True)
        yield
        run(0, width // SPLIT // 2, write_w1(group * 4))
        for slot in range(2):
            emit(stage_w1.at[slot], gw1_ref.at[pl.ds(0, 4)], out_sems.at[2, slot], True)

    swaps = []
    step_through([flow(chunk) for chunk in range(CHUNKS)], fill())
    query = pl.ds(0, HEAD_DIM)
    far_query = far(qkv_ref.at[halo_src, query], qkv_ref.at[halo_dst, query], 12)
    dout_src = pl.ds(pl.multiple_of(near_edge, 32), REACH)
    dout_dst = pl.ds(pl.multiple_of(far_edge, 32), REACH)
    far_dout = far(dout_ref.at[dout_src, :], dout_ref.at[dout_dst, :], 9)
    run(0, width // SPLIT, write_wo)
    for slot in range(2):
        emit(stage_ref.at[slot, 0:HEAD_DIM, :], gwo_ref.at[:, columns_at(0)], out_sems.at[4, slot], True)
    far_dout.wait()
    far_query.wait()
    for copy in swaps:
        copy.wait()


def layer(tokens, cotangent, wq, wk, wv, w1, w2, wo, vector, lengths):
    f32, bf16 = jnp.float32, jnp.bfloat16
    block, width = tokens.shape
    rows = block // CHUNKS
    unit_rows = w2.shape[0]
    units = 2 * unit_rows
    half_rows = rows * GROUP // 2
    own_rows = GROUP * block
    weight_rows = wo.shape[0]
    peers = GROUP - 1
    vmem = pl.BlockSpec(memory_space=pltpu.VMEM)
    anywhere = pl.BlockSpec(memory_space=pl.ANY)
    smem = pl.BlockSpec(memory_space=pltpu.SMEM)
    sems = pltpu.SemaphoreType.DMA
    shape = jax.ShapeDtypeStruct

    def slots(*lead):
        return pltpu.VMEM(lead + (rows, width), bf16)

    return pl.pallas_call(
        layer_kernel,
        out_shape=[
            shape((block, width), bf16),
            shape((block, width), f32),
            shape((8, width), f32),
            shape((8, units), f32),
            shape((unit_rows, width), f32),
            shape((unit_rows, width), bf16),
            shape((unit_rows, width), bf16),
            shape((2 * GROUP, weight_rows, units), bf16),
            shape((HEAD_DIM, width), f32),
            shape((CHUNKS, 2, 2, 2, 2, rows, width), bf16),
            shape((CHUNKS, 2, 2, 2, 2, rows, width), bf16),
            shape((own_rows + HALO + 2 * PAD, 3 * HEAD_DIM), bf16),
            shape((own_rows + HALO, HEAD_DIM), bf16),
            shape((2, GROUP, weight_rows, 3 * HEAD_DIM), bf16),
        ],
        in_specs=[vmem] * 2 + [anywhere] * 6 + [vmem, smem],
        out_specs=[vmem] * 4 + [anywhere] * 7 + [vmem] * 3,
        scratch_shapes=[
            slots(CHUNKS, 2, 2, 2, 2), slots(CHUNKS, 2, 2, 2, 2),
            slots(CHUNKS, 2, 2, 2), slots(2, 2, 2, 2), slots(CHUNKS, 2, 2, 2),
            slots(CHUNKS, 2, 2), slots(CHUNKS, 2), slots(CHUNKS),
            pltpu.VMEM((own_rows, units), f32),
            pltpu.VMEM((half_rows, units), bf16),
            pltpu.VMEM((units, own_rows), bf16),
            pltpu.VMEM((half_rows, units), bf16),
            pltpu.VMEM((units, own_rows), bf16),
            pltpu.VMEM((own_rows, HEAD_DIM), bf16),
            pltpu.VMEM((HEAD_DIM, own_rows), bf16),
            pltpu.VMEM((block, width), f32),
            pltpu.VMEM((block, width), f32),
            pltpu.VMEM((block, width), f32),
            pltpu.VMEM((block, 128), f32),
            pltpu.VMEM((2, GROUP, weight_rows, units), bf16),
            pltpu.VMEM((2, unit_rows, width), bf16),
            pltpu.VMEM((2, 2, weight_rows, width), bf16),
            pltpu.VMEM((2, GROUP, 8, 128), f32),
            pltpu.VMEM((8, width), f32),
            pltpu.VMEM((8, width), f32),
            pltpu.VMEM((8, units), f32),
            pltpu.VMEM((2, SPLIT, SPLIT), f32),
            pltpu.VMEM((2, SPLIT, SPLIT), bf16),
            pltpu.VMEM((2, 4, SPLIT // 4, units), bf16),
            pltpu.VMEM((1, own_rows + HALO), f32),
            pltpu.VMEM((1, own_rows + HALO + 2 * PAD), f32),
            sems((STAGES, CHUNKS, 4, 3)), sems((STAGES, CHUNKS, 4, 3)),
            sems((STAGES, CHUNKS)), sems((STAGES, CHUNKS)),
            sems((5,)), sems((5, peers)), sems((5, peers)),
            sems((peers,)), sems((peers,)),
            sems((13,)), sems((13,)), sems((3,)), sems((5, 2)), sems((3, CHUNKS)),
        ],
        compiler_params=pltpu.CompilerParams(
            collective_id=4, has_side_effects=True, vmem_limit_bytes=63 << 20
        ),
        name="layer",
    )(tokens, cotangent, wq, wk, wv, w1, w2, wo, vector, lengths)


def tail_kernel(
    qkv_ref, dout_ref, wqkv_ref, dres_ref, gwo_ref, vecg_ref, gb1_ref, lengths_ref,
    x_all, gw1_ref, w2_own, w2_early,
    input_ref, out_q, out_k, out_v, out_wo, out_w1, out_w2, vec_ref,
    xs_ref, own_part, far_part, pair_in, in_one, in_two, in_three, res_ref,
    dqkv_ref, dk_sum, dv_sum, dqkv_t, gq_own, gq_far, gq_here, gq_there,
    w1_here, w1_there, w2_sum, w2_in, wo_low, wo_in, wo_pair, wo_pair_in,
    blocks_ref, arrived, theirs, far_vec_in,
    queries_ref, keys_ref,
    hop_send, hop_recv, pair_send, pair_recv, load_sems,
    block_local, block_send, block_recv, there_send, there_recv, far_send, far_recv,
):
    f32, low = jnp.float32, qkv_ref.dtype
    block, width = dres_ref.shape
    rows = block // TAIL_CHUNKS
    weight_rows = out_q.shape[0]
    scale = HEAD_DIM ** (-0.5)
    group, base, mine, others, across, there = group_places()
    net = Traffic((hop_send, hop_recv, pair_send, pair_recv), TAIL_PLANS)
    core, chip = net.core, mine // 2
    enter(others + there)

    def far(src, dst, at, device=across):
        copy = push(src, dst, far_send.at[at], far_recv.at[at], device)
        copy.start()
        return copy

    def load(src, dst, at):
        copy = pltpu.make_async_copy(src, dst, load_sems.at[at])
        copy.start()
        return copy

    far_wo = push(
        wo_low, wo_in, far_send.at[0], far_recv.at[0], core * GROUP + 2 * chip + core
    )

    @pl.when(core != group)
    def _():
        wo_low[...] = gwo_ref[...].astype(low)
        far_wo.start()

    def blocks(pairs, at):
        here = slice(at, at + len(pairs))
        return exchange_blocks(
            pairs, (block_local.at[here], block_send.at[here], block_recv.at[here]),
            base, mine, others,
        )

    first = pl.ds(pl.multiple_of((1 - group) * GROUP, GROUP), GROUP)
    w1_far = far_blocks(
        gw1_ref.at[first], w1_there, there_send.at[0], there_recv.at[0], group, mine
    )
    own_first = pl.ds(pl.multiple_of(group * GROUP, GROUP), GROUP)
    w1_blocks = blocks([(gw1_ref.at[own_first], w1_here)], 1)
    x_loads = [load(x_all.at[at], xs_ref.at[at], at) for at in range(CHUNKS)]
    loads = [
        load(w2_own, w2_sum, CHUNKS),
        load(w2_early, w2_in, CHUNKS + 1),
    ]
    own_rows = GROUP * block
    write_segments(lengths_ref, group * (own_rows - HALO), keys_ref, queries_ref)
    dk_sum[...] = jnp.zeros_like(dk_sum)
    dv_sum[...] = jnp.zeros_like(dv_sum)

    def attend_back_tile(tile):
        place = pl.multiple_of(tile * TILE, TILE)
        window = pl.ds(place, WINDOW)
        queries, keys, probs = tile_probs(qkv_ref, queries_ref, keys_ref, tile)
        values = qkv_ref[window, 2 * HEAD_DIM : 3 * HEAD_DIM]
        grads = dout_ref[pl.ds(place, TILE), :]
        grad_probs = lax.dot_general(grads, values, NT, preferred_element_type=f32)
        inner = jnp.sum(probs * grad_probs, -1, keepdims=True)
        grad_scores = (probs * (grad_probs - inner)).astype(low)
        grad_q = jnp.dot(grad_scores, keys, preferred_element_type=f32)
        dqkv_ref[pl.ds(place, TILE), 0:HEAD_DIM] = (grad_q * scale).astype(low)
        dk_sum[window, :] += lax.dot_general(grad_scores, queries, TN, preferred_element_type=f32)
        dv_sum[window, :] += lax.dot_general(
            probs.astype(low), grads, TN, preferred_element_type=f32
        )

    def attend_back_two(at, carry):
        attend_back_tile(2 * at)
        attend_back_tile(2 * at + 1)
        return carry

    ext_rows = dout_ref.shape[0]
    lax.fori_loop(0, ext_rows // TILE // 2, attend_back_two, 0)
    inside = slice(PAD, PAD + ext_rows)
    dqkv_ref[:, HEAD_DIM : 2 * HEAD_DIM] = (dk_sum[inside, :] * scale).astype(low)
    dqkv_ref[:, 2 * HEAD_DIM : 3 * HEAD_DIM] = dv_sum[inside, :].astype(low)

    def rows_of(chunk, side, rows):
        places = [
            group * HALO + (slot * 2 + side) * block + chunk * rows for slot in range(GROUP // 2)
        ]
        return jnp.concatenate(
            [dqkv_ref[pl.ds(pl.multiple_of(place, rows), rows), :] for place in places], 0
        )

    x_rows = block // CHUNKS
    x_half = x_rows * GROUP // 2
    bias = jnp.zeros((1, 3 * HEAD_DIM), f32)
    for chunk in range(CHUNKS):
        for side in range(2):
            part = rows_of(chunk, side, x_rows).astype(f32)
            bias = bias + jnp.sum(part, 0, keepdims=True)
            here = slice((chunk * 2 + side) * x_half, (chunk * 2 + side + 1) * x_half)
            dqkv_t[:, here] = part.T.astype(low)

    for copy in x_loads:
        copy.wait()

    def product(at):
        columns = pl.ds(pl.multiple_of(at * SPLIT, SPLIT), SPLIT)
        total = None
        for chunk in range(CHUNKS):
            for side in range(2):
                here = slice((chunk * 2 + side) * x_half, (chunk * 2 + side + 1) * x_half)
                right = xs_ref[chunk, side, :, :, :, :, columns].reshape(x_half, SPLIT)
                term = jnp.dot(dqkv_t[:, here], right, preferred_element_type=f32)
                total = term if total is None else total + term
        return total.T

    quarter = width // SPLIT // 2

    def tile_of(ref, first):
        def body(at, carry):
            total = product(first + at).astype(low)
            ref[pl.ds(pl.multiple_of(at * 4, 4), 4)] = total.reshape(4, SPLIT // 4, 3 * HEAD_DIM)
            return carry

        lax.fori_loop(0, quarter, body, 0)

    tile_of(gq_far, (1 - group) * quarter)
    qkv_far = far_blocks(gq_far, gq_there, there_send.at[1], there_recv.at[1], group, mine)

    blocks_ref[...] = jnp.zeros_like(blocks_ref)
    lane = lax.broadcasted_iota(jnp.int32, (1, 128), 1)

    def pieces_of(low_row, high_row):
        return (
            jnp.where(lane < 64, low_row, pltpu.roll(high_row, 64, 1)),
            jnp.where(lane < 64, pltpu.roll(low_row, 64, 1), high_row),
        )

    for tile in range(GROUP):
        here = slice(tile * 128, tile * 128 + 128)
        for at, (low_row, high_row) in enumerate(((3, 4), (5, 0), (1, 2))):
            to = tile // 8 * 8 + 1 + at
            both = pieces_of(vecg_ref[low_row : low_row + 1, here], vecg_ref[high_row : high_row + 1, here])
            for odd in range(2):
                blocks_ref[tile % 8 * 2 + odd, to : to + 1, :] = both[odd]
    for half in range(2):
        for part in range(2):
            to = half * 8 + 4 + part
            here = slice((half * 2 + part) * 128, (half * 2 + part + 1) * 128)
            blocks_ref[mine, to : to + 1, :] = gb1_ref[0:1, here]
    bias_q, bias_v = bias[:, 0:HEAD_DIM], bias[:, 2 * HEAD_DIM : 3 * HEAD_DIM]
    both = pieces_of(bias_q, bias_v)
    for odd in range(2):
        blocks_ref[2 * chip + odd, pl.ds(core * 8, 1), :] = both[odd]

    vec_blocks = blocks([(blocks_ref, arrived)], 0)

    def input_part(chunk, side, dst):
        left = rows_of(chunk, side, rows)

        def body(at, carry):
            weight = wqkv_ref[at // 4, pl.ds(at % 4 * 4, 4)].reshape(SPLIT, 3 * HEAD_DIM)
            part = lax.dot_general(left, weight, NT, preferred_element_type=f32)
            columns = pl.ds(pl.multiple_of(at * SPLIT, SPLIT), SPLIT)
            dst[:, :, :, :, columns] = part.astype(low).reshape(2, 2, 2, rows, SPLIT)
            return carry

        lax.fori_loop(0, width // SPLIT, body, 0)

    def flow(chunk):
        def finish(row, columns, total):
            res_ref[pl.ds(pl.multiple_of(chunk * rows + row, 32), 32), columns] = total

        incoming = (in_one.at[chunk], in_two.at[chunk], in_three.at[chunk])
        other = far_part.at[chunk % 2]
        input_part(chunk, 1 - core, other)
        share = net.share(other, pair_in.at[chunk], 0, chunk)
        input_part(chunk, core, own_part.at[chunk])
        yield
        yield from net.scatter(
            own_part.at[chunk], pair_in.at[chunk], incoming, share, 0, chunk, finish
        )
        here = slice(chunk * rows, (chunk + 1) * rows)
        input_ref[here, :] = (dres_ref[here, :] + res_ref[here, :]).astype(low)

    def fill():
        yield
        yield
        for copy in loads:
            copy.wait()
        out_w2[...] = w2_sum[...] + w2_in[...].astype(f32)
        yield
        tile_of(gq_own, group * quarter)
        state["qkv"] = blocks([(gq_own, gq_here)], 2)
        yield
        for copy in vec_blocks:
            copy.wait()
        total = arrived[0]
        for at in range(1, GROUP):
            total = total + arrived[at]
        first, second = total[:8], total[8:]
        theirs[...] = jnp.where(group == 0, second, first)
        vec_ref[...] = jnp.where(group == 0, first, second)
        state["vec"] = far(theirs, far_vec_in, 3)

    state = {}
    step_through([flow(chunk) for chunk in range(TAIL_CHUNKS)], fill())

    share_wo = push(wo_pair, wo_pair_in, far_send.at[4], far_recv.at[4], net.pair)

    @pl.when(core == group)
    def _():
        far_wo.wait_recv()
        total = gwo_ref[...] + wo_in[...].astype(f32)
        first, second = total[:weight_rows], total[weight_rows:]
        out_wo[...] = jnp.where(core == 0, first, second)
        wo_pair[...] = jnp.where(core == 0, second, first)
        share_wo.start()

    state["vec"].wait()
    vec_ref[...] += far_vec_in[...]

    @pl.when(core != group)
    def _():
        far_wo.wait_send()
        share_wo.wait_recv()
        out_wo[...] = wo_pair_in[...]

    @pl.when(core == group)
    def _():
        share_wo.wait_send()

    for copy in w1_blocks + w1_far:
        copy.wait()
    unit_rows = out_w2.shape[0]
    for at in range(GROUP):
        for part in range(2):
            here = slice(part * unit_rows, (part + 1) * unit_rows)
            to = (part * GROUP + at) * unit_rows
            out_w1[:, to : to + unit_rows] = w1_here[at, :, here].astype(f32) + w1_there[
                at, :, here
            ].astype(f32)
    for copy in state["qkv"] + qkv_far:
        copy.wait()
    for at in range(GROUP):
        to = (at % 2 * 8 + at // 2) * HEAD_DIM
        for part, ref in enumerate((out_q, out_k, out_v)):
            here = slice(part * HEAD_DIM, (part + 1) * HEAD_DIM)
            ref[:, to : to + HEAD_DIM] = gq_here[at, :, here].astype(f32) + gq_there[
                at, :, here
            ].astype(f32)


def layer_tail(
    qkv, dout, wqkv, dres, gwo, vecg, gb1, lengths, x_all, gw1, w2_own, w2_early
):
    f32, bf16 = jnp.float32, jnp.bfloat16
    block, width = dres.shape
    rows = block // TAIL_CHUNKS
    weight_rows = wqkv.shape[2]
    units = gw1.shape[2]
    unit_rows = units // 2
    own_rows = GROUP * block
    peers = GROUP - 1
    vmem = pl.BlockSpec(memory_space=pltpu.VMEM)
    anywhere = pl.BlockSpec(memory_space=pl.ANY)
    smem = pl.BlockSpec(memory_space=pltpu.SMEM)
    sems = pltpu.SemaphoreType.DMA
    shape, scratch = jax.ShapeDtypeStruct, pltpu.VMEM
    heads = 3 * HEAD_DIM

    def slots(*lead):
        return scratch(lead + (rows, width), bf16)

    return pl.pallas_call(
        tail_kernel,
        out_shape=[
            shape((block, width), bf16),
            shape((weight_rows, width), f32),
            shape((weight_rows, width), f32),
            shape((weight_rows, width), f32),
            shape((weight_rows, width), f32),
            shape((weight_rows, GROUP * units), f32),
            shape((unit_rows, width), f32),
            shape((8, 128), f32),
        ],
        in_specs=[vmem] * 7 + [smem] + [anywhere] * 4,
        out_specs=[vmem] * 8,
        scratch_shapes=[
            scratch(x_all.shape, bf16),
            slots(TAIL_CHUNKS, 2, 2, 2), slots(2, 2, 2, 2), slots(TAIL_CHUNKS, 2, 2, 2),
            slots(TAIL_CHUNKS, 2, 2), slots(TAIL_CHUNKS, 2), slots(TAIL_CHUNKS),
            scratch((block, width), f32),
            scratch((own_rows + HALO, heads), bf16),
            scratch(qkv.shape[:1] + (HEAD_DIM,), f32),
            scratch(qkv.shape[:1] + (HEAD_DIM,), f32),
            scratch((heads, own_rows), bf16),
            scratch((GROUP, weight_rows, heads), bf16),
            scratch((GROUP, weight_rows, heads), bf16),
            scratch((GROUP, weight_rows, heads), bf16),
            scratch((GROUP, weight_rows, heads), bf16),
            scratch((GROUP, weight_rows, units), bf16),
            scratch((GROUP, weight_rows, units), bf16),
            scratch((unit_rows, width), f32),
            scratch((unit_rows, width), bf16),
            scratch((HEAD_DIM, width), bf16),
            scratch((HEAD_DIM, width), bf16),
            scratch((weight_rows, width), f32),
            scratch((weight_rows, width), f32),
            scratch((GROUP, 16, 128), f32),
            scratch((GROUP, 16, 128), f32),
            scratch((8, 128), f32),
            scratch((8, 128), f32),
            pltpu.VMEM((1, own_rows + HALO), f32),
            pltpu.VMEM((1, own_rows + HALO + 2 * PAD), f32),
            sems((1, TAIL_CHUNKS, 4, 3)), sems((1, TAIL_CHUNKS, 4, 3)),
            sems((1, TAIL_CHUNKS)), sems((1, TAIL_CHUNKS)),
            sems((CHUNKS + 2,)), sems((3,)), sems((3, peers)), sems((3, peers)),
            sems((2, GROUP)), sems((2, GROUP)), sems((5,)), sems((5,)),
        ],
        compiler_params=pltpu.CompilerParams(
            collective_id=5, has_side_effects=True, vmem_limit_bytes=63 << 20
        ),
        name="layer_tail",
    )(qkv, dout, wqkv, dres, gwo, vecg, gb1, lengths, x_all, gw1, w2_own, w2_early)


def grouped_device(
    tokens,
    cotangent,
    lengths,
    wq,
    bq,
    wk,
    wv,
    bv,
    wo,
    bo,
    norm1_gain,
    norm1_bias,
    w1,
    b1,
    w2,
    b2,
    norm2_gain,
    norm2_bias,
):
    f32 = jnp.float32
    vectors = [bq, bv, bo, norm1_gain, norm1_bias, b2, norm2_gain, norm2_bias, b1]
    sizes = [item.shape[0] for item in vectors]
    vector, at = jnp.zeros((1024,), f32), 0
    for item, size in zip(vectors, sizes):
        vector = vector + jnp.pad(item.astype(f32), (at, 1024 - at - size))
        at += size
    vector = vector.reshape(8, 128)

    (
        output, grad_resid_one, vec_grads, grad_b1, w2_own, _, w2_early, grad_w1, grad_wo,
        all_tokens, _, qkv, grad_out, full_qkv,
    ) = layer(tokens, cotangent, wq, wk, wv, w1, w2, wo, vector, lengths)

    input_grad, out_q, out_k, out_v, out_wo, out_w1, out_w2, sums = layer_tail(
        qkv, grad_out, full_qkv, grad_resid_one, grad_wo, vec_grads, grad_b1, lengths,
        all_tokens, grad_w1, w2_own, w2_early,
    )
    sums, at = sums.reshape(-1), 0
    small = []
    for size in sizes:
        small.append(sums[at : at + size])
        at += size
    out_bq, out_bv, out_bo, out_g1, out_s1, out_b2, out_g2, out_s2, out_b1 = small
    return (
        output, input_grad, out_q, out_bq, out_k, out_v, out_bv, out_wo, out_bo, out_g1, out_s1,
        out_w1, out_b1, out_w2, out_b2, out_g2, out_s2,
    )


def solution(mesh):
    in_specs = (
        P("dp", None),
        P("dp", None),
        P(),
        P("dp", None),
        P("dp"),
        P("dp", None),
        P("dp", None),
        P("dp"),
        P("dp", None),
        P("dp"),
        P("dp"),
        P("dp"),
        P("dp", None),
        P("dp"),
        P("dp", None),
        P("dp"),
        P("dp"),
        P("dp"),
    )
    out_specs = (
        P("dp", None),
        P("dp", None),
        P("dp", None),
        P("dp"),
        P("dp", None),
        P("dp", None),
        P("dp"),
        P("dp", None),
        P("dp"),
        P("dp"),
        P("dp"),
        P("dp", None),
        P("dp"),
        P("dp", None),
        P("dp"),
        P("dp"),
        P("dp"),
    )
    two_groups = mesh.shape["dp"] == 2 * GROUP
    return jax.shard_map(
        grouped_device if two_groups else per_device, mesh=mesh, in_specs=in_specs, out_specs=out_specs, check_vma=False
    )
```
